32 devices in a mesh: ctx: 8 (over z, y), fsdp: 4 (over x, core).
Axes of the slice: x: 2, y: 2, z: 4, core: 2. Of those that a mesh axis runs over, the one named last changes fastest.
Arguments:
- byte_ids: int32 [16, 2048], P('fsdp', 'ctx'), may hold values from 0 to 258
- doc_ids: int32 [16, 2048], P('fsdp', 'ctx'), may hold values from 0 to 4, never falling along the last dimension, each value on 1 to 1024 neighbouring positions
- rel_bucket: int32 [2047], replicated, may hold values from 0 to 31
- table: float32 [259, 768], replicated, may hold values from -6 to 6
- conv_w: float32 [4, 768], replicated, may hold values from -3 to 3
- score_w: float32 [768], replicated, may hold values from -0.4375 to 0.4375
- gain_one: float32 [768], replicated, may hold values from 0.1 to 1.9
- gain_two: float32 [768], replicated, may hold values from 0.1 to 1.9
- rel_bias: float32 [32, 12], replicated, may hold values from -4 to 4
- query_master: float32 [768, 768], P('fsdp'), may hold values from -0.078125 to 0.078125
- key_master: float32 [768, 768], P('fsdp'), may hold values from -0.078125 to 0.078125
- value_master: float32 [768, 768], P('fsdp'), may hold values from -0.21875 to 0.21875
- out_master: float32 [768, 768], P('fsdp'), may hold values from -2.5 to 2.5
- gate_master: float32 [768, 2048], P('fsdp'), may hold values from -0.21875 to 0.21875
- up_master: float32 [768, 2048], P('fsdp'), may hold values from -0.21875 to 0.21875
- down_master: float32 [2048, 768], P('fsdp'), may hold values from -0.1875 to 0.1875
- out_cotangent: bfloat16 [1024, 16, 768], P('ctx', 'fsdp'), may hold values from -6 to 6
Outputs:
- output: bfloat16 [1024, 16, 768], P('ctx', 'fsdp')
- grad_table: float32 [259, 768], replicated
- grad_conv: float32 [4, 768], replicated
- grad_score: float32 [768], replicated
- grad_gain_one: float32 [768], replicated
- grad_gain_two: float32 [768], replicated
- grad_rel_bias: float32 [32, 12], replicated
- grad_query: float32 [768, 768], P('fsdp')
- grad_key: float32 [768, 768], P('fsdp')
- grad_value: float32 [768, 768], P('fsdp')
- grad_out_proj: float32 [768, 768], P('fsdp')
- grad_gate: float32 [768, 2048], P('fsdp')
- grad_up: float32 [768, 2048], P('fsdp')
- grad_down: float32 [2048, 768], P('fsdp')
The draws below stay inside these ranges and needn't reach their ends.
Inputs may be any that keep to these rules, and one draw needn't show every extreme that they name: `doc_ids`: along each sequence the document numbers never fall, so each document is one run of bytes.
All inputs are finite; a program needn't handle non-finite values.
Results may differ from the reference program's by a relative error of at most 0.02.
Values may be sent and summed in bfloat16 or wider, within the bound.
No kernel may reach another device: no remote copies, remote signals or barrier semaphores. Data moves between devices by JAX's collectives and lax.ppermute only.
A program may use at most 256 MiB of HBM per device.

```python
import math
import jax
import jax.numpy as jnp
import numpy as np
from jax import lax

D = 768
FF = 2048
H = 12
DH = 64
VOCAB = 259
NB = 32
L = 2048
T_SEQ = 1024
NSEQ = 16


def plant(drawn, own_key, low, largest):
    longest = drawn.shape.index(max(drawn.shape))
    spots = []
    for shift in (0, 1):
        where = [jax.random.randint(jax.random.fold_in(own_key, axis), (), 0, length) for axis, length in enumerate(drawn.shape)]
        where[longest] = (where[longest] + shift) % drawn.shape[longest]
        spots.append(tuple(where))
    return drawn.at[spots[0]].set(low).at[spots[1]].set(largest)


def steps_of(own_key, dims, cuts, least, high):
    gain = 1.0
    for dim, blocks in cuts:
        steps = jax.random.uniform(jax.random.fold_in(jax.random.fold_in(own_key, 6), dim), (blocks,), jnp.float32, least / len(cuts), high / len(cuts))
        gain = gain * jnp.repeat(jnp.exp(steps), dims[dim] // blocks).reshape((-1,) + (1,) * (len(dims) - 1 - dim))
    return gain


def rank_bounds(number_of, lean):
    weights = [(1 << 20) // math.isqrt(standing ** lean) + 1 for standing in range(1, number_of + 1)]
    scale = 1 + sum(weights) // (1 << 30)
    return np.cumsum(np.array([max(1, weight // scale) for weight in weights]))


def ranked_ids(rng, dims, count, lean):
    listing = rank_bounds(count, lean)
    ticket = jax.random.randint(jax.random.fold_in(rng, 1), dims, 0, int(listing[count - 1]))
    grade = jnp.searchsorted(jnp.asarray(listing, jnp.int32), ticket, side="right")
    return jax.random.permutation(jax.random.fold_in(rng, 2), count)[grade].astype(jnp.int32)


def length_profile(amount, total, limit, slope):
    loads = [(1 << 20) // math.isqrt(rank ** slope) + 1 for rank in range(2, amount + 1)]
    rest, holding = total - limit - (amount - 1), [1] * (amount - 1)
    while rest > 0:
        movable = [i for i in range(amount - 1) if holding[i] < limit]
        mass, remaining = sum([loads[i] for i in movable]), rest
        for i in movable:
            extra = min(limit - holding[i], max(1, remaining * loads[i] // mass), rest)
            holding[i] = holding[i] + extra
            rest = rest - extra
    return np.array([limit] + holding)


def ragged(key, count, total, most, skew):
    if count == 2:
        one = jax.random.randint(key, (), max(1, total - most), min(most, total - 1) + 1)
        return jnp.stack([one, total - one])
    sizes = jnp.asarray(length_profile(count, total, most, skew), jnp.int32)
    pairs = (count - 1) // 2
    donor, taker = sizes[1:1 + 2 * pairs:2], sizes[2:2 + 2 * pairs:2]
    margin = jnp.minimum(donor - 1, most - taker)
    moved = jax.random.randint(jax.random.fold_in(key, 1), (pairs,), 0, 1 << 20) % (margin + 1)
    sizes = sizes.at[1:1 + 2 * pairs:2].set(donor - moved).at[2:2 + 2 * pairs:2].set(taker + moved)
    return sizes[jax.random.permutation(jax.random.fold_in(key, 2), count)]


def bell_draw(rng, dims, spread, bound, cuts=(), kind=jnp.bfloat16):
    gain = steps_of(rng, dims, cuts, -0.22, 0.18) if cuts else 1.0
    entries = jax.random.normal(rng, dims, jnp.float32) * spread * gain
    return jnp.minimum(jnp.maximum(entries, -bound), bound).astype(kind)


def setup_inputs(seed: int = 0) -> dict:
    key_of = jax.random.split(jax.random.key(seed), 18)
    byte_ids = plant(ranked_ids(key_of[0], (NSEQ, L), VOCAB, 2), jax.random.fold_in(key_of[0], 3), 0, VOCAB - 1).astype(jnp.int32)
    doc_ids = jax.vmap(lambda own: jnp.searchsorted(jnp.cumsum(ragged(own, max(3, L // 512 + 1), L, min(2000, L // 2), 1)), jnp.arange(L), side="right"))(jax.random.split(key_of[1], NSEQ)).reshape((NSEQ, L)).astype(jnp.int32)
    rel_bucket = plant(jax.random.randint(key_of[2], (2 * T_SEQ - 1,), 0, NB), jax.random.fold_in(key_of[2], 1), 0, NB - 1).astype(jnp.int32)
    table = bell_draw(key_of[3], (VOCAB, D), 1.0, 6.0, (), jnp.float32)
    conv_w = bell_draw(key_of[4], (4, D), 0.5, 3.0, (), jnp.float32)
    score_w = bell_draw(key_of[5], (D,), (D // 4) ** -0.5, 0.4375, (), jnp.float32)
    gain_one = jnp.clip(1.0 + 0.18 * jax.random.normal(key_of[6], (D,), jnp.float32), 0.1, 1.9)
    gain_two = jnp.clip(1.0 + 0.18 * jax.random.normal(key_of[7], (D,), jnp.float32), 0.1, 1.9)
    rel_bias = bell_draw(key_of[8], (NB, H), 1.0, 4.0, (), jnp.float32)
    query_master = bell_draw(key_of[9], (D, H * DH), (8 * D) ** -0.5, 0.078125, ((0, 4),), jnp.float32)
    key_master = bell_draw(key_of[10], (D, H * DH), (8 * D) ** -0.5, 0.078125, ((0, 4),), jnp.float32)
    value_master = bell_draw(key_of[11], (D, H * DH), D ** -0.5, 0.21875, ((0, 4),), jnp.float32)
    out_master = bell_draw(key_of[12], (H * DH, D), (max(D // 128, 1)) ** -0.5, 2.5, ((0, 4),), jnp.float32)
    gate_master = bell_draw(key_of[13], (D, FF), D ** -0.5, 0.21875, ((0, 4),), jnp.float32)
    up_master = bell_draw(key_of[14], (D, FF), D ** -0.5, 0.21875, ((0, 4),), jnp.float32)
    down_master = bell_draw(key_of[15], (FF, D), (FF // 2) ** -0.5, 0.1875, ((0, 4),), jnp.float32)
    out_cotangent = bell_draw(key_of[16], (T_SEQ, NSEQ, D), 1.0, 6.0, ((0, 8), (1, 4)))
    return {"byte_ids": byte_ids, "doc_ids": doc_ids, "rel_bucket": rel_bucket, "table": table, "conv_w": conv_w, "score_w": score_w, "gain_one": gain_one, "gain_two": gain_two, "rel_bias": rel_bias, "query_master": query_master, "key_master": key_master, "value_master": value_master, "out_master": out_master, "gate_master": gate_master, "up_master": up_master, "down_master": down_master, "out_cotangent": out_cotangent}


@jax.custom_vjp
def low(v):
    return lax.optimization_barrier(v.astype(jnp.bfloat16)).astype(jnp.float32)

@jax.custom_vjp
def low_back(v):
    return v

def low_keep(v):
    return (low(v), None)

def low_pass(kept, grad):
    return (grad,)

def back_keep(v):
    return (v, None)

def back_low(kept, grad):
    return (low(grad),)
low.defvjp(low_keep, low_pass)
low_back.defvjp(back_keep, back_low)

def rms_scale(values, gain_vec):
    return values * lax.rsqrt(lax.optimization_barrier(jnp.mean(values * values, axis=-1, keepdims=True)) + 1e-06) * gain_vec

def matmul(left, right):
    return jnp.dot(left, right, precision=lax.Precision.HIGHEST, preferred_element_type=jnp.float32)

def forward(params, byte_row, doc_row, rel_bucket):
    table, conv_w, score_w, gain_one, gain_two, rel_bias, query_master, key_master, value_master, out_master, gate_master, up_master, down_master = params
    embedded = jnp.take(table, byte_row, axis=0)
    padded = jnp.pad(embedded, ((3, 0), (0, 0)))
    conv_out = padded[0:L] * conv_w[0]
    for offset in range(1, 4):
        conv_out = conv_out + padded[offset:offset + L] * conv_w[offset]
    extra_rows = -L % 12
    conv_ext = jnp.pad(conv_out, ((0, extra_rows), (0, 0)))
    pooled_list = []
    for width in range(1, 5):
        means = lax.optimization_barrier(jnp.mean(conv_ext.reshape(-1, width, D), axis=1))
        pooled_list.append(jnp.repeat(means, width, axis=0)[:L])
    stacked = jnp.stack(pooled_list)
    logits = jnp.einsum('bld,d->bl', stacked, score_w, precision=lax.Precision.HIGHEST)
    mixing = jax.nn.softmax(logits, axis=0)
    mixed = lax.optimization_barrier(jnp.sum(mixing[:, :, None] * stacked, axis=0))
    tokens = lax.optimization_barrier(jnp.mean(mixed.reshape(T_SEQ, 2, D), axis=1))
    norm_one = low(rms_scale(tokens, gain_one))
    query_rows = low(low_back(matmul(norm_one, low(query_master))))
    key_rows = low(low_back(matmul(norm_one, low(key_master))))
    value_rows = low(low_back(matmul(norm_one, low(value_master))))
    query4 = query_rows.reshape(T_SEQ, H, DH)
    key4 = key_rows.reshape(T_SEQ, H, DH)
    value4 = value_rows.reshape(T_SEQ, H, DH)
    token_docs = doc_row[::2]
    index_grid = (jnp.arange(T_SEQ)[None, :] - jnp.arange(T_SEQ)[:, None] + T_SEQ - 1).astype(jnp.int32)
    buckets = jnp.take(rel_bucket, index_grid)
    pos_bias = jnp.transpose(jnp.take(rel_bias, buckets, axis=0), (2, 0, 1))
    scores = jnp.einsum('qhe,khe->hqk', query4, key4, precision=lax.Precision.HIGHEST) + pos_bias
    scores = low_back(scores)
    allowed = token_docs[:, None] == token_docs[None, :]
    scores = jnp.where(allowed[None], scores, -1e+30)
    row_best = lax.optimization_barrier(jnp.max(scores, axis=-1, keepdims=True))
    weights = jnp.exp(scores - row_best)
    row_total = lax.optimization_barrier(jnp.sum(weights, axis=-1, keepdims=True))
    attended = jnp.einsum('hqk,khe->hqe', low(weights), value4, precision=lax.Precision.HIGHEST) / row_total
    attended = jnp.transpose(attended, (1, 0, 2)).reshape(T_SEQ, H * DH)
    attended = low(low_back(attended))
    branch = low_back(matmul(attended, low(out_master)))
    resid = tokens + branch
    norm_two = low(rms_scale(resid, gain_two))
    gate_pre = low_back(matmul(norm_two, low(gate_master)))
    up_pre = low_back(matmul(norm_two, low(up_master)))
    hidden = low(jax.nn.gelu(gate_pre, approximate=True) * up_pre)
    down_out = low_back(matmul(hidden, low(down_master)))
    return resid + down_out

def reference(byte_ids, doc_ids, rel_bucket, table, conv_w, score_w, gain_one, gain_two, rel_bias, query_master, key_master, value_master, out_master, gate_master, up_master, down_master, out_cotangent):
    params = (table.astype(jnp.float32), conv_w.astype(jnp.float32), score_w.astype(jnp.float32), gain_one.astype(jnp.float32), gain_two.astype(jnp.float32), rel_bias.astype(jnp.float32), query_master.astype(jnp.float32), key_master.astype(jnp.float32), value_master.astype(jnp.float32), out_master.astype(jnp.float32), gate_master.astype(jnp.float32), up_master.astype(jnp.float32), down_master.astype(jnp.float32))
    cotangent = jnp.transpose(out_cotangent.astype(jnp.float32), (1, 0, 2))

    def per_sequence(totals, inputs):
        byte_row, doc_row, cot_row = inputs

        def run_forward(param_set):
            return forward(param_set, byte_row, doc_row, rel_bucket)
        out_row, pullback = jax.vjp(run_forward, params)
        grads = pullback(cot_row)[0]
        return (jax.tree.map(jnp.add, totals, grads), out_row)
    zero_grads = jax.tree.map(jnp.zeros_like, params)
    totals, out_rows = lax.scan(per_sequence, zero_grads, (byte_ids, doc_ids, cotangent))
    output = jnp.transpose(out_rows, (1, 0, 2)).astype(jnp.bfloat16)
    return (output, totals[0], totals[1], totals[2], totals[3], totals[4], totals[5], totals[6], totals[7], totals[8], totals[9], totals[10], totals[11], totals[12])
```

```python
import functools

import jax
import jax.numpy as jnp
from jax import lax
from jax.experimental import pallas as pl
from jax.experimental.pallas import tpu as pltpu
from jax.sharding import PartitionSpec as P

f32 = jnp.float32
bf16 = jnp.bfloat16
LANE = 128
BLK = 128
VMEM_CAP = 60 * 1024 * 1024
HIGH = lax.Precision.HIGHEST
NT = (((1,), (1,)), ((), ()))
NN = (((1,), (0,)), ((), ()))


def lane_iota(rows):
    return lax.broadcasted_iota(jnp.int32, (rows, LANE), 1)


def block_sum(value, width, lane):
    def ahead(v, n):
        return pltpu.roll(v, LANE - n, 1)

    def behind(v, n):
        return pltpu.roll(v, n, 1)

    if width == 1:
        return value
    if width == 3:
        lead = value + ahead(value, 1) + ahead(value, 2)
        phase = lane % 3
        return jnp.where(phase == 0, lead, jnp.where(phase == 1, behind(lead, 1), behind(lead, 2)))
    pair = value + jnp.where(lane % 2 == 0, ahead(value, 1), behind(value, 1))
    if width == 2:
        return pair
    return pair + jnp.where(lane % 4 < 2, ahead(pair, 2), behind(pair, 2))


def pick(value, lane_index):
    return value[:, lane_index : lane_index + 1]


def byte_forward_kernel(
    total_bytes,
    ids_ref,
    hi_ref,
    lo_ref,
    conv_w_ref,
    score_ref,
    gain_ref,
    tok_ref,
    norm_ref,
    conv_ref,
    mix_ref,
    emb,
    flat,
):
    groups = conv_ref.shape[1]
    width = conv_ref.shape[2]
    tiles = width // LANE
    token_count = norm_ref.shape[0]
    vocab_pad = hi_ref.shape[0]
    ids_cols = jnp.transpose(ids_ref[...].astype(f32))
    vocab = lax.broadcasted_iota(jnp.int32, (groups, vocab_pad), 1).astype(f32)
    for r in range(15):
        onehot = (ids_cols[0:groups, r : r + 1] == vocab).astype(bf16)
        emb[r] = jnp.dot(onehot, hi_ref[...], preferred_element_type=f32) + jnp.dot(
            onehot, lo_ref[...], preferred_element_type=f32
        )
    lane = lane_iota(8)

    def chunk(i, masked):
        r0 = pl.multiple_of(i * 8, 8)
        rows = pl.ds(r0, 8)
        sums = [jnp.zeros((8, LANE), f32) for _ in range(12)]
        for tile in range(tiles):
            cols = slice(tile * LANE, (tile + 1) * LANE)
            taps = [conv_w_ref[k : k + 1, cols] for k in range(4)]
            piece = [emb[r, rows, cols] for r in range(15)]
            score = score_ref[0:1, cols]
            for r in range(12):
                value = (
                    piece[r] * taps[0]
                    + piece[r + 1] * taps[1]
                    + piece[r + 2] * taps[2]
                    + piece[r + 3] * taps[3]
                )
                if masked:
                    group = r0 + lax.broadcasted_iota(jnp.int32, (8, LANE), 0)
                    value = jnp.where(group * 12 + r < total_bytes, value, 0.0)
                conv_ref[r, rows, cols] = value
                sums[r] = sums[r] + value * score
        packed = jnp.zeros((8, LANE), f32)
        for r in range(12):
            packed = jnp.where(lane == r, jnp.sum(sums[r], axis=1, keepdims=True), packed)
        logits = [block_sum(packed, b, lane) * (1.0 / b) for b in range(1, 5)]
        best = jnp.maximum(jnp.maximum(logits[0], logits[1]), jnp.maximum(logits[2], logits[3]))
        parts = [jnp.exp(value - best) for value in logits]
        total = parts[0] + parts[1] + parts[2] + parts[3]
        mix = [part / total for part in parts]
        for b in range(4):
            mix_ref[b, rows, :] = mix[b]
        half_one = mix[0] * 0.5
        pair_two = block_sum(mix[1], 2, lane) * 0.25
        single_three = mix[2] * (1.0 / 6.0)
        pair_three = block_sum(mix[2], 2, lane) * (1.0 / 6.0)
        pair_four = block_sum(mix[3], 2, lane) * 0.125
        coef_one = [pick(half_one, r) for r in range(12)]
        coef_two = [pick(pair_two, 2 * j) for j in range(6)]
        coef_four = [pick(pair_four, 2 * j) for j in range(6)]
        coef_three = []
        for j in range(6):
            if j % 3 == 1:
                coef_three.append((pick(single_three, 2 * j), pick(single_three, 2 * j + 1)))
            else:
                coef_three.append((pick(pair_three, 2 * j), None))
        for tile in range(tiles):
            cols = slice(tile * LANE, (tile + 1) * LANE)
            conv = [conv_ref[r, rows, cols] for r in range(12)]
            two = [conv[2 * j] + conv[2 * j + 1] for j in range(6)]
            three = [conv[3 * q] + conv[3 * q + 1] + conv[3 * q + 2] for q in range(4)]
            four = [two[2 * q] + two[2 * q + 1] for q in range(3)]
            for j in range(6):
                a, b = 2 * j, 2 * j + 1
                value = coef_one[a] * conv[a] + coef_one[b] * conv[b]
                value = value + coef_two[j] * two[j] + coef_four[j] * four[j // 2]
                value = value + coef_three[j][0] * three[a // 3]
                if j % 3 == 1:
                    value = value + coef_three[j][1] * three[b // 3]
                flat[tile, pl.ds(6 * r0 + j, 8, stride=6), :] = value

    whole = (total_bytes // 12) // 8

    def plain(i, carry):
        chunk(i, False)
        return carry

    lax.fori_loop(0, whole, plain, 0)
    for i in range(whole, groups // 8):
        chunk(i, True)

    def norm(i, carry):
        rows = pl.ds(pl.multiple_of(i * 16, 16), 16)
        value = jnp.concatenate([flat[tile, rows, :] for tile in range(tiles)], axis=1)
        tok_ref[rows, :] = value
        scale = lax.rsqrt(jnp.mean(value * value, axis=1, keepdims=True) + 1e-06)
        norm_ref[rows, :] = (value * scale * gain_ref[...]).astype(bf16)
        return carry

    lax.fori_loop(0, token_count // 16, norm, 0)


def phase_ids(ids_row, total_bytes):
    groups = -(-total_bytes // 12)
    padded = jnp.pad(ids_row, (0, 12 * groups - total_bytes), constant_values=-1)
    phases = jnp.transpose(padded.reshape(groups, 12))
    before = jnp.pad(phases[9:12, :-1], ((0, 0), (1, 0)), constant_values=-1)
    lanes = -(-groups // LANE) * LANE
    both = jnp.concatenate([before, phases], axis=0)
    return jnp.pad(both, ((0, 1), (0, lanes - groups)), constant_values=-1)


def byte_forward(ids, hi, lo, conv_w, score_w, gain_one, total_bytes):
    width = conv_w.shape[1]
    token_count = total_bytes // 2
    groups = -(-(-(-total_bytes // 12)) // 16) * 16
    return pl.pallas_call(
        functools.partial(byte_forward_kernel, total_bytes),
        out_shape=(
            jax.ShapeDtypeStruct((token_count, width), f32),
            jax.ShapeDtypeStruct((token_count, width), bf16),
            jax.ShapeDtypeStruct((12, groups, width), f32),
            jax.ShapeDtypeStruct((4, groups, LANE), f32),
        ),
        scratch_shapes=[
            pltpu.VMEM((15, groups, width), f32),
            pltpu.VMEM((width // LANE, 6 * groups, LANE), f32),
        ],
        compiler_params=pltpu.CompilerParams(vmem_limit_bytes=VMEM_CAP),
        name="byte_forward",
    )(ids, hi, lo, conv_w, score_w.reshape(1, width), gain_one.reshape(1, width))


def byte_backward_kernel(
    total_bytes,
    first_ref,
    ids_ref,
    tok_ref,
    dnorm_ref,
    dres_ref,
    conv_ref,
    mix_ref,
    table_ref,
    conv_w_ref,
    score_ref,
    gain_ref,
    out_ref,
    dtok,
    dconv,
    onehot,
):
    groups = conv_ref.shape[1]
    width = conv_ref.shape[2]
    tiles = width // LANE
    token_count = dnorm_ref.shape[0]
    vocab_rows = onehot.shape[0]
    lanes = ids_ref.shape[1]
    gain = gain_ref[...]

    def norm_back(i, acc):
        rows = pl.ds(pl.multiple_of(i * 8, 8), 8)
        value = tok_ref[rows, :]
        grad = dnorm_ref[rows, :]
        scale = lax.rsqrt(jnp.mean(value * value, axis=1, keepdims=True) + 1e-06)
        grad_gain = grad * gain
        inner = jnp.mean(value * grad_gain, axis=1, keepdims=True)
        total = 0.5 * scale * grad_gain - value * (0.5 * scale * scale * scale * inner)
        for tile in range(tiles):
            dtok[tile, rows, :] = total[:, tile * LANE : (tile + 1) * LANE]
        return acc + grad * value * scale

    gain_acc = lax.fori_loop(0, token_count // 8, norm_back, jnp.zeros((8, width), f32))
    rest = dtok.shape[1] - token_count
    dtok[:, token_count:, :] = jnp.zeros((tiles, rest, LANE), f32)
    for slot in range(dres_ref.shape[0]):
        start = pl.multiple_of(first_ref[slot] * BLK, BLK)

        def add(i, carry, slot=slot, start=start):
            r = pl.multiple_of(i * 8, 8)
            rows = pl.ds(start + r, 8)
            more = 0.5 * dres_ref[slot, pl.ds(r, 8), :]
            for tile in range(tiles):
                dtok[tile, rows, :] = (
                    dtok[tile, rows, :] + more[:, tile * LANE : (tile + 1) * LANE]
                )
            return carry

        lax.fori_loop(0, BLK // 8, add, 0)
    vocab = lax.broadcasted_iota(jnp.int32, (vocab_rows, lanes), 0)
    for r in range(15):
        onehot[:, r * lanes : (r + 1) * lanes] = (vocab == ids_ref[r : r + 1, :]).astype(bf16)
    for r in range(12):
        dconv[r * lanes + groups : (r + 1) * lanes, :] = jnp.zeros((lanes - groups, width), bf16)
    lane = lane_iota(8)

    def scalars(r0):
        rows = pl.ds(r0, 8)
        one = [jnp.zeros((8, LANE), f32) for _ in range(12)]
        cross = [jnp.zeros((8, LANE), f32) for _ in range(6)]
        tri = [jnp.zeros((8, LANE), f32) for _ in range(8)]
        for tile in range(tiles):
            cols = slice(tile * LANE, (tile + 1) * LANE)
            conv = [conv_ref[r, rows, cols] for r in range(12)]
            grad = [dtok[tile, pl.ds(6 * r0 + j, 8, stride=6), :] for j in range(6)]
            two = [conv[2 * j] + conv[2 * j + 1] for j in range(6)]
            three = [conv[3 * q] + conv[3 * q + 1] + conv[3 * q + 2] for q in range(4)]
            for r in range(12):
                one[r] = one[r] + conv[r] * grad[r // 2]
            slot = 0
            for j in range(6):
                cross[j] = cross[j] + two[j ^ 1] * grad[j]
                for q in sorted({(2 * j) // 3, (2 * j + 1) // 3}):
                    tri[slot] = tri[slot] + three[q] * grad[j]
                    slot += 1
        inner_one = jnp.zeros((8, LANE), f32)
        for r in range(12):
            inner_one = jnp.where(lane == r, jnp.sum(one[r], axis=1, keepdims=True), inner_one)
        inner_cross = jnp.zeros((8, LANE), f32)
        for j in range(6):
            inner_cross = jnp.where(
                lane // 2 == j, jnp.sum(cross[j], axis=1, keepdims=True), inner_cross
            )
        inner_three = jnp.zeros((8, LANE), f32)
        slot = 0
        for j in range(6):
            for q in sorted({(2 * j) // 3, (2 * j + 1) // 3}):
                here = (lane // 2 == j) & (lane // 3 == q)
                inner_three = jnp.where(
                    here, jnp.sum(tri[slot], axis=1, keepdims=True), inner_three
                )
                slot += 1
        inner_two = block_sum(inner_one, 2, lane)
        mix = [mix_ref[b, rows, :] for b in range(4)]
        d_mix = [
            inner_one,
            inner_two * 0.5,
            inner_three * (1.0 / 3.0),
            (inner_two + inner_cross) * 0.25,
        ]
        mean = mix[0] * d_mix[0] + mix[1] * d_mix[1] + mix[2] * d_mix[2] + mix[3] * d_mix[3]
        d_logit = [mix[b] * (d_mix[b] - mean) for b in range(4)]
        d_logit = [jnp.where(lane < 12, value, 0.0) for value in d_logit]
        slope = d_logit[0]
        for b in range(2, 5):
            slope = slope + block_sum(d_logit[b - 1], b, lane) * (1.0 / b)
        pair_two = block_sum(mix[1], 2, lane) * 0.5
        single_three = mix[2] * (1.0 / 3.0)
        pair_three = block_sum(mix[2], 2, lane) * (1.0 / 3.0)
        pair_four = block_sum(mix[3], 2, lane) * 0.25
        return mix[0], pair_two, single_three, pair_three, pair_four, slope

    def spread(r0, coefs, tile, masked, score_acc):
        one, pair_two, single_three, pair_three, pair_four, slope = coefs
        rows = pl.ds(r0, 8)
        cols = slice(tile * LANE, (tile + 1) * LANE)
        grad = [dtok[tile, pl.ds(6 * r0 + j, 8, stride=6), :] for j in range(6)]
        score = score_ref[0:1, cols]
        four = [
            pick(pair_four, 4 * q) * grad[2 * q] + pick(pair_four, 4 * q + 2) * grad[2 * q + 1]
            for q in range(3)
        ]
        three = []
        for q in range(4):
            a = 3 * q
            if a % 2 == 0:
                three.append(
                    pick(pair_three, a) * grad[a // 2]
                    + pick(single_three, a + 2) * grad[a // 2 + 1]
                )
            else:
                three.append(
                    pick(single_three, a) * grad[a // 2]
                    + pick(pair_three, a + 1) * grad[a // 2 + 1]
                )
        result = []
        for r in range(12):
            weight = pick(slope, r)
            own = (pick(one, r) + pick(pair_two, r)) * grad[r // 2]
            value = own + three[r // 3] + four[r // 4] + weight * score
            score_acc = score_acc + weight * conv_ref[r, rows, cols]
            if masked:
                group = r0 + lax.broadcasted_iota(jnp.int32, (8, LANE), 0)
                value = jnp.where(group * 12 + r < total_bytes, value, 0.0)
            result.append(value)
        return result, score_acc

    def chunk(i, accs, masked):
        r0 = pl.multiple_of(i * 16, 16)
        r1 = pl.multiple_of(i * 16 + 8, 8)
        low_coefs = scalars(r0)
        high_coefs = scalars(r1)
        new = []
        for tile in range(tiles):
            cols = slice(tile * LANE, (tile + 1) * LANE)
            low, acc = spread(r0, low_coefs, tile, masked, accs[tile])
            high, acc = spread(r1, high_coefs, tile, masked, acc)
            new.append(acc)
            for r in range(12):
                both = jnp.concatenate([low[r], high[r]], axis=0).astype(bf16)
                dconv[pl.ds(pl.multiple_of(r * lanes + r0, 16), 16), cols] = both
        return tuple(new)

    accs = tuple(jnp.zeros((8, LANE), f32) for _ in range(tiles))
    whole = (total_bytes // 12) // 16
    accs = lax.fori_loop(0, whole, lambda i, a: chunk(i, a, False), accs)
    for i in range(whole, groups // 16):
        accs = chunk(i, accs, True)
    tail = [jnp.zeros((1, width), f32) for _ in range(8)]
    for k in range(4):
        part = jnp.dot(
            onehot[:, k * lanes : (k + 12) * lanes], dconv[...], preferred_element_type=f32
        )
        if k == 0:
            out_ref[0:vocab_rows, :] = part * conv_w_ref[k : k + 1, :]
        else:
            out_ref[0:vocab_rows, :] = out_ref[0:vocab_rows, :] + part * conv_w_ref[k : k + 1, :]
        tail[k] = jnp.sum(part * table_ref[...], axis=0, keepdims=True)
    tail[4] = jnp.sum(jnp.concatenate(accs, axis=1), axis=0, keepdims=True)
    tail[5] = jnp.sum(gain_acc, axis=0, keepdims=True)
    out_ref[vocab_rows:, :] = jnp.concatenate(tail, axis=0)


def byte_backward(
    first, ids, tokens, d_norm, d_resid, conv, mix, table, conv_w, score_w, gain_one, total_bytes
):
    width = conv.shape[2]
    groups = conv.shape[1]
    lanes = ids.shape[1]
    vocab_rows = table.shape[0]
    return pl.pallas_call(
        functools.partial(byte_backward_kernel, total_bytes),
        out_shape=jax.ShapeDtypeStruct((vocab_rows + 8, width), f32),
        in_specs=[pl.BlockSpec(memory_space=pltpu.SMEM)]
        + [pl.BlockSpec(memory_space=pltpu.VMEM)] * 10,
        scratch_shapes=[
            pltpu.VMEM((width // LANE, 6 * groups, LANE), f32),
            pltpu.VMEM((12 * lanes, width), bf16),
            pltpu.VMEM((vocab_rows, 15 * lanes), bf16),
        ],
        compiler_params=pltpu.CompilerParams(vmem_limit_bytes=VMEM_CAP),
        name="byte_backward",
    )(
        first,
        ids,
        tokens,
        d_norm,
        d_resid,
        conv,
        mix,
        table,
        conv_w,
        score_w.reshape(1, width),
        gain_one.reshape(1, width),
    )


def head_mask(value, head):
    half = value.shape[1] // 2
    lane = lax.broadcasted_iota(jnp.int32, value.shape, 1)
    keep = lane < half if head == 0 else lane >= half
    return jnp.where(keep, value, jnp.zeros_like(value))


def two_heads(value):
    return jnp.concatenate([head_mask(value, 0), head_mask(value, 1)], axis=0)


def doc_operands(docs_ref, known, barred):
    blocks = docs_ref.shape[0]
    cols = jnp.transpose(docs_ref[...].astype(f32))
    lane = lane_iota(BLK).astype(f32)
    for b in range(blocks):
        same = cols[:, b : b + 1] == lane
        known[b * BLK : (b + 1) * BLK, :] = same.astype(bf16)
        barred[b * BLK : (b + 1) * BLK, :] = jnp.where(
            same | (lane >= 16.0), 0.0, -1e30
        ).astype(bf16)


def bias_tiles(buckets_ref, rel_ref, tiles):
    count = tiles.shape[0]
    blocks = buckets_ref.shape[0] // 2
    reach = count // 2
    levels = rel_ref.shape[1]
    level = lax.broadcasted_iota(jnp.int32, (levels, 2 * BLK), 0)
    for n in range(count):
        row = blocks - 1 - (n - reach)
        bucket = jnp.concatenate(
            [buckets_ref[row : row + 1, :], buckets_ref[row + 1 : row + 2, :]], axis=1
        )
        onehot = (level == bucket).astype(f32)
        values = lax.dot_general(
            rel_ref[...], onehot, NN, precision=HIGH, preferred_element_type=f32
        )
        for head in range(2):
            spread = jnp.broadcast_to(values[head : head + 1, :], (BLK, 2 * BLK))
            rolled = pltpu.roll(spread, BLK + 1, 1, stride=1, stride_axis=0)
            tiles[n, :, head * BLK : (head + 1) * BLK] = rolled[:, :BLK]


def attend_kernel(
    lead_ref,
    low_ref,
    high_ref,
    q_ref,
    k_ref,
    v_ref,
    docs_ref,
    buckets_ref,
    rel_ref,
    out_ref,
    low_out_ref,
    log_ref,
    known,
    barred,
    tiles,
    v_turned,
    held,
):
    reach = tiles.shape[0] // 2
    slots = q_ref.shape[0] // BLK

    @pl.when(pl.program_id(0) == 0)
    def _():
        doc_operands(docs_ref, known, barred)

    bias_tiles(buckets_ref, rel_ref.at[0], tiles)
    v_turned[...] = jnp.transpose(v_ref[...])
    for slot in range(slots):
        block = lead_ref[slot]
        first = low_ref[slot]
        last = high_ref[slot]
        base = pl.multiple_of(block * BLK, BLK)
        q_two = two_heads(q_ref[slot * BLK : (slot + 1) * BLK, :])
        bar = barred[pl.ds(base, BLK), :]
        q_full = jnp.concatenate([q_two, jnp.concatenate([bar, bar], axis=0)], axis=1)

        def score(kb, best):
            rows = pl.ds(pl.multiple_of(kb * BLK, BLK), BLK)
            k_full = jnp.concatenate([k_ref[rows, :], known[rows, :]], axis=1)
            value = lax.dot_general(k_full, q_full, NT, preferred_element_type=f32)
            value = value + tiles[kb - block + reach]
            held[kb - first] = value
            return jnp.maximum(best, jnp.max(value.reshape(BLK // 8, 8, 2 * BLK), axis=0))

        best = lax.fori_loop(first, last, score, jnp.full((8, 2 * BLK), -3e38, f32))
        best = jnp.max(best, axis=0, keepdims=True)

        def gather(kb, state):
            total, accum = state
            weight = jnp.exp(held[kb - first] - best)
            total = total + jnp.sum(weight.reshape(BLK // 8, 8, 2 * BLK), axis=0)
            cols = pl.ds(pl.multiple_of(kb * BLK, BLK), BLK)
            accum = accum + jnp.dot(
                v_turned[:, cols], weight.astype(bf16), preferred_element_type=f32
            )
            return total, accum

        total, accum = lax.fori_loop(
            first,
            last,
            gather,
            (jnp.zeros((8, 2 * BLK), f32), jnp.zeros((BLK, 2 * BLK), f32)),
        )
        total = jnp.sum(total, axis=0, keepdims=True)
        accum = accum / total
        half = BLK // 2
        both = jnp.concatenate([accum[:half, :BLK], accum[half:, BLK:]], axis=0)
        both = jnp.transpose(both)
        out_ref[slot * BLK : (slot + 1) * BLK, :] = both
        low_out_ref[slot * BLK : (slot + 1) * BLK, :] = both.astype(bf16)
        log_ref[0, slot : slot + 1, :] = best + jnp.log(total)


def attend(lead, low, high, q, k, v, docs, buckets, rel):
    rows, width = q.shape
    keys = k.shape[0]
    pairs = width // BLK
    blocks = docs.shape[0]
    slots = rows // BLK
    reach = blocks // 2
    smem = pl.BlockSpec(memory_space=pltpu.SMEM)

    def cols(count):
        return pl.BlockSpec((count, BLK), lambda i: (0, i))

    def whole(array):
        return pl.BlockSpec(array.shape, lambda i: (0,) * array.ndim)

    return pl.pallas_call(
        attend_kernel,
        grid=(pairs,),
        out_shape=(
            jax.ShapeDtypeStruct((rows, width), f32),
            jax.ShapeDtypeStruct((rows, width), bf16),
            jax.ShapeDtypeStruct((pairs, slots, 2 * BLK), f32),
        ),
        in_specs=[
            smem,
            smem,
            smem,
            cols(rows),
            cols(keys),
            cols(keys),
            whole(docs),
            whole(buckets),
            pl.BlockSpec((1,) + rel.shape[1:], lambda i: (i, 0, 0)),
        ],
        out_specs=(
            cols(rows),
            cols(rows),
            pl.BlockSpec((1, slots, 2 * BLK), lambda i: (i, 0, 0)),
        ),
        scratch_shapes=[
            pltpu.VMEM((keys, BLK), bf16),
            pltpu.VMEM((keys, BLK), bf16),
            pltpu.VMEM((2 * reach + 1, BLK, 2 * BLK), f32),
            pltpu.VMEM((BLK, keys), bf16),
            pltpu.VMEM((blocks, BLK, 2 * BLK), f32),
        ],
        compiler_params=pltpu.CompilerParams(vmem_limit_bytes=VMEM_CAP),
        name="attend",
    )(lead, low, high, q, k, v, docs, buckets, rel)


def attend_back_kernel(
    lead_ref,
    low_ref,
    high_ref,
    q_ref,
    k_ref,
    v_ref,
    g_ref,
    out_ref,
    log_ref,
    docs_ref,
    buckets_ref,
    rel_ref,
    dq_ref,
    dk_ref,
    dv_ref,
    dbias_ref,
    known,
    barred,
    tiles,
    k_turned,
    dk_acc,
    dv_acc,
    d_tiles,
):
    reach = tiles.shape[0] // 2
    count = tiles.shape[0]
    blocks = docs_ref.shape[0]
    slots = q_ref.shape[0] // BLK
    half = BLK // 2

    @pl.when(pl.program_id(0) == 0)
    def _():
        doc_operands(docs_ref, known, barred)

    bias_tiles(buckets_ref, rel_ref.at[0], tiles)
    k_turned[...] = jnp.transpose(k_ref[...])
    dk_acc[...] = jnp.zeros_like(dk_acc)
    dv_acc[...] = jnp.zeros_like(dv_acc)
    d_tiles[...] = jnp.zeros_like(d_tiles)
    sub = lax.broadcasted_iota(jnp.int32, (8, BLK), 0)
    lane = lane_iota(8)
    chooser = jnp.where((lane // half) == sub, 1.0, 0.0)
    for slot in range(slots):
        block = lead_ref[slot]
        first = low_ref[slot]
        last = high_ref[slot]
        base = pl.multiple_of(block * BLK, BLK)
        own = slice(slot * BLK, (slot + 1) * BLK)
        q_two = two_heads(q_ref[own, :])
        g_two = two_heads(g_ref[own, :])
        bar = barred[pl.ds(base, BLK), :]
        q_full = jnp.concatenate([q_two, jnp.concatenate([bar, bar], axis=0)], axis=1)
        product = g_ref[own, :].astype(f32) * out_ref[own, :]
        delta = lax.dot_general(chooser, product, NT, precision=HIGH, preferred_element_type=f32)
        delta = jnp.concatenate([delta[0:1, :], delta[1:2, :]], axis=1)
        log_total = log_ref[0, slot : slot + 1, :]

        def step(kb, dq):
            rows = pl.ds(pl.multiple_of(kb * BLK, BLK), BLK)
            k_full = jnp.concatenate([k_ref[rows, :], known[rows, :]], axis=1)
            value = lax.dot_general(k_full, q_full, NT, preferred_element_type=f32)
            prob = jnp.exp(value + tiles[kb - block + reach] - log_total)
            d_prob = lax.dot_general(v_ref[rows, :], g_two, NT, preferred_element_type=f32)
            d_score = prob * (d_prob - delta)
            d_tiles[kb - block + reach] = d_tiles[kb - block + reach] + d_score
            d_low = d_score.astype(bf16)
            dv_acc[rows, :] = dv_acc[rows, :] + jnp.dot(
                prob.astype(bf16), g_two, preferred_element_type=f32
            )
            dk_acc[rows, :] = dk_acc[rows, :] + jnp.dot(
                d_low, q_two, preferred_element_type=f32
            )
            return dq + jnp.dot(k_turned[:, rows], d_low, preferred_element_type=f32)

        dq = lax.fori_loop(first, last, step, jnp.zeros((BLK, 2 * BLK), f32))
        both = jnp.concatenate([dq[:half, :BLK], dq[half:, BLK:]], axis=0)
        dq_ref[own, :] = jnp.transpose(both).astype(bf16)
    dk_ref[...] = dk_acc[...].astype(bf16)
    dv_ref[...] = dv_acc[...].astype(bf16)
    levels = rel_ref.shape[2]
    level = lax.broadcasted_iota(jnp.int32, (levels, 2 * BLK), 0)
    total = jnp.zeros((8, levels), f32)
    pad = jnp.zeros((BLK, BLK), f32)
    mirror = (
        lax.broadcasted_iota(jnp.int32, (BLK, BLK), 0)
        + lax.broadcasted_iota(jnp.int32, (BLK, BLK), 1)
        == BLK - 1
    ).astype(bf16)
    for n in range(count):
        flipped = jnp.dot(mirror, d_tiles[n].astype(bf16), preferred_element_type=f32)
        row = blocks - 1 - (n - reach)
        bucket = jnp.concatenate(
            [buckets_ref[row : row + 1, :], buckets_ref[row + 1 : row + 2, :]], axis=1
        )
        onehot = (level == bucket).astype(f32)
        sums = []
        for head in range(2):
            part = flipped[:, head * BLK : (head + 1) * BLK]
            wide = jnp.concatenate([part, pad], axis=1)
            rolled = pltpu.roll(wide, 0, 1, stride=1, stride_axis=0)
            sums.append(jnp.sum(rolled, axis=0, keepdims=True))
        stacked = jnp.concatenate(sums + [jnp.zeros((6, 2 * BLK), f32)], axis=0)
        total = total + lax.dot_general(
            stacked, onehot, NT, precision=HIGH, preferred_element_type=f32
        )
    dbias_ref[0] = total


def attend_back(lead, low, high, q, k, v, g, out, log, docs, buckets, rel):
    rows, width = q.shape
    keys = k.shape[0]
    pairs = width // BLK
    blocks = docs.shape[0]
    slots = rows // BLK
    reach = blocks // 2
    levels = rel.shape[2]
    smem = pl.BlockSpec(memory_space=pltpu.SMEM)

    def cols(count):
        return pl.BlockSpec((count, BLK), lambda i: (0, i))

    def whole(array):
        return pl.BlockSpec(array.shape, lambda i: (0,) * array.ndim)

    def lead_block(shape):
        return pl.BlockSpec((1,) + shape, lambda i: (i,) + (0,) * len(shape))

    return pl.pallas_call(
        attend_back_kernel,
        grid=(pairs,),
        out_shape=(
            jax.ShapeDtypeStruct((rows, width), bf16),
            jax.ShapeDtypeStruct((keys, width), bf16),
            jax.ShapeDtypeStruct((keys, width), bf16),
            jax.ShapeDtypeStruct((pairs, 8, levels), f32),
        ),
        in_specs=[
            smem,
            smem,
            smem,
            cols(rows),
            cols(keys),
            cols(keys),
            cols(rows),
            cols(rows),
            lead_block((slots, 2 * BLK)),
            whole(docs),
            whole(buckets),
            lead_block(rel.shape[1:]),
        ],
        out_specs=(cols(rows), cols(keys), cols(keys), lead_block((8, levels))),
        scratch_shapes=[
            pltpu.VMEM((keys, BLK), bf16),
            pltpu.VMEM((keys, BLK), bf16),
            pltpu.VMEM((2 * reach + 1, BLK, 2 * BLK), f32),
            pltpu.VMEM((BLK, keys), bf16),
            pltpu.VMEM((keys, BLK), f32),
            pltpu.VMEM((keys, BLK), f32),
            pltpu.VMEM((2 * reach + 1, BLK, 2 * BLK), f32),
        ],
        compiler_params=pltpu.CompilerParams(vmem_limit_bytes=VMEM_CAP),
        name="attend_back",
    )(lead, low, high, q, k, v, g, out, log, docs, buckets, rel)


def attention_tables(docs, rel_bucket, rel_bias, lead):
    blocks = docs.shape[0]
    starts = docs[:, 0]
    ends = docs[:, -1]
    own_start = jnp.take(starts, lead)
    own_end = jnp.take(ends, lead)
    low = jnp.sum((ends[None, :] < own_start[:, None]).astype(jnp.int32), axis=1)
    high = jnp.sum((starts[None, :] <= own_end[:, None]).astype(jnp.int32), axis=1)
    buckets = jnp.pad(jnp.flip(rel_bucket), (0, 1)).reshape(2 * blocks, BLK)
    levels, heads = rel_bias.shape
    rel = jnp.transpose(rel_bias).reshape(heads // 2, 2, levels)
    rel = jnp.pad(rel, ((0, 0), (0, 6), (0, 0)))
    return low, high, buckets, rel


def bits_of(count):
    bits = count.bit_length() - 1
    assert 1 << bits == count
    return bits


def swap(value, axis, bit):
    count = lax.axis_size(axis)
    return lax.ppermute(value, axis, [(i, i ^ (1 << bit)) for i in range(count)])


def ordered(mine, other, index, bit, axis=0):
    upper = ((index >> bit) & 1) == 1
    return jnp.concatenate(
        [jnp.where(upper, other, mine), jnp.where(upper, mine, other)], axis=axis
    )


def gather_small(value, axis):
    index = lax.axis_index(axis)
    value = value[None]
    for bit in range(bits_of(lax.axis_size(axis))):
        value = ordered(value, swap(value, axis, bit), index, bit)
    return value


def gather_rows(shard, axis):
    count = lax.axis_size(axis)
    index = lax.axis_index(axis)
    parts = [(0, shard)]
    for bit in reversed(range(bits_of(count))):
        parts = parts + [(j | (1 << bit), swap(part, axis, bit)) for j, part in parts]
    rows = shard.shape[0]
    result = jnp.zeros((rows * count,) + shard.shape[1:], shard.dtype)
    for j, part in parts:
        result = lax.dynamic_update_slice_in_dim(result, part, (index ^ j) * rows, axis=0)
    return result


def half_step(value, axis, bit, dim):
    index = lax.axis_index(axis)
    own = (index >> bit) & 1
    size = value.shape[dim] // 2
    keep = lax.dynamic_slice_in_dim(value, own * size, size, dim)
    send = lax.dynamic_slice_in_dim(value, (1 - own) * size, size, dim)
    other = swap(send.astype(bf16), axis, bit)
    return (keep.astype(f32) + other.astype(f32)).astype(bf16)


def reduce_rows(value, scatter_axis, sum_axis):
    count = lax.axis_size(scatter_axis)
    bits = bits_of(count)
    rows = value.shape[0] // count
    value = value.reshape((2,) * bits + (rows,) + value.shape[1:])
    for bit in range(bits):
        value = half_step(value, scatter_axis, bit, bits - 1 - bit)
    value = value.reshape((rows,) + value.shape[bits + 1 :])
    steps = bits_of(lax.axis_size(sum_axis))
    done = 0
    while done < steps and value.shape[0] % 2 == 0:
        value = half_step(value, sum_axis, done, 0)
        done += 1
    for bit in range(done, steps):
        value = (value.astype(f32) + swap(value, sum_axis, bit).astype(f32)).astype(bf16)
    index = lax.axis_index(sum_axis)
    for bit in reversed(range(done)):
        value = ordered(value, swap(value, sum_axis, bit), index, bit)
    return value


def reduce_all(value, axes):
    stages = [(axis, bit) for axis in axes for bit in range(bits_of(lax.axis_size(axis)))]
    halved = []
    for axis, bit in stages:
        if value.shape[0] % 2 == 0:
            value = half_step(value, axis, bit, 0)
            halved.append((axis, bit))
        else:
            value = (value.astype(f32) + swap(value, axis, bit).astype(f32)).astype(bf16)
    for axis, bit in reversed(halved):
        value = ordered(value, swap(value, axis, bit), lax.axis_index(axis), bit)
    return value


def rms_scale(values, gain_vec):
    return values * lax.rsqrt(jnp.mean(values * values, axis=-1, keepdims=True) + 1e-06) * gain_vec


def gelu_product(gate_pre, up_pre):
    return jax.nn.gelu(gate_pre, approximate=True) * up_pre


def local(
    byte_ids,
    doc_ids,
    rel_bucket,
    table,
    conv_w,
    score_w,
    gain_one,
    gain_two,
    rel_bias,
    query_master,
    key_master,
    value_master,
    out_master,
    gate_master,
    up_master,
    down_master,
    out_cotangent,
):
    ctx_count = lax.axis_size("ctx")
    ctx_index = lax.axis_index("ctx")
    seq_count, byte_count = byte_ids.shape
    total_bytes = byte_count * ctx_count
    width = table.shape[1]
    vocab = table.shape[0]
    hidden_width = gate_master.shape[1]
    levels, heads = rel_bias.shape
    share = ctx_count // seq_count
    assert share * seq_count == ctx_count and byte_count == 2 * BLK
    seq = ctx_index // share
    part = ctx_index % share
    near = [seq ^ slot for slot in range(seq_count)]
    lead = jnp.stack([share * other + part for other in near]).astype(jnp.int32)
    rows = seq_count * BLK

    both = jnp.stack([byte_ids, doc_ids], axis=1)
    both = gather_small(both, "ctx")
    both = lax.dynamic_index_in_dim(both, seq, 1, keepdims=False)
    ids = both[:, 0].reshape(total_bytes)
    docs = both[:, 1, ::2]

    qkv_low = jnp.concatenate([query_master, key_master, value_master], axis=1).astype(bf16)
    ogu_low = jnp.concatenate([out_master, gate_master, up_master], axis=1).astype(bf16)
    down_low = down_master.astype(bf16)
    qkv = gather_rows(qkv_low, "fsdp")
    ogu = gather_rows(ogu_low, "fsdp")
    down_weight = gather_rows(down_low, "fsdp")
    query_weight = qkv[:, :width]
    key_weight = qkv[:, width : 2 * width]
    value_weight = qkv[:, 2 * width :]
    out_weight = ogu[:, :width]
    gate_up = ogu[:, width:]

    def to_owner(block, slot):
        if slot == 0:
            return block
        pairs = []
        for c in range(ctx_count):
            pairs.append((c, ((c // share) ^ slot) * share + c % share))
        return lax.ppermute(block, "ctx", pairs)

    cotangent = jnp.concatenate(
        [
            to_owner(lax.dynamic_index_in_dim(out_cotangent, near[s], 1, keepdims=False), s)
            for s in range(seq_count)
        ],
        axis=0,
    )

    phases = phase_ids(ids, total_bytes)
    table_wide = jnp.pad(table, ((0, -vocab % LANE), (0, 0)))
    table_hi = lax.reduce_precision(table_wide, 8, 7)
    table_lo = (table_wide - table_hi).astype(bf16)
    tokens, norm_one, conv, mix = byte_forward(
        phases, table_hi.astype(bf16), table_lo, conv_w, score_w, gain_one, total_bytes
    )

    def own_rows(array):
        return jnp.concatenate(
            [lax.dynamic_slice_in_dim(array, lead[s] * BLK, BLK, 0) for s in range(seq_count)],
            axis=0,
        )

    tokens_own = own_rows(tokens)
    norm_own = own_rows(norm_one)

    queries = jnp.dot(norm_own, query_weight, preferred_element_type=f32).astype(bf16)
    keys = jnp.dot(norm_one, key_weight, preferred_element_type=f32).astype(bf16)
    values = jnp.dot(norm_one, value_weight, preferred_element_type=f32).astype(bf16)
    low, high, buckets, rel = attention_tables(docs, rel_bucket, rel_bias, lead)
    attended, attended_low, log_total = attend(
        lead, low, high, queries, keys, values, docs, buckets, rel
    )

    resid = tokens_own + jnp.dot(attended_low, out_weight, preferred_element_type=f32)
    norm_two = rms_scale(resid, gain_two).astype(bf16)
    gate_pre = jnp.dot(norm_two, gate_up[:, :hidden_width], preferred_element_type=f32)
    up_pre = jnp.dot(norm_two, gate_up[:, hidden_width:], preferred_element_type=f32)
    hidden = gelu_product(gate_pre, up_pre).astype(bf16)
    output = (resid + jnp.dot(hidden, down_weight, preferred_element_type=f32)).astype(bf16)
    output = output.reshape(seq_count, BLK, width)
    arrived = jnp.stack([to_owner(output[s], s) for s in range(seq_count)])
    output = jnp.stack(
        [lax.dynamic_index_in_dim(arrived, seq ^ s, 0, keepdims=False) for s in range(seq_count)],
        axis=1,
    )

    grad_down = jnp.einsum("rf,rd->fd", hidden, cotangent, preferred_element_type=f32)
    grad_down = reduce_rows(grad_down.astype(bf16), "fsdp", "ctx")
    d_hidden = jnp.einsum("rd,fd->rf", cotangent, down_weight, preferred_element_type=f32)
    _, gelu_pull = jax.vjp(gelu_product, gate_pre, up_pre)
    d_gate, d_up = gelu_pull(d_hidden)
    d_both = jnp.concatenate([d_gate.astype(bf16), d_up.astype(bf16)], axis=1)
    grad_gu = jnp.einsum("rd,rf->df", norm_two, d_both, preferred_element_type=f32)
    grad_gu = reduce_rows(grad_gu.astype(bf16), "fsdp", "ctx")
    d_norm_two = jnp.einsum("rf,df->rd", d_both, gate_up, preferred_element_type=f32)
    _, norm_pull_two = jax.vjp(rms_scale, resid, gain_two)
    d_resid_norm, grad_gain_two = norm_pull_two(d_norm_two)
    d_resid = cotangent.astype(f32) + d_resid_norm
    d_branch = d_resid.astype(bf16)
    grad_out = jnp.einsum("ra,rd->ad", attended_low, d_branch, preferred_element_type=f32)
    d_attended = jnp.einsum("rd,ad->ra", d_branch, out_weight, preferred_element_type=f32)
    d_attended = d_attended.astype(bf16)

    d_queries, d_keys, d_values, d_bias = attend_back(
        lead,
        low,
        high,
        queries,
        keys,
        values,
        d_attended,
        attended,
        log_total,
        docs,
        buckets,
        rel,
    )
    grad_qkv = jnp.concatenate(
        [
            jnp.einsum("rd,ra->da", norm_own, d_queries, preferred_element_type=f32),
            jnp.einsum("rd,ra->da", norm_one, d_keys, preferred_element_type=f32),
            jnp.einsum("rd,ra->da", norm_one, d_values, preferred_element_type=f32),
            grad_out,
        ],
        axis=1,
    )
    grad_qkv = reduce_rows(grad_qkv.astype(bf16), "fsdp", "ctx")
    d_norm_query = jnp.einsum("ra,da->rd", d_queries, query_weight, preferred_element_type=f32)
    d_norm_one = jnp.einsum(
        "ra,da->rd", d_keys, key_weight, preferred_element_type=f32
    ) + jnp.einsum("ra,da->rd", d_values, value_weight, preferred_element_type=f32)
    for s in range(seq_count):
        start = lead[s] * BLK
        old = lax.dynamic_slice_in_dim(d_norm_one, start, BLK, 0)
        d_norm_one = lax.dynamic_update_slice_in_dim(
            d_norm_one, old + d_norm_query[s * BLK : (s + 1) * BLK], start, 0
        )

    vocab_rows = -(-vocab // 16) * 16
    table_tall = jnp.pad(table, ((0, vocab_rows - vocab), (0, 0)))
    small = byte_backward(
        lead,
        phases,
        tokens,
        d_norm_one,
        d_resid.reshape(seq_count, BLK, width),
        conv,
        mix,
        table_tall,
        conv_w,
        score_w,
        gain_one,
        total_bytes,
    )
    bias_grad = jnp.transpose(d_bias[:, :2].reshape(heads, levels)).reshape(1, levels * heads)
    bias_grad = jnp.pad(bias_grad, ((0, 0), (0, width - levels * heads)))
    small = jnp.concatenate([small[: vocab_rows + 6], grad_gain_two[None], bias_grad], axis=0)
    small = jnp.pad(small, ((0, -small.shape[0] % 32), (0, 0))).astype(bf16)
    small = reduce_all(small, ("fsdp", "ctx")).astype(f32)
    top = vocab_rows
    return (
        output,
        small[:vocab],
        small[top : top + 4],
        small[top + 4],
        small[top + 5],
        small[top + 6],
        small[top + 7, : levels * heads].reshape(levels, heads),
        grad_qkv[:, :width].astype(f32),
        grad_qkv[:, width : 2 * width].astype(f32),
        grad_qkv[:, 2 * width : 3 * width].astype(f32),
        grad_qkv[:, 3 * width :].astype(f32),
        grad_gu[:, :hidden_width].astype(f32),
        grad_gu[:, hidden_width:].astype(f32),
        grad_down.astype(f32),
    )


def solution(mesh):
    placed = (
        P("fsdp", "ctx"),
        P("fsdp", "ctx"),
        P(),
        P(),
        P(),
        P(),
        P(),
        P(),
        P(),
        P("fsdp", None),
        P("fsdp", None),
        P("fsdp", None),
        P("fsdp", None),
        P("fsdp", None),
        P("fsdp", None),
        P("fsdp", None),
        P("ctx", "fsdp", None),
    )
    return jax.shard_map(
        local,
        mesh=mesh,
        in_specs=placed,
        out_specs=(
            P("ctx", "fsdp", None),
            P(),
            P(),
            P(),
            P(),
            P(),
            P(),
            P("fsdp", None),
            P("fsdp", None),
            P("fsdp", None),
            P("fsdp", None),
            P("fsdp", None),
            P("fsdp", None),
            P("fsdp", None),
        ),
        check_vma=False,
    )
```

```python
import functools

import jax
import jax.numpy as jnp
from jax import lax
from jax.experimental import pallas as pl
from jax.experimental.pallas import tpu as pltpu
from jax.sharding import PartitionSpec as P

f32 = jnp.float32
bf16 = jnp.bfloat16
LANE = 128
BLK = 128
VMEM_CAP = 60 * 1024 * 1024
HIGH = lax.Precision.HIGHEST
NT = (((1,), (1,)), ((), ()))
NN = (((1,), (0,)), ((), ()))


def lane_iota(rows):
    return lax.broadcasted_iota(jnp.int32, (rows, LANE), 1)


def block_sum(value, width, lane):
    def ahead(v, n):
        return pltpu.roll(v, LANE - n, 1)

    def behind(v, n):
        return pltpu.roll(v, n, 1)

    if width == 1:
        return value
    if width == 3:
        lead = value + ahead(value, 1) + ahead(value, 2)
        phase = lane % 3
        return jnp.where(phase == 0, lead, jnp.where(phase == 1, behind(lead, 1), behind(lead, 2)))
    pair = value + jnp.where(lane % 2 == 0, ahead(value, 1), behind(value, 1))
    if width == 2:
        return pair
    return pair + jnp.where(lane % 4 < 2, ahead(pair, 2), behind(pair, 2))


def pick(value, lane_index):
    return value[:, lane_index : lane_index + 1]


def byte_forward_kernel(
    total_bytes,
    ids_ref,
    table_ref,
    conv_w_ref,
    score_ref,
    gain_ref,
    tok_ref,
    norm_ref,
    conv_ref,
    mix_ref,
    hi_ref,
    lo_ref,
    emb,
    flat,
):
    groups = conv_ref.shape[1]
    width = conv_ref.shape[2]
    tiles = width // LANE
    token_count = norm_ref.shape[0]
    vocab_pad = hi_ref.shape[0]
    high = table_ref[...].astype(bf16)
    hi_ref[...] = high
    lo_ref[...] = (table_ref[...] - high.astype(f32)).astype(bf16)
    ids_cols = jnp.transpose(ids_ref[...].astype(f32))
    vocab = lax.broadcasted_iota(jnp.int32, (groups, vocab_pad), 1).astype(f32)
    for r in range(15):
        onehot = (ids_cols[0:groups, r : r + 1] == vocab).astype(bf16)
        emb[r] = jnp.dot(onehot, hi_ref[...], preferred_element_type=f32) + jnp.dot(
            onehot, lo_ref[...], preferred_element_type=f32
        )
    lane = lane_iota(8)

    def chunk(i, masked):
        r0 = pl.multiple_of(i * 8, 8)
        rows = pl.ds(r0, 8)
        sums = [jnp.zeros((8, LANE), f32) for _ in range(12)]
        for tile in range(tiles):
            cols = slice(tile * LANE, (tile + 1) * LANE)
            taps = [conv_w_ref[k : k + 1, cols] for k in range(4)]
            piece = [emb[r, rows, cols] for r in range(15)]
            score = score_ref[0:1, cols]
            for r in range(12):
                value = (
                    piece[r] * taps[0]
                    + piece[r + 1] * taps[1]
                    + piece[r + 2] * taps[2]
                    + piece[r + 3] * taps[3]
                )
                if masked:
                    group = r0 + lax.broadcasted_iota(jnp.int32, (8, LANE), 0)
                    value = jnp.where(group * 12 + r < total_bytes, value, 0.0)
                conv_ref[r, rows, cols] = value
                sums[r] = sums[r] + value * score
        packed = jnp.zeros((8, LANE), f32)
        for r in range(12):
            packed = jnp.where(lane == r, jnp.sum(sums[r], axis=1, keepdims=True), packed)
        logits = [block_sum(packed, b, lane) * (1.0 / b) for b in range(1, 5)]
        best = jnp.maximum(jnp.maximum(logits[0], logits[1]), jnp.maximum(logits[2], logits[3]))
        parts = [jnp.exp(value - best) for value in logits]
        total = parts[0] + parts[1] + parts[2] + parts[3]
        mix = [part / total for part in parts]
        for b in range(4):
            mix_ref[b, rows, :] = mix[b]
        half_one = mix[0] * 0.5
        pair_two = block_sum(mix[1], 2, lane) * 0.25
        single_three = mix[2] * (1.0 / 6.0)
        pair_three = block_sum(mix[2], 2, lane) * (1.0 / 6.0)
        pair_four = block_sum(mix[3], 2, lane) * 0.125
        coef_one = [pick(half_one, r) for r in range(12)]
        coef_two = [pick(pair_two, 2 * j) for j in range(6)]
        coef_four = [pick(pair_four, 2 * j) for j in range(6)]
        coef_three = []
        for j in range(6):
            if j % 3 == 1:
                coef_three.append((pick(single_three, 2 * j), pick(single_three, 2 * j + 1)))
            else:
                coef_three.append((pick(pair_three, 2 * j), None))
        for tile in range(tiles):
            cols = slice(tile * LANE, (tile + 1) * LANE)
            conv = [conv_ref[r, rows, cols] for r in range(12)]
            two = [conv[2 * j] + conv[2 * j + 1] for j in range(6)]
            three = [conv[3 * q] + conv[3 * q + 1] + conv[3 * q + 2] for q in range(4)]
            four = [two[2 * q] + two[2 * q + 1] for q in range(3)]
            for j in range(6):
                a, b = 2 * j, 2 * j + 1
                value = coef_one[a] * conv[a] + coef_one[b] * conv[b]
                value = value + coef_two[j] * two[j] + coef_four[j] * four[j // 2]
                value = value + coef_three[j][0] * three[a // 3]
                if j % 3 == 1:
                    value = value + coef_three[j][1] * three[b // 3]
                flat[tile, pl.ds(6 * r0 + j, 8, stride=6), :] = value

    whole = (total_bytes // 12) // 8

    def plain(i, carry):
        chunk(i, False)
        return carry

    lax.fori_loop(0, whole, plain, 0)
    for i in range(whole, groups // 8):
        chunk(i, True)

    def norm(i, carry):
        rows = pl.ds(pl.multiple_of(i * 16, 16), 16)
        value = jnp.concatenate([flat[tile, rows, :] for tile in range(tiles)], axis=1)
        tok_ref[rows, :] = value
        scale = lax.rsqrt(jnp.mean(value * value, axis=1, keepdims=True) + 1e-06)
        norm_ref[rows, :] = (value * scale * gain_ref[...]).astype(bf16)
        return carry

    lax.fori_loop(0, token_count // 16, norm, 0)


def phase_ids(ids_row, total_bytes):
    groups = -(-total_bytes // 12)
    padded = jnp.pad(ids_row, (0, 12 * groups - total_bytes), constant_values=-1)
    phases = jnp.transpose(padded.reshape(groups, 12))
    before = jnp.pad(phases[9:12, :-1], ((0, 0), (1, 0)), constant_values=-1)
    lanes = -(-groups // LANE) * LANE
    both = jnp.concatenate([before, phases], axis=0)
    return jnp.pad(both, ((0, 1), (0, lanes - groups)), constant_values=-1)


def byte_forward(ids, table, conv_w, score_w, gain_one, total_bytes):
    width = conv_w.shape[1]
    token_count = total_bytes // 2
    groups = -(-(-(-total_bytes // 12)) // 16) * 16
    return pl.pallas_call(
        functools.partial(byte_forward_kernel, total_bytes),
        out_shape=(
            jax.ShapeDtypeStruct((token_count, width), f32),
            jax.ShapeDtypeStruct((token_count, width), bf16),
            jax.ShapeDtypeStruct((12, groups, width), f32),
            jax.ShapeDtypeStruct((4, groups, LANE), f32),
        ),
        scratch_shapes=[
            pltpu.VMEM(table.shape, bf16),
            pltpu.VMEM(table.shape, bf16),
            pltpu.VMEM((15, groups, width), f32),
            pltpu.VMEM((width // LANE, 6 * groups, LANE), f32),
        ],
        compiler_params=pltpu.CompilerParams(vmem_limit_bytes=VMEM_CAP),
        cost_estimate=pl.CostEstimate(flops=20_000_000_000, transcendentals=0, bytes_accessed=1 << 24),
        name="byte_forward",
    )(ids, table, conv_w, score_w.reshape(1, width), gain_one.reshape(1, width))


def byte_backward_kernel(
    total_bytes,
    first_ref,
    ids_ref,
    tok_ref,
    dnorm_ref,
    dres_ref,
    conv_ref,
    mix_ref,
    table_ref,
    conv_w_ref,
    score_ref,
    gain_ref,
    out_ref,
    dtok,
    dconv,
    onehot,
):
    groups = conv_ref.shape[1]
    width = conv_ref.shape[2]
    tiles = width // LANE
    token_count = dnorm_ref.shape[0]
    vocab_rows = onehot.shape[0]
    lanes = ids_ref.shape[1]
    gain = gain_ref[...]

    def norm_back(i, acc):
        rows = pl.ds(pl.multiple_of(i * 8, 8), 8)
        value = tok_ref[rows, :]
        grad = dnorm_ref[rows, :]
        scale = lax.rsqrt(jnp.mean(value * value, axis=1, keepdims=True) + 1e-06)
        grad_gain = grad * gain
        inner = jnp.mean(value * grad_gain, axis=1, keepdims=True)
        total = 0.5 * scale * grad_gain - value * (0.5 * scale * scale * scale * inner)
        for tile in range(tiles):
            dtok[tile, rows, :] = total[:, tile * LANE : (tile + 1) * LANE]
        return acc + grad * value * scale

    gain_acc = lax.fori_loop(0, token_count // 8, norm_back, jnp.zeros((8, width), f32))
    rest = dtok.shape[1] - token_count
    dtok[:, token_count:, :] = jnp.zeros((tiles, rest, LANE), f32)
    for slot in range(dres_ref.shape[0]):
        start = pl.multiple_of(first_ref[slot] * BLK, BLK)

        def add(i, carry, slot=slot, start=start):
            r = pl.multiple_of(i * 8, 8)
            rows = pl.ds(start + r, 8)
            more = 0.5 * dres_ref[slot, pl.ds(r, 8), :]
            for tile in range(tiles):
                dtok[tile, rows, :] = (
                    dtok[tile, rows, :] + more[:, tile * LANE : (tile + 1) * LANE]
                )
            return carry

        lax.fori_loop(0, BLK // 8, add, 0)
    vocab = lax.broadcasted_iota(jnp.int32, (vocab_rows, lanes), 0)
    for r in range(15):
        onehot[:, r * lanes : (r + 1) * lanes] = (vocab == ids_ref[r : r + 1, :]).astype(bf16)
    for r in range(12):
        dconv[r * lanes + groups : (r + 1) * lanes, :] = jnp.zeros((lanes - groups, width), bf16)
    lane = lane_iota(8)

    def scalars(r0):
        rows = pl.ds(r0, 8)
        one = [jnp.zeros((8, LANE), f32) for _ in range(12)]
        cross = [jnp.zeros((8, LANE), f32) for _ in range(6)]
        tri = [jnp.zeros((8, LANE), f32) for _ in range(8)]
        for tile in range(tiles):
            cols = slice(tile * LANE, (tile + 1) * LANE)
            conv = [conv_ref[r, rows, cols] for r in range(12)]
            grad = [dtok[tile, pl.ds(6 * r0 + j, 8, stride=6), :] for j in range(6)]
            two = [conv[2 * j] + conv[2 * j + 1] for j in range(6)]
            three = [conv[3 * q] + conv[3 * q + 1] + conv[3 * q + 2] for q in range(4)]
            for r in range(12):
                one[r] = one[r] + conv[r] * grad[r // 2]
            slot = 0
            for j in range(6):
                cross[j] = cross[j] + two[j ^ 1] * grad[j]
                for q in sorted({(2 * j) // 3, (2 * j + 1) // 3}):
                    tri[slot] = tri[slot] + three[q] * grad[j]
                    slot += 1
        inner_one = jnp.zeros((8, LANE), f32)
        for r in range(12):
            inner_one = jnp.where(lane == r, jnp.sum(one[r], axis=1, keepdims=True), inner_one)
        inner_cross = jnp.zeros((8, LANE), f32)
        for j in range(6):
            inner_cross = jnp.where(
                lane // 2 == j, jnp.sum(cross[j], axis=1, keepdims=True), inner_cross
            )
        inner_three = jnp.zeros((8, LANE), f32)
        slot = 0
        for j in range(6):
            for q in sorted({(2 * j) // 3, (2 * j + 1) // 3}):
                here = (lane // 2 == j) & (lane // 3 == q)
                inner_three = jnp.where(
                    here, jnp.sum(tri[slot], axis=1, keepdims=True), inner_three
                )
                slot += 1
        inner_two = block_sum(inner_one, 2, lane)
        mix = [mix_ref[b, rows, :] for b in range(4)]
        d_mix = [
            inner_one,
            inner_two * 0.5,
            inner_three * (1.0 / 3.0),
            (inner_two + inner_cross) * 0.25,
        ]
        mean = mix[0] * d_mix[0] + mix[1] * d_mix[1] + mix[2] * d_mix[2] + mix[3] * d_mix[3]
        d_logit = [mix[b] * (d_mix[b] - mean) for b in range(4)]
        d_logit = [jnp.where(lane < 12, value, 0.0) for value in d_logit]
        slope = d_logit[0]
        for b in range(2, 5):
            slope = slope + block_sum(d_logit[b - 1], b, lane) * (1.0 / b)
        pair_two = block_sum(mix[1], 2, lane) * 0.5
        single_three = mix[2] * (1.0 / 3.0)
        pair_three = block_sum(mix[2], 2, lane) * (1.0 / 3.0)
        pair_four = block_sum(mix[3], 2, lane) * 0.25
        return mix[0], pair_two, single_three, pair_three, pair_four, slope

    def spread(r0, coefs, tile, masked, score_acc):
        one, pair_two, single_three, pair_three, pair_four, slope = coefs
        rows = pl.ds(r0, 8)
        cols = slice(tile * LANE, (tile + 1) * LANE)
        grad = [dtok[tile, pl.ds(6 * r0 + j, 8, stride=6), :] for j in range(6)]
        score = score_ref[0:1, cols]
        four = [
            pick(pair_four, 4 * q) * grad[2 * q] + pick(pair_four, 4 * q + 2) * grad[2 * q + 1]
            for q in range(3)
        ]
        three = []
        for q in range(4):
            a = 3 * q
            if a % 2 == 0:
                three.append(
                    pick(pair_three, a) * grad[a // 2]
                    + pick(single_three, a + 2) * grad[a // 2 + 1]
                )
            else:
                three.append(
                    pick(single_three, a) * grad[a // 2]
                    + pick(pair_three, a + 1) * grad[a // 2 + 1]
                )
        result = []
        for r in range(12):
            weight = pick(slope, r)
            own = (pick(one, r) + pick(pair_two, r)) * grad[r // 2]
            value = own + three[r // 3] + four[r // 4] + weight * score
            score_acc = score_acc + weight * conv_ref[r, rows, cols]
            if masked:
                group = r0 + lax.broadcasted_iota(jnp.int32, (8, LANE), 0)
                value = jnp.where(group * 12 + r < total_bytes, value, 0.0)
            result.append(value)
        return result, score_acc

    def chunk(i, accs, masked):
        r0 = pl.multiple_of(i * 16, 16)
        r1 = pl.multiple_of(i * 16 + 8, 8)
        low_coefs = scalars(r0)
        high_coefs = scalars(r1)
        new = []
        for tile in range(tiles):
            cols = slice(tile * LANE, (tile + 1) * LANE)
            low, acc = spread(r0, low_coefs, tile, masked, accs[tile])
            high, acc = spread(r1, high_coefs, tile, masked, acc)
            new.append(acc)
            for r in range(12):
                both = jnp.concatenate([low[r], high[r]], axis=0).astype(bf16)
                dconv[pl.ds(pl.multiple_of(r * lanes + r0, 16), 16), cols] = both
        return tuple(new)

    accs = tuple(jnp.zeros((8, LANE), f32) for _ in range(tiles))
    whole = (total_bytes // 12) // 16
    accs = lax.fori_loop(0, whole, lambda i, a: chunk(i, a, False), accs)
    for i in range(whole, groups // 16):
        accs = chunk(i, accs, True)
    tail = [jnp.zeros((1, width), f32) for _ in range(8)]
    for k in range(4):
        part = jnp.dot(
            onehot[:, k * lanes : (k + 12) * lanes], dconv[...], preferred_element_type=f32
        )
        if k == 0:
            out_ref[0:vocab_rows, :] = part * conv_w_ref[k : k + 1, :]
        else:
            out_ref[0:vocab_rows, :] = out_ref[0:vocab_rows, :] + part * conv_w_ref[k : k + 1, :]
        tail[k] = jnp.sum(part * table_ref[0:vocab_rows, :], axis=0, keepdims=True)
    tail[4] = jnp.sum(jnp.concatenate(accs, axis=1), axis=0, keepdims=True)
    tail[5] = jnp.sum(gain_acc, axis=0, keepdims=True)
    out_ref[vocab_rows:, :] = jnp.concatenate(tail, axis=0)


def byte_backward(
    first,
    ids,
    tokens,
    d_norm,
    d_resid,
    conv,
    mix,
    table,
    vocab_rows,
    conv_w,
    score_w,
    gain_one,
    total_bytes,
):
    width = conv.shape[2]
    groups = conv.shape[1]
    lanes = ids.shape[1]
    return pl.pallas_call(
        functools.partial(byte_backward_kernel, total_bytes),
        out_shape=jax.ShapeDtypeStruct((vocab_rows + 8, width), f32),
        in_specs=[pl.BlockSpec(memory_space=pltpu.SMEM)]
        + [pl.BlockSpec(memory_space=pltpu.VMEM)] * 10,
        scratch_shapes=[
            pltpu.VMEM((width // LANE, 6 * groups, LANE), f32),
            pltpu.VMEM((12 * lanes, width), bf16),
            pltpu.VMEM((vocab_rows, 15 * lanes), bf16),
        ],
        compiler_params=pltpu.CompilerParams(vmem_limit_bytes=VMEM_CAP),
        cost_estimate=pl.CostEstimate(flops=20_000_000_000, transcendentals=0, bytes_accessed=1 << 24),
        name="byte_backward",
    )(
        first,
        ids,
        tokens,
        d_norm,
        d_resid,
        conv,
        mix,
        table,
        conv_w,
        score_w.reshape(1, width),
        gain_one.reshape(1, width),
    )


def head_mask(value, head):
    half = value.shape[1] // 2
    lane = lax.broadcasted_iota(jnp.int32, value.shape, 1)
    keep = lane < half if head == 0 else lane >= half
    return jnp.where(keep, value, jnp.zeros_like(value))


def two_heads(value):
    return jnp.concatenate([head_mask(value, 0), head_mask(value, 1)], axis=0)


def doc_operands(docs_ref, known, barred):
    blocks = docs_ref.shape[0]
    cols = jnp.transpose(docs_ref[...].astype(f32))
    lane = lane_iota(BLK).astype(f32)
    for b in range(blocks):
        same = cols[:, b : b + 1] == lane
        known[b * BLK : (b + 1) * BLK, :] = same.astype(bf16)
        barred[b * BLK : (b + 1) * BLK, :] = jnp.where(
            same | (lane >= 16.0), 0.0, -1e30
        ).astype(bf16)


def bias_tiles(buckets_ref, rel_ref, tiles):
    count = tiles.shape[0]
    blocks = buckets_ref.shape[0] // 2
    reach = count // 2
    levels = rel_ref.shape[1]
    level = lax.broadcasted_iota(jnp.int32, (levels, 2 * BLK), 0)
    for n in range(count):
        row = blocks - 1 - (n - reach)
        bucket = jnp.concatenate(
            [buckets_ref[row : row + 1, :], buckets_ref[row + 1 : row + 2, :]], axis=1
        )
        onehot = (level == bucket).astype(f32)
        values = lax.dot_general(
            rel_ref[...], onehot, NN, precision=HIGH, preferred_element_type=f32
        )
        for head in range(2):
            spread = jnp.broadcast_to(values[head : head + 1, :], (BLK, 2 * BLK))
            rolled = pltpu.roll(spread, BLK + 1, 1, stride=1, stride_axis=0)
            tiles[n, :, head * BLK : (head + 1) * BLK] = rolled[:, :BLK]


def attend_kernel(
    lead_ref,
    low_ref,
    high_ref,
    q_ref,
    k_ref,
    v_ref,
    docs_ref,
    buckets_ref,
    rel_ref,
    out_ref,
    low_out_ref,
    log_ref,
    known,
    barred,
    tiles,
    v_turned,
    held,
):
    reach = tiles.shape[0] // 2
    slots = q_ref.shape[0] // BLK

    @pl.when(pl.program_id(0) == 0)
    def _():
        doc_operands(docs_ref, known, barred)

    bias_tiles(buckets_ref, rel_ref.at[0], tiles)
    v_turned[...] = jnp.transpose(v_ref[...])
    for slot in range(slots):
        block = lead_ref[slot]
        first = low_ref[slot]
        last = high_ref[slot]
        base = pl.multiple_of(block * BLK, BLK)
        q_two = two_heads(q_ref[slot * BLK : (slot + 1) * BLK, :])
        bar = barred[pl.ds(base, BLK), :]
        q_full = jnp.concatenate([q_two, jnp.concatenate([bar, bar], axis=0)], axis=1)

        def score(kb, best):
            rows = pl.ds(pl.multiple_of(kb * BLK, BLK), BLK)
            k_full = jnp.concatenate([k_ref[rows, :], known[rows, :]], axis=1)
            value = lax.dot_general(k_full, q_full, NT, preferred_element_type=f32)
            value = value + tiles[kb - block + reach]
            held[kb - first] = value
            return jnp.maximum(best, jnp.max(value.reshape(BLK // 8, 8, 2 * BLK), axis=0))

        best = lax.fori_loop(first, last, score, jnp.full((8, 2 * BLK), -3e38, f32))
        best = jnp.max(best, axis=0, keepdims=True)

        def gather(kb, state):
            total, accum = state
            weight = jnp.exp(held[kb - first] - best)
            total = total + jnp.sum(weight.reshape(BLK // 8, 8, 2 * BLK), axis=0)
            cols = pl.ds(pl.multiple_of(kb * BLK, BLK), BLK)
            accum = accum + jnp.dot(
                v_turned[:, cols], weight.astype(bf16), preferred_element_type=f32
            )
            return total, accum

        total, accum = lax.fori_loop(
            first,
            last,
            gather,
            (jnp.zeros((8, 2 * BLK), f32), jnp.zeros((BLK, 2 * BLK), f32)),
        )
        total = jnp.sum(total, axis=0, keepdims=True)
        accum = accum / total
        half = BLK // 2
        both = jnp.concatenate([accum[:half, :BLK], accum[half:, BLK:]], axis=0)
        both = jnp.transpose(both)
        out_ref[slot * BLK : (slot + 1) * BLK, :] = both
        low_out_ref[slot * BLK : (slot + 1) * BLK, :] = both.astype(bf16)
        log_ref[0, slot : slot + 1, :] = best + jnp.log(total)


def attend(lead, low, high, q, k, v, docs, buckets, rel):
    rows, width = q.shape
    keys = k.shape[0]
    pairs = width // BLK
    blocks = docs.shape[0]
    slots = rows // BLK
    reach = blocks // 2
    smem = pl.BlockSpec(memory_space=pltpu.SMEM)

    def cols(count):
        return pl.BlockSpec((count, BLK), lambda i: (0, i))

    def whole(array):
        return pl.BlockSpec(array.shape, lambda i: (0,) * array.ndim)

    return pl.pallas_call(
        attend_kernel,
        grid=(pairs,),
        out_shape=(
            jax.ShapeDtypeStruct((rows, width), f32),
            jax.ShapeDtypeStruct((rows, width), bf16),
            jax.ShapeDtypeStruct((pairs, slots, 2 * BLK), f32),
        ),
        in_specs=[
            smem,
            smem,
            smem,
            cols(rows),
            cols(keys),
            cols(keys),
            whole(docs),
            whole(buckets),
            pl.BlockSpec((1,) + rel.shape[1:], lambda i: (i, 0, 0)),
        ],
        out_specs=(
            cols(rows),
            cols(rows),
            pl.BlockSpec((1, slots, 2 * BLK), lambda i: (i, 0, 0)),
        ),
        scratch_shapes=[
            pltpu.VMEM((keys, BLK), bf16),
            pltpu.VMEM((keys, BLK), bf16),
            pltpu.VMEM((2 * reach + 1, BLK, 2 * BLK), f32),
            pltpu.VMEM((BLK, keys), bf16),
            pltpu.VMEM((blocks, BLK, 2 * BLK), f32),
        ],
        compiler_params=pltpu.CompilerParams(vmem_limit_bytes=VMEM_CAP),
        cost_estimate=pl.CostEstimate(flops=25_000_000_000, transcendentals=0, bytes_accessed=1 << 23),
        name="attend",
    )(lead, low, high, q, k, v, docs, buckets, rel)


def attend_back_kernel(
    lead_ref,
    low_ref,
    high_ref,
    q_ref,
    k_ref,
    v_ref,
    g_ref,
    out_ref,
    log_ref,
    docs_ref,
    buckets_ref,
    rel_ref,
    dq_ref,
    dk_ref,
    dv_ref,
    dbias_ref,
    known,
    barred,
    tiles,
    k_turned,
    dk_acc,
    dv_acc,
    d_tiles,
):
    reach = tiles.shape[0] // 2
    count = tiles.shape[0]
    blocks = docs_ref.shape[0]
    slots = q_ref.shape[0] // BLK
    half = BLK // 2

    @pl.when(pl.program_id(0) == 0)
    def _():
        doc_operands(docs_ref, known, barred)

    bias_tiles(buckets_ref, rel_ref.at[0], tiles)
    k_turned[...] = jnp.transpose(k_ref[...])
    dk_acc[...] = jnp.zeros_like(dk_acc)
    dv_acc[...] = jnp.zeros_like(dv_acc)
    d_tiles[...] = jnp.zeros_like(d_tiles)
    sub = lax.broadcasted_iota(jnp.int32, (8, BLK), 0)
    lane = lane_iota(8)
    chooser = jnp.where((lane // half) == sub, 1.0, 0.0)
    for slot in range(slots):
        block = lead_ref[slot]
        first = low_ref[slot]
        last = high_ref[slot]
        base = pl.multiple_of(block * BLK, BLK)
        own = slice(slot * BLK, (slot + 1) * BLK)
        q_two = two_heads(q_ref[own, :])
        g_two = two_heads(g_ref[own, :])
        bar = barred[pl.ds(base, BLK), :]
        q_full = jnp.concatenate([q_two, jnp.concatenate([bar, bar], axis=0)], axis=1)
        product = g_ref[own, :].astype(f32) * out_ref[own, :]
        delta = lax.dot_general(chooser, product, NT, precision=HIGH, preferred_element_type=f32)
        delta = jnp.concatenate([delta[0:1, :], delta[1:2, :]], axis=1)
        log_total = log_ref[0, slot : slot + 1, :]

        def step(kb, dq):
            rows = pl.ds(pl.multiple_of(kb * BLK, BLK), BLK)
            k_full = jnp.concatenate([k_ref[rows, :], known[rows, :]], axis=1)
            value = lax.dot_general(k_full, q_full, NT, preferred_element_type=f32)
            prob = jnp.exp(value + tiles[kb - block + reach] - log_total)
            d_prob = lax.dot_general(v_ref[rows, :], g_two, NT, preferred_element_type=f32)
            d_score = prob * (d_prob - delta)
            d_tiles[kb - block + reach] = d_tiles[kb - block + reach] + d_score
            d_low = d_score.astype(bf16)
            dv_acc[rows, :] = dv_acc[rows, :] + jnp.dot(
                prob.astype(bf16), g_two, preferred_element_type=f32
            )
            dk_acc[rows, :] = dk_acc[rows, :] + jnp.dot(
                d_low, q_two, preferred_element_type=f32
            )
            return dq + jnp.dot(k_turned[:, rows], d_low, preferred_element_type=f32)

        dq = lax.fori_loop(first, last, step, jnp.zeros((BLK, 2 * BLK), f32))
        both = jnp.concatenate([dq[:half, :BLK], dq[half:, BLK:]], axis=0)
        dq_ref[own, :] = jnp.transpose(both).astype(bf16)
    dk_ref[...] = dk_acc[...].astype(bf16)
    dv_ref[...] = dv_acc[...].astype(bf16)
    levels = rel_ref.shape[2]
    level = lax.broadcasted_iota(jnp.int32, (levels, 2 * BLK), 0)
    total = jnp.zeros((8, levels), f32)
    pad = jnp.zeros((BLK, BLK), f32)
    mirror = (
        lax.broadcasted_iota(jnp.int32, (BLK, BLK), 0)
        + lax.broadcasted_iota(jnp.int32, (BLK, BLK), 1)
        == BLK - 1
    ).astype(bf16)
    for n in range(count):
        flipped = jnp.dot(mirror, d_tiles[n].astype(bf16), preferred_element_type=f32)
        row = blocks - 1 - (n - reach)
        bucket = jnp.concatenate(
            [buckets_ref[row : row + 1, :], buckets_ref[row + 1 : row + 2, :]], axis=1
        )
        onehot = (level == bucket).astype(f32)
        sums = []
        for head in range(2):
            part = flipped[:, head * BLK : (head + 1) * BLK]
            wide = jnp.concatenate([part, pad], axis=1)
            rolled = pltpu.roll(wide, 0, 1, stride=1, stride_axis=0)
            sums.append(jnp.sum(rolled, axis=0, keepdims=True))
        stacked = jnp.concatenate(sums + [jnp.zeros((6, 2 * BLK), f32)], axis=0)
        total = total + lax.dot_general(
            stacked, onehot, NT, precision=HIGH, preferred_element_type=f32
        )
    dbias_ref[0] = total


def attend_back(lead, low, high, q, k, v, g, out, log, docs, buckets, rel):
    rows, width = q.shape
    keys = k.shape[0]
    pairs = width // BLK
    blocks = docs.shape[0]
    slots = rows // BLK
    reach = blocks // 2
    levels = rel.shape[2]
    smem = pl.BlockSpec(memory_space=pltpu.SMEM)

    def cols(count):
        return pl.BlockSpec((count, BLK), lambda i: (0, i))

    def whole(array):
        return pl.BlockSpec(array.shape, lambda i: (0,) * array.ndim)

    def lead_block(shape):
        return pl.BlockSpec((1,) + shape, lambda i: (i,) + (0,) * len(shape))

    return pl.pallas_call(
        attend_back_kernel,
        grid=(pairs,),
        out_shape=(
            jax.ShapeDtypeStruct((rows, width), bf16),
            jax.ShapeDtypeStruct((keys, width), bf16),
            jax.ShapeDtypeStruct((keys, width), bf16),
            jax.ShapeDtypeStruct((pairs, 8, levels), f32),
        ),
        in_specs=[
            smem,
            smem,
            smem,
            cols(rows),
            cols(keys),
            cols(keys),
            cols(rows),
            cols(rows),
            lead_block((slots, 2 * BLK)),
            whole(docs),
            whole(buckets),
            lead_block(rel.shape[1:]),
        ],
        out_specs=(cols(rows), cols(keys), cols(keys), lead_block((8, levels))),
        scratch_shapes=[
            pltpu.VMEM((keys, BLK), bf16),
            pltpu.VMEM((keys, BLK), bf16),
            pltpu.VMEM((2 * reach + 1, BLK, 2 * BLK), f32),
            pltpu.VMEM((BLK, keys), bf16),
            pltpu.VMEM((keys, BLK), f32),
            pltpu.VMEM((keys, BLK), f32),
            pltpu.VMEM((2 * reach + 1, BLK, 2 * BLK), f32),
        ],
        compiler_params=pltpu.CompilerParams(vmem_limit_bytes=VMEM_CAP),
        cost_estimate=pl.CostEstimate(flops=35_000_000_000, transcendentals=0, bytes_accessed=1 << 23),
        name="attend_back",
    )(lead, low, high, q, k, v, g, out, log, docs, buckets, rel)


def attention_tables(docs, rel_bucket, rel_bias, lead):
    blocks = docs.shape[0]
    starts = docs[:, 0]
    ends = docs[:, -1]
    mine = (lead[:, None] == jnp.arange(blocks)[None, :]).astype(jnp.int32)
    own_start = jnp.sum(mine * starts[None, :], axis=1)
    own_end = jnp.sum(mine * ends[None, :], axis=1)
    low = jnp.sum((ends[None, :] < own_start[:, None]).astype(jnp.int32), axis=1)
    high = jnp.sum((starts[None, :] <= own_end[:, None]).astype(jnp.int32), axis=1)
    buckets = jnp.pad(jnp.flip(rel_bucket), (0, 1)).reshape(2 * blocks, BLK)
    levels, heads = rel_bias.shape
    rel = jnp.transpose(rel_bias).reshape(heads // 2, 2, levels)
    return low, high, buckets, rel


def bits_of(count):
    bits = count.bit_length() - 1
    assert 1 << bits == count
    return bits


def swap(value, axis, bit):
    count = lax.axis_size(axis)
    return lax.ppermute(value, axis, [(i, i ^ (1 << bit)) for i in range(count)])


def ordered(mine, other, index, bit, axis=0):
    upper = ((index >> bit) & 1) == 1
    return jnp.concatenate(
        [jnp.where(upper, other, mine), jnp.where(upper, mine, other)], axis=axis
    )


def gather_small(value, axis):
    index = lax.axis_index(axis)
    value = value[None]
    for bit in range(bits_of(lax.axis_size(axis))):
        value = ordered(value, swap(value, axis, bit), index, bit)
    return value


def gather_rows(shard, axis):
    count = lax.axis_size(axis)
    index = lax.axis_index(axis)
    parts = [(0, shard)]
    for bit in reversed(range(bits_of(count))):
        parts = parts + [(j | (1 << bit), swap(part, axis, bit)) for j, part in parts]
    rows = shard.shape[0]
    result = jnp.zeros((rows * count,) + shard.shape[1:], shard.dtype)
    for j, part in parts:
        result = lax.dynamic_update_slice_in_dim(result, part, (index ^ j) * rows, axis=0)
    return result


def add_low(left, right):
    return (left.astype(f32) + right.astype(f32)).astype(bf16)


def piece(value, index, dim=0):
    return lax.dynamic_index_in_dim(value, index, dim, keepdims=False)


def scatter_step(value, axis, bit, dim):
    own = (lax.axis_index(axis) >> bit) & 1
    other = swap(piece(value, 1 - own, dim), axis, bit)
    return add_low(piece(value, own, dim), other)


def rest_sum(value, axis):
    count = lax.axis_size(axis)
    index = lax.axis_index(axis)
    mine = index // 2
    total = piece(value, mine).astype(f32)
    for j in range(1, count // 2):
        pairs = [(i, ((i // 2) ^ j) * 2 + i % 2) for i in range(count)]
        total = total + lax.ppermute(piece(value, mine ^ j), axis, pairs).astype(f32)
    return total.astype(bf16)


def reduce_rows(value, scatter_axis, sum_axis):
    count = lax.axis_size(scatter_axis)
    bits = bits_of(count)
    rows = value.shape[0] // count
    value = value.reshape((2,) * bits + (rows,) + value.shape[1:])
    value = yield value
    for bit in range(bits):
        value = yield scatter_step(value, scatter_axis, bit, bits - 1 - bit)
    count = lax.axis_size(sum_axis)
    value = value.reshape((count // 2, 2, rows // count) + value.shape[1:])
    value = yield scatter_step(value, sum_axis, 0, 1)
    value = yield rest_sum(value, sum_axis)
    yield lax.all_gather(value, sum_axis, axis=0, tiled=True)


class Chain:
    def __init__(self, value):
        self.steps = reduce_rows(value, "fsdp", "ctx")
        self.value = next(self.steps)

    def advance(self, value):
        self.value = self.steps.send(value)

    def finish(self):
        for value in self.steps_left():
            self.value = value
        return self.value.astype(f32)

    def steps_left(self):
        while True:
            try:
                yield self.steps.send(self.value)
            except StopIteration:
                return


def gate(anchor, *chains):
    joined = lax.optimization_barrier((anchor,) + tuple(chain.value for chain in chains))
    for chain, value in zip(chains, joined[1:]):
        chain.advance(value)
    return joined[0]


def reduce_small(value):
    fsdp_bits = bits_of(lax.axis_size("fsdp"))
    count = lax.axis_size("ctx")
    rows, width = value.shape
    value = value.reshape(2, count // 2, 2 * rows // (2 * count), width)
    value = scatter_step(value, "fsdp", 0, 0)
    value = rest_sum(value, "ctx")
    value = add_low(value, swap(value, "ctx", 0))
    for bit in range(1, fsdp_bits):
        value = add_low(value, swap(value, "fsdp", bit))
    mine = lax.axis_index("ctx") // 2
    parts = [(0, value)]
    for j in range(1, count // 2):
        pairs = [(i, ((i // 2) ^ j) * 2 + i % 2) for i in range(count)]
        parts.append((j, lax.ppermute(value, "ctx", pairs)))
    whole = jnp.zeros((count // 2,) + value.shape, value.dtype)
    for j, part in parts:
        whole = lax.dynamic_update_index_in_dim(whole, part, mine ^ j, 0)
    whole = whole.reshape((rows // 2, width))
    return ordered(whole, swap(whole, "fsdp", 0), lax.axis_index("fsdp"), 0)


def rms_scale(values, gain_vec):
    return values * lax.rsqrt(jnp.mean(values * values, axis=-1, keepdims=True) + 1e-06) * gain_vec


def gelu_product(gate_pre, up_pre):
    return jax.nn.gelu(gate_pre, approximate=True) * up_pre


def local(
    byte_ids,
    doc_ids,
    rel_bucket,
    table,
    conv_w,
    score_w,
    gain_one,
    gain_two,
    rel_bias,
    query_master,
    key_master,
    value_master,
    out_master,
    gate_master,
    up_master,
    down_master,
    out_cotangent,
):
    ctx_count = lax.axis_size("ctx")
    ctx_index = lax.axis_index("ctx")
    seq_count, byte_count = byte_ids.shape
    total_bytes = byte_count * ctx_count
    width = table.shape[1]
    vocab = table.shape[0]
    hidden_width = gate_master.shape[1]
    levels, heads = rel_bias.shape
    share = ctx_count // seq_count
    assert share * seq_count == ctx_count and byte_count == 2 * BLK
    seq = ctx_index // share
    part = ctx_index % share
    near = [seq ^ slot for slot in range(seq_count)]
    lead = jnp.stack([share * other + part for other in near]).astype(jnp.int32)
    rows = seq_count * BLK

    qkv_low = jnp.concatenate([query_master, key_master, value_master], axis=1).astype(bf16)
    both = jnp.stack([byte_ids, doc_ids], axis=1)
    both, qkv_low = lax.optimization_barrier((both, qkv_low))
    qkv = gather_rows(qkv_low, "fsdp")
    both = gather_small(both, "ctx")
    both, out_master, gate_master, up_master, down_master = lax.optimization_barrier(
        (both, out_master, gate_master, up_master, down_master)
    )
    both = piece(both, seq, 1)
    ids = both[:, 0].reshape(total_bytes)
    docs = both[:, 1, ::2]
    ogu_low = jnp.concatenate([out_master, gate_master, up_master], axis=1).astype(bf16)
    down_low = down_master.astype(bf16)
    ogu = gather_rows(ogu_low, "fsdp")
    down_weight = gather_rows(down_low, "fsdp")
    query_weight = qkv[:, :width]
    key_weight = qkv[:, width : 2 * width]
    value_weight = qkv[:, 2 * width :]
    out_weight = ogu[:, :width]
    gate_up = ogu[:, width:]

    def to_owner(block, slot):
        if slot == 0:
            return block
        pairs = []
        for c in range(ctx_count):
            pairs.append((c, ((c // share) ^ slot) * share + c % share))
        return lax.ppermute(block, "ctx", pairs)

    cotangent = jnp.concatenate(
        [
            to_owner(lax.dynamic_index_in_dim(out_cotangent, near[s], 1, keepdims=False), s)
            for s in range(seq_count)
        ],
        axis=0,
    )

    phases = phase_ids(ids, total_bytes)
    table_wide = jnp.pad(table, ((0, -vocab % LANE), (0, 0)))
    tokens, norm_one, conv, mix = byte_forward(
        phases, table_wide, conv_w, score_w, gain_one, total_bytes
    )

    def own_rows(array):
        return jnp.concatenate(
            [lax.dynamic_slice_in_dim(array, lead[s] * BLK, BLK, 0) for s in range(seq_count)],
            axis=0,
        )

    tokens_own = own_rows(tokens)
    norm_own = own_rows(norm_one)

    queries = jnp.dot(norm_own, query_weight, preferred_element_type=f32).astype(bf16)
    keys = jnp.dot(norm_one, key_weight, preferred_element_type=f32).astype(bf16)
    values = jnp.dot(norm_one, value_weight, preferred_element_type=f32).astype(bf16)
    low, high, buckets, rel = attention_tables(docs, rel_bucket, rel_bias, lead)
    attended, attended_low, log_total = attend(
        lead, low, high, queries, keys, values, docs, buckets, rel
    )

    resid = tokens_own + jnp.dot(attended_low, out_weight, preferred_element_type=f32)
    norm_two = rms_scale(resid, gain_two).astype(bf16)
    gate_pre = jnp.dot(norm_two, gate_up[:, :hidden_width], preferred_element_type=f32)
    up_pre = jnp.dot(norm_two, gate_up[:, hidden_width:], preferred_element_type=f32)
    hidden = gelu_product(gate_pre, up_pre).astype(bf16)
    output = (resid + jnp.dot(hidden, down_weight, preferred_element_type=f32)).astype(bf16)
    output = output.reshape(seq_count, BLK, width)
    arrived = jnp.stack([to_owner(output[s], s) for s in range(seq_count)])
    output = jnp.stack(
        [lax.dynamic_index_in_dim(arrived, seq ^ s, 0, keepdims=False) for s in range(seq_count)],
        axis=1,
    )

    grad_down = jnp.einsum("rf,rd->fd", hidden, cotangent, preferred_element_type=f32)
    down_chain = Chain(grad_down.astype(bf16))
    cotangent = gate(cotangent, down_chain)
    d_hidden = jnp.einsum("rd,fd->rf", cotangent, down_weight, preferred_element_type=f32)
    _, gelu_pull = jax.vjp(gelu_product, gate_pre, up_pre)
    d_gate, d_up = gelu_pull(d_hidden)
    d_both = jnp.concatenate([d_gate.astype(bf16), d_up.astype(bf16)], axis=1)
    d_both = gate(d_both, down_chain)
    grad_gu = jnp.einsum("rd,rf->df", norm_two, d_both, preferred_element_type=f32)
    gu_chain = Chain(grad_gu.astype(bf16))
    d_both = gate(d_both, gu_chain)
    d_norm_two = jnp.einsum("rf,df->rd", d_both, gate_up, preferred_element_type=f32)
    _, norm_pull_two = jax.vjp(rms_scale, resid, gain_two)
    d_resid_norm, grad_gain_two = norm_pull_two(d_norm_two)
    d_resid = cotangent.astype(f32) + d_resid_norm
    d_branch = d_resid.astype(bf16)
    d_attended = jnp.einsum("rd,ad->ra", d_branch, out_weight, preferred_element_type=f32)
    d_attended = gate(d_attended.astype(bf16), gu_chain, down_chain)

    d_queries, d_keys, d_values, d_bias = attend_back(
        lead,
        low,
        high,
        queries,
        keys,
        values,
        d_attended,
        attended,
        log_total,
        docs,
        buckets,
        rel,
    )
    d_queries = gate(d_queries, gu_chain, down_chain)
    grad_qkv = jnp.concatenate(
        [
            jnp.einsum("rd,ra->da", norm_own, d_queries, preferred_element_type=f32),
            jnp.einsum("rd,ra->da", norm_one, d_keys, preferred_element_type=f32),
            jnp.einsum("rd,ra->da", norm_one, d_values, preferred_element_type=f32),
            jnp.einsum("ra,rd->ad", attended_low, d_branch, preferred_element_type=f32),
        ],
        axis=1,
    )
    qkv_chain = Chain(grad_qkv.astype(bf16))
    d_queries, d_keys, d_values = gate(
        (d_queries, d_keys, d_values), qkv_chain, down_chain
    )
    d_norm_query = jnp.einsum("ra,da->rd", d_queries, query_weight, preferred_element_type=f32)
    d_norm_one = jnp.einsum(
        "ra,da->rd", d_keys, key_weight, preferred_element_type=f32
    ) + jnp.einsum("ra,da->rd", d_values, value_weight, preferred_element_type=f32)
    for s in range(seq_count):
        start = lead[s] * BLK
        old = lax.dynamic_slice_in_dim(d_norm_one, start, BLK, 0)
        d_norm_one = lax.dynamic_update_slice_in_dim(
            d_norm_one, old + d_norm_query[s * BLK : (s + 1) * BLK], start, 0
        )
    d_norm_one = gate(d_norm_one, qkv_chain, gu_chain)

    vocab_rows = -(-vocab // 16) * 16
    small = byte_backward(
        lead,
        phases,
        tokens,
        d_norm_one,
        d_resid.reshape(seq_count, BLK, width),
        conv,
        mix,
        table_wide,
        vocab_rows,
        conv_w,
        score_w,
        gain_one,
        total_bytes,
    )
    bias_grad = jnp.transpose(d_bias[:, :2].reshape(heads, levels)).reshape(1, levels * heads)
    bias_grad = jnp.pad(bias_grad, ((0, 0), (0, width - levels * heads)))
    small = jnp.concatenate([small[: vocab_rows + 6], grad_gain_two[None], bias_grad], axis=0)
    small = jnp.pad(small, ((0, -small.shape[0] % (8 * ctx_count)), (0, 0))).astype(bf16)
    small = gate(small, qkv_chain, gu_chain)
    small = reduce_small(small).astype(f32)
    grad_down = down_chain.finish()
    grad_gu = gu_chain.finish()
    grad_qkv = qkv_chain.finish()
    top = vocab_rows
    return (
        output,
        small[:vocab],
        small[top : top + 4],
        small[top + 4],
        small[top + 5],
        small[top + 6],
        small[top + 7, : levels * heads].reshape(levels, heads),
        grad_qkv[:, :width],
        grad_qkv[:, width : 2 * width],
        grad_qkv[:, 2 * width : 3 * width],
        grad_qkv[:, 3 * width :],
        grad_gu[:, :hidden_width],
        grad_gu[:, hidden_width:],
        grad_down,
    )


def solution(mesh):
    placed = (
        P("fsdp", "ctx"),
        P("fsdp", "ctx"),
        P(),
        P(),
        P(),
        P(),
        P(),
        P(),
        P(),
        P("fsdp", None),
        P("fsdp", None),
        P("fsdp", None),
        P("fsdp", None),
        P("fsdp", None),
        P("fsdp", None),
        P("fsdp", None),
        P("ctx", "fsdp", None),
    )
    return jax.shard_map(
        local,
        mesh=mesh,
        in_specs=placed,
        out_specs=(
            P("ctx", "fsdp", None),
            P(),
            P(),
            P(),
            P(),
            P(),
            P(),
            P("fsdp", None),
            P("fsdp", None),
            P("fsdp", None),
            P("fsdp", None),
            P("fsdp", None),
            P("fsdp", None),
            P("fsdp", None),
        ),
        check_vma=False,
    )
```

```python
import functools

import jax
import jax.numpy as jnp
from jax import lax
from jax.experimental import pallas as pl
from jax.experimental.pallas import tpu as pltpu
from jax.sharding import PartitionSpec as P

f32 = jnp.float32
bf16 = jnp.bfloat16
LANE = 128
BLK = 128
VMEM_CAP = 60 * 1024 * 1024
HIGH = lax.Precision.HIGHEST
NT = (((1,), (1,)), ((), ()))
NN = (((1,), (0,)), ((), ()))
LIGHT = pl.CostEstimate(flops=1, transcendentals=0, bytes_accessed=1)


def lane_iota(rows):
    return lax.broadcasted_iota(jnp.int32, (rows, LANE), 1)


def block_sum(value, width, lane):
    def ahead(v, n):
        return pltpu.roll(v, LANE - n, 1)

    def behind(v, n):
        return pltpu.roll(v, n, 1)

    if width == 1:
        return value
    if width == 3:
        lead = value + ahead(value, 1) + ahead(value, 2)
        phase = lane % 3
        return jnp.where(phase == 0, lead, jnp.where(phase == 1, behind(lead, 1), behind(lead, 2)))
    pair = value + jnp.where(lane % 2 == 0, ahead(value, 1), behind(value, 1))
    if width == 2:
        return pair
    return pair + jnp.where(lane % 4 < 2, ahead(pair, 2), behind(pair, 2))


def pick(value, lane_index):
    return value[:, lane_index : lane_index + 1]


def byte_forward_kernel(
    total_bytes,
    seq_ref,
    lead_ref,
    both_ref,
    table_ref,
    conv_w_ref,
    score_ref,
    gain_ref,
    tok_ref,
    norm_ref,
    norm_own_ref,
    conv_ref,
    mix_ref,
    ids_ref,
    known_ref,
    barred_ref,
    hi_ref,
    lo_ref,
    emb,
    flat,
    spread,
):
    groups = conv_ref.shape[1]
    width = conv_ref.shape[2]
    tiles = width // LANE
    token_count = norm_ref.shape[0]
    vocab_pad = table_ref.shape[0]
    row_lanes = ids_ref.shape[1]
    seq = seq_ref[0]
    high = table_ref[...].astype(bf16)
    hi_ref[...] = high
    lo_ref[...] = (table_ref[...] - high.astype(f32)).astype(bf16)
    lane_f = lane_iota(BLK).astype(f32)
    chunk_bytes = both_ref.shape[3]

    def lay(kind, first):
        for block in range(both_ref.shape[0]):
            row = both_ref[block, seq, kind : kind + 1, :].astype(f32)
            for half in range(chunk_bytes // LANE):
                part = jnp.broadcast_to(row[:, half * LANE : (half + 1) * LANE], (LANE, LANE))
                start = first + block * chunk_bytes + half * LANE
                spread[start : start + LANE, :] = jnp.transpose(part)

    lay(1, 0)
    for block in range(token_count // BLK):
        docs = spread[pl.ds(block * 2 * BLK, BLK, stride=2), :]
        same = docs == lane_f
        rows = slice(block * BLK, (block + 1) * BLK)
        known_ref[rows, :] = same.astype(bf16)
        barred_ref[rows, :] = jnp.where(same | (lane_f >= 16.0), 0.0, -1e30).astype(bf16)
    lay(0, 16)
    none = jnp.full((16, LANE), -1.0, f32)
    spread[0:16, :] = none
    tail = spread.shape[0] - total_bytes - 16
    spread[total_bytes + 16 :, :] = jnp.full((tail, LANE), -1.0, f32)
    lane_g = lane_iota(groups).astype(f32)
    for r in range(15):
        here = spread[pl.ds(13 + r, row_lanes, stride=12), :]
        turned = [
            jnp.transpose(here[n * LANE : (n + 1) * LANE, :])[0:1, :]
            for n in range(row_lanes // LANE)
        ]
        ids_ref[r : r + 1, :] = jnp.concatenate(turned, axis=1)
        onehot = jnp.concatenate(
            [
                (here[0:groups, :] == lane_g + n * LANE).astype(bf16)
                for n in range(vocab_pad // LANE)
            ],
            axis=1,
        )
        emb[r] = jnp.dot(onehot, hi_ref[...], preferred_element_type=f32) + jnp.dot(
            onehot, lo_ref[...], preferred_element_type=f32
        )
    ids_ref[15:16, :] = jnp.full((1, row_lanes), -1.0, f32)
    lane = lane_iota(8)

    def chunk(i, masked):
        r0 = pl.multiple_of(i * 8, 8)
        rows = pl.ds(r0, 8)
        sums = [jnp.zeros((8, LANE), f32) for _ in range(12)]
        for tile in range(tiles):
            cols = slice(tile * LANE, (tile + 1) * LANE)
            taps = [conv_w_ref[k : k + 1, cols] for k in range(4)]
            piece = [emb[r, rows, cols] for r in range(15)]
            score = score_ref[0:1, cols]
            for r in range(12):
                value = (
                    piece[r] * taps[0]
                    + piece[r + 1] * taps[1]
                    + piece[r + 2] * taps[2]
                    + piece[r + 3] * taps[3]
                )
                if masked:
                    group = r0 + lax.broadcasted_iota(jnp.int32, (8, LANE), 0)
                    value = jnp.where(group * 12 + r < total_bytes, value, 0.0)
                conv_ref[r, rows, cols] = value
                sums[r] = sums[r] + value * score
        packed = jnp.zeros((8, LANE), f32)
        for r in range(12):
            packed = jnp.where(lane == r, jnp.sum(sums[r], axis=1, keepdims=True), packed)
        logits = [block_sum(packed, b, lane) * (1.0 / b) for b in range(1, 5)]
        best = jnp.maximum(jnp.maximum(logits[0], logits[1]), jnp.maximum(logits[2], logits[3]))
        parts = [jnp.exp(value - best) for value in logits]
        total = parts[0] + parts[1] + parts[2] + parts[3]
        mix = [part / total for part in parts]
        for b in range(4):
            mix_ref[b, rows, :] = mix[b]
        half_one = mix[0] * 0.5
        pair_two = block_sum(mix[1], 2, lane) * 0.25
        single_three = mix[2] * (1.0 / 6.0)
        pair_three = block_sum(mix[2], 2, lane) * (1.0 / 6.0)
        pair_four = block_sum(mix[3], 2, lane) * 0.125
        coef_one = [pick(half_one, r) for r in range(12)]
        coef_two = [pick(pair_two, 2 * j) for j in range(6)]
        coef_four = [pick(pair_four, 2 * j) for j in range(6)]
        coef_three = []
        for j in range(6):
            if j % 3 == 1:
                coef_three.append((pick(single_three, 2 * j), pick(single_three, 2 * j + 1)))
            else:
                coef_three.append((pick(pair_three, 2 * j), None))
        for tile in range(tiles):
            cols = slice(tile * LANE, (tile + 1) * LANE)
            conv = [conv_ref[r, rows, cols] for r in range(12)]
            two = [conv[2 * j] + conv[2 * j + 1] for j in range(6)]
            three = [conv[3 * q] + conv[3 * q + 1] + conv[3 * q + 2] for q in range(4)]
            four = [two[2 * q] + two[2 * q + 1] for q in range(3)]
            for j in range(6):
                a, b = 2 * j, 2 * j + 1
                value = coef_one[a] * conv[a] + coef_one[b] * conv[b]
                value = value + coef_two[j] * two[j] + coef_four[j] * four[j // 2]
                value = value + coef_three[j][0] * three[a // 3]
                if j % 3 == 1:
                    value = value + coef_three[j][1] * three[b // 3]
                flat[tile, pl.ds(6 * r0 + j, 8, stride=6), :] = value

    whole = (total_bytes // 12) // 8

    def plain(i, carry):
        chunk(i, False)
        return carry

    lax.fori_loop(0, whole, plain, 0)
    for i in range(whole, groups // 8):
        chunk(i, True)

    def norm(i, carry):
        rows = pl.ds(pl.multiple_of(i * 16, 16), 16)
        value = jnp.concatenate([flat[tile, rows, :] for tile in range(tiles)], axis=1)
        tok_ref[rows, :] = value
        scale = lax.rsqrt(jnp.mean(value * value, axis=1, keepdims=True) + 1e-06)
        norm_ref[rows, :] = (value * scale * gain_ref[...]).astype(bf16)
        return carry

    lax.fori_loop(0, token_count // 16, norm, 0)
    for slot in range(norm_own_ref.shape[0] // BLK):
        start = pl.multiple_of(lead_ref[slot] * BLK, BLK)
        norm_own_ref[slot * BLK : (slot + 1) * BLK, :] = norm_ref[pl.ds(start, BLK), :]


def byte_forward(seq, lead, both, table, conv_w, score_w, gain_one, total_bytes):
    width = conv_w.shape[1]
    token_count = total_bytes // 2
    least = -(-total_bytes // 12)
    groups = -(-least // 16) * 16
    row_lanes = -(-least // LANE) * LANE
    smem = pl.BlockSpec(memory_space=pltpu.SMEM)
    vmem = pl.BlockSpec(memory_space=pltpu.VMEM)
    return pl.pallas_call(
        functools.partial(byte_forward_kernel, total_bytes),
        out_shape=(
            jax.ShapeDtypeStruct((token_count, width), f32),
            jax.ShapeDtypeStruct((token_count, width), bf16),
            jax.ShapeDtypeStruct((lead.shape[0] * BLK, width), bf16),
            jax.ShapeDtypeStruct((12, groups, width), f32),
            jax.ShapeDtypeStruct((4, groups, LANE), f32),
            jax.ShapeDtypeStruct((16, row_lanes), f32),
            jax.ShapeDtypeStruct((token_count, LANE), bf16),
            jax.ShapeDtypeStruct((token_count, LANE), bf16),
        ),
        in_specs=[smem, smem] + [vmem] * 5,
        scratch_shapes=[
            pltpu.VMEM(table.shape, bf16),
            pltpu.VMEM(table.shape, bf16),
            pltpu.VMEM((15, groups, width), f32),
            pltpu.VMEM((width // LANE, 6 * groups, LANE), f32),
            pltpu.VMEM((12 * row_lanes + 32, LANE), f32),
        ],
        compiler_params=pltpu.CompilerParams(vmem_limit_bytes=VMEM_CAP),
        cost_estimate=LIGHT,
        name="byte_forward",
    )(
        seq,
        lead,
        both,
        table,
        conv_w,
        score_w.reshape(1, width),
        gain_one.reshape(1, width),
    )


def byte_backward_kernel(
    total_bytes,
    first_ref,
    ids_ref,
    tok_ref,
    dnorm_ref,
    dres_ref,
    conv_ref,
    mix_ref,
    table_ref,
    conv_w_ref,
    score_ref,
    gain_ref,
    out_ref,
    dtok,
    dconv,
    onehot,
):
    groups = conv_ref.shape[1]
    width = conv_ref.shape[2]
    tiles = width // LANE
    token_count = dnorm_ref.shape[0]
    vocab_rows = onehot.shape[0]
    lanes = ids_ref.shape[1]
    gain = gain_ref[...]

    def norm_back(i, acc):
        rows = pl.ds(pl.multiple_of(i * 8, 8), 8)
        value = tok_ref[rows, :]
        grad = dnorm_ref[rows, :]
        scale = lax.rsqrt(jnp.mean(value * value, axis=1, keepdims=True) + 1e-06)
        grad_gain = grad * gain
        inner = jnp.mean(value * grad_gain, axis=1, keepdims=True)
        total = 0.5 * scale * grad_gain - value * (0.5 * scale * scale * scale * inner)
        for tile in range(tiles):
            dtok[tile, rows, :] = total[:, tile * LANE : (tile + 1) * LANE]
        return acc + grad * value * scale

    gain_acc = lax.fori_loop(0, token_count // 8, norm_back, jnp.zeros((8, width), f32))
    rest = dtok.shape[1] - token_count
    dtok[:, token_count:, :] = jnp.zeros((tiles, rest, LANE), f32)
    for slot in range(dres_ref.shape[0]):
        start = pl.multiple_of(first_ref[slot] * BLK, BLK)

        def add(i, carry, slot=slot, start=start):
            r = pl.multiple_of(i * 8, 8)
            rows = pl.ds(start + r, 8)
            more = 0.5 * dres_ref[slot, pl.ds(r, 8), :]
            for tile in range(tiles):
                dtok[tile, rows, :] = (
                    dtok[tile, rows, :] + more[:, tile * LANE : (tile + 1) * LANE]
                )
            return carry

        lax.fori_loop(0, BLK // 8, add, 0)
    vocab = lax.broadcasted_iota(jnp.int32, (vocab_rows, lanes), 0).astype(f32)
    for r in range(15):
        onehot[:, r * lanes : (r + 1) * lanes] = (vocab == ids_ref[r : r + 1, :]).astype(bf16)
    for r in range(12):
        dconv[r * lanes + groups : (r + 1) * lanes, :] = jnp.zeros((lanes - groups, width), bf16)
    lane = lane_iota(8)

    def scalars(r0):
        rows = pl.ds(r0, 8)
        one = [jnp.zeros((8, LANE), f32) for _ in range(12)]
        cross = [jnp.zeros((8, LANE), f32) for _ in range(6)]
        tri = [jnp.zeros((8, LANE), f32) for _ in range(8)]
        for tile in range(tiles):
            cols = slice(tile * LANE, (tile + 1) * LANE)
            conv = [conv_ref[r, rows, cols] for r in range(12)]
            grad = [dtok[tile, pl.ds(6 * r0 + j, 8, stride=6), :] for j in range(6)]
            two = [conv[2 * j] + conv[2 * j + 1] for j in range(6)]
            three = [conv[3 * q] + conv[3 * q + 1] + conv[3 * q + 2] for q in range(4)]
            for r in range(12):
                one[r] = one[r] + conv[r] * grad[r // 2]
            slot = 0
            for j in range(6):
                cross[j] = cross[j] + two[j ^ 1] * grad[j]
                for q in sorted({(2 * j) // 3, (2 * j + 1) // 3}):
                    tri[slot] = tri[slot] + three[q] * grad[j]
                    slot += 1
        inner_one = jnp.zeros((8, LANE), f32)
        for r in range(12):
            inner_one = jnp.where(lane == r, jnp.sum(one[r], axis=1, keepdims=True), inner_one)
        inner_cross = jnp.zeros((8, LANE), f32)
        for j in range(6):
            inner_cross = jnp.where(
                lane // 2 == j, jnp.sum(cross[j], axis=1, keepdims=True), inner_cross
            )
        inner_three = jnp.zeros((8, LANE), f32)
        slot = 0
        for j in range(6):
            for q in sorted({(2 * j) // 3, (2 * j + 1) // 3}):
                here = (lane // 2 == j) & (lane // 3 == q)
                inner_three = jnp.where(
                    here, jnp.sum(tri[slot], axis=1, keepdims=True), inner_three
                )
                slot += 1
        inner_two = block_sum(inner_one, 2, lane)
        mix = [mix_ref[b, rows, :] for b in range(4)]
        d_mix = [
            inner_one,
            inner_two * 0.5,
            inner_three * (1.0 / 3.0),
            (inner_two + inner_cross) * 0.25,
        ]
        mean = mix[0] * d_mix[0] + mix[1] * d_mix[1] + mix[2] * d_mix[2] + mix[3] * d_mix[3]
        d_logit = [mix[b] * (d_mix[b] - mean) for b in range(4)]
        d_logit = [jnp.where(lane < 12, value, 0.0) for value in d_logit]
        slope = d_logit[0]
        for b in range(2, 5):
            slope = slope + block_sum(d_logit[b - 1], b, lane) * (1.0 / b)
        pair_two = block_sum(mix[1], 2, lane) * 0.5
        single_three = mix[2] * (1.0 / 3.0)
        pair_three = block_sum(mix[2], 2, lane) * (1.0 / 3.0)
        pair_four = block_sum(mix[3], 2, lane) * 0.25
        return mix[0], pair_two, single_three, pair_three, pair_four, slope

    def spread(r0, coefs, tile, masked, score_acc):
        one, pair_two, single_three, pair_three, pair_four, slope = coefs
        rows = pl.ds(r0, 8)
        cols = slice(tile * LANE, (tile + 1) * LANE)
        grad = [dtok[tile, pl.ds(6 * r0 + j, 8, stride=6), :] for j in range(6)]
        score = score_ref[0:1, cols]
        four = [
            pick(pair_four, 4 * q) * grad[2 * q] + pick(pair_four, 4 * q + 2) * grad[2 * q + 1]
            for q in range(3)
        ]
        three = []
        for q in range(4):
            a = 3 * q
            if a % 2 == 0:
                three.append(
                    pick(pair_three, a) * grad[a // 2]
                    + pick(single_three, a + 2) * grad[a // 2 + 1]
                )
            else:
                three.append(
                    pick(single_three, a) * grad[a // 2]
                    + pick(pair_three, a + 1) * grad[a // 2 + 1]
                )
        result = []
        for r in range(12):
            weight = pick(slope, r)
            own = (pick(one, r) + pick(pair_two, r)) * grad[r // 2]
            value = own + three[r // 3] + four[r // 4] + weight * score
            score_acc = score_acc + weight * conv_ref[r, rows, cols]
            if masked:
                group = r0 + lax.broadcasted_iota(jnp.int32, (8, LANE), 0)
                value = jnp.where(group * 12 + r < total_bytes, value, 0.0)
            result.append(value)
        return result, score_acc

    def chunk(i, accs, masked):
        r0 = pl.multiple_of(i * 16, 16)
        r1 = pl.multiple_of(i * 16 + 8, 8)
        low_coefs = scalars(r0)
        high_coefs = scalars(r1)
        new = []
        for tile in range(tiles):
            cols = slice(tile * LANE, (tile + 1) * LANE)
            low, acc = spread(r0, low_coefs, tile, masked, accs[tile])
            high, acc = spread(r1, high_coefs, tile, masked, acc)
            new.append(acc)
            for r in range(12):
                both = jnp.concatenate([low[r], high[r]], axis=0).astype(bf16)
                dconv[pl.ds(pl.multiple_of(r * lanes + r0, 16), 16), cols] = both
        return tuple(new)

    accs = tuple(jnp.zeros((8, LANE), f32) for _ in range(tiles))
    whole = (total_bytes // 12) // 16
    accs = lax.fori_loop(0, whole, lambda i, a: chunk(i, a, False), accs)
    for i in range(whole, groups // 16):
        accs = chunk(i, accs, True)
    tail = [jnp.zeros((1, width), f32) for _ in range(8)]
    for k in range(4):
        part = jnp.dot(
            onehot[:, k * lanes : (k + 12) * lanes], dconv[...], preferred_element_type=f32
        )
        if k == 0:
            out_ref[0:vocab_rows, :] = part * conv_w_ref[k : k + 1, :]
        else:
            out_ref[0:vocab_rows, :] = out_ref[0:vocab_rows, :] + part * conv_w_ref[k : k + 1, :]
        tail[k] = jnp.sum(part * table_ref[0:vocab_rows, :], axis=0, keepdims=True)
    tail[4] = jnp.sum(jnp.concatenate(accs, axis=1), axis=0, keepdims=True)
    tail[5] = jnp.sum(gain_acc, axis=0, keepdims=True)
    out_ref[vocab_rows:, :] = jnp.concatenate(tail, axis=0)


def byte_backward(
    first,
    ids,
    tokens,
    d_norm,
    d_resid,
    conv,
    mix,
    table,
    vocab_rows,
    conv_w,
    score_w,
    gain_one,
    total_bytes,
):
    width = conv.shape[2]
    groups = conv.shape[1]
    lanes = ids.shape[1]
    return pl.pallas_call(
        functools.partial(byte_backward_kernel, total_bytes),
        out_shape=jax.ShapeDtypeStruct((vocab_rows + 8, width), f32),
        in_specs=[pl.BlockSpec(memory_space=pltpu.SMEM)]
        + [pl.BlockSpec(memory_space=pltpu.VMEM)] * 10,
        scratch_shapes=[
            pltpu.VMEM((width // LANE, 6 * groups, LANE), f32),
            pltpu.VMEM((12 * lanes, width), bf16),
            pltpu.VMEM((vocab_rows, 15 * lanes), bf16),
        ],
        compiler_params=pltpu.CompilerParams(vmem_limit_bytes=VMEM_CAP),
        cost_estimate=LIGHT,
        name="byte_backward",
    )(
        first,
        ids,
        tokens,
        d_norm,
        d_resid,
        conv,
        mix,
        table,
        conv_w,
        score_w.reshape(1, width),
        gain_one.reshape(1, width),
    )


def head_mask(value, head):
    half = value.shape[1] // 2
    lane = lax.broadcasted_iota(jnp.int32, value.shape, 1)
    keep = lane < half if head == 0 else lane >= half
    return jnp.where(keep, value, jnp.zeros_like(value))


def two_heads(value):
    return jnp.concatenate([head_mask(value, 0), head_mask(value, 1)], axis=0)


def bias_tiles(buckets_ref, rel_ref, tiles):
    count = tiles.shape[0]
    blocks = buckets_ref.shape[0] // 2
    reach = count // 2
    levels = rel_ref.shape[1]
    level = lax.broadcasted_iota(jnp.int32, (levels, 2 * BLK), 0)
    for n in range(count):
        row = blocks - 1 - (n - reach)
        bucket = jnp.concatenate(
            [buckets_ref[row : row + 1, :], buckets_ref[row + 1 : row + 2, :]], axis=1
        )
        onehot = (level == bucket).astype(f32)
        values = lax.dot_general(
            rel_ref[...], onehot, NN, precision=HIGH, preferred_element_type=f32
        )
        for head in range(2):
            spread = jnp.broadcast_to(values[head : head + 1, :], (BLK, 2 * BLK))
            rolled = pltpu.roll(spread, BLK + 1, 1, stride=1, stride_axis=0)
            tiles[n, :, head * BLK : (head + 1) * BLK] = rolled[:, :BLK]


def attend_kernel(
    lead_ref,
    low_ref,
    high_ref,
    q_ref,
    k_ref,
    v_ref,
    known,
    barred,
    buckets_ref,
    rel_ref,
    out_ref,
    low_out_ref,
    log_ref,
    tiles,
    v_turned,
    held,
):
    reach = tiles.shape[0] // 2
    slots = q_ref.shape[0] // BLK

    bias_tiles(buckets_ref, rel_ref.at[0], tiles)
    v_turned[...] = jnp.transpose(v_ref[...])
    for slot in range(slots):
        block = lead_ref[slot]
        first = low_ref[slot]
        last = high_ref[slot]
        base = pl.multiple_of(block * BLK, BLK)
        q_two = two_heads(q_ref[slot * BLK : (slot + 1) * BLK, :])
        bar = barred[pl.ds(base, BLK), :]
        q_full = jnp.concatenate([q_two, jnp.concatenate([bar, bar], axis=0)], axis=1)

        def score(kb, best):
            rows = pl.ds(pl.multiple_of(kb * BLK, BLK), BLK)
            k_full = jnp.concatenate([k_ref[rows, :], known[rows, :]], axis=1)
            value = lax.dot_general(k_full, q_full, NT, preferred_element_type=f32)
            value = value + tiles[kb - block + reach]
            held[kb - first] = value
            return jnp.maximum(best, jnp.max(value.reshape(BLK // 8, 8, 2 * BLK), axis=0))

        best = lax.fori_loop(first, last, score, jnp.full((8, 2 * BLK), -3e38, f32))
        best = jnp.max(best, axis=0, keepdims=True)

        def gather(kb, state):
            total, accum = state
            weight = jnp.exp(held[kb - first] - best)
            total = total + jnp.sum(weight.reshape(BLK // 8, 8, 2 * BLK), axis=0)
            cols = pl.ds(pl.multiple_of(kb * BLK, BLK), BLK)
            accum = accum + jnp.dot(
                v_turned[:, cols], weight.astype(bf16), preferred_element_type=f32
            )
            return total, accum

        total, accum = lax.fori_loop(
            first,
            last,
            gather,
            (jnp.zeros((8, 2 * BLK), f32), jnp.zeros((BLK, 2 * BLK), f32)),
        )
        total = jnp.sum(total, axis=0, keepdims=True)
        accum = accum / total
        half = BLK // 2
        both = jnp.concatenate([accum[:half, :BLK], accum[half:, BLK:]], axis=0)
        both = jnp.transpose(both)
        out_ref[slot * BLK : (slot + 1) * BLK, :] = both
        low_out_ref[slot * BLK : (slot + 1) * BLK, :] = both.astype(bf16)
        log_ref[0, slot : slot + 1, :] = best + jnp.log(total)


def attend(lead, low, high, q, k, v, known, barred, buckets, rel):
    rows, width = q.shape
    keys = k.shape[0]
    pairs = width // BLK
    blocks = keys // BLK
    slots = rows // BLK
    reach = blocks // 2
    smem = pl.BlockSpec(memory_space=pltpu.SMEM)

    def cols(count):
        return pl.BlockSpec((count, BLK), lambda i: (0, i))

    def whole(array):
        return pl.BlockSpec(array.shape, lambda i: (0,) * array.ndim)

    return pl.pallas_call(
        attend_kernel,
        grid=(pairs,),
        out_shape=(
            jax.ShapeDtypeStruct((rows, width), f32),
            jax.ShapeDtypeStruct((rows, width), bf16),
            jax.ShapeDtypeStruct((pairs, slots, 2 * BLK), f32),
        ),
        in_specs=[
            smem,
            smem,
            smem,
            cols(rows),
            cols(keys),
            cols(keys),
            whole(known),
            whole(barred),
            whole(buckets),
            pl.BlockSpec((1,) + rel.shape[1:], lambda i: (i, 0, 0)),
        ],
        out_specs=(
            cols(rows),
            cols(rows),
            pl.BlockSpec((1, slots, 2 * BLK), lambda i: (i, 0, 0)),
        ),
        scratch_shapes=[
            pltpu.VMEM((2 * reach + 1, BLK, 2 * BLK), f32),
            pltpu.VMEM((BLK, keys), bf16),
            pltpu.VMEM((blocks, BLK, 2 * BLK), f32),
        ],
        compiler_params=pltpu.CompilerParams(vmem_limit_bytes=VMEM_CAP),
        cost_estimate=LIGHT,
        name="attend",
    )(lead, low, high, q, k, v, known, barred, buckets, rel)


def attend_back_kernel(
    lead_ref,
    low_ref,
    high_ref,
    q_ref,
    k_ref,
    v_ref,
    g_ref,
    out_ref,
    log_ref,
    known,
    barred,
    buckets_ref,
    rel_ref,
    dq_ref,
    dk_ref,
    dv_ref,
    dbias_ref,
    tiles,
    k_turned,
    dk_acc,
    dv_acc,
    d_tiles,
):
    reach = tiles.shape[0] // 2
    count = tiles.shape[0]
    blocks = k_ref.shape[0] // BLK
    slots = q_ref.shape[0] // BLK
    half = BLK // 2

    bias_tiles(buckets_ref, rel_ref.at[0], tiles)
    k_turned[...] = jnp.transpose(k_ref[...])
    dk_acc[...] = jnp.zeros_like(dk_acc)
    dv_acc[...] = jnp.zeros_like(dv_acc)
    d_tiles[...] = jnp.zeros_like(d_tiles)
    sub = lax.broadcasted_iota(jnp.int32, (8, BLK), 0)
    lane = lane_iota(8)
    chooser = jnp.where((lane // half) == sub, 1.0, 0.0)
    for slot in range(slots):
        block = lead_ref[slot]
        first = low_ref[slot]
        last = high_ref[slot]
        base = pl.multiple_of(block * BLK, BLK)
        own = slice(slot * BLK, (slot + 1) * BLK)
        q_two = two_heads(q_ref[own, :])
        g_two = two_heads(g_ref[own, :])
        bar = barred[pl.ds(base, BLK), :]
        q_full = jnp.concatenate([q_two, jnp.concatenate([bar, bar], axis=0)], axis=1)
        product = g_ref[own, :].astype(f32) * out_ref[own, :]
        delta = lax.dot_general(chooser, product, NT, precision=HIGH, preferred_element_type=f32)
        delta = jnp.concatenate([delta[0:1, :], delta[1:2, :]], axis=1)
        log_total = log_ref[0, slot : slot + 1, :]

        def step(kb, dq):
            rows = pl.ds(pl.multiple_of(kb * BLK, BLK), BLK)
            k_full = jnp.concatenate([k_ref[rows, :], known[rows, :]], axis=1)
            value = lax.dot_general(k_full, q_full, NT, preferred_element_type=f32)
            prob = jnp.exp(value + tiles[kb - block + reach] - log_total)
            d_prob = lax.dot_general(v_ref[rows, :], g_two, NT, preferred_element_type=f32)
            d_score = prob * (d_prob - delta)
            d_tiles[kb - block + reach] = d_tiles[kb - block + reach] + d_score
            d_low = d_score.astype(bf16)
            dv_acc[rows, :] = dv_acc[rows, :] + jnp.dot(
                prob.astype(bf16), g_two, preferred_element_type=f32
            )
            dk_acc[rows, :] = dk_acc[rows, :] + jnp.dot(
                d_low, q_two, preferred_element_type=f32
            )
            return dq + jnp.dot(k_turned[:, rows], d_low, preferred_element_type=f32)

        dq = lax.fori_loop(first, last, step, jnp.zeros((BLK, 2 * BLK), f32))
        both = jnp.concatenate([dq[:half, :BLK], dq[half:, BLK:]], axis=0)
        dq_ref[own, :] = jnp.transpose(both).astype(bf16)
    dk_ref[...] = dk_acc[...].astype(bf16)
    dv_ref[...] = dv_acc[...].astype(bf16)
    levels = rel_ref.shape[2]
    level = lax.broadcasted_iota(jnp.int32, (levels, 2 * BLK), 0)
    total = jnp.zeros((8, levels), f32)
    pad = jnp.zeros((BLK, BLK), f32)
    mirror = (
        lax.broadcasted_iota(jnp.int32, (BLK, BLK), 0)
        + lax.broadcasted_iota(jnp.int32, (BLK, BLK), 1)
        == BLK - 1
    ).astype(bf16)
    for n in range(count):
        flipped = jnp.dot(mirror, d_tiles[n].astype(bf16), preferred_element_type=f32)
        row = blocks - 1 - (n - reach)
        bucket = jnp.concatenate(
            [buckets_ref[row : row + 1, :], buckets_ref[row + 1 : row + 2, :]], axis=1
        )
        onehot = (level == bucket).astype(f32)
        sums = []
        for head in range(2):
            part = flipped[:, head * BLK : (head + 1) * BLK]
            wide = jnp.concatenate([part, pad], axis=1)
            rolled = pltpu.roll(wide, 0, 1, stride=1, stride_axis=0)
            sums.append(jnp.sum(rolled, axis=0, keepdims=True))
        stacked = jnp.concatenate(sums + [jnp.zeros((6, 2 * BLK), f32)], axis=0)
        total = total + lax.dot_general(
            stacked, onehot, NT, precision=HIGH, preferred_element_type=f32
        )
    dbias_ref[0] = total


def attend_back(lead, low, high, q, k, v, g, out, log, known, barred, buckets, rel):
    rows, width = q.shape
    keys = k.shape[0]
    pairs = width // BLK
    blocks = keys // BLK
    slots = rows // BLK
    reach = blocks // 2
    levels = rel.shape[2]
    smem = pl.BlockSpec(memory_space=pltpu.SMEM)

    def cols(count):
        return pl.BlockSpec((count, BLK), lambda i: (0, i))

    def whole(array):
        return pl.BlockSpec(array.shape, lambda i: (0,) * array.ndim)

    def lead_block(shape):
        return pl.BlockSpec((1,) + shape, lambda i: (i,) + (0,) * len(shape))

    return pl.pallas_call(
        attend_back_kernel,
        grid=(pairs,),
        out_shape=(
            jax.ShapeDtypeStruct((rows, width), bf16),
            jax.ShapeDtypeStruct((keys, width), bf16),
            jax.ShapeDtypeStruct((keys, width), bf16),
            jax.ShapeDtypeStruct((pairs, 8, levels), f32),
        ),
        in_specs=[
            smem,
            smem,
            smem,
            cols(rows),
            cols(keys),
            cols(keys),
            cols(rows),
            cols(rows),
            lead_block((slots, 2 * BLK)),
            whole(known),
            whole(barred),
            whole(buckets),
            lead_block(rel.shape[1:]),
        ],
        out_specs=(cols(rows), cols(keys), cols(keys), lead_block((8, levels))),
        scratch_shapes=[
            pltpu.VMEM((2 * reach + 1, BLK, 2 * BLK), f32),
            pltpu.VMEM((BLK, keys), bf16),
            pltpu.VMEM((keys, BLK), f32),
            pltpu.VMEM((keys, BLK), f32),
            pltpu.VMEM((2 * reach + 1, BLK, 2 * BLK), f32),
        ],
        compiler_params=pltpu.CompilerParams(vmem_limit_bytes=VMEM_CAP),
        cost_estimate=LIGHT,
        name="attend_back",
    )(lead, low, high, q, k, v, g, out, log, known, barred, buckets, rel)


def attention_tables(starts, ends, rel_bucket, rel_bias, lead):
    blocks = starts.shape[0]
    mine = (lead[:, None] == jnp.arange(blocks)[None, :]).astype(jnp.int32)
    own_start = jnp.sum(mine * starts[None, :], axis=1)
    own_end = jnp.sum(mine * ends[None, :], axis=1)
    low = jnp.sum((ends[None, :] < own_start[:, None]).astype(jnp.int32), axis=1)
    high = jnp.sum((starts[None, :] <= own_end[:, None]).astype(jnp.int32), axis=1)
    buckets = jnp.pad(jnp.flip(rel_bucket), (0, 1)).reshape(2 * blocks, BLK)
    levels, heads = rel_bias.shape
    rel = jnp.transpose(rel_bias).reshape(heads // 2, 2, levels)
    return low, high, buckets, rel


def pack_kernel(*refs):
    outs = [ref for ref in refs if ref.dtype == bf16]
    masters = [ref for ref in refs if ref.dtype == f32]
    at = 0
    for out in outs:
        col = 0
        while col < out.shape[1]:
            wide = masters[at].shape[1]
            out[:, col : col + wide] = masters[at][...].astype(bf16)
            col += wide
            at += 1


def pack(groups):
    steps = 1
    while all(group[0].shape[0] % (32 * steps) == 0 for group in groups) and steps < 4:
        steps *= 2

    def spec(array):
        return pl.BlockSpec((array.shape[0] // steps, array.shape[1]), lambda i: (i, 0))

    outs = tuple(
        jax.ShapeDtypeStruct((group[0].shape[0], sum(a.shape[1] for a in group)), bf16)
        for group in groups
    )
    arrays = [array for group in groups for array in group]
    return pl.pallas_call(
        pack_kernel,
        grid=(steps,),
        out_shape=outs,
        in_specs=[spec(array) for array in arrays],
        out_specs=tuple(spec(out) for out in outs),
        compiler_params=pltpu.CompilerParams(vmem_limit_bytes=VMEM_CAP),
        cost_estimate=LIGHT,
        name="pack",
    )(*arrays)


def bits_of(count):
    bits = count.bit_length() - 1
    assert 1 << bits == count
    return bits


def swap(value, axis, bit):
    count = lax.axis_size(axis)
    return lax.ppermute(value, axis, [(i, i ^ (1 << bit)) for i in range(count)])


def ordered(mine, other, index, bit, axis=0):
    upper = ((index >> bit) & 1) == 1
    return jnp.concatenate(
        [jnp.where(upper, other, mine), jnp.where(upper, mine, other)], axis=axis
    )


def gather_small(value, axis):
    index = lax.axis_index(axis)
    value = value[None]
    for bit in range(bits_of(lax.axis_size(axis))):
        value = ordered(value, swap(value, axis, bit), index, bit)
    return value


def gather_rows(shard, axis):
    count = lax.axis_size(axis)
    index = lax.axis_index(axis)
    parts = [(0, shard)]
    for bit in reversed(range(bits_of(count))):
        parts = parts + [(j | (1 << bit), swap(part, axis, bit)) for j, part in parts]
    rows = shard.shape[0]
    result = jnp.zeros((rows * count,) + shard.shape[1:], shard.dtype)
    for j, part in parts:
        result = lax.dynamic_update_slice_in_dim(result, part, (index ^ j) * rows, axis=0)
    return result


def add_low(left, right):
    return (left.astype(f32) + right.astype(f32)).astype(bf16)


def piece(value, index, dim=0):
    return lax.dynamic_index_in_dim(value, index, dim, keepdims=False)


def scatter_step(value, axis, bit, dim):
    own = (lax.axis_index(axis) >> bit) & 1
    other = swap(piece(value, 1 - own, dim), axis, bit)
    return add_low(piece(value, own, dim), other)


def rest_sum(value, axis):
    count = lax.axis_size(axis)
    index = lax.axis_index(axis)
    mine = index // 2
    total = piece(value, mine).astype(f32)
    for j in range(1, count // 2):
        pairs = [(i, ((i // 2) ^ j) * 2 + i % 2) for i in range(count)]
        total = total + lax.ppermute(piece(value, mine ^ j), axis, pairs).astype(f32)
    return total.astype(bf16)


def rest_gather(value, axis):
    count = lax.axis_size(axis)
    index = lax.axis_index(axis)
    whole = jnp.zeros((count // 2,) + value.shape, value.dtype)
    for j in range(count // 2):
        part = value
        if j:
            pairs = [(i, ((i // 2) ^ j) * 2 + i % 2) for i in range(count)]
            part = lax.ppermute(value, axis, pairs)
        whole = lax.dynamic_update_index_in_dim(whole, part, (index // 2) ^ j, 0)
    other = swap(whole, axis, 0)
    upper = index % 2 == 1
    both = jnp.stack([jnp.where(upper, other, whole), jnp.where(upper, whole, other)], axis=1)
    return both.reshape((count * value.shape[0],) + value.shape[1:])


def reduce_rows(value, scatter_axis, sum_axis):
    count = lax.axis_size(scatter_axis)
    bits = bits_of(count)
    rows = value.shape[0] // count
    value = value.reshape((2,) * bits + (rows,) + value.shape[1:])
    value = yield value
    for bit in range(bits):
        value = yield scatter_step(value, scatter_axis, bit, bits - 1 - bit)
    count = lax.axis_size(sum_axis)
    value = value.reshape((count // 2, 2, rows // count) + value.shape[1:])
    value = yield scatter_step(value, sum_axis, 0, 1)
    value = yield rest_sum(value, sum_axis)
    yield rest_gather(value, sum_axis)


class Chain:
    def __init__(self, value):
        self.steps = reduce_rows(value, "fsdp", "ctx")
        self.value = next(self.steps)

    def advance(self, value):
        self.value = self.steps.send(value)

    def finish(self):
        for value in self.steps_left():
            self.value = value
        return self.value.astype(f32)

    def steps_left(self):
        while True:
            try:
                yield self.steps.send(self.value)
            except StopIteration:
                return


def gate(anchor, *chains):
    joined = lax.optimization_barrier((anchor,) + tuple(chain.value for chain in chains))
    for chain, value in zip(chains, joined[1:]):
        chain.advance(value)
    return joined[0]


def reduce_small(value):
    fsdp_bits = bits_of(lax.axis_size("fsdp"))
    count = lax.axis_size("ctx")
    rows, width = value.shape
    value = value.reshape(2, count // 2, 2 * rows // (2 * count), width)
    value = scatter_step(value, "fsdp", 0, 0)
    value = rest_sum(value, "ctx")
    value = add_low(value, swap(value, "ctx", 0))
    for bit in range(1, fsdp_bits):
        value = add_low(value, swap(value, "fsdp", bit))
    mine = lax.axis_index("ctx") // 2
    parts = [(0, value)]
    for j in range(1, count // 2):
        pairs = [(i, ((i // 2) ^ j) * 2 + i % 2) for i in range(count)]
        parts.append((j, lax.ppermute(value, "ctx", pairs)))
    whole = jnp.zeros((count // 2,) + value.shape, value.dtype)
    for j, part in parts:
        whole = lax.dynamic_update_index_in_dim(whole, part, mine ^ j, 0)
    whole = whole.reshape((rows // 2, width))
    return ordered(whole, swap(whole, "fsdp", 0), lax.axis_index("fsdp"), 0)


def rms_scale(values, gain_vec):
    return values * lax.rsqrt(jnp.mean(values * values, axis=-1, keepdims=True) + 1e-06) * gain_vec


def gelu_product(gate_pre, up_pre):
    return jax.nn.gelu(gate_pre, approximate=True) * up_pre


def local(
    byte_ids,
    doc_ids,
    rel_bucket,
    table,
    conv_w,
    score_w,
    gain_one,
    gain_two,
    rel_bias,
    query_master,
    key_master,
    value_master,
    out_master,
    gate_master,
    up_master,
    down_master,
    out_cotangent,
):
    ctx_count = lax.axis_size("ctx")
    ctx_index = lax.axis_index("ctx")
    seq_count, byte_count = byte_ids.shape
    total_bytes = byte_count * ctx_count
    width = table.shape[1]
    vocab = table.shape[0]
    hidden_width = gate_master.shape[1]
    levels, heads = rel_bias.shape
    share = ctx_count // seq_count
    assert share * seq_count == ctx_count and byte_count == 2 * BLK
    seq = ctx_index // share
    part = ctx_index % share
    near = [seq ^ slot for slot in range(seq_count)]
    lead = jnp.stack([share * other + part for other in near]).astype(jnp.int32)
    rows = seq_count * BLK

    (qkv_low,) = pack([[query_master, key_master, value_master]])
    both = jnp.stack([byte_ids, doc_ids], axis=1)
    both, qkv_low = lax.optimization_barrier((both, qkv_low))
    qkv = gather_rows(qkv_low, "fsdp")
    both = gather_small(both, "ctx")
    ogu_low, down_low = pack([[out_master, gate_master, up_master], [down_master]])
    both, ogu_low, down_low = lax.optimization_barrier((both, ogu_low, down_low))
    ogu = gather_rows(ogu_low, "fsdp")
    down_weight = gather_rows(down_low, "fsdp")
    query_weight = qkv[:, :width]
    key_weight = qkv[:, width : 2 * width]
    value_weight = qkv[:, 2 * width :]
    out_weight = ogu[:, :width]
    gate_up = ogu[:, width:]

    def to_owner(block, slot):
        if slot == 0:
            return block
        pairs = []
        for c in range(ctx_count):
            pairs.append((c, ((c // share) ^ slot) * share + c % share))
        return lax.ppermute(block, "ctx", pairs)

    cotangent = jnp.concatenate(
        [
            to_owner(lax.dynamic_index_in_dim(out_cotangent, near[s], 1, keepdims=False), s)
            for s in range(seq_count)
        ],
        axis=0,
    )

    table_wide = jnp.pad(table, ((0, -vocab % LANE), (0, 0)))
    tokens, norm_one, norm_own, conv, mix, phases, known, barred = byte_forward(
        seq[None], lead, both, table_wide, conv_w, score_w, gain_one, total_bytes
    )
    tokens_own = jnp.concatenate(
        [lax.dynamic_slice_in_dim(tokens, lead[s] * BLK, BLK, 0) for s in range(seq_count)], axis=0
    )

    queries = jnp.dot(norm_own, query_weight, preferred_element_type=f32).astype(bf16)
    keys = jnp.dot(norm_one, key_weight, preferred_element_type=f32).astype(bf16)
    values = jnp.dot(norm_one, value_weight, preferred_element_type=f32).astype(bf16)
    docs = piece(both[:, :, 1], seq, 1)
    low, high, buckets, rel = attention_tables(
        docs[:, 0], docs[:, 2 * BLK - 2], rel_bucket, rel_bias, lead
    )
    attended, attended_low, log_total = attend(
        lead, low, high, queries, keys, values, known, barred, buckets, rel
    )

    resid = tokens_own + jnp.dot(attended_low, out_weight, preferred_element_type=f32)
    norm_two = rms_scale(resid, gain_two).astype(bf16)
    gate_pre = jnp.dot(norm_two, gate_up[:, :hidden_width], preferred_element_type=f32)
    up_pre = jnp.dot(norm_two, gate_up[:, hidden_width:], preferred_element_type=f32)
    hidden = gelu_product(gate_pre, up_pre).astype(bf16)
    output = (resid + jnp.dot(hidden, down_weight, preferred_element_type=f32)).astype(bf16)
    output = output.reshape(seq_count, BLK, width)
    arrived = jnp.stack([to_owner(output[s], s) for s in range(seq_count)])
    output = jnp.stack(
        [lax.dynamic_index_in_dim(arrived, seq ^ s, 0, keepdims=False) for s in range(seq_count)],
        axis=1,
    )

    grad_down = jnp.einsum("rf,rd->fd", hidden, cotangent, preferred_element_type=f32)
    down_chain = Chain(grad_down.astype(bf16))
    cotangent = gate(cotangent, down_chain)
    d_hidden = jnp.einsum("rd,fd->rf", cotangent, down_weight, preferred_element_type=f32)
    _, gelu_pull = jax.vjp(gelu_product, gate_pre, up_pre)
    d_gate, d_up = gelu_pull(d_hidden)
    d_both = jnp.concatenate([d_gate.astype(bf16), d_up.astype(bf16)], axis=1)
    d_both = gate(d_both, down_chain)
    grad_gu = jnp.einsum("rd,rf->df", norm_two, d_both, preferred_element_type=f32)
    gu_chain = Chain(grad_gu.astype(bf16))
    d_both = gate(d_both, gu_chain)
    d_norm_two = jnp.einsum("rf,df->rd", d_both, gate_up, preferred_element_type=f32)
    _, norm_pull_two = jax.vjp(rms_scale, resid, gain_two)
    d_resid_norm, grad_gain_two = norm_pull_two(d_norm_two)
    d_resid = cotangent.astype(f32) + d_resid_norm
    d_branch = d_resid.astype(bf16)
    d_attended = jnp.einsum("rd,ad->ra", d_branch, out_weight, preferred_element_type=f32)
    d_attended = gate(d_attended.astype(bf16), gu_chain, down_chain)

    d_queries, d_keys, d_values, d_bias = attend_back(
        lead,
        low,
        high,
        queries,
        keys,
        values,
        d_attended,
        attended,
        log_total,
        known,
        barred,
        buckets,
        rel,
    )
    d_queries = gate(d_queries, gu_chain, down_chain)
    grad_qkv = jnp.concatenate(
        [
            jnp.einsum("rd,ra->da", norm_own, d_queries, preferred_element_type=f32),
            jnp.einsum("rd,ra->da", norm_one, d_keys, preferred_element_type=f32),
            jnp.einsum("rd,ra->da", norm_one, d_values, preferred_element_type=f32),
            jnp.einsum("ra,rd->ad", attended_low, d_branch, preferred_element_type=f32),
        ],
        axis=1,
    )
    qkv_chain = Chain(grad_qkv.astype(bf16))
    d_queries, d_keys, d_values = gate(
        (d_queries, d_keys, d_values), qkv_chain, down_chain
    )
    d_norm_query = jnp.einsum("ra,da->rd", d_queries, query_weight, preferred_element_type=f32)
    d_norm_one = jnp.einsum(
        "ra,da->rd", d_keys, key_weight, preferred_element_type=f32
    ) + jnp.einsum("ra,da->rd", d_values, value_weight, preferred_element_type=f32)
    for s in range(seq_count):
        start = lead[s] * BLK
        old = lax.dynamic_slice_in_dim(d_norm_one, start, BLK, 0)
        d_norm_one = lax.dynamic_update_slice_in_dim(
            d_norm_one, old + d_norm_query[s * BLK : (s + 1) * BLK], start, 0
        )
    d_norm_one = gate(d_norm_one, qkv_chain, gu_chain)

    vocab_rows = -(-vocab // 16) * 16
    small = byte_backward(
        lead,
        phases,
        tokens,
        d_norm_one,
        d_resid.reshape(seq_count, BLK, width),
        conv,
        mix,
        table_wide,
        vocab_rows,
        conv_w,
        score_w,
        gain_one,
        total_bytes,
    )
    bias_grad = jnp.transpose(d_bias[:, :2].reshape(heads, levels)).reshape(1, levels * heads)
    bias_grad = jnp.pad(bias_grad, ((0, 0), (0, width - levels * heads)))
    small = jnp.concatenate([small[: vocab_rows + 6], grad_gain_two[None], bias_grad], axis=0)
    small = jnp.pad(small, ((0, -small.shape[0] % (8 * ctx_count)), (0, 0))).astype(bf16)
    small = gate(small, qkv_chain, gu_chain)
    small = reduce_small(small).astype(f32)
    grad_down = down_chain.finish()
    grad_gu = gu_chain.finish()
    grad_qkv = qkv_chain.finish()
    top = vocab_rows
    return (
        output,
        small[:vocab],
        small[top : top + 4],
        small[top + 4],
        small[top + 5],
        small[top + 6],
        small[top + 7, : levels * heads].reshape(levels, heads),
        grad_qkv[:, :width],
        grad_qkv[:, width : 2 * width],
        grad_qkv[:, 2 * width : 3 * width],
        grad_qkv[:, 3 * width :],
        grad_gu[:, :hidden_width],
        grad_gu[:, hidden_width:],
        grad_down,
    )


def solution(mesh):
    placed = (
        P("fsdp", "ctx"),
        P("fsdp", "ctx"),
        P(),
        P(),
        P(),
        P(),
        P(),
        P(),
        P(),
        P("fsdp", None),
        P("fsdp", None),
        P("fsdp", None),
        P("fsdp", None),
        P("fsdp", None),
        P("fsdp", None),
        P("fsdp", None),
        P("ctx", "fsdp", None),
    )
    return jax.shard_map(
        local,
        mesh=mesh,
        in_specs=placed,
        out_specs=(
            P("ctx", "fsdp", None),
            P(),
            P(),
            P(),
            P(),
            P(),
            P(),
            P("fsdp", None),
            P("fsdp", None),
            P("fsdp", None),
            P("fsdp", None),
            P("fsdp", None),
            P("fsdp", None),
            P("fsdp", None),
        ),
        check_vma=False,
    )
```

```python
import functools

import jax
import jax.numpy as jnp
from jax import lax
from jax.experimental import pallas as pl
from jax.experimental.pallas import tpu as pltpu
from jax.sharding import PartitionSpec as P

f32 = jnp.float32
bf16 = jnp.bfloat16
LANE = 128
BLK = 128
VMEM_CAP = 60 * 1024 * 1024
HIGH = lax.Precision.HIGHEST
NT = (((1,), (1,)), ((), ()))
NN = (((1,), (0,)), ((), ()))
LIGHT = pl.CostEstimate(flops=1, transcendentals=0, bytes_accessed=1)


def lane_iota(rows):
    return lax.broadcasted_iota(jnp.int32, (rows, LANE), 1)


def block_sum(value, width, lane):
    def ahead(v, n):
        return pltpu.roll(v, LANE - n, 1)

    def behind(v, n):
        return pltpu.roll(v, n, 1)

    if width == 1:
        return value
    if width == 3:
        lead = value + ahead(value, 1) + ahead(value, 2)
        phase = lane % 3
        return jnp.where(phase == 0, lead, jnp.where(phase == 1, behind(lead, 1), behind(lead, 2)))
    pair = value + jnp.where(lane % 2 == 0, ahead(value, 1), behind(value, 1))
    if width == 2:
        return pair
    return pair + jnp.where(lane % 4 < 2, ahead(pair, 2), behind(pair, 2))


def pick(value, lane_index):
    return value[:, lane_index : lane_index + 1]


def byte_forward_kernel(
    total_bytes,
    seq_ref,
    lead_ref,
    both_ref,
    table_ref,
    conv_w_ref,
    score_ref,
    gain_ref,
    tok_ref,
    norm_ref,
    norm_own_ref,
    conv_ref,
    mix_ref,
    ids_ref,
    known_ref,
    barred_ref,
    hi_ref,
    lo_ref,
    emb,
    flat,
    spread,
):
    groups = conv_ref.shape[1]
    width = conv_ref.shape[2]
    tiles = width // LANE
    token_count = norm_ref.shape[0]
    vocab_pad = table_ref.shape[0]
    row_lanes = ids_ref.shape[1]
    seq = seq_ref[0]
    high = table_ref[...].astype(bf16)
    hi_ref[...] = high
    lo_ref[...] = (table_ref[...] - high.astype(f32)).astype(bf16)
    lane_f = lane_iota(BLK).astype(f32)
    chunk_bytes = both_ref.shape[3]

    def lay(kind, first):
        for block in range(both_ref.shape[0]):
            row = both_ref[block, seq, kind : kind + 1, :].astype(f32)
            for half in range(chunk_bytes // LANE):
                part = jnp.broadcast_to(row[:, half * LANE : (half + 1) * LANE], (LANE, LANE))
                start = first + block * chunk_bytes + half * LANE
                spread[start : start + LANE, :] = jnp.transpose(part)

    lay(1, 0)
    for block in range(token_count // BLK):
        docs = spread[pl.ds(block * 2 * BLK, BLK, stride=2), :]
        same = docs == lane_f
        rows = slice(block * BLK, (block + 1) * BLK)
        known_ref[rows, :] = same.astype(bf16)
        barred_ref[rows, :] = jnp.where(same | (lane_f >= 16.0), 0.0, -1e30).astype(bf16)
    lay(0, 16)
    none = jnp.full((16, LANE), -1.0, f32)
    spread[0:16, :] = none
    tail = spread.shape[0] - total_bytes - 16
    spread[total_bytes + 16 :, :] = jnp.full((tail, LANE), -1.0, f32)
    lane_g = lane_iota(groups).astype(f32)
    for r in range(15):
        here = spread[pl.ds(13 + r, row_lanes, stride=12), :]
        turned = [
            jnp.transpose(here[n * LANE : (n + 1) * LANE, :])[0:1, :]
            for n in range(row_lanes // LANE)
        ]
        ids_ref[r : r + 1, :] = jnp.concatenate(turned, axis=1)
        onehot = jnp.concatenate(
            [
                (here[0:groups, :] == lane_g + n * LANE).astype(bf16)
                for n in range(vocab_pad // LANE)
            ],
            axis=1,
        )
        emb[r] = jnp.dot(onehot, hi_ref[...], preferred_element_type=f32) + jnp.dot(
            onehot, lo_ref[...], preferred_element_type=f32
        )
    ids_ref[15:16, :] = jnp.full((1, row_lanes), -1.0, f32)
    lane = lane_iota(8)

    def chunk(i, masked):
        r0 = pl.multiple_of(i * 8, 8)
        rows = pl.ds(r0, 8)
        sums = [jnp.zeros((8, LANE), f32) for _ in range(12)]
        for tile in range(tiles):
            cols = slice(tile * LANE, (tile + 1) * LANE)
            taps = [conv_w_ref[k : k + 1, cols] for k in range(4)]
            piece = [emb[r, rows, cols] for r in range(15)]
            score = score_ref[0:1, cols]
            for r in range(12):
                value = (
                    piece[r] * taps[0]
                    + piece[r + 1] * taps[1]
                    + piece[r + 2] * taps[2]
                    + piece[r + 3] * taps[3]
                )
                if masked:
                    group = r0 + lax.broadcasted_iota(jnp.int32, (8, LANE), 0)
                    value = jnp.where(group * 12 + r < total_bytes, value, 0.0)
                conv_ref[r, rows, cols] = value
                sums[r] = sums[r] + value * score
        packed = jnp.zeros((8, LANE), f32)
        for r in range(12):
            packed = jnp.where(lane == r, jnp.sum(sums[r], axis=1, keepdims=True), packed)
        logits = [block_sum(packed, b, lane) * (1.0 / b) for b in range(1, 5)]
        best = jnp.maximum(jnp.maximum(logits[0], logits[1]), jnp.maximum(logits[2], logits[3]))
        parts = [jnp.exp(value - best) for value in logits]
        total = parts[0] + parts[1] + parts[2] + parts[3]
        mix = [part / total for part in parts]
        for b in range(4):
            mix_ref[b, rows, :] = mix[b]
        half_one = mix[0] * 0.5
        pair_two = block_sum(mix[1], 2, lane) * 0.25
        single_three = mix[2] * (1.0 / 6.0)
        pair_three = block_sum(mix[2], 2, lane) * (1.0 / 6.0)
        pair_four = block_sum(mix[3], 2, lane) * 0.125
        coef_one = [pick(half_one, r) for r in range(12)]
        coef_two = [pick(pair_two, 2 * j) for j in range(6)]
        coef_four = [pick(pair_four, 2 * j) for j in range(6)]
        coef_three = []
        for j in range(6):
            if j % 3 == 1:
                coef_three.append((pick(single_three, 2 * j), pick(single_three, 2 * j + 1)))
            else:
                coef_three.append((pick(pair_three, 2 * j), None))
        for tile in range(tiles):
            cols = slice(tile * LANE, (tile + 1) * LANE)
            conv = [conv_ref[r, rows, cols] for r in range(12)]
            two = [conv[2 * j] + conv[2 * j + 1] for j in range(6)]
            three = [conv[3 * q] + conv[3 * q + 1] + conv[3 * q + 2] for q in range(4)]
            four = [two[2 * q] + two[2 * q + 1] for q in range(3)]
            for j in range(6):
                a, b = 2 * j, 2 * j + 1
                value = coef_one[a] * conv[a] + coef_one[b] * conv[b]
                value = value + coef_two[j] * two[j] + coef_four[j] * four[j // 2]
                value = value + coef_three[j][0] * three[a // 3]
                if j % 3 == 1:
                    value = value + coef_three[j][1] * three[b // 3]
                flat[tile, pl.ds(6 * r0 + j, 8, stride=6), :] = value

    whole = (total_bytes // 12) // 8

    def plain(i, carry):
        chunk(i, False)
        return carry

    lax.fori_loop(0, whole, plain, 0)
    for i in range(whole, groups // 8):
        chunk(i, True)

    def norm(i, carry):
        rows = pl.ds(pl.multiple_of(i * 16, 16), 16)
        value = jnp.concatenate([flat[tile, rows, :] for tile in range(tiles)], axis=1)
        tok_ref[rows, :] = value
        scale = lax.rsqrt(jnp.mean(value * value, axis=1, keepdims=True) + 1e-06)
        norm_ref[rows, :] = (value * scale * gain_ref[...]).astype(bf16)
        return carry

    lax.fori_loop(0, token_count // 16, norm, 0)
    for slot in range(norm_own_ref.shape[0] // BLK):
        start = pl.multiple_of(lead_ref[slot] * BLK, BLK)
        norm_own_ref[slot * BLK : (slot + 1) * BLK, :] = norm_ref[pl.ds(start, BLK), :]


def byte_forward(seq, lead, both, table, conv_w, score_w, gain_one, total_bytes):
    width = conv_w.shape[1]
    token_count = total_bytes // 2
    least = -(-total_bytes // 12)
    groups = -(-least // 16) * 16
    row_lanes = -(-least // LANE) * LANE
    smem = pl.BlockSpec(memory_space=pltpu.SMEM)
    vmem = pl.BlockSpec(memory_space=pltpu.VMEM)
    return pl.pallas_call(
        functools.partial(byte_forward_kernel, total_bytes),
        out_shape=(
            jax.ShapeDtypeStruct((token_count, width), f32),
            jax.ShapeDtypeStruct((token_count, width), bf16),
            jax.ShapeDtypeStruct((lead.shape[0] * BLK, width), bf16),
            jax.ShapeDtypeStruct((12, groups, width), f32),
            jax.ShapeDtypeStruct((4, groups, LANE), f32),
            jax.ShapeDtypeStruct((16, row_lanes), f32),
            jax.ShapeDtypeStruct((token_count, LANE), bf16),
            jax.ShapeDtypeStruct((token_count, LANE), bf16),
        ),
        in_specs=[smem, smem] + [vmem] * 5,
        scratch_shapes=[
            pltpu.VMEM(table.shape, bf16),
            pltpu.VMEM(table.shape, bf16),
            pltpu.VMEM((15, groups, width), f32),
            pltpu.VMEM((width // LANE, 6 * groups, LANE), f32),
            pltpu.VMEM((12 * row_lanes + 32, LANE), f32),
        ],
        compiler_params=pltpu.CompilerParams(vmem_limit_bytes=VMEM_CAP),
        cost_estimate=LIGHT,
        name="byte_forward",
    )(
        seq,
        lead,
        both,
        table,
        conv_w,
        score_w.reshape(1, width),
        gain_one.reshape(1, width),
    )


def byte_backward_kernel(
    total_bytes,
    first_ref,
    ids_ref,
    tok_ref,
    dnorm_ref,
    dres_ref,
    conv_ref,
    mix_ref,
    table_ref,
    conv_w_ref,
    score_ref,
    gain_ref,
    out_ref,
    dtok,
    dconv,
    onehot,
):
    groups = conv_ref.shape[1]
    width = conv_ref.shape[2]
    tiles = width // LANE
    token_count = dnorm_ref.shape[0]
    vocab_rows = onehot.shape[0]
    lanes = ids_ref.shape[1]
    gain = gain_ref[...]

    def norm_back(i, acc):
        rows = pl.ds(pl.multiple_of(i * 8, 8), 8)
        value = tok_ref[rows, :]
        grad = dnorm_ref[rows, :]
        scale = lax.rsqrt(jnp.mean(value * value, axis=1, keepdims=True) + 1e-06)
        grad_gain = grad * gain
        inner = jnp.mean(value * grad_gain, axis=1, keepdims=True)
        total = 0.5 * scale * grad_gain - value * (0.5 * scale * scale * scale * inner)
        for tile in range(tiles):
            dtok[tile, rows, :] = total[:, tile * LANE : (tile + 1) * LANE]
        return acc + grad * value * scale

    gain_acc = lax.fori_loop(0, token_count // 8, norm_back, jnp.zeros((8, width), f32))
    rest = dtok.shape[1] - token_count
    dtok[:, token_count:, :] = jnp.zeros((tiles, rest, LANE), f32)
    for slot in range(dres_ref.shape[0]):
        start = pl.multiple_of(first_ref[slot] * BLK, BLK)

        def add(i, carry, slot=slot, start=start):
            r = pl.multiple_of(i * 8, 8)
            rows = pl.ds(start + r, 8)
            more = 0.5 * dres_ref[slot, pl.ds(r, 8), :]
            for tile in range(tiles):
                dtok[tile, rows, :] = (
                    dtok[tile, rows, :] + more[:, tile * LANE : (tile + 1) * LANE]
                )
            return carry

        lax.fori_loop(0, BLK // 8, add, 0)
    vocab = lax.broadcasted_iota(jnp.int32, (vocab_rows, lanes), 0).astype(f32)
    for r in range(15):
        onehot[:, r * lanes : (r + 1) * lanes] = (vocab == ids_ref[r : r + 1, :]).astype(bf16)
    for r in range(12):
        dconv[r * lanes + groups : (r + 1) * lanes, :] = jnp.zeros((lanes - groups, width), bf16)
    lane = lane_iota(8)

    def scalars(r0):
        rows = pl.ds(r0, 8)
        one = [jnp.zeros((8, LANE), f32) for _ in range(12)]
        cross = [jnp.zeros((8, LANE), f32) for _ in range(6)]
        tri = [jnp.zeros((8, LANE), f32) for _ in range(8)]
        for tile in range(tiles):
            cols = slice(tile * LANE, (tile + 1) * LANE)
            conv = [conv_ref[r, rows, cols] for r in range(12)]
            grad = [dtok[tile, pl.ds(6 * r0 + j, 8, stride=6), :] for j in range(6)]
            two = [conv[2 * j] + conv[2 * j + 1] for j in range(6)]
            three = [conv[3 * q] + conv[3 * q + 1] + conv[3 * q + 2] for q in range(4)]
            for r in range(12):
                one[r] = one[r] + conv[r] * grad[r // 2]
            slot = 0
            for j in range(6):
                cross[j] = cross[j] + two[j ^ 1] * grad[j]
                for q in sorted({(2 * j) // 3, (2 * j + 1) // 3}):
                    tri[slot] = tri[slot] + three[q] * grad[j]
                    slot += 1
        inner_one = jnp.zeros((8, LANE), f32)
        for r in range(12):
            inner_one = jnp.where(lane == r, jnp.sum(one[r], axis=1, keepdims=True), inner_one)
        inner_cross = jnp.zeros((8, LANE), f32)
        for j in range(6):
            inner_cross = jnp.where(
                lane // 2 == j, jnp.sum(cross[j], axis=1, keepdims=True), inner_cross
            )
        inner_three = jnp.zeros((8, LANE), f32)
        slot = 0
        for j in range(6):
            for q in sorted({(2 * j) // 3, (2 * j + 1) // 3}):
                here = (lane // 2 == j) & (lane // 3 == q)
                inner_three = jnp.where(
                    here, jnp.sum(tri[slot], axis=1, keepdims=True), inner_three
                )
                slot += 1
        inner_two = block_sum(inner_one, 2, lane)
        mix = [mix_ref[b, rows, :] for b in range(4)]
        d_mix = [
            inner_one,
            inner_two * 0.5,
            inner_three * (1.0 / 3.0),
            (inner_two + inner_cross) * 0.25,
        ]
        mean = mix[0] * d_mix[0] + mix[1] * d_mix[1] + mix[2] * d_mix[2] + mix[3] * d_mix[3]
        d_logit = [mix[b] * (d_mix[b] - mean) for b in range(4)]
        d_logit = [jnp.where(lane < 12, value, 0.0) for value in d_logit]
        slope = d_logit[0]
        for b in range(2, 5):
            slope = slope + block_sum(d_logit[b - 1], b, lane) * (1.0 / b)
        pair_two = block_sum(mix[1], 2, lane) * 0.5
        single_three = mix[2] * (1.0 / 3.0)
        pair_three = block_sum(mix[2], 2, lane) * (1.0 / 3.0)
        pair_four = block_sum(mix[3], 2, lane) * 0.25
        return mix[0], pair_two, single_three, pair_three, pair_four, slope

    def spread(r0, coefs, tile, masked, score_acc):
        one, pair_two, single_three, pair_three, pair_four, slope = coefs
        rows = pl.ds(r0, 8)
        cols = slice(tile * LANE, (tile + 1) * LANE)
        grad = [dtok[tile, pl.ds(6 * r0 + j, 8, stride=6), :] for j in range(6)]
        score = score_ref[0:1, cols]
        four = [
            pick(pair_four, 4 * q) * grad[2 * q] + pick(pair_four, 4 * q + 2) * grad[2 * q + 1]
            for q in range(3)
        ]
        three = []
        for q in range(4):
            a = 3 * q
            if a % 2 == 0:
                three.append(
                    pick(pair_three, a) * grad[a // 2]
                    + pick(single_three, a + 2) * grad[a // 2 + 1]
                )
            else:
                three.append(
                    pick(single_three, a) * grad[a // 2]
                    + pick(pair_three, a + 1) * grad[a // 2 + 1]
                )
        result = []
        for r in range(12):
            weight = pick(slope, r)
            own = (pick(one, r) + pick(pair_two, r)) * grad[r // 2]
            value = own + three[r // 3] + four[r // 4] + weight * score
            score_acc = score_acc + weight * conv_ref[r, rows, cols]
            if masked:
                group = r0 + lax.broadcasted_iota(jnp.int32, (8, LANE), 0)
                value = jnp.where(group * 12 + r < total_bytes, value, 0.0)
            result.append(value)
        return result, score_acc

    def chunk(i, accs, masked):
        r0 = pl.multiple_of(i * 16, 16)
        r1 = pl.multiple_of(i * 16 + 8, 8)
        low_coefs = scalars(r0)
        high_coefs = scalars(r1)
        new = []
        for tile in range(tiles):
            cols = slice(tile * LANE, (tile + 1) * LANE)
            low, acc = spread(r0, low_coefs, tile, masked, accs[tile])
            high, acc = spread(r1, high_coefs, tile, masked, acc)
            new.append(acc)
            for r in range(12):
                both = jnp.concatenate([low[r], high[r]], axis=0).astype(bf16)
                dconv[pl.ds(pl.multiple_of(r * lanes + r0, 16), 16), cols] = both
        return tuple(new)

    accs = tuple(jnp.zeros((8, LANE), f32) for _ in range(tiles))
    whole = (total_bytes // 12) // 16
    accs = lax.fori_loop(0, whole, lambda i, a: chunk(i, a, False), accs)
    for i in range(whole, groups // 16):
        accs = chunk(i, accs, True)
    tail = [jnp.zeros((1, width), f32) for _ in range(8)]
    for k in range(4):
        part = jnp.dot(
            onehot[:, k * lanes : (k + 12) * lanes], dconv[...], preferred_element_type=f32
        )
        if k == 0:
            out_ref[0:vocab_rows, :] = part * conv_w_ref[k : k + 1, :]
        else:
            out_ref[0:vocab_rows, :] = out_ref[0:vocab_rows, :] + part * conv_w_ref[k : k + 1, :]
        tail[k] = jnp.sum(part * table_ref[0:vocab_rows, :], axis=0, keepdims=True)
    tail[4] = jnp.sum(jnp.concatenate(accs, axis=1), axis=0, keepdims=True)
    tail[5] = jnp.sum(gain_acc, axis=0, keepdims=True)
    out_ref[vocab_rows:, :] = jnp.concatenate(tail, axis=0)


def byte_backward(
    first,
    ids,
    tokens,
    d_norm,
    d_resid,
    conv,
    mix,
    table,
    vocab_rows,
    conv_w,
    score_w,
    gain_one,
    total_bytes,
):
    width = conv.shape[2]
    groups = conv.shape[1]
    lanes = ids.shape[1]
    return pl.pallas_call(
        functools.partial(byte_backward_kernel, total_bytes),
        out_shape=jax.ShapeDtypeStruct((vocab_rows + 8, width), f32),
        in_specs=[pl.BlockSpec(memory_space=pltpu.SMEM)]
        + [pl.BlockSpec(memory_space=pltpu.VMEM)] * 10,
        scratch_shapes=[
            pltpu.VMEM((width // LANE, 6 * groups, LANE), f32),
            pltpu.VMEM((12 * lanes, width), bf16),
            pltpu.VMEM((vocab_rows, 15 * lanes), bf16),
        ],
        compiler_params=pltpu.CompilerParams(vmem_limit_bytes=VMEM_CAP),
        cost_estimate=LIGHT,
        name="byte_backward",
    )(
        first,
        ids,
        tokens,
        d_norm,
        d_resid,
        conv,
        mix,
        table,
        conv_w,
        score_w.reshape(1, width),
        gain_one.reshape(1, width),
    )


def head_mask(value, head):
    half = value.shape[1] // 2
    lane = lax.broadcasted_iota(jnp.int32, value.shape, 1)
    keep = lane < half if head == 0 else lane >= half
    return jnp.where(keep, value, jnp.zeros_like(value))


def two_heads(value):
    return jnp.concatenate([head_mask(value, 0), head_mask(value, 1)], axis=0)


def bias_tiles(buckets_ref, rel_ref, tiles):
    count = tiles.shape[0]
    blocks = buckets_ref.shape[0] // 2
    reach = count // 2
    levels = rel_ref.shape[1]
    level = lax.broadcasted_iota(jnp.int32, (levels, 2 * BLK), 0)
    for n in range(count):
        row = blocks - 1 - (n - reach)
        bucket = jnp.concatenate(
            [buckets_ref[row : row + 1, :], buckets_ref[row + 1 : row + 2, :]], axis=1
        )
        onehot = (level == bucket).astype(f32)
        values = lax.dot_general(
            rel_ref[...], onehot, NN, precision=HIGH, preferred_element_type=f32
        )
        for head in range(2):
            spread = jnp.broadcast_to(values[head : head + 1, :], (BLK, 2 * BLK))
            rolled = pltpu.roll(spread, BLK + 1, 1, stride=1, stride_axis=0)
            tiles[n, :, head * BLK : (head + 1) * BLK] = rolled[:, :BLK]


def attend_kernel(
    lead_ref,
    low_ref,
    high_ref,
    q_ref,
    k_ref,
    v_ref,
    known,
    barred,
    buckets_ref,
    rel_ref,
    out_ref,
    low_out_ref,
    log_ref,
    tiles,
    v_turned,
    held,
):
    reach = tiles.shape[0] // 2
    slots = q_ref.shape[0] // BLK

    bias_tiles(buckets_ref, rel_ref.at[0], tiles)
    v_turned[...] = jnp.transpose(v_ref[...])
    for slot in range(slots):
        block = lead_ref[slot]
        first = low_ref[slot]
        last = high_ref[slot]
        base = pl.multiple_of(block * BLK, BLK)
        q_two = two_heads(q_ref[slot * BLK : (slot + 1) * BLK, :])
        bar = barred[pl.ds(base, BLK), :]
        q_full = jnp.concatenate([q_two, jnp.concatenate([bar, bar], axis=0)], axis=1)

        def score(kb, best):
            rows = pl.ds(pl.multiple_of(kb * BLK, BLK), BLK)
            k_full = jnp.concatenate([k_ref[rows, :], known[rows, :]], axis=1)
            value = lax.dot_general(k_full, q_full, NT, preferred_element_type=f32)
            value = value + tiles[kb - block + reach]
            held[kb - first] = value
            return jnp.maximum(best, jnp.max(value.reshape(BLK // 8, 8, 2 * BLK), axis=0))

        best = lax.fori_loop(first, last, score, jnp.full((8, 2 * BLK), -3e38, f32))
        best = jnp.max(best, axis=0, keepdims=True)

        def gather(kb, state):
            total, accum = state
            weight = jnp.exp(held[kb - first] - best)
            total = total + jnp.sum(weight.reshape(BLK // 8, 8, 2 * BLK), axis=0)
            cols = pl.ds(pl.multiple_of(kb * BLK, BLK), BLK)
            accum = accum + jnp.dot(
                v_turned[:, cols], weight.astype(bf16), preferred_element_type=f32
            )
            return total, accum

        total, accum = lax.fori_loop(
            first,
            last,
            gather,
            (jnp.zeros((8, 2 * BLK), f32), jnp.zeros((BLK, 2 * BLK), f32)),
        )
        total = jnp.sum(total, axis=0, keepdims=True)
        accum = accum / total
        half = BLK // 2
        both = jnp.concatenate([accum[:half, :BLK], accum[half:, BLK:]], axis=0)
        both = jnp.transpose(both)
        out_ref[slot * BLK : (slot + 1) * BLK, :] = both
        low_out_ref[slot * BLK : (slot + 1) * BLK, :] = both.astype(bf16)
        log_ref[0, slot : slot + 1, :] = best + jnp.log(total)


def attend(lead, low, high, q, k, v, known, barred, buckets, rel):
    rows, width = q.shape
    keys = k.shape[0]
    pairs = width // BLK
    blocks = keys // BLK
    slots = rows // BLK
    reach = blocks // 2
    smem = pl.BlockSpec(memory_space=pltpu.SMEM)

    def cols(count):
        return pl.BlockSpec((count, BLK), lambda i: (0, i))

    def whole(array):
        return pl.BlockSpec(array.shape, lambda i: (0,) * array.ndim)

    return pl.pallas_call(
        attend_kernel,
        grid=(pairs,),
        out_shape=(
            jax.ShapeDtypeStruct((rows, width), f32),
            jax.ShapeDtypeStruct((rows, width), bf16),
            jax.ShapeDtypeStruct((pairs, slots, 2 * BLK), f32),
        ),
        in_specs=[
            smem,
            smem,
            smem,
            cols(rows),
            cols(keys),
            cols(keys),
            whole(known),
            whole(barred),
            whole(buckets),
            pl.BlockSpec((1,) + rel.shape[1:], lambda i: (i, 0, 0)),
        ],
        out_specs=(
            cols(rows),
            cols(rows),
            pl.BlockSpec((1, slots, 2 * BLK), lambda i: (i, 0, 0)),
        ),
        scratch_shapes=[
            pltpu.VMEM((2 * reach + 1, BLK, 2 * BLK), f32),
            pltpu.VMEM((BLK, keys), bf16),
            pltpu.VMEM((blocks, BLK, 2 * BLK), f32),
        ],
        compiler_params=pltpu.CompilerParams(vmem_limit_bytes=VMEM_CAP),
        cost_estimate=LIGHT,
        name="attend",
    )(lead, low, high, q, k, v, known, barred, buckets, rel)


def attend_back_kernel(
    lead_ref,
    low_ref,
    high_ref,
    q_ref,
    k_ref,
    v_ref,
    g_ref,
    out_ref,
    log_ref,
    known,
    barred,
    buckets_ref,
    rel_ref,
    dq_ref,
    dk_ref,
    dv_ref,
    dbias_ref,
    tiles,
    k_turned,
    dk_acc,
    dv_acc,
    d_tiles,
):
    reach = tiles.shape[0] // 2
    count = tiles.shape[0]
    blocks = k_ref.shape[0] // BLK
    slots = q_ref.shape[0] // BLK
    half = BLK // 2

    bias_tiles(buckets_ref, rel_ref.at[0], tiles)
    k_turned[...] = jnp.transpose(k_ref[...])
    dk_acc[...] = jnp.zeros_like(dk_acc)
    dv_acc[...] = jnp.zeros_like(dv_acc)
    d_tiles[...] = jnp.zeros_like(d_tiles)
    sub = lax.broadcasted_iota(jnp.int32, (8, BLK), 0)
    lane = lane_iota(8)
    chooser = jnp.where((lane // half) == sub, 1.0, 0.0)
    for slot in range(slots):
        block = lead_ref[slot]
        first = low_ref[slot]
        last = high_ref[slot]
        base = pl.multiple_of(block * BLK, BLK)
        own = slice(slot * BLK, (slot + 1) * BLK)
        q_two = two_heads(q_ref[own, :])
        g_two = two_heads(g_ref[own, :])
        bar = barred[pl.ds(base, BLK), :]
        q_full = jnp.concatenate([q_two, jnp.concatenate([bar, bar], axis=0)], axis=1)
        product = g_ref[own, :].astype(f32) * out_ref[own, :]
        delta = lax.dot_general(chooser, product, NT, precision=HIGH, preferred_element_type=f32)
        delta = jnp.concatenate([delta[0:1, :], delta[1:2, :]], axis=1)
        log_total = log_ref[0, slot : slot + 1, :]

        def step(kb, dq):
            rows = pl.ds(pl.multiple_of(kb * BLK, BLK), BLK)
            k_full = jnp.concatenate([k_ref[rows, :], known[rows, :]], axis=1)
            value = lax.dot_general(k_full, q_full, NT, preferred_element_type=f32)
            prob = jnp.exp(value + tiles[kb - block + reach] - log_total)
            d_prob = lax.dot_general(v_ref[rows, :], g_two, NT, preferred_element_type=f32)
            d_score = prob * (d_prob - delta)
            d_tiles[kb - block + reach] = d_tiles[kb - block + reach] + d_score
            d_low = d_score.astype(bf16)
            dv_acc[rows, :] = dv_acc[rows, :] + jnp.dot(
                prob.astype(bf16), g_two, preferred_element_type=f32
            )
            dk_acc[rows, :] = dk_acc[rows, :] + jnp.dot(
                d_low, q_two, preferred_element_type=f32
            )
            return dq + jnp.dot(k_turned[:, rows], d_low, preferred_element_type=f32)

        dq = lax.fori_loop(first, last, step, jnp.zeros((BLK, 2 * BLK), f32))
        both = jnp.concatenate([dq[:half, :BLK], dq[half:, BLK:]], axis=0)
        dq_ref[own, :] = jnp.transpose(both).astype(bf16)
    dk_ref[...] = dk_acc[...].astype(bf16)
    dv_ref[...] = dv_acc[...].astype(bf16)
    levels = rel_ref.shape[2]
    level = lax.broadcasted_iota(jnp.int32, (levels, 2 * BLK), 0)
    total = jnp.zeros((8, levels), f32)
    pad = jnp.zeros((BLK, BLK), f32)
    mirror = (
        lax.broadcasted_iota(jnp.int32, (BLK, BLK), 0)
        + lax.broadcasted_iota(jnp.int32, (BLK, BLK), 1)
        == BLK - 1
    ).astype(bf16)
    for n in range(count):
        flipped = jnp.dot(mirror, d_tiles[n].astype(bf16), preferred_element_type=f32)
        row = blocks - 1 - (n - reach)
        bucket = jnp.concatenate(
            [buckets_ref[row : row + 1, :], buckets_ref[row + 1 : row + 2, :]], axis=1
        )
        onehot = (level == bucket).astype(f32)
        sums = []
        for head in range(2):
            part = flipped[:, head * BLK : (head + 1) * BLK]
            wide = jnp.concatenate([part, pad], axis=1)
            rolled = pltpu.roll(wide, 0, 1, stride=1, stride_axis=0)
            sums.append(jnp.sum(rolled, axis=0, keepdims=True))
        stacked = jnp.concatenate(sums + [jnp.zeros((6, 2 * BLK), f32)], axis=0)
        total = total + lax.dot_general(
            stacked, onehot, NT, precision=HIGH, preferred_element_type=f32
        )
    dbias_ref[0] = total


def attend_back(first, pairs, lead, low, high, q, k, v, g, out, log, known, barred, buckets, rel):
    rows, width = q.shape
    keys = k.shape[0]
    width = pairs * BLK
    blocks = keys // BLK
    slots = rows // BLK
    reach = blocks // 2
    levels = rel.shape[2]
    smem = pl.BlockSpec(memory_space=pltpu.SMEM)

    def cols(count):
        return pl.BlockSpec((count, BLK), lambda i: (0, i + first))

    def fresh(count):
        return pl.BlockSpec((count, BLK), lambda i: (0, i))

    def whole(array):
        return pl.BlockSpec(array.shape, lambda i: (0,) * array.ndim)

    def lead_block(shape):
        return pl.BlockSpec((1,) + shape, lambda i: (i + first,) + (0,) * len(shape))

    return pl.pallas_call(
        attend_back_kernel,
        grid=(pairs,),
        out_shape=(
            jax.ShapeDtypeStruct((rows, width), bf16),
            jax.ShapeDtypeStruct((keys, width), bf16),
            jax.ShapeDtypeStruct((keys, width), bf16),
            jax.ShapeDtypeStruct((pairs, 8, levels), f32),
        ),
        in_specs=[
            smem,
            smem,
            smem,
            cols(rows),
            cols(keys),
            cols(keys),
            cols(rows),
            cols(rows),
            lead_block((slots, 2 * BLK)),
            whole(known),
            whole(barred),
            whole(buckets),
            lead_block(rel.shape[1:]),
        ],
        out_specs=(
            fresh(rows),
            fresh(keys),
            fresh(keys),
            pl.BlockSpec((1, 8, levels), lambda i: (i, 0, 0)),
        ),
        scratch_shapes=[
            pltpu.VMEM((2 * reach + 1, BLK, 2 * BLK), f32),
            pltpu.VMEM((BLK, keys), bf16),
            pltpu.VMEM((keys, BLK), f32),
            pltpu.VMEM((keys, BLK), f32),
            pltpu.VMEM((2 * reach + 1, BLK, 2 * BLK), f32),
        ],
        compiler_params=pltpu.CompilerParams(vmem_limit_bytes=VMEM_CAP),
        cost_estimate=LIGHT,
        name="attend_back",
    )(lead, low, high, q, k, v, g, out, log, known, barred, buckets, rel)


def attention_tables(starts, ends, rel_bucket, rel_bias, lead):
    blocks = starts.shape[0]
    mine = (lead[:, None] == jnp.arange(blocks)[None, :]).astype(jnp.int32)
    own_start = jnp.sum(mine * starts[None, :], axis=1)
    own_end = jnp.sum(mine * ends[None, :], axis=1)
    low = jnp.sum((ends[None, :] < own_start[:, None]).astype(jnp.int32), axis=1)
    high = jnp.sum((starts[None, :] <= own_end[:, None]).astype(jnp.int32), axis=1)
    buckets = jnp.pad(jnp.flip(rel_bucket), (0, 1)).reshape(2 * blocks, BLK)
    levels, heads = rel_bias.shape
    rel = jnp.transpose(rel_bias).reshape(heads // 2, 2, levels)
    return low, high, buckets, rel


def pack_kernel(*refs):
    outs = [ref for ref in refs if ref.dtype == bf16]
    masters = [ref for ref in refs if ref.dtype == f32]
    at = 0
    for out in outs:
        col = 0
        while col < out.shape[1]:
            wide = masters[at].shape[1]
            out[:, col : col + wide] = masters[at][...].astype(bf16)
            col += wide
            at += 1


def pack(groups):
    steps = 1
    while all(group[0].shape[0] % (32 * steps) == 0 for group in groups) and steps < 4:
        steps *= 2

    def spec(array):
        return pl.BlockSpec((array.shape[0] // steps, array.shape[1]), lambda i: (i, 0))

    outs = tuple(
        jax.ShapeDtypeStruct((group[0].shape[0], sum(a.shape[1] for a in group)), bf16)
        for group in groups
    )
    arrays = [array for group in groups for array in group]
    return pl.pallas_call(
        pack_kernel,
        grid=(steps,),
        out_shape=outs,
        in_specs=[spec(array) for array in arrays],
        out_specs=tuple(spec(out) for out in outs),
        compiler_params=pltpu.CompilerParams(vmem_limit_bytes=VMEM_CAP),
        cost_estimate=LIGHT,
        name="pack",
    )(*arrays)


TN = (((0,), (0,)), ((), ()))


def fetch_rows(index, parts, whole, sems):
    rows = parts[0].shape[0]
    copies = []
    for j, part in enumerate(parts):
        start = pl.multiple_of((index ^ j) * rows, rows)
        copies.append(pltpu.make_async_copy(part, whole.at[pl.ds(start, rows), :], sems.at[j]))
    return copies


def project_kernel(count, index_ref, *refs):
    parts = refs[:count]
    norm_ref, own_ref, q_ref, k_ref, v_ref, whole_ref, whole, sems, done = refs[count:]
    width = norm_ref.shape[1]
    copies = fetch_rows(index_ref[0], parts, whole, sems)
    for copy in copies:
        copy.start()
    for copy in copies:
        copy.wait()
    keep = pltpu.make_async_copy(whole, whole_ref, done)
    keep.start()
    for out, rows, col in ((q_ref, own_ref, 0), (k_ref, norm_ref, 1), (v_ref, norm_ref, 2)):
        weight = whole[:, col * width : (col + 1) * width]
        for block in range(rows.shape[0] // 256):
            part = slice(block * 256, (block + 1) * 256)
            out[part, :] = jnp.dot(rows[part, :], weight, preferred_element_type=f32).astype(bf16)
    keep.wait()


def project(index, parts, norm, own):
    count = len(parts)
    width = norm.shape[1]
    full = (parts[0].shape[0] * count, parts[0].shape[1])
    vmem = pl.BlockSpec(memory_space=pltpu.VMEM)
    anywhere = pl.BlockSpec(memory_space=pl.ANY)
    return pl.pallas_call(
        functools.partial(project_kernel, count),
        out_shape=(
            jax.ShapeDtypeStruct(own.shape, bf16),
            jax.ShapeDtypeStruct(norm.shape, bf16),
            jax.ShapeDtypeStruct(norm.shape, bf16),
            jax.ShapeDtypeStruct(full, bf16),
        ),
        in_specs=[pl.BlockSpec(memory_space=pltpu.SMEM)] + [anywhere] * count + [vmem] * 2,
        out_specs=(vmem, vmem, vmem, anywhere),
        scratch_shapes=[
            pltpu.VMEM(full, bf16),
            pltpu.SemaphoreType.DMA((count,)),
            pltpu.SemaphoreType.DMA,
        ],
        compiler_params=pltpu.CompilerParams(vmem_limit_bytes=VMEM_CAP),
        cost_estimate=LIGHT,
        name="project",
    )(index, *parts, norm, own)


def project_back_kernel(halves, lead_ref, norm_ref, own_ref, whole_ref, *refs):
    grad_ref, dnorm_ref = refs[3 * halves :]
    width = norm_ref.shape[1]
    part_width = width // halves
    for half in range(halves):
        for col in range(3):
            rows = own_ref if col == 0 else norm_ref
            here = slice(col * width + half * part_width, col * width + (half + 1) * part_width)
            grad_ref[:, here] = lax.dot_general(
                rows[...], refs[3 * half + col][...], TN, preferred_element_type=f32
            ).astype(bf16)
    for block in range(norm_ref.shape[0] // 256):
        part = slice(block * 256, (block + 1) * 256)
        total = None
        for half in range(halves):
            for col in (1, 2):
                here = slice(col * width + half * part_width, col * width + (half + 1) * part_width)
                term = lax.dot_general(
                    refs[3 * half + col][part, :],
                    whole_ref[:, here],
                    NT,
                    preferred_element_type=f32,
                )
                total = term if total is None else total + term
        dnorm_ref[part, :] = total
    for slot in range(own_ref.shape[0] // BLK):
        rows = pl.ds(pl.multiple_of(lead_ref[slot] * BLK, BLK), BLK)
        total = dnorm_ref[rows, :]
        for half in range(halves):
            total = total + lax.dot_general(
                refs[3 * half][slot * BLK : (slot + 1) * BLK, :],
                whole_ref[:, half * part_width : (half + 1) * part_width],
                NT,
                preferred_element_type=f32,
            )
        dnorm_ref[rows, :] = total


def project_back(lead, norm, own, whole, halves):
    vmem = pl.BlockSpec(memory_space=pltpu.VMEM)
    grads = [grad for half in halves for grad in half]
    return pl.pallas_call(
        functools.partial(project_back_kernel, len(halves)),
        out_shape=(
            jax.ShapeDtypeStruct(whole.shape, bf16),
            jax.ShapeDtypeStruct(norm.shape, f32),
        ),
        in_specs=[pl.BlockSpec(memory_space=pltpu.SMEM)] + [vmem] * (3 + len(grads)),
        out_specs=(vmem, vmem),
        compiler_params=pltpu.CompilerParams(vmem_limit_bytes=VMEM_CAP),
        cost_estimate=LIGHT,
        name="project_back",
    )(lead, norm, own, whole, *grads)


ROOT = 0.7978845608028654
CUBE = 0.044715


def feed_kernel(count, index_ref, *refs):
    upper = refs[:count]
    lower = refs[count : 2 * count]
    (
        tok_ref,
        att_ref,
        cot_ref,
        gain_ref,
        out_ref,
        d_att_ref,
        d_resid_ref,
        gain_grad_ref,
        left_ref,
        right_ref,
        ogu,
        down,
        store,
        resid,
        norm,
        d_norm,
        total,
        hid,
        d_gate,
        d_up,
        sems_upper,
        sems_lower,
        sems_store,
    ) = refs[2 * count :]
    rows, width = tok_ref.shape
    hidden = down.shape[0]
    copies_upper = fetch_rows(index_ref[0], upper, ogu, sems_upper)
    copies_lower = fetch_rows(index_ref[0], lower, down, sems_lower)
    for copy in copies_upper + copies_lower:
        copy.start()
    for copy in copies_upper:
        copy.wait()
    gain = gain_ref[...]
    row_step = 128
    tile = 512
    for block in range(rows // row_step):
        part = slice(block * row_step, (block + 1) * row_step)
        value = tok_ref[part, :] + jnp.dot(
            att_ref[part, :], ogu[:, :width], preferred_element_type=f32
        )
        resid[part, :] = value
        scale = lax.rsqrt(jnp.mean(value * value, axis=1, keepdims=True) + 1e-06)
        norm[part, :] = (value * scale * gain).astype(bf16)
    for copy in copies_lower:
        copy.wait()
    for n in range(hidden // tile):
        here = slice(n * tile, (n + 1) * tile)
        gate_cols = slice(width + n * tile, width + (n + 1) * tile)
        up_cols = slice(width + hidden + n * tile, width + hidden + (n + 1) * tile)
        for block in range(rows // row_step):
            part = slice(block * row_step, (block + 1) * row_step)
            gate_pre = jnp.dot(norm[part, :], ogu[:, gate_cols], preferred_element_type=f32)
            up_pre = jnp.dot(norm[part, :], ogu[:, up_cols], preferred_element_type=f32)
            d_hidden = lax.dot_general(
                cot_ref[part, :], down[here, :], NT, preferred_element_type=f32
            )
            square = gate_pre * gate_pre
            bent = jnp.tanh(ROOT * gate_pre * (1.0 + CUBE * square))
            half = 0.5 + 0.5 * bent
            gelu = gate_pre * half
            slope = half + (0.5 * ROOT) * gate_pre * (1.0 - bent * bent) * (
                1.0 + (3.0 * CUBE) * square
            )
            low = (gelu * up_pre).astype(bf16)
            d_gate_low = (d_hidden * up_pre * slope).astype(bf16)
            d_up_low = (d_hidden * gelu).astype(bf16)
            hid[part, :] = low
            d_gate[part, :] = d_gate_low
            d_up[part, :] = d_up_low
            add = jnp.dot(low, down[here, :], preferred_element_type=f32)
            back = lax.dot_general(
                d_gate_low, ogu[:, gate_cols], NT, preferred_element_type=f32
            ) + lax.dot_general(d_up_low, ogu[:, up_cols], NT, preferred_element_type=f32)
            if n == 0:
                total[part, :] = resid[part, :] + add
                d_norm[part, :] = back
            else:
                total[part, :] = total[part, :] + add
                d_norm[part, :] = d_norm[part, :] + back
        store[:, gate_cols] = lax.dot_general(
            norm[...], d_gate[...], TN, preferred_element_type=f32
        ).astype(bf16)
        store[:, up_cols] = lax.dot_general(
            norm[...], d_up[...], TN, preferred_element_type=f32
        ).astype(bf16)
        part = lax.dot_general(
            hid[...], cot_ref[...], TN, preferred_element_type=f32
        ).astype(bf16)
        for low_row, low_col, row, size in down_pieces(width // count, hidden // count, width):
            for device in range(count):
                source = device * (hidden // count) + low_row
                if n * tile <= source < (n + 1) * tile:
                    source = source - n * tile
                    target = device * (width // count) + row
                    col = width + 2 * hidden + low_col[1]
                    store[target : target + size, col : col + LANE] = part[
                        source : source + size, low_col[0] : low_col[0] + LANE
                    ]
    gain_sum = jnp.zeros((1, width), f32)
    for block in range(rows // row_step):
        part = slice(block * row_step, (block + 1) * row_step)
        out_ref[part, :] = total[part, :].astype(bf16)
        value = resid[part, :]
        grad = d_norm[part, :]
        scale = lax.rsqrt(jnp.mean(value * value, axis=1, keepdims=True) + 1e-06)
        scaled = grad * gain
        inner = jnp.mean(value * scaled, axis=1, keepdims=True)
        d_value = (
            cot_ref[part, :].astype(f32)
            + scale * scaled
            - value * (scale * scale * scale * inner)
        )
        gain_sum = gain_sum + jnp.sum(grad * value * scale, axis=0, keepdims=True)
        d_resid_ref[part, :] = d_value
        d_low = d_value.astype(bf16)
        norm[part, :] = d_low
        d_att_ref[part, :] = lax.dot_general(
            d_low, ogu[:, :width], NT, preferred_element_type=f32
        ).astype(bf16)
    gain_grad_ref[...] = gain_sum
    store[:, :width] = lax.dot_general(
        att_ref[...], norm[...], TN, preferred_element_type=f32
    ).astype(bf16)
    half = store.shape[1] // 2
    copies = [
        pltpu.make_async_copy(store.at[:, :half], left_ref, sems_store.at[0]),
        pltpu.make_async_copy(store.at[:, half:], right_ref, sems_store.at[1]),
    ]
    for copy in copies:
        copy.start()
    for copy in copies:
        copy.wait()


def down_pieces(rows, tall, width):
    size = 16
    while tall % (2 * size) == 0 and rows % (2 * size) == 0:
        size *= 2
    pieces = []
    for q in range(tall * (width // LANE) // size):
        there = (q % (tall // size)) * size
        here = (q % (rows // size)) * size
        pieces.append((there, (q // (tall // size) * LANE, q // (rows // size) * LANE), here, size))
    return pieces


def unpack_kernel(hidden, left_ref, right_ref, qkv_ref, *outs):
    rows = left_ref.shape[0]
    half = left_ref.shape[1]
    width = outs[0].shape[1]
    for n in range(3):
        outs[n][...] = qkv_ref[:, n * width : (n + 1) * width].astype(f32)

    def column(first, last):
        parts = []
        if first < half:
            parts.append((left_ref, first, min(last, half), 0))
        if last > half:
            begin = max(first, half)
            parts.append((right_ref, begin - half, last - half, begin - first))
        return parts

    spans = ((0, width), (width, width + hidden), (width + hidden, width + 2 * hidden))
    for out, (first, last) in zip(outs[3:6], spans):
        for ref, begin, end, at in column(first, last):
            out[:, at : at + end - begin] = ref[:, begin:end].astype(f32)
    base = width + 2 * hidden - half
    for there, (col_there, col_here), here, size in down_pieces(rows, outs[6].shape[0], width):
        outs[6][there : there + size, col_there : col_there + LANE] = right_ref[
            here : here + size, base + col_here : base + col_here + LANE
        ].astype(f32)


def unpack(left, right, qkv, hidden, tall):
    rows = left.shape[0]
    width = qkv.shape[1] // 3
    shapes = [(rows, width)] * 4 + [(rows, hidden)] * 2 + [(tall, width)]
    return pl.pallas_call(
        functools.partial(unpack_kernel, hidden),
        out_shape=tuple(jax.ShapeDtypeStruct(shape, f32) for shape in shapes),
        compiler_params=pltpu.CompilerParams(vmem_limit_bytes=VMEM_CAP),
        cost_estimate=LIGHT,
        name="unpack",
    )(left, right, qkv)


def feed(index, upper, lower, tokens, attended, cotangent, gain):
    count = len(upper)
    rows, width = tokens.shape
    full_upper = (upper[0].shape[0] * count, upper[0].shape[1])
    full_lower = (lower[0].shape[0] * count, width)
    hidden = full_lower[0]
    columns = width + 3 * hidden
    vmem = pl.BlockSpec(memory_space=pltpu.VMEM)
    anywhere = pl.BlockSpec(memory_space=pl.ANY)
    tile = 512
    return pl.pallas_call(
        functools.partial(feed_kernel, count),
        out_shape=(
            jax.ShapeDtypeStruct((rows, width), bf16),
            jax.ShapeDtypeStruct((rows, width), bf16),
            jax.ShapeDtypeStruct((rows, width), f32),
            jax.ShapeDtypeStruct((1, width), f32),
            jax.ShapeDtypeStruct((width, columns // 2), bf16),
            jax.ShapeDtypeStruct((width, columns // 2), bf16),
        ),
        in_specs=[pl.BlockSpec(memory_space=pltpu.SMEM)]
        + [anywhere] * (2 * count)
        + [vmem] * 4,
        out_specs=(vmem,) * 4 + (anywhere,) * 2,
        scratch_shapes=[
            pltpu.VMEM(full_upper, bf16),
            pltpu.VMEM(full_lower, bf16),
            pltpu.VMEM((width, columns), bf16),
            pltpu.VMEM((rows, width), f32),
            pltpu.VMEM((rows, width), bf16),
            pltpu.VMEM((rows, width), f32),
            pltpu.VMEM((rows, width), f32),
            pltpu.VMEM((rows, tile), bf16),
            pltpu.VMEM((rows, tile), bf16),
            pltpu.VMEM((rows, tile), bf16),
            pltpu.SemaphoreType.DMA((count,)),
            pltpu.SemaphoreType.DMA((count,)),
            pltpu.SemaphoreType.DMA((2,)),
        ],
        compiler_params=pltpu.CompilerParams(vmem_limit_bytes=VMEM_CAP),
        cost_estimate=LIGHT,
        name="feed",
    )(index, *upper, *lower, tokens, attended, cotangent, gain.reshape(1, width))


def bits_of(count):
    bits = count.bit_length() - 1
    assert 1 << bits == count
    return bits


def swap(value, axis, bit):
    count = lax.axis_size(axis)
    return lax.ppermute(value, axis, [(i, i ^ (1 << bit)) for i in range(count)])


def ordered(mine, other, index, bit, axis=0):
    upper = ((index >> bit) & 1) == 1
    return jnp.concatenate(
        [jnp.where(upper, other, mine), jnp.where(upper, mine, other)], axis=axis
    )


def gather_small(value, axis):
    index = lax.axis_index(axis)
    value = value[None]
    for bit in range(bits_of(lax.axis_size(axis))):
        value = ordered(value, swap(value, axis, bit), index, bit)
    return value


def first_swap(shard, axis):
    bit = bits_of(lax.axis_size(axis)) - 1
    return [(0, shard), (1 << bit, swap(shard, axis, bit))]


def other_swaps(parts, axis):
    for bit in reversed(range(bits_of(lax.axis_size(axis)) - 1)):
        parts = parts + [(j | (1 << bit), swap(part, axis, bit)) for j, part in parts]
    return [part for _, part in sorted(parts, key=lambda pair: pair[0])]


def after(anchor, part):
    j, array = part
    anchor, array = lax.optimization_barrier((anchor, array))
    return anchor, (j, array)


def add_low(left, right):
    return (left.astype(f32) + right.astype(f32)).astype(bf16)


def piece(value, index, dim=0):
    return lax.dynamic_index_in_dim(value, index, dim, keepdims=False)


def scatter_step(value, axis, bit, dim):
    own = (lax.axis_index(axis) >> bit) & 1
    other = swap(piece(value, 1 - own, dim), axis, bit)
    return add_low(piece(value, own, dim), other)


def rest_sum(value, axis):
    count = lax.axis_size(axis)
    index = lax.axis_index(axis)
    mine = index // 2
    total = piece(value, mine).astype(f32)
    for j in range(1, count // 2):
        pairs = [(i, ((i // 2) ^ j) * 2 + i % 2) for i in range(count)]
        total = total + lax.ppermute(piece(value, mine ^ j), axis, pairs).astype(f32)
    return total.astype(bf16)


def rest_gather(value, axis):
    count = lax.axis_size(axis)
    index = lax.axis_index(axis)
    whole = jnp.zeros((count // 2,) + value.shape, value.dtype)
    for j in range(count // 2):
        part = value
        if j:
            pairs = [(i, ((i // 2) ^ j) * 2 + i % 2) for i in range(count)]
            part = lax.ppermute(value, axis, pairs)
        whole = lax.dynamic_update_index_in_dim(whole, part, (index // 2) ^ j, 0)
    return whole


def pair_gather(whole, axis):
    other = swap(whole, axis, 0)
    upper = lax.axis_index(axis) % 2 == 1
    both = jnp.stack([jnp.where(upper, other, whole), jnp.where(upper, whole, other)], axis=1)
    return both.reshape((2 * whole.shape[0] * whole.shape[1],) + whole.shape[2:])


def reduce_rows(value, scatter_axis, sum_axis):
    count = lax.axis_size(scatter_axis)
    bits = bits_of(count)
    rows = value.shape[0] // count
    value = value.reshape((2,) * bits + (rows,) + value.shape[1:])
    value = yield value
    for bit in range(bits):
        value = yield scatter_step(value, scatter_axis, bit, bits - 1 - bit)
    count = lax.axis_size(sum_axis)
    value = value.reshape((count // 2, 2, rows // count) + value.shape[1:])
    value = yield scatter_step(value, sum_axis, 0, 1)
    value = yield rest_sum(value, sum_axis)
    value = yield rest_gather(value, sum_axis)
    yield pair_gather(value, sum_axis)


class Chain:
    def __init__(self, value):
        self.steps = reduce_rows(value, "fsdp", "ctx")
        self.value = next(self.steps)

    def advance(self, value):
        self.value = self.steps.send(value)

    def finish(self):
        for value in self.steps_left():
            self.value = value
        return self.value

    def steps_left(self):
        while True:
            try:
                yield self.steps.send(self.value)
            except StopIteration:
                return


def gate(anchor, *chains):
    joined = lax.optimization_barrier((anchor,) + tuple(chain.value for chain in chains))
    for chain, value in zip(chains, joined[1:]):
        chain.advance(value)
    return joined[0]


def reduce_small(value):
    fsdp_bits = bits_of(lax.axis_size("fsdp"))
    count = lax.axis_size("ctx")
    rows, width = value.shape
    value = value.reshape(2, count // 2, 2 * rows // (2 * count), width)
    value = scatter_step(value, "fsdp", 0, 0)
    value = rest_sum(value, "ctx")
    value = add_low(value, swap(value, "ctx", 0))
    for bit in range(1, fsdp_bits):
        value = add_low(value, swap(value, "fsdp", bit))
    whole = rest_gather(value, "ctx")
    whole = whole.reshape((rows // 2, width))
    return ordered(whole, swap(whole, "fsdp", 0), lax.axis_index("fsdp"), 0)


def local(
    byte_ids,
    doc_ids,
    rel_bucket,
    table,
    conv_w,
    score_w,
    gain_one,
    gain_two,
    rel_bias,
    query_master,
    key_master,
    value_master,
    out_master,
    gate_master,
    up_master,
    down_master,
    out_cotangent,
):
    ctx_count = lax.axis_size("ctx")
    ctx_index = lax.axis_index("ctx")
    seq_count, byte_count = byte_ids.shape
    total_bytes = byte_count * ctx_count
    width = table.shape[1]
    vocab = table.shape[0]
    hidden_width = gate_master.shape[1]
    levels, heads = rel_bias.shape
    share = ctx_count // seq_count
    assert share * seq_count == ctx_count and byte_count == 2 * BLK
    seq = ctx_index // share
    part = ctx_index % share
    near = [seq ^ slot for slot in range(seq_count)]
    lead = jnp.stack([share * other + part for other in near]).astype(jnp.int32)
    rows = seq_count * BLK

    (qkv_low,) = pack([[query_master, key_master, value_master]])
    both = jnp.stack([byte_ids, doc_ids], axis=1)
    both, qkv_low = lax.optimization_barrier((both, qkv_low))
    qkv_parts = first_swap(qkv_low, "fsdp")
    both = gather_small(both, "ctx")
    (both, out_master), qkv_parts[1] = after((both, out_master), qkv_parts[1])
    ogu_low, down_low = pack([[out_master, gate_master, up_master], [down_master]])
    both, ogu_low, down_low = lax.optimization_barrier((both, ogu_low, down_low))
    down_parts = first_swap(down_low, "fsdp")
    ogu_parts = first_swap(ogu_low, "fsdp")
    shard = lax.axis_index("fsdp")[None]

    def to_owner(block, slot):
        if slot == 0:
            return block
        pairs = []
        for c in range(ctx_count):
            pairs.append((c, ((c // share) ^ slot) * share + c % share))
        return lax.ppermute(block, "ctx", pairs)

    cotangent = jnp.concatenate(
        [
            to_owner(lax.dynamic_index_in_dim(out_cotangent, near[s], 1, keepdims=False), s)
            for s in range(seq_count)
        ],
        axis=0,
    )

    table_wide = jnp.pad(table, ((0, -vocab % LANE), (0, 0)))
    tokens, norm_one, norm_own, conv, mix, phases, known, barred = byte_forward(
        seq[None], lead, both, table_wide, conv_w, score_w, gain_one, total_bytes
    )
    tokens_own = jnp.concatenate(
        [lax.dynamic_slice_in_dim(tokens, lead[s] * BLK, BLK, 0) for s in range(seq_count)], axis=0
    )

    norm_one, down_parts[1] = after(norm_one, down_parts[1])
    norm_one, cotangent = lax.optimization_barrier((norm_one, cotangent))
    queries, keys, values, qkv = project(shard, other_swaps(qkv_parts, "fsdp"), norm_one, norm_own)
    docs = piece(both[:, :, 1], seq, 1)
    low, high, buckets, rel = attention_tables(
        docs[:, 0], docs[:, 2 * BLK - 2], rel_bucket, rel_bias, lead
    )
    attended, attended_low, log_total = attend(
        lead, low, high, queries, keys, values, known, barred, buckets, rel
    )

    attended_low, ogu_parts[1] = after(attended_low, ogu_parts[1])
    output, d_attended, d_resid, grad_gain_two, grad_left, grad_right = feed(
        shard,
        other_swaps(ogu_parts, "fsdp"),
        other_swaps(down_parts, "fsdp"),
        tokens_own,
        attended_low,
        cotangent,
        gain_two,
    )
    left = Chain(grad_left)
    right = Chain(grad_right)
    left.advance(left.value)
    d_attended = gate(d_attended, left)
    right.advance(right.value)
    output = output.reshape(seq_count, BLK, width)
    arrived = jnp.stack([to_owner(output[s], s) for s in range(seq_count)])
    output = jnp.stack(
        [lax.dynamic_index_in_dim(arrived, seq ^ s, 0, keepdims=False) for s in range(seq_count)],
        axis=1,
    )

    pairs = heads // 2
    cut = pairs // 2
    halves = []
    for first, count in ((0, cut), (cut, pairs - cut)):
        if first:
            d_attended = gate(d_attended, left)
        else:
            d_attended = gate(d_attended, right)
        *grads, d_bias = attend_back(
            first,
            count,
            lead,
            low,
            high,
            queries,
            keys,
            values,
            d_attended,
            attended,
            log_total,
            known,
            barred,
            buckets,
            rel,
        )
        halves.append((grads, d_bias))
        d_attended, _ = lax.optimization_barrier((d_attended, grads[0]))
    d_bias = jnp.concatenate([half[1] for half in halves], axis=0)
    norm_own, halves = gate((norm_own, [half[0] for half in halves]), left, right)
    grad_qkv, d_norm_one = project_back(lead, norm_one, norm_own, qkv, halves)
    qkv_chain = Chain(grad_qkv)
    qkv_chain.advance(qkv_chain.value)
    d_norm_one = gate(d_norm_one, qkv_chain, left, right)

    vocab_rows = -(-vocab // 16) * 16
    small = byte_backward(
        lead,
        phases,
        tokens,
        d_norm_one,
        d_resid.reshape(seq_count, BLK, width),
        conv,
        mix,
        table_wide,
        vocab_rows,
        conv_w,
        score_w,
        gain_one,
        total_bytes,
    )
    bias_grad = jnp.transpose(d_bias[:, :2].reshape(heads, levels)).reshape(1, levels * heads)
    bias_grad = jnp.pad(bias_grad, ((0, 0), (0, width - levels * heads)))
    small = jnp.concatenate([small[: vocab_rows + 6], grad_gain_two, bias_grad], axis=0)
    small = jnp.pad(small, ((0, -small.shape[0] % (8 * ctx_count)), (0, 0))).astype(bf16)
    small = gate(small, qkv_chain, left, right)
    small = reduce_small(small).astype(f32)
    grads = unpack(
        left.finish(), right.finish(), qkv_chain.finish(), hidden_width, down_master.shape[0]
    )
    top = vocab_rows
    return (
        output,
        small[:vocab],
        small[top : top + 4],
        small[top + 4],
        small[top + 5],
        small[top + 6],
        small[top + 7, : levels * heads].reshape(levels, heads),
        *grads,
    )


def solution(mesh):
    placed = (
        P("fsdp", "ctx"),
        P("fsdp", "ctx"),
        P(),
        P(),
        P(),
        P(),
        P(),
        P(),
        P(),
        P("fsdp", None),
        P("fsdp", None),
        P("fsdp", None),
        P("fsdp", None),
        P("fsdp", None),
        P("fsdp", None),
        P("fsdp", None),
        P("ctx", "fsdp", None),
    )
    return jax.shard_map(
        local,
        mesh=mesh,
        in_specs=placed,
        out_specs=(
            P("ctx", "fsdp", None),
            P(),
            P(),
            P(),
            P(),
            P(),
            P(),
            P("fsdp", None),
            P("fsdp", None),
            P("fsdp", None),
            P("fsdp", None),
            P("fsdp", None),
            P("fsdp", None),
            P("fsdp", None),
        ),
        check_vma=False,
    )
```

```python
import functools

import jax
import jax.numpy as jnp
from jax import lax
from jax.experimental import pallas as pl
from jax.experimental.pallas import tpu as pltpu
from jax.sharding import PartitionSpec as P

f32 = jnp.float32
bf16 = jnp.bfloat16
LANE = 128
BLK = 128
VMEM_CAP = 60 * 1024 * 1024
HIGH = lax.Precision.HIGHEST
NT = (((1,), (1,)), ((), ()))
NN = (((1,), (0,)), ((), ()))
LIGHT = pl.CostEstimate(flops=1, transcendentals=0, bytes_accessed=1)


def lane_iota(rows):
    return lax.broadcasted_iota(jnp.int32, (rows, LANE), 1)


def block_sum(value, width, lane):
    def ahead(v, n):
        return pltpu.roll(v, LANE - n, 1)

    def behind(v, n):
        return pltpu.roll(v, n, 1)

    if width == 1:
        return value
    if width == 3:
        lead = value + ahead(value, 1) + ahead(value, 2)
        phase = lane % 3
        return jnp.where(phase == 0, lead, jnp.where(phase == 1, behind(lead, 1), behind(lead, 2)))
    pair = value + jnp.where(lane % 2 == 0, ahead(value, 1), behind(value, 1))
    if width == 2:
        return pair
    return pair + jnp.where(lane % 4 < 2, ahead(pair, 2), behind(pair, 2))


def pick(value, lane_index):
    return value[:, lane_index : lane_index + 1]


def byte_forward_kernel(
    total_bytes,
    seq_ref,
    lead_ref,
    both_ref,
    table_ref,
    conv_w_ref,
    score_ref,
    gain_ref,
    tok_ref,
    norm_ref,
    norm_own_ref,
    tok_own_ref,
    conv_ref,
    mix_ref,
    ids_ref,
    known_ref,
    barred_ref,
    hi_ref,
    lo_ref,
    emb,
    flat,
    spread,
):
    groups = conv_ref.shape[1]
    width = conv_ref.shape[2]
    tiles = width // LANE
    token_count = norm_ref.shape[0]
    vocab_pad = table_ref.shape[0]
    row_lanes = ids_ref.shape[1]
    seq = seq_ref[0]
    high = table_ref[...].astype(bf16)
    hi_ref[...] = high
    lo_ref[...] = (table_ref[...] - high.astype(f32)).astype(bf16)
    lane_f = lane_iota(BLK).astype(f32)
    chunk_bytes = both_ref.shape[3]

    def lay(kind, first):
        for block in range(both_ref.shape[0]):
            row = both_ref[block, seq, kind : kind + 1, :].astype(f32)
            for half in range(chunk_bytes // LANE):
                part = jnp.broadcast_to(row[:, half * LANE : (half + 1) * LANE], (LANE, LANE))
                start = first + block * chunk_bytes + half * LANE
                spread[start : start + LANE, :] = jnp.transpose(part)

    lay(1, 0)
    for block in range(token_count // BLK):
        docs = spread[pl.ds(block * 2 * BLK, BLK, stride=2), :]
        same = docs == lane_f
        rows = slice(block * BLK, (block + 1) * BLK)
        known_ref[rows, :] = same.astype(bf16)
        barred_ref[rows, :] = jnp.where(same | (lane_f >= 16.0), 0.0, -1e30).astype(bf16)
    lay(0, 16)
    none = jnp.full((16, LANE), -1.0, f32)
    spread[0:16, :] = none
    tail = spread.shape[0] - total_bytes - 16
    spread[total_bytes + 16 :, :] = jnp.full((tail, LANE), -1.0, f32)
    lane_g = lane_iota(groups).astype(f32)
    for r in range(15):
        here = spread[pl.ds(13 + r, row_lanes, stride=12), :]
        turned = [
            jnp.transpose(here[n * LANE : (n + 1) * LANE, :])[0:1, :]
            for n in range(row_lanes // LANE)
        ]
        ids_ref[r : r + 1, :] = jnp.concatenate(turned, axis=1)
        onehot = jnp.concatenate(
            [
                (here[0:groups, :] == lane_g + n * LANE).astype(bf16)
                for n in range(vocab_pad // LANE)
            ],
            axis=1,
        )
        emb[r] = jnp.dot(onehot, hi_ref[...], preferred_element_type=f32) + jnp.dot(
            onehot, lo_ref[...], preferred_element_type=f32
        )
    ids_ref[15:16, :] = jnp.full((1, row_lanes), -1.0, f32)
    lane = lane_iota(8)

    def chunk(i, masked):
        r0 = pl.multiple_of(i * 8, 8)
        rows = pl.ds(r0, 8)
        sums = [jnp.zeros((8, LANE), f32) for _ in range(12)]
        for tile in range(tiles):
            cols = slice(tile * LANE, (tile + 1) * LANE)
            taps = [conv_w_ref[k : k + 1, cols] for k in range(4)]
            piece = [emb[r, rows, cols] for r in range(15)]
            score = score_ref[0:1, cols]
            for r in range(12):
                value = (
                    piece[r] * taps[0]
                    + piece[r + 1] * taps[1]
                    + piece[r + 2] * taps[2]
                    + piece[r + 3] * taps[3]
                )
                if masked:
                    group = r0 + lax.broadcasted_iota(jnp.int32, (8, LANE), 0)
                    value = jnp.where(group * 12 + r < total_bytes, value, 0.0)
                conv_ref[r, rows, cols] = value
                sums[r] = sums[r] + value * score
        packed = jnp.zeros((8, LANE), f32)
        for r in range(12):
            packed = jnp.where(lane == r, jnp.sum(sums[r], axis=1, keepdims=True), packed)
        logits = [block_sum(packed, b, lane) * (1.0 / b) for b in range(1, 5)]
        best = jnp.maximum(jnp.maximum(logits[0], logits[1]), jnp.maximum(logits[2], logits[3]))
        parts = [jnp.exp(value - best) for value in logits]
        total = parts[0] + parts[1] + parts[2] + parts[3]
        mix = [part / total for part in parts]
        for b in range(4):
            mix_ref[b, rows, :] = mix[b]
        half_one = mix[0] * 0.5
        pair_two = block_sum(mix[1], 2, lane) * 0.25
        single_three = mix[2] * (1.0 / 6.0)
        pair_three = block_sum(mix[2], 2, lane) * (1.0 / 6.0)
        pair_four = block_sum(mix[3], 2, lane) * 0.125
        coef_one = [pick(half_one, r) for r in range(12)]
        coef_two = [pick(pair_two, 2 * j) for j in range(6)]
        coef_four = [pick(pair_four, 2 * j) for j in range(6)]
        coef_three = []
        for j in range(6):
            if j % 3 == 1:
                coef_three.append((pick(single_three, 2 * j), pick(single_three, 2 * j + 1)))
            else:
                coef_three.append((pick(pair_three, 2 * j), None))
        for tile in range(tiles):
            cols = slice(tile * LANE, (tile + 1) * LANE)
            conv = [conv_ref[r, rows, cols] for r in range(12)]
            two = [conv[2 * j] + conv[2 * j + 1] for j in range(6)]
            three = [conv[3 * q] + conv[3 * q + 1] + conv[3 * q + 2] for q in range(4)]
            four = [two[2 * q] + two[2 * q + 1] for q in range(3)]
            for j in range(6):
                a, b = 2 * j, 2 * j + 1
                value = coef_one[a] * conv[a] + coef_one[b] * conv[b]
                value = value + coef_two[j] * two[j] + coef_four[j] * four[j // 2]
                value = value + coef_three[j][0] * three[a // 3]
                if j % 3 == 1:
                    value = value + coef_three[j][1] * three[b // 3]
                flat[tile, pl.ds(6 * r0 + j, 8, stride=6), :] = value

    whole = (total_bytes // 12) // 8

    def plain(i, carry):
        chunk(i, False)
        return carry

    lax.fori_loop(0, whole, plain, 0)
    for i in range(whole, groups // 8):
        chunk(i, True)

    def norm(i, carry):
        rows = pl.ds(pl.multiple_of(i * 16, 16), 16)
        value = jnp.concatenate([flat[tile, rows, :] for tile in range(tiles)], axis=1)
        tok_ref[rows, :] = value
        scale = lax.rsqrt(jnp.mean(value * value, axis=1, keepdims=True) + 1e-06)
        norm_ref[rows, :] = (value * scale * gain_ref[...]).astype(bf16)
        return carry

    lax.fori_loop(0, token_count // 16, norm, 0)
    for slot in range(norm_own_ref.shape[0] // BLK):
        start = pl.multiple_of(lead_ref[slot] * BLK, BLK)
        norm_own_ref[slot * BLK : (slot + 1) * BLK, :] = norm_ref[pl.ds(start, BLK), :]
        tok_own_ref[slot * BLK : (slot + 1) * BLK, :] = tok_ref[pl.ds(start, BLK), :]


def byte_forward(seq, lead, both, table, conv_w, score_w, gain_one, total_bytes):
    width = conv_w.shape[1]
    token_count = total_bytes // 2
    least = -(-total_bytes // 12)
    groups = -(-least // 16) * 16
    row_lanes = -(-least // LANE) * LANE
    smem = pl.BlockSpec(memory_space=pltpu.SMEM)
    vmem = pl.BlockSpec(memory_space=pltpu.VMEM)
    return pl.pallas_call(
        functools.partial(byte_forward_kernel, total_bytes),
        out_shape=(
            jax.ShapeDtypeStruct((token_count, width), f32),
            jax.ShapeDtypeStruct((token_count, width), bf16),
            jax.ShapeDtypeStruct((lead.shape[0] * BLK, width), bf16),
            jax.ShapeDtypeStruct((lead.shape[0] * BLK, width), f32),
            jax.ShapeDtypeStruct((12, groups, width), f32),
            jax.ShapeDtypeStruct((4, groups, LANE), f32),
            jax.ShapeDtypeStruct((16, row_lanes), f32),
            jax.ShapeDtypeStruct((token_count, LANE), bf16),
            jax.ShapeDtypeStruct((token_count, LANE), bf16),
        ),
        in_specs=[smem, smem] + [vmem] * 5,
        scratch_shapes=[
            pltpu.VMEM(table.shape, bf16),
            pltpu.VMEM(table.shape, bf16),
            pltpu.VMEM((15, groups, width), f32),
            pltpu.VMEM((width // LANE, 6 * groups, LANE), f32),
            pltpu.VMEM((12 * row_lanes + 32, LANE), f32),
        ],
        compiler_params=pltpu.CompilerParams(vmem_limit_bytes=VMEM_CAP),
        cost_estimate=LIGHT,
        name="byte_forward",
    )(
        seq,
        lead,
        both,
        table,
        conv_w,
        score_w,
        gain_one,
    )


def byte_backward_kernel(
    total_bytes,
    first_ref,
    ids_ref,
    tok_ref,
    dnorm_ref,
    dres_ref,
    conv_ref,
    mix_ref,
    table_ref,
    conv_w_ref,
    score_ref,
    gain_ref,
    out_ref,
    dtok,
    dconv,
    onehot,
):
    groups = conv_ref.shape[1]
    width = conv_ref.shape[2]
    tiles = width // LANE
    token_count = dnorm_ref.shape[0]
    vocab_rows = onehot.shape[0]
    lanes = ids_ref.shape[1]
    gain = gain_ref[...]

    def norm_back(i, acc):
        rows = pl.ds(pl.multiple_of(i * 8, 8), 8)
        value = tok_ref[rows, :]
        grad = dnorm_ref[rows, :]
        scale = lax.rsqrt(jnp.mean(value * value, axis=1, keepdims=True) + 1e-06)
        grad_gain = grad * gain
        inner = jnp.mean(value * grad_gain, axis=1, keepdims=True)
        total = 0.5 * scale * grad_gain - value * (0.5 * scale * scale * scale * inner)
        for tile in range(tiles):
            dtok[tile, rows, :] = total[:, tile * LANE : (tile + 1) * LANE]
        return acc + grad * value * scale

    gain_acc = lax.fori_loop(0, token_count // 8, norm_back, jnp.zeros((8, width), f32))
    rest = dtok.shape[1] - token_count
    dtok[:, token_count:, :] = jnp.zeros((tiles, rest, LANE), f32)
    for slot in range(dres_ref.shape[0]):
        start = pl.multiple_of(first_ref[slot] * BLK, BLK)

        def add(i, carry, slot=slot, start=start):
            r = pl.multiple_of(i * 8, 8)
            rows = pl.ds(start + r, 8)
            more = 0.5 * dres_ref[slot, pl.ds(r, 8), :]
            for tile in range(tiles):
                dtok[tile, rows, :] = (
                    dtok[tile, rows, :] + more[:, tile * LANE : (tile + 1) * LANE]
                )
            return carry

        lax.fori_loop(0, BLK // 8, add, 0)
    vocab = lax.broadcasted_iota(jnp.int32, (vocab_rows, lanes), 0).astype(f32)
    for r in range(15):
        onehot[:, r * lanes : (r + 1) * lanes] = (vocab == ids_ref[r : r + 1, :]).astype(bf16)
    for r in range(12):
        dconv[r * lanes + groups : (r + 1) * lanes, :] = jnp.zeros((lanes - groups, width), bf16)
    lane = lane_iota(8)

    def scalars(r0):
        rows = pl.ds(r0, 8)
        one = [jnp.zeros((8, LANE), f32) for _ in range(12)]
        cross = [jnp.zeros((8, LANE), f32) for _ in range(6)]
        tri = [jnp.zeros((8, LANE), f32) for _ in range(8)]
        for tile in range(tiles):
            cols = slice(tile * LANE, (tile + 1) * LANE)
            conv = [conv_ref[r, rows, cols] for r in range(12)]
            grad = [dtok[tile, pl.ds(6 * r0 + j, 8, stride=6), :] for j in range(6)]
            two = [conv[2 * j] + conv[2 * j + 1] for j in range(6)]
            three = [conv[3 * q] + conv[3 * q + 1] + conv[3 * q + 2] for q in range(4)]
            for r in range(12):
                one[r] = one[r] + conv[r] * grad[r // 2]
            slot = 0
            for j in range(6):
                cross[j] = cross[j] + two[j ^ 1] * grad[j]
                for q in sorted({(2 * j) // 3, (2 * j + 1) // 3}):
                    tri[slot] = tri[slot] + three[q] * grad[j]
                    slot += 1
        inner_one = jnp.zeros((8, LANE), f32)
        for r in range(12):
            inner_one = jnp.where(lane == r, jnp.sum(one[r], axis=1, keepdims=True), inner_one)
        inner_cross = jnp.zeros((8, LANE), f32)
        for j in range(6):
            inner_cross = jnp.where(
                lane // 2 == j, jnp.sum(cross[j], axis=1, keepdims=True), inner_cross
            )
        inner_three = jnp.zeros((8, LANE), f32)
        slot = 0
        for j in range(6):
            for q in sorted({(2 * j) // 3, (2 * j + 1) // 3}):
                here = (lane // 2 == j) & (lane // 3 == q)
                inner_three = jnp.where(
                    here, jnp.sum(tri[slot], axis=1, keepdims=True), inner_three
                )
                slot += 1
        inner_two = block_sum(inner_one, 2, lane)
        mix = [mix_ref[b, rows, :] for b in range(4)]
        d_mix = [
            inner_one,
            inner_two * 0.5,
            inner_three * (1.0 / 3.0),
            (inner_two + inner_cross) * 0.25,
        ]
        mean = mix[0] * d_mix[0] + mix[1] * d_mix[1] + mix[2] * d_mix[2] + mix[3] * d_mix[3]
        d_logit = [mix[b] * (d_mix[b] - mean) for b in range(4)]
        d_logit = [jnp.where(lane < 12, value, 0.0) for value in d_logit]
        slope = d_logit[0]
        for b in range(2, 5):
            slope = slope + block_sum(d_logit[b - 1], b, lane) * (1.0 / b)
        pair_two = block_sum(mix[1], 2, lane) * 0.5
        single_three = mix[2] * (1.0 / 3.0)
        pair_three = block_sum(mix[2], 2, lane) * (1.0 / 3.0)
        pair_four = block_sum(mix[3], 2, lane) * 0.25
        return mix[0], pair_two, single_three, pair_three, pair_four, slope

    def spread(r0, coefs, tile, masked, score_acc):
        one, pair_two, single_three, pair_three, pair_four, slope = coefs
        rows = pl.ds(r0, 8)
        cols = slice(tile * LANE, (tile + 1) * LANE)
        grad = [dtok[tile, pl.ds(6 * r0 + j, 8, stride=6), :] for j in range(6)]
        score = score_ref[0:1, cols]
        four = [
            pick(pair_four, 4 * q) * grad[2 * q] + pick(pair_four, 4 * q + 2) * grad[2 * q + 1]
            for q in range(3)
        ]
        three = []
        for q in range(4):
            a = 3 * q
            if a % 2 == 0:
                three.append(
                    pick(pair_three, a) * grad[a // 2]
                    + pick(single_three, a + 2) * grad[a // 2 + 1]
                )
            else:
                three.append(
                    pick(single_three, a) * grad[a // 2]
                    + pick(pair_three, a + 1) * grad[a // 2 + 1]
                )
        result = []
        for r in range(12):
            weight = pick(slope, r)
            own = (pick(one, r) + pick(pair_two, r)) * grad[r // 2]
            value = own + three[r // 3] + four[r // 4] + weight * score
            score_acc = score_acc + weight * conv_ref[r, rows, cols]
            if masked:
                group = r0 + lax.broadcasted_iota(jnp.int32, (8, LANE), 0)
                value = jnp.where(group * 12 + r < total_bytes, value, 0.0)
            result.append(value)
        return result, score_acc

    def chunk(i, accs, masked):
        r0 = pl.multiple_of(i * 16, 16)
        r1 = pl.multiple_of(i * 16 + 8, 8)
        low_coefs = scalars(r0)
        high_coefs = scalars(r1)
        new = []
        for tile in range(tiles):
            cols = slice(tile * LANE, (tile + 1) * LANE)
            low, acc = spread(r0, low_coefs, tile, masked, accs[tile])
            high, acc = spread(r1, high_coefs, tile, masked, acc)
            new.append(acc)
            for r in range(12):
                both = jnp.concatenate([low[r], high[r]], axis=0).astype(bf16)
                dconv[pl.ds(pl.multiple_of(r * lanes + r0, 16), 16), cols] = both
        return tuple(new)

    accs = tuple(jnp.zeros((8, LANE), f32) for _ in range(tiles))
    whole = (total_bytes // 12) // 16
    accs = lax.fori_loop(0, whole, lambda i, a: chunk(i, a, False), accs)
    for i in range(whole, groups // 16):
        accs = chunk(i, accs, True)
    tail = [jnp.zeros((1, width), f32) for _ in range(8)]
    for k in range(4):
        part = jnp.dot(
            onehot[:, k * lanes : (k + 12) * lanes], dconv[...], preferred_element_type=f32
        )
        if k == 0:
            out_ref[0:vocab_rows, :] = part * conv_w_ref[k : k + 1, :]
        else:
            out_ref[0:vocab_rows, :] = out_ref[0:vocab_rows, :] + part * conv_w_ref[k : k + 1, :]
        tail[k] = jnp.sum(part * table_ref[0:vocab_rows, :], axis=0, keepdims=True)
    tail[4] = jnp.sum(jnp.concatenate(accs, axis=1), axis=0, keepdims=True)
    tail[5] = jnp.sum(gain_acc, axis=0, keepdims=True)
    out_ref[vocab_rows:, :] = jnp.concatenate(tail, axis=0)


def byte_backward(
    first,
    ids,
    tokens,
    d_norm,
    d_resid,
    conv,
    mix,
    table,
    vocab_rows,
    conv_w,
    score_w,
    gain_one,
    total_bytes,
):
    width = conv.shape[2]
    groups = conv.shape[1]
    lanes = ids.shape[1]
    return pl.pallas_call(
        functools.partial(byte_backward_kernel, total_bytes),
        out_shape=jax.ShapeDtypeStruct((vocab_rows + 8, width), f32),
        in_specs=[pl.BlockSpec(memory_space=pltpu.SMEM)]
        + [pl.BlockSpec(memory_space=pltpu.VMEM)] * 10,
        scratch_shapes=[
            pltpu.VMEM((width // LANE, 6 * groups, LANE), f32),
            pltpu.VMEM((12 * lanes, width), bf16),
            pltpu.VMEM((vocab_rows, 15 * lanes), bf16),
        ],
        compiler_params=pltpu.CompilerParams(vmem_limit_bytes=VMEM_CAP),
        cost_estimate=LIGHT,
        name="byte_backward",
    )(
        first,
        ids,
        tokens,
        d_norm,
        d_resid,
        conv,
        mix,
        table,
        conv_w,
        score_w,
        gain_one,
    )


def head_mask(value, head):
    half = value.shape[1] // 2
    lane = lax.broadcasted_iota(jnp.int32, value.shape, 1)
    keep = lane < half if head == 0 else lane >= half
    return jnp.where(keep, value, jnp.zeros_like(value))


def two_heads(value):
    return jnp.concatenate([head_mask(value, 0), head_mask(value, 1)], axis=0)


def bias_tiles(buckets_ref, rel_ref, tiles):
    count = tiles.shape[0]
    blocks = buckets_ref.shape[0] // 2
    reach = count // 2
    levels = rel_ref.shape[1]
    level = lax.broadcasted_iota(jnp.int32, (levels, 2 * BLK), 0)
    for n in range(count):
        row = blocks - 1 - (n - reach)
        bucket = jnp.concatenate(
            [buckets_ref[row : row + 1, :], buckets_ref[row + 1 : row + 2, :]], axis=1
        )
        onehot = (level == bucket).astype(f32)
        values = lax.dot_general(
            rel_ref[...], onehot, NN, precision=HIGH, preferred_element_type=f32
        )
        for head in range(2):
            spread = jnp.broadcast_to(values[head : head + 1, :], (BLK, 2 * BLK))
            rolled = pltpu.roll(spread, BLK + 1, 1, stride=1, stride_axis=0)
            tiles[n, :, head * BLK : (head + 1) * BLK] = rolled[:, :BLK]


def attend_kernel(
    lead_ref,
    low_ref,
    high_ref,
    q_ref,
    k_ref,
    v_ref,
    known,
    barred,
    buckets_ref,
    rel_ref,
    out_ref,
    low_out_ref,
    log_ref,
    tiles,
    v_turned,
    held,
):
    reach = tiles.shape[0] // 2
    slots = q_ref.shape[0] // BLK

    bias_tiles(buckets_ref, rel_ref.at[0], tiles)
    v_turned[...] = jnp.transpose(v_ref[...])
    for slot in range(slots):
        block = lead_ref[slot]
        first = low_ref[slot]
        last = high_ref[slot]
        base = pl.multiple_of(block * BLK, BLK)
        q_two = two_heads(q_ref[slot * BLK : (slot + 1) * BLK, :])
        bar = barred[pl.ds(base, BLK), :]
        q_full = jnp.concatenate([q_two, jnp.concatenate([bar, bar], axis=0)], axis=1)

        def score(kb, best):
            rows = pl.ds(pl.multiple_of(kb * BLK, BLK), BLK)
            k_full = jnp.concatenate([k_ref[rows, :], known[rows, :]], axis=1)
            value = lax.dot_general(k_full, q_full, NT, preferred_element_type=f32)
            value = value + tiles[kb - block + reach]
            held[kb - first] = value
            return jnp.maximum(best, jnp.max(value.reshape(BLK // 8, 8, 2 * BLK), axis=0))

        best = lax.fori_loop(first, last, score, jnp.full((8, 2 * BLK), -3e38, f32))
        best = jnp.max(best, axis=0, keepdims=True)

        def gather(kb, state):
            total, accum = state
            weight = jnp.exp(held[kb - first] - best)
            total = total + jnp.sum(weight.reshape(BLK // 8, 8, 2 * BLK), axis=0)
            cols = pl.ds(pl.multiple_of(kb * BLK, BLK), BLK)
            accum = accum + jnp.dot(
                v_turned[:, cols], weight.astype(bf16), preferred_element_type=f32
            )
            return total, accum

        total, accum = lax.fori_loop(
            first,
            last,
            gather,
            (jnp.zeros((8, 2 * BLK), f32), jnp.zeros((BLK, 2 * BLK), f32)),
        )
        total = jnp.sum(total, axis=0, keepdims=True)
        accum = accum / total
        half = BLK // 2
        both = jnp.concatenate([accum[:half, :BLK], accum[half:, BLK:]], axis=0)
        both = jnp.transpose(both)
        out_ref[slot * BLK : (slot + 1) * BLK, :] = both
        low_out_ref[slot * BLK : (slot + 1) * BLK, :] = both.astype(bf16)
        log_ref[0, slot : slot + 1, :] = best + jnp.log(total)


def attend(lead, low, high, q, k, v, known, barred, buckets, rel):
    rows, width = q.shape
    keys = k.shape[0]
    pairs = width // BLK
    blocks = keys // BLK
    slots = rows // BLK
    reach = blocks // 2
    smem = pl.BlockSpec(memory_space=pltpu.SMEM)

    def cols(count):
        return pl.BlockSpec((count, BLK), lambda i: (0, i))

    def whole(array):
        return pl.BlockSpec(array.shape, lambda i: (0,) * array.ndim)

    return pl.pallas_call(
        attend_kernel,
        grid=(pairs,),
        out_shape=(
            jax.ShapeDtypeStruct((rows, width), f32),
            jax.ShapeDtypeStruct((rows, width), bf16),
            jax.ShapeDtypeStruct((pairs, slots, 2 * BLK), f32),
        ),
        in_specs=[
            smem,
            smem,
            smem,
            cols(rows),
            cols(keys),
            cols(keys),
            whole(known),
            whole(barred),
            whole(buckets),
            pl.BlockSpec((1,) + rel.shape[1:], lambda i: (i, 0, 0)),
        ],
        out_specs=(
            cols(rows),
            cols(rows),
            pl.BlockSpec((1, slots, 2 * BLK), lambda i: (i, 0, 0)),
        ),
        scratch_shapes=[
            pltpu.VMEM((2 * reach + 1, BLK, 2 * BLK), f32),
            pltpu.VMEM((BLK, keys), bf16),
            pltpu.VMEM((blocks, BLK, 2 * BLK), f32),
        ],
        compiler_params=pltpu.CompilerParams(vmem_limit_bytes=VMEM_CAP),
        cost_estimate=LIGHT,
        name="attend",
    )(lead, low, high, q, k, v, known, barred, buckets, rel)


def attend_back_kernel(
    lead_ref,
    low_ref,
    high_ref,
    q_ref,
    k_ref,
    v_ref,
    g_ref,
    out_ref,
    log_ref,
    known,
    barred,
    buckets_ref,
    rel_ref,
    dq_ref,
    dk_ref,
    dv_ref,
    dbias_ref,
    tiles,
    k_turned,
    dk_acc,
    dv_acc,
    d_tiles,
):
    reach = tiles.shape[0] // 2
    count = tiles.shape[0]
    blocks = k_ref.shape[0] // BLK
    slots = q_ref.shape[0] // BLK
    half = BLK // 2

    bias_tiles(buckets_ref, rel_ref.at[0], tiles)
    k_turned[...] = jnp.transpose(k_ref[...])
    dk_acc[...] = jnp.zeros_like(dk_acc)
    dv_acc[...] = jnp.zeros_like(dv_acc)
    d_tiles[...] = jnp.zeros_like(d_tiles)
    sub = lax.broadcasted_iota(jnp.int32, (8, BLK), 0)
    lane = lane_iota(8)
    chooser = jnp.where((lane // half) == sub, 1.0, 0.0)
    for slot in range(slots):
        block = lead_ref[slot]
        first = low_ref[slot]
        last = high_ref[slot]
        base = pl.multiple_of(block * BLK, BLK)
        own = slice(slot * BLK, (slot + 1) * BLK)
        q_two = two_heads(q_ref[own, :])
        g_two = two_heads(g_ref[own, :])
        bar = barred[pl.ds(base, BLK), :]
        q_full = jnp.concatenate([q_two, jnp.concatenate([bar, bar], axis=0)], axis=1)
        product = g_ref[own, :].astype(f32) * out_ref[own, :]
        delta = lax.dot_general(chooser, product, NT, precision=HIGH, preferred_element_type=f32)
        delta = jnp.concatenate([delta[0:1, :], delta[1:2, :]], axis=1)
        log_total = log_ref[0, slot : slot + 1, :]

        def step(kb, dq):
            rows = pl.ds(pl.multiple_of(kb * BLK, BLK), BLK)
            k_full = jnp.concatenate([k_ref[rows, :], known[rows, :]], axis=1)
            value = lax.dot_general(k_full, q_full, NT, preferred_element_type=f32)
            prob = jnp.exp(value + tiles[kb - block + reach] - log_total)
            d_prob = lax.dot_general(v_ref[rows, :], g_two, NT, preferred_element_type=f32)
            d_score = prob * (d_prob - delta)
            d_tiles[kb - block + reach] = d_tiles[kb - block + reach] + d_score
            d_low = d_score.astype(bf16)
            dv_acc[rows, :] = dv_acc[rows, :] + jnp.dot(
                prob.astype(bf16), g_two, preferred_element_type=f32
            )
            dk_acc[rows, :] = dk_acc[rows, :] + jnp.dot(
                d_low, q_two, preferred_element_type=f32
            )
            return dq + jnp.dot(k_turned[:, rows], d_low, preferred_element_type=f32)

        dq = lax.fori_loop(first, last, step, jnp.zeros((BLK, 2 * BLK), f32))
        both = jnp.concatenate([dq[:half, :BLK], dq[half:, BLK:]], axis=0)
        dq_ref[own, :] = jnp.transpose(both).astype(bf16)
    dk_ref[...] = dk_acc[...].astype(bf16)
    dv_ref[...] = dv_acc[...].astype(bf16)
    levels = rel_ref.shape[2]
    level = lax.broadcasted_iota(jnp.int32, (levels, 2 * BLK), 0)
    total = jnp.zeros((8, levels), f32)
    pad = jnp.zeros((BLK, BLK), f32)
    mirror = (
        lax.broadcasted_iota(jnp.int32, (BLK, BLK), 0)
        + lax.broadcasted_iota(jnp.int32, (BLK, BLK), 1)
        == BLK - 1
    ).astype(bf16)
    for n in range(count):
        flipped = jnp.dot(mirror, d_tiles[n].astype(bf16), preferred_element_type=f32)
        row = blocks - 1 - (n - reach)
        bucket = jnp.concatenate(
            [buckets_ref[row : row + 1, :], buckets_ref[row + 1 : row + 2, :]], axis=1
        )
        onehot = (level == bucket).astype(f32)
        sums = []
        for head in range(2):
            part = flipped[:, head * BLK : (head + 1) * BLK]
            wide = jnp.concatenate([part, pad], axis=1)
            rolled = pltpu.roll(wide, 0, 1, stride=1, stride_axis=0)
            sums.append(jnp.sum(rolled, axis=0, keepdims=True))
        stacked = jnp.concatenate(sums + [jnp.zeros((6, 2 * BLK), f32)], axis=0)
        total = total + lax.dot_general(
            stacked, onehot, NT, precision=HIGH, preferred_element_type=f32
        )
    dbias_ref[0] = total


def attend_back(first, pairs, lead, low, high, q, k, v, g, out, log, known, barred, buckets, rel):
    rows, width = q.shape
    keys = k.shape[0]
    width = pairs * BLK
    blocks = keys // BLK
    slots = rows // BLK
    reach = blocks // 2
    levels = rel.shape[2]
    smem = pl.BlockSpec(memory_space=pltpu.SMEM)

    def cols(count):
        return pl.BlockSpec((count, BLK), lambda i: (0, i + first))

    def fresh(count):
        return pl.BlockSpec((count, BLK), lambda i: (0, i))

    def whole(array):
        return pl.BlockSpec(array.shape, lambda i: (0,) * array.ndim)

    def lead_block(shape):
        return pl.BlockSpec((1,) + shape, lambda i: (i + first,) + (0,) * len(shape))

    return pl.pallas_call(
        attend_back_kernel,
        grid=(pairs,),
        out_shape=(
            jax.ShapeDtypeStruct((rows, width), bf16),
            jax.ShapeDtypeStruct((keys, width), bf16),
            jax.ShapeDtypeStruct((keys, width), bf16),
            jax.ShapeDtypeStruct((pairs, 8, levels), f32),
        ),
        in_specs=[
            smem,
            smem,
            smem,
            cols(rows),
            cols(keys),
            cols(keys),
            cols(rows),
            cols(rows),
            lead_block((slots, 2 * BLK)),
            whole(known),
            whole(barred),
            whole(buckets),
            lead_block(rel.shape[1:]),
        ],
        out_specs=(
            fresh(rows),
            fresh(keys),
            fresh(keys),
            pl.BlockSpec((1, 8, levels), lambda i: (i, 0, 0)),
        ),
        scratch_shapes=[
            pltpu.VMEM((2 * reach + 1, BLK, 2 * BLK), f32),
            pltpu.VMEM((BLK, keys), bf16),
            pltpu.VMEM((keys, BLK), f32),
            pltpu.VMEM((keys, BLK), f32),
            pltpu.VMEM((2 * reach + 1, BLK, 2 * BLK), f32),
        ],
        compiler_params=pltpu.CompilerParams(vmem_limit_bytes=VMEM_CAP),
        cost_estimate=LIGHT,
        name="attend_back",
    )(lead, low, high, q, k, v, g, out, log, known, barred, buckets, rel)


def attention_tables(starts, ends, rel_bucket, rel_bias, lead):
    blocks = starts.shape[0]
    mine = (lead[:, None] == jnp.arange(blocks)[None, :]).astype(jnp.int32)
    own_start = jnp.sum(mine * starts[None, :], axis=1)
    own_end = jnp.sum(mine * ends[None, :], axis=1)
    low = jnp.sum((ends[None, :] < own_start[:, None]).astype(jnp.int32), axis=1)
    high = jnp.sum((starts[None, :] <= own_end[:, None]).astype(jnp.int32), axis=1)
    buckets = jnp.pad(jnp.flip(rel_bucket), (0, 1)).reshape(2 * blocks, BLK)
    levels, heads = rel_bias.shape
    rel = jnp.transpose(rel_bias).reshape(heads // 2, 2, levels)
    return low, high, buckets, rel


def pack_kernel(*refs):
    outs = [ref for ref in refs if ref.dtype == bf16]
    masters = [ref for ref in refs if ref.dtype == f32]
    at = 0
    for out in outs:
        col = 0
        while col < out.shape[1]:
            wide = masters[at].shape[1]
            out[:, col : col + wide] = masters[at][...].astype(bf16)
            col += wide
            at += 1


def pack(groups):
    steps = 1
    while all(group[0].shape[0] % (32 * steps) == 0 for group in groups) and steps < 4:
        steps *= 2

    def spec(array):
        return pl.BlockSpec((array.shape[0] // steps, array.shape[1]), lambda i: (i, 0))

    outs = tuple(
        jax.ShapeDtypeStruct((group[0].shape[0], sum(a.shape[1] for a in group)), bf16)
        for group in groups
    )
    arrays = [array for group in groups for array in group]
    return pl.pallas_call(
        pack_kernel,
        grid=(steps,),
        out_shape=outs,
        in_specs=[spec(array) for array in arrays],
        out_specs=tuple(spec(out) for out in outs),
        compiler_params=pltpu.CompilerParams(vmem_limit_bytes=VMEM_CAP),
        cost_estimate=LIGHT,
        name="pack",
    )(*arrays)


TN = (((0,), (0,)), ((), ()))


def fetch_rows(index, parts, whole, sems):
    rows = parts[0].shape[0]
    copies = []
    for j, part in enumerate(parts):
        start = pl.multiple_of((index ^ j) * rows, rows)
        copies.append(pltpu.make_async_copy(part, whole.at[pl.ds(start, rows), :], sems.at[j]))
    return copies


def project_kernel(count, index_ref, *refs):
    parts = refs[:count]
    norm_ref, own_ref, q_ref, k_ref, v_ref, whole_ref, whole, sems, done = refs[count:]
    width = norm_ref.shape[1]
    copies = fetch_rows(index_ref[0], parts, whole, sems)
    for copy in copies:
        copy.start()
    for copy in copies:
        copy.wait()
    keep = pltpu.make_async_copy(whole, whole_ref, done)
    keep.start()
    for out, rows, col in ((q_ref, own_ref, 0), (k_ref, norm_ref, 1), (v_ref, norm_ref, 2)):
        weight = whole[:, col * width : (col + 1) * width]
        for block in range(rows.shape[0] // 256):
            part = slice(block * 256, (block + 1) * 256)
            out[part, :] = jnp.dot(rows[part, :], weight, preferred_element_type=f32).astype(bf16)
    keep.wait()


def project(index, parts, norm, own):
    count = len(parts)
    width = norm.shape[1]
    full = (parts[0].shape[0] * count, parts[0].shape[1])
    vmem = pl.BlockSpec(memory_space=pltpu.VMEM)
    anywhere = pl.BlockSpec(memory_space=pl.ANY)
    return pl.pallas_call(
        functools.partial(project_kernel, count),
        out_shape=(
            jax.ShapeDtypeStruct(own.shape, bf16),
            jax.ShapeDtypeStruct(norm.shape, bf16),
            jax.ShapeDtypeStruct(norm.shape, bf16),
            jax.ShapeDtypeStruct(full, bf16),
        ),
        in_specs=[pl.BlockSpec(memory_space=pltpu.SMEM)] + [anywhere] * count + [vmem] * 2,
        out_specs=(vmem, vmem, vmem, anywhere),
        scratch_shapes=[
            pltpu.VMEM(full, bf16),
            pltpu.SemaphoreType.DMA((count,)),
            pltpu.SemaphoreType.DMA,
        ],
        compiler_params=pltpu.CompilerParams(vmem_limit_bytes=VMEM_CAP),
        cost_estimate=LIGHT,
        name="project",
    )(index, *parts, norm, own)


def project_back_kernel(count, halves, index_ref, lead_ref, norm_ref, own_ref, whole_ref, *refs):
    keep_ref, send_ref, dnorm_ref, grad_ref, sems = refs[3 * halves :]
    width = norm_ref.shape[1]
    part_width = width // halves
    for half in range(halves):
        for col in range(3):
            rows = own_ref if col == 0 else norm_ref
            here = slice(col * width + half * part_width, col * width + (half + 1) * part_width)
            grad_ref[:, here] = lax.dot_general(
                rows[...], refs[3 * half + col][...], TN, preferred_element_type=f32
            ).astype(bf16)
    for block in range(norm_ref.shape[0] // 256):
        part = slice(block * 256, (block + 1) * 256)
        total = None
        for half in range(halves):
            for col in (1, 2):
                here = slice(col * width + half * part_width, col * width + (half + 1) * part_width)
                term = lax.dot_general(
                    refs[3 * half + col][part, :],
                    whole_ref[:, here],
                    NT,
                    preferred_element_type=f32,
                )
                total = term if total is None else total + term
        dnorm_ref[part, :] = total
    for slot in range(own_ref.shape[0] // BLK):
        rows = pl.ds(pl.multiple_of(lead_ref[slot] * BLK, BLK), BLK)
        total = dnorm_ref[rows, :]
        for half in range(halves):
            total = total + lax.dot_general(
                refs[3 * half][slot * BLK : (slot + 1) * BLK, :],
                whole_ref[:, half * part_width : (half + 1) * part_width],
                NT,
                preferred_element_type=f32,
            )
        dnorm_ref[rows, :] = total
    scatter_rows(
        index_ref[0], count, ((grad_ref, 0, grad_ref.shape[1], keep_ref, send_ref),), sems
    )


def project_back(index, count, lead, norm, own, whole, halves):
    vmem = pl.BlockSpec(memory_space=pltpu.VMEM)
    anywhere = pl.BlockSpec(memory_space=pl.ANY)
    smem = pl.BlockSpec(memory_space=pltpu.SMEM)
    grads = [grad for half in halves for grad in half]
    part = jax.ShapeDtypeStruct((count // 2, whole.shape[0] // count, whole.shape[1]), bf16)
    return pl.pallas_call(
        functools.partial(project_back_kernel, count, len(halves)),
        out_shape=(part, part, jax.ShapeDtypeStruct(norm.shape, f32)),
        in_specs=[smem] * 2 + [vmem] * (3 + len(grads)),
        out_specs=(anywhere, anywhere, vmem),
        scratch_shapes=[pltpu.VMEM(whole.shape, bf16), pltpu.SemaphoreType.DMA((count,))],
        compiler_params=pltpu.CompilerParams(vmem_limit_bytes=VMEM_CAP),
        cost_estimate=LIGHT,
        name="project_back",
    )(index, lead, norm, own, whole, *grads)


ROOT = 0.7978845608028654
CUBE = 0.044715


def feed_kernel(count, index_ref, *refs):
    upper = refs[:count]
    lower = refs[count : 2 * count]
    (
        tok_ref,
        att_ref,
        cot_ref,
        gain_ref,
        out_ref,
        d_att_ref,
        d_resid_ref,
        gain_grad_ref,
        left_keep,
        left_send,
        right_keep,
        right_send,
        ogu,
        down,
        store,
        resid,
        norm,
        d_norm,
        total,
        hid,
        d_gate,
        d_up,
        sems_upper,
        sems_lower,
        sems_store,
    ) = refs[2 * count :]
    rows, width = tok_ref.shape
    hidden = down.shape[0]
    copies_upper = fetch_rows(index_ref[0], upper, ogu, sems_upper)
    copies_lower = fetch_rows(index_ref[0], lower, down, sems_lower)
    for copy in copies_upper + copies_lower:
        copy.start()
    for copy in copies_upper:
        copy.wait()
    gain = gain_ref[...]
    row_step = 128
    tile = 512
    for block in range(rows // row_step):
        part = slice(block * row_step, (block + 1) * row_step)
        value = tok_ref[part, :] + jnp.dot(
            att_ref[part, :], ogu[:, :width], preferred_element_type=f32
        )
        resid[part, :] = value
        scale = lax.rsqrt(jnp.mean(value * value, axis=1, keepdims=True) + 1e-06)
        norm[part, :] = (value * scale * gain).astype(bf16)
    for copy in copies_lower:
        copy.wait()
    for n in range(hidden // tile):
        here = slice(n * tile, (n + 1) * tile)
        gate_cols = slice(width + n * tile, width + (n + 1) * tile)
        up_cols = slice(width + hidden + n * tile, width + hidden + (n + 1) * tile)
        for block in range(rows // row_step):
            part = slice(block * row_step, (block + 1) * row_step)
            gate_pre = jnp.dot(norm[part, :], ogu[:, gate_cols], preferred_element_type=f32)
            up_pre = jnp.dot(norm[part, :], ogu[:, up_cols], preferred_element_type=f32)
            d_hidden = lax.dot_general(
                cot_ref[part, :], down[here, :], NT, preferred_element_type=f32
            )
            square = gate_pre * gate_pre
            bent = jnp.tanh(ROOT * gate_pre * (1.0 + CUBE * square))
            half = 0.5 + 0.5 * bent
            gelu = gate_pre * half
            slope = half + (0.5 * ROOT) * gate_pre * (1.0 - bent * bent) * (
                1.0 + (3.0 * CUBE) * square
            )
            low = (gelu * up_pre).astype(bf16)
            d_gate_low = (d_hidden * up_pre * slope).astype(bf16)
            d_up_low = (d_hidden * gelu).astype(bf16)
            hid[part, :] = low
            d_gate[part, :] = d_gate_low
            d_up[part, :] = d_up_low
            add = jnp.dot(low, down[here, :], preferred_element_type=f32)
            back = lax.dot_general(
                d_gate_low, ogu[:, gate_cols], NT, preferred_element_type=f32
            ) + lax.dot_general(d_up_low, ogu[:, up_cols], NT, preferred_element_type=f32)
            if n == 0:
                total[part, :] = resid[part, :] + add
                d_norm[part, :] = back
            else:
                total[part, :] = total[part, :] + add
                d_norm[part, :] = d_norm[part, :] + back
        store[:, gate_cols] = lax.dot_general(
            norm[...], d_gate[...], TN, preferred_element_type=f32
        ).astype(bf16)
        store[:, up_cols] = lax.dot_general(
            norm[...], d_up[...], TN, preferred_element_type=f32
        ).astype(bf16)
        part = lax.dot_general(
            hid[...], cot_ref[...], TN, preferred_element_type=f32
        ).astype(bf16)
        for low_row, low_col, row, size in down_pieces(width // count, hidden // count, width):
            for device in range(count):
                source = device * (hidden // count) + low_row
                if n * tile <= source < (n + 1) * tile:
                    source = source - n * tile
                    target = device * (width // count) + row
                    col = width + 2 * hidden + low_col[1]
                    store[target : target + size, col : col + LANE] = part[
                        source : source + size, low_col[0] : low_col[0] + LANE
                    ]
    gain_sum = jnp.zeros((1, width), f32)
    for block in range(rows // row_step):
        part = slice(block * row_step, (block + 1) * row_step)
        out_ref[part, :] = total[part, :].astype(bf16)
        value = resid[part, :]
        grad = d_norm[part, :]
        scale = lax.rsqrt(jnp.mean(value * value, axis=1, keepdims=True) + 1e-06)
        scaled = grad * gain
        inner = jnp.mean(value * scaled, axis=1, keepdims=True)
        d_value = (
            cot_ref[part, :].astype(f32)
            + scale * scaled
            - value * (scale * scale * scale * inner)
        )
        gain_sum = gain_sum + jnp.sum(grad * value * scale, axis=0, keepdims=True)
        d_resid_ref[part, :] = d_value
        d_low = d_value.astype(bf16)
        norm[part, :] = d_low
        d_att_ref[part, :] = lax.dot_general(
            d_low, ogu[:, :width], NT, preferred_element_type=f32
        ).astype(bf16)
    gain_grad_ref[...] = gain_sum
    store[:, :width] = lax.dot_general(
        att_ref[...], norm[...], TN, preferred_element_type=f32
    ).astype(bf16)
    half = store.shape[1] // 2
    scatter_rows(
        index_ref[0],
        count,
        ((store, 0, half, left_keep, left_send), (store, half, half, right_keep, right_send)),
        sems_store,
    )


def scatter_rows(index, count, jobs, sems):
    rows = jobs[0][0].shape[0] // count
    waits = []
    for n, (source, first, wide, keep, send) in enumerate(jobs):
        for device in range(count):
            other = index ^ device
            part = source.at[device * rows : (device + 1) * rows, first : first + wide]
            sem = sems.at[n * count + device]

            @pl.when(other % 2 == 0)
            def _():
                pltpu.make_async_copy(part, keep.at[other // 2], sem).start()

            @pl.when(other % 2 == 1)
            def _():
                pltpu.make_async_copy(part, send.at[other // 2], sem).start()

            waits.append(pltpu.make_async_copy(part, keep.at[0], sem))
    for wait in waits:
        wait.wait()


def down_pieces(rows, tall, width):
    size = 16
    while tall % (2 * size) == 0 and rows % (2 * size) == 0:
        size *= 2
    pieces = []
    for q in range(tall * (width // LANE) // size):
        there = (q % (tall // size)) * size
        here = (q % (rows // size)) * size
        pieces.append((there, (q // (tall // size) * LANE, q // (rows // size) * LANE), here, size))
    return pieces


def unpack_kernel(hidden, left_ref, right_ref, qkv_ref, *outs):
    rows = left_ref.shape[0]
    half = left_ref.shape[1]
    width = outs[0].shape[1]
    for n in range(3):
        outs[n][...] = qkv_ref[:, n * width : (n + 1) * width].astype(f32)

    def column(first, last):
        parts = []
        if first < half:
            parts.append((left_ref, first, min(last, half), 0))
        if last > half:
            begin = max(first, half)
            parts.append((right_ref, begin - half, last - half, begin - first))
        return parts

    spans = ((0, width), (width, width + hidden), (width + hidden, width + 2 * hidden))
    for out, (first, last) in zip(outs[3:6], spans):
        for ref, begin, end, at in column(first, last):
            out[:, at : at + end - begin] = ref[:, begin:end].astype(f32)
    base = width + 2 * hidden - half
    for there, (col_there, col_here), here, size in down_pieces(rows, outs[6].shape[0], width):
        outs[6][there : there + size, col_there : col_there + LANE] = right_ref[
            here : here + size, base + col_here : base + col_here + LANE
        ].astype(f32)


def unpack(left, right, qkv, hidden, tall):
    rows = left.shape[0]
    width = qkv.shape[1] // 3
    shapes = [(rows, width)] * 4 + [(rows, hidden)] * 2 + [(tall, width)]
    return pl.pallas_call(
        functools.partial(unpack_kernel, hidden),
        out_shape=tuple(jax.ShapeDtypeStruct(shape, f32) for shape in shapes),
        compiler_params=pltpu.CompilerParams(vmem_limit_bytes=VMEM_CAP),
        cost_estimate=LIGHT,
        name="unpack",
    )(left, right, qkv)


def feed(index, upper, lower, tokens, attended, cotangent, gain):
    count = len(upper)
    rows, width = tokens.shape
    full_upper = (upper[0].shape[0] * count, upper[0].shape[1])
    full_lower = (lower[0].shape[0] * count, width)
    hidden = full_lower[0]
    columns = width + 3 * hidden
    vmem = pl.BlockSpec(memory_space=pltpu.VMEM)
    anywhere = pl.BlockSpec(memory_space=pl.ANY)
    tile = 512
    return pl.pallas_call(
        functools.partial(feed_kernel, count),
        out_shape=(
            jax.ShapeDtypeStruct((rows, width), bf16),
            jax.ShapeDtypeStruct((rows, width), bf16),
            jax.ShapeDtypeStruct((rows, width), f32),
            jax.ShapeDtypeStruct((1, width), f32),
            *[jax.ShapeDtypeStruct((count // 2, width // count, columns // 2), bf16)] * 4,
        ),
        in_specs=[pl.BlockSpec(memory_space=pltpu.SMEM)]
        + [anywhere] * (2 * count)
        + [vmem] * 4,
        out_specs=(vmem,) * 4 + (anywhere,) * 4,
        scratch_shapes=[
            pltpu.VMEM(full_upper, bf16),
            pltpu.VMEM(full_lower, bf16),
            pltpu.VMEM((width, columns), bf16),
            pltpu.VMEM((rows, width), f32),
            pltpu.VMEM((rows, width), bf16),
            pltpu.VMEM((rows, width), f32),
            pltpu.VMEM((rows, width), f32),
            pltpu.VMEM((rows, tile), bf16),
            pltpu.VMEM((rows, tile), bf16),
            pltpu.VMEM((rows, tile), bf16),
            pltpu.SemaphoreType.DMA((count,)),
            pltpu.SemaphoreType.DMA((count,)),
            pltpu.SemaphoreType.DMA((2 * count,)),
        ],
        compiler_params=pltpu.CompilerParams(vmem_limit_bytes=VMEM_CAP),
        cost_estimate=LIGHT,
        name="feed",
    )(index, *upper, *lower, tokens, attended, cotangent, gain.reshape(1, width))


def bits_of(count):
    bits = count.bit_length() - 1
    assert 1 << bits == count
    return bits


def swap(value, axis, bit):
    count = lax.axis_size(axis)
    return lax.ppermute(value, axis, [(i, i ^ (1 << bit)) for i in range(count)])


def ordered(mine, other, index, bit, axis=0):
    upper = ((index >> bit) & 1) == 1
    return jnp.concatenate(
        [jnp.where(upper, other, mine), jnp.where(upper, mine, other)], axis=axis
    )


def gather_small(value, axis):
    index = lax.axis_index(axis)
    value = value[None]
    for bit in range(bits_of(lax.axis_size(axis))):
        value = ordered(value, swap(value, axis, bit), index, bit)
    return value


def first_swap(shard, axis):
    bit = bits_of(lax.axis_size(axis)) - 1
    return [(0, shard), (1 << bit, swap(shard, axis, bit))]


def other_swaps(parts, axis):
    for bit in reversed(range(bits_of(lax.axis_size(axis)) - 1)):
        parts = parts + [(j | (1 << bit), swap(part, axis, bit)) for j, part in parts]
    return [part for _, part in sorted(parts, key=lambda pair: pair[0])]


def after(anchor, part):
    j, array = part
    anchor, array = lax.optimization_barrier((anchor, array))
    return anchor, (j, array)


def add_low(left, right):
    return (left.astype(f32) + right.astype(f32)).astype(bf16)


def piece(value, index, dim=0):
    return lax.dynamic_index_in_dim(value, index, dim, keepdims=False)


def scatter_step(value, axis, bit, dim):
    own = (lax.axis_index(axis) >> bit) & 1
    other = swap(piece(value, 1 - own, dim), axis, bit)
    return add_low(piece(value, own, dim), other)


def rest_sum(value, axis):
    count = lax.axis_size(axis)
    index = lax.axis_index(axis)
    mine = index // 2
    total = piece(value, mine).astype(f32)
    for j in range(1, count // 2):
        pairs = [(i, ((i // 2) ^ j) * 2 + i % 2) for i in range(count)]
        total = total + lax.ppermute(piece(value, mine ^ j), axis, pairs).astype(f32)
    return total.astype(bf16)


def rest_gather(value, axis):
    count = lax.axis_size(axis)
    index = lax.axis_index(axis)
    whole = jnp.zeros((count // 2,) + value.shape, value.dtype)
    for j in range(count // 2):
        part = value
        if j:
            pairs = [(i, ((i // 2) ^ j) * 2 + i % 2) for i in range(count)]
            part = lax.ppermute(value, axis, pairs)
        whole = lax.dynamic_update_index_in_dim(whole, part, (index // 2) ^ j, 0)
    return whole


def pair_gather(whole, axis):
    other = swap(whole, axis, 0)
    upper = lax.axis_index(axis) % 2 == 1
    both = jnp.stack([jnp.where(upper, other, whole), jnp.where(upper, whole, other)], axis=1)
    return both.reshape((2 * whole.shape[0] * whole.shape[1],) + whole.shape[2:])


class Chain:
    def __init__(self, keep, send, whole_sum=False):
        self.whole_sum = whole_sum
        self.steps = self.run(keep, send)
        self.value = next(self.steps)

    def run(self, keep, send):
        bits = bits_of(lax.axis_size("fsdp"))
        for bit in range(bits):
            other = swap(send, "fsdp", bit)
            if bit == bits - 1:
                break
            left = keep.shape[0] // 2
            split = (left, 2) + keep.shape[1:]
            keep, other = keep.reshape(split), other.reshape(split)
            send = add_low(keep[:, 1], other[:, 1])
            keep = keep[:, 0].astype(f32) + other[:, 0].astype(f32)
            (keep, send) = yield (keep, send)
        total = yield add_low(keep, other)[0]
        if self.whole_sum:
            yield lax.psum(total, "ctx")
            return
        count = lax.axis_size("ctx")
        total = total.reshape((count // 2, 2, total.shape[0] // count) + total.shape[1:])
        total = yield scatter_step(total, "ctx", 0, 1)
        total = yield rest_sum(total, "ctx")
        total = yield rest_gather(total, "ctx")
        yield pair_gather(total, "ctx")

    def advance(self, value):
        self.value = self.steps.send(value)

    def finish(self):
        while True:
            try:
                self.advance(self.value)
            except StopIteration:
                return self.value


def gate(anchor, *chains):
    joined = lax.optimization_barrier((anchor,) + tuple(chain.value for chain in chains))
    for chain, value in zip(chains, joined[1:]):
        chain.advance(value)
    return joined[0]


def reduce_small(value, early):
    fsdp_bits = bits_of(lax.axis_size("fsdp"))
    count = lax.axis_size("ctx")
    rows, width = value.shape
    value = value.reshape(2, count // 2, 2 * rows // (2 * count), width)
    value = scatter_step(value, "fsdp", 0, 0)
    value = rest_sum(value, "ctx")
    value, early.value = lax.optimization_barrier((value, early.value))
    value = add_low(value, swap(value, "ctx", 0))
    for bit in range(1, fsdp_bits):
        value = add_low(value, swap(value, "fsdp", bit))
    whole = rest_gather(value, "ctx")
    whole = whole.reshape((rows // 2, width))
    return ordered(whole, swap(whole, "fsdp", 0), lax.axis_index("fsdp"), 0)


def local(
    byte_ids,
    doc_ids,
    rel_bucket,
    table,
    conv_w,
    score_w,
    gain_one,
    gain_two,
    rel_bias,
    query_master,
    key_master,
    value_master,
    out_master,
    gate_master,
    up_master,
    down_master,
    out_cotangent,
):
    ctx_count = lax.axis_size("ctx")
    ctx_index = lax.axis_index("ctx")
    seq_count, byte_count = byte_ids.shape
    total_bytes = byte_count * ctx_count
    width = table.shape[1]
    vocab = table.shape[0]
    hidden_width = gate_master.shape[1]
    levels, heads = rel_bias.shape
    share = ctx_count // seq_count
    assert share * seq_count == ctx_count and byte_count == 2 * BLK
    seq = ctx_index // share
    part = ctx_index % share
    near = [seq ^ slot for slot in range(seq_count)]
    lead = jnp.stack([share * other + part for other in near]).astype(jnp.int32)
    rows = seq_count * BLK

    qkv_low, down_low, ogu_low = pack(
        [[query_master, key_master, value_master], [down_master], [out_master, gate_master, up_master]]
    )
    both = jnp.stack([byte_ids, doc_ids], axis=1)
    both, qkv_low = lax.optimization_barrier((both, qkv_low))
    qkv_parts = first_swap(qkv_low, "fsdp")
    both = gather_small(both, "ctx")
    both, qkv_parts[1] = after(both, qkv_parts[1])
    both, down_low = lax.optimization_barrier((both, down_low))
    shard = lax.axis_index("fsdp")[None]
    shards = lax.axis_size("fsdp")

    def to_owner(block, slot):
        if slot == 0:
            return block
        pairs = []
        for c in range(ctx_count):
            pairs.append((c, ((c // share) ^ slot) * share + c % share))
        return lax.ppermute(block, "ctx", pairs)

    table_wide = jnp.pad(table, ((0, -vocab % LANE), (0, 0)))
    score_row = score_w.reshape(1, width)
    gain_row = gain_one.reshape(1, width)
    seq_row = seq[None]
    tokens, norm_one, norm_own, tokens_own, conv, mix, phases, known, barred = byte_forward(
        seq_row, lead, both, table_wide, conv_w, score_row, gain_row, total_bytes
    )
    down_parts = first_swap(down_low, "fsdp")
    qkv_parts = other_swaps(qkv_parts, "fsdp")
    queries, keys, values, qkv = project(shard, qkv_parts, norm_one, norm_own)
    blocks = [to_owner(piece(out_cotangent, near[s], 1), s) for s in range(seq_count)]
    queries, ogu_low, blocks, down_parts = lax.optimization_barrier(
        (queries, ogu_low, blocks, [part for _, part in down_parts])
    )
    down_parts = [(0, down_parts[0]), (shards // 2, down_parts[1])]
    docs = piece(both[:, :, 1], seq, 1)
    low, high, buckets, rel = attention_tables(
        docs[:, 0], docs[:, 2 * BLK - 2], rel_bucket, rel_bias, lead
    )
    ogu_parts = first_swap(ogu_low, "fsdp")
    down_parts = other_swaps(down_parts, "fsdp")
    attended, attended_low, log_total = attend(
        lead, low, high, queries, keys, values, known, barred, buckets, rel
    )
    cotangent = jnp.concatenate(blocks, axis=0)

    attended_low, ogu_parts[1] = after(attended_low, ogu_parts[1])
    output, d_attended, d_resid, grad_gain_two, *grads = feed(
        shard,
        other_swaps(ogu_parts, "fsdp"),
        down_parts,
        tokens_own,
        attended_low,
        cotangent,
        gain_two,
    )
    left = Chain(*grads[:2], whole_sum=True)
    right = Chain(*grads[2:])
    d_attended = gate(d_attended, left, right)

    output = output.reshape(seq_count, BLK, width)
    arrived = [to_owner(output[s], s) for s in range(seq_count)]

    pairs = heads // 2
    cut = pairs // 2
    halves = []
    for first, count in ((0, cut), (cut, pairs - cut)):
        if first:
            d_attended = gate(d_attended, left)
            d_attended, arrived = lax.optimization_barrier((d_attended, arrived))
            arrived = jnp.stack(arrived)
            output = jnp.stack([piece(arrived, seq ^ s) for s in range(seq_count)], axis=1)
        *grads, d_bias = attend_back(
            first,
            count,
            lead,
            low,
            high,
            queries,
            keys,
            values,
            d_attended,
            attended,
            log_total,
            known,
            barred,
            buckets,
            rel,
        )
        halves.append((grads, d_bias))
        d_attended, _ = lax.optimization_barrier((d_attended, grads[0]))
    d_bias = jnp.concatenate([half[1] for half in halves], axis=0)
    norm_own, halves = gate((norm_own, [half[0] for half in halves]), right)
    keep, send, d_norm_one = project_back(shard, shards, lead, norm_one, norm_own, qkv, halves)
    qkv_chain = Chain(keep, send)
    d_norm_one = gate(d_norm_one, qkv_chain, right)

    vocab_rows = -(-vocab // 16) * 16
    d_resid = d_resid.reshape(seq_count, BLK, width)
    small = byte_backward(
        lead,
        phases,
        tokens,
        d_norm_one,
        d_resid,
        conv,
        mix,
        table_wide,
        vocab_rows,
        conv_w,
        score_row,
        gain_row,
        total_bytes,
    )
    bias_grad = jnp.transpose(d_bias[:, :2].reshape(heads, levels)).reshape(1, levels * heads)
    bias_grad = jnp.pad(bias_grad, ((0, 0), (0, width - levels * heads)))
    small = jnp.concatenate([small[: vocab_rows + 6], grad_gain_two, bias_grad], axis=0)
    small = jnp.pad(small, ((0, -small.shape[0] % (8 * ctx_count)), (0, 0))).astype(bf16)
    small = gate(small, qkv_chain, right)
    small = reduce_small(small, left).astype(f32)
    grads = unpack(
        left.finish(), right.finish(), qkv_chain.finish(), hidden_width, down_master.shape[0]
    )
    top = vocab_rows
    return (
        output,
        small[:vocab],
        small[top : top + 4],
        small[top + 4],
        small[top + 5],
        small[top + 6],
        small[top + 7, : levels * heads].reshape(levels, heads),
        *grads,
    )


def solution(mesh):
    placed = (
        P("fsdp", "ctx"),
        P("fsdp", "ctx"),
        P(),
        P(),
        P(),
        P(),
        P(),
        P(),
        P(),
        P("fsdp", None),
        P("fsdp", None),
        P("fsdp", None),
        P("fsdp", None),
        P("fsdp", None),
        P("fsdp", None),
        P("fsdp", None),
        P("ctx", "fsdp", None),
    )
    return jax.shard_map(
        local,
        mesh=mesh,
        in_specs=placed,
        out_specs=(
            P("ctx", "fsdp", None),
            P(),
            P(),
            P(),
            P(),
            P(),
            P(),
            P("fsdp", None),
            P("fsdp", None),
            P("fsdp", None),
            P("fsdp", None),
            P("fsdp", None),
            P("fsdp", None),
            P("fsdp", None),
        ),
        check_vma=False,
    )
```

```python
import functools

import jax
import jax.numpy as jnp
from jax import lax
from jax.experimental import pallas as pl
from jax.experimental.pallas import tpu as pltpu
from jax.sharding import PartitionSpec as P

f32 = jnp.float32
bf16 = jnp.bfloat16
LANE = 128
BLK = 128
VMEM_CAP = 60 * 1024 * 1024
HIGH = lax.Precision.HIGHEST
NT = (((1,), (1,)), ((), ()))
NN = (((1,), (0,)), ((), ()))
LIGHT = pl.CostEstimate(flops=1, transcendentals=0, bytes_accessed=1)


def lane_iota(rows):
    return lax.broadcasted_iota(jnp.int32, (rows, LANE), 1)


def block_sum(value, width, lane):
    def ahead(v, n):
        return pltpu.roll(v, LANE - n, 1)

    def behind(v, n):
        return pltpu.roll(v, n, 1)

    if width == 1:
        return value
    if width == 3:
        lead = value + ahead(value, 1) + ahead(value, 2)
        phase = lane % 3
        return jnp.where(phase == 0, lead, jnp.where(phase == 1, behind(lead, 1), behind(lead, 2)))
    pair = value + jnp.where(lane % 2 == 0, ahead(value, 1), behind(value, 1))
    if width == 2:
        return pair
    return pair + jnp.where(lane % 4 < 2, ahead(pair, 2), behind(pair, 2))


def pick(value, lane_index):
    return value[:, lane_index : lane_index + 1]


def byte_forward_kernel(
    total_bytes,
    seq_ref,
    lead_ref,
    both_ref,
    table_ref,
    conv_w_ref,
    score_ref,
    gain_ref,
    tok_ref,
    norm_ref,
    norm_own_ref,
    tok_own_ref,
    conv_ref,
    mix_ref,
    ids_ref,
    known_ref,
    barred_ref,
    hi_ref,
    lo_ref,
    emb,
    flat,
    spread,
):
    groups = conv_ref.shape[1]
    width = conv_ref.shape[2]
    tiles = width // LANE
    token_count = norm_ref.shape[0]
    vocab_pad = table_ref.shape[0]
    row_lanes = ids_ref.shape[1]
    seq = seq_ref[0]
    high = table_ref[...].astype(bf16)
    hi_ref[...] = high
    lo_ref[...] = (table_ref[...] - high.astype(f32)).astype(bf16)
    lane_f = lane_iota(BLK).astype(f32)
    chunk_bytes = both_ref.shape[3]

    def lay(kind, first):
        for block in range(both_ref.shape[0]):
            row = both_ref[block, seq, kind : kind + 1, :].astype(f32)
            for half in range(chunk_bytes // LANE):
                part = jnp.broadcast_to(row[:, half * LANE : (half + 1) * LANE], (LANE, LANE))
                start = first + block * chunk_bytes + half * LANE
                spread[start : start + LANE, :] = jnp.transpose(part)

    lay(1, 0)
    for block in range(token_count // BLK):
        docs = spread[pl.ds(block * 2 * BLK, BLK, stride=2), :]
        same = docs == lane_f
        rows = slice(block * BLK, (block + 1) * BLK)
        known_ref[rows, :] = same.astype(bf16)
        barred_ref[rows, :] = jnp.where(same | (lane_f >= 16.0), 0.0, -1e30).astype(bf16)
    lay(0, 16)
    none = jnp.full((16, LANE), -1.0, f32)
    spread[0:16, :] = none
    tail = spread.shape[0] - total_bytes - 16
    spread[total_bytes + 16 :, :] = jnp.full((tail, LANE), -1.0, f32)
    lane_g = lane_iota(groups).astype(f32)
    for r in range(15):
        here = spread[pl.ds(13 + r, row_lanes, stride=12), :]
        turned = [
            jnp.transpose(here[n * LANE : (n + 1) * LANE, :])[0:1, :]
            for n in range(row_lanes // LANE)
        ]
        ids_ref[r : r + 1, :] = jnp.concatenate(turned, axis=1)
        onehot = jnp.concatenate(
            [
                (here[0:groups, :] == lane_g + n * LANE).astype(bf16)
                for n in range(vocab_pad // LANE)
            ],
            axis=1,
        )
        emb[r] = jnp.dot(onehot, hi_ref[...], preferred_element_type=f32) + jnp.dot(
            onehot, lo_ref[...], preferred_element_type=f32
        )
    ids_ref[15:16, :] = jnp.full((1, row_lanes), -1.0, f32)
    lane = lane_iota(8)

    def chunk(i, masked):
        r0 = pl.multiple_of(i * 8, 8)
        rows = pl.ds(r0, 8)
        sums = [jnp.zeros((8, LANE), f32) for _ in range(12)]
        for tile in range(tiles):
            cols = slice(tile * LANE, (tile + 1) * LANE)
            taps = [conv_w_ref[k : k + 1, cols] for k in range(4)]
            piece = [emb[r, rows, cols] for r in range(15)]
            score = score_ref[0:1, cols]
            for r in range(12):
                value = (
                    piece[r] * taps[0]
                    + piece[r + 1] * taps[1]
                    + piece[r + 2] * taps[2]
                    + piece[r + 3] * taps[3]
                )
                if masked:
                    group = r0 + lax.broadcasted_iota(jnp.int32, (8, LANE), 0)
                    value = jnp.where(group * 12 + r < total_bytes, value, 0.0)
                conv_ref[r, rows, cols] = value
                sums[r] = sums[r] + value * score
        packed = jnp.zeros((8, LANE), f32)
        for r in range(12):
            packed = jnp.where(lane == r, jnp.sum(sums[r], axis=1, keepdims=True), packed)
        logits = [block_sum(packed, b, lane) * (1.0 / b) for b in range(1, 5)]
        best = jnp.maximum(jnp.maximum(logits[0], logits[1]), jnp.maximum(logits[2], logits[3]))
        parts = [jnp.exp(value - best) for value in logits]
        total = parts[0] + parts[1] + parts[2] + parts[3]
        mix = [part / total for part in parts]
        for b in range(4):
            mix_ref[b, rows, :] = mix[b]
        half_one = mix[0] * 0.5
        pair_two = block_sum(mix[1], 2, lane) * 0.25
        single_three = mix[2] * (1.0 / 6.0)
        pair_three = block_sum(mix[2], 2, lane) * (1.0 / 6.0)
        pair_four = block_sum(mix[3], 2, lane) * 0.125
        coef_one = [pick(half_one, r) for r in range(12)]
        coef_two = [pick(pair_two, 2 * j) for j in range(6)]
        coef_four = [pick(pair_four, 2 * j) for j in range(6)]
        coef_three = []
        for j in range(6):
            if j % 3 == 1:
                coef_three.append((pick(single_three, 2 * j), pick(single_three, 2 * j + 1)))
            else:
                coef_three.append((pick(pair_three, 2 * j), None))
        for tile in range(tiles):
            cols = slice(tile * LANE, (tile + 1) * LANE)
            conv = [conv_ref[r, rows, cols] for r in range(12)]
            two = [conv[2 * j] + conv[2 * j + 1] for j in range(6)]
            three = [conv[3 * q] + conv[3 * q + 1] + conv[3 * q + 2] for q in range(4)]
            four = [two[2 * q] + two[2 * q + 1] for q in range(3)]
            for j in range(6):
                a, b = 2 * j, 2 * j + 1
                value = coef_one[a] * conv[a] + coef_one[b] * conv[b]
                value = value + coef_two[j] * two[j] + coef_four[j] * four[j // 2]
                value = value + coef_three[j][0] * three[a // 3]
                if j % 3 == 1:
                    value = value + coef_three[j][1] * three[b // 3]
                flat[tile, pl.ds(6 * r0 + j, 8, stride=6), :] = value

    whole = (total_bytes // 12) // 8

    def plain(i, carry):
        chunk(i, False)
        return carry

    lax.fori_loop(0, whole, plain, 0)
    for i in range(whole, groups // 8):
        chunk(i, True)

    def norm(i, carry):
        rows = pl.ds(pl.multiple_of(i * 16, 16), 16)
        value = jnp.concatenate([flat[tile, rows, :] for tile in range(tiles)], axis=1)
        tok_ref[rows, :] = value
        scale = lax.rsqrt(jnp.mean(value * value, axis=1, keepdims=True) + 1e-06)
        norm_ref[rows, :] = (value * scale * gain_ref[...]).astype(bf16)
        return carry

    lax.fori_loop(0, token_count // 16, norm, 0)
    for slot in range(norm_own_ref.shape[0] // BLK):
        start = pl.multiple_of(lead_ref[slot] * BLK, BLK)
        norm_own_ref[slot * BLK : (slot + 1) * BLK, :] = norm_ref[pl.ds(start, BLK), :]
        tok_own_ref[slot * BLK : (slot + 1) * BLK, :] = tok_ref[pl.ds(start, BLK), :]


def byte_forward(seq, lead, both, table, conv_w, score_w, gain_one, total_bytes):
    width = conv_w.shape[1]
    token_count = total_bytes // 2
    least = -(-total_bytes // 12)
    groups = -(-least // 16) * 16
    row_lanes = -(-least // LANE) * LANE
    smem = pl.BlockSpec(memory_space=pltpu.SMEM)
    vmem = pl.BlockSpec(memory_space=pltpu.VMEM)
    return pl.pallas_call(
        functools.partial(byte_forward_kernel, total_bytes),
        out_shape=(
            jax.ShapeDtypeStruct((token_count, width), f32),
            jax.ShapeDtypeStruct((token_count, width), bf16),
            jax.ShapeDtypeStruct((lead.shape[0] * BLK, width), bf16),
            jax.ShapeDtypeStruct((lead.shape[0] * BLK, width), f32),
            jax.ShapeDtypeStruct((12, groups, width), f32),
            jax.ShapeDtypeStruct((4, groups, LANE), f32),
            jax.ShapeDtypeStruct((16, row_lanes), f32),
            jax.ShapeDtypeStruct((token_count, LANE), bf16),
            jax.ShapeDtypeStruct((token_count, LANE), bf16),
        ),
        in_specs=[smem, smem] + [vmem] * 5,
        scratch_shapes=[
            pltpu.VMEM(table.shape, bf16),
            pltpu.VMEM(table.shape, bf16),
            pltpu.VMEM((15, groups, width), f32),
            pltpu.VMEM((width // LANE, 6 * groups, LANE), f32),
            pltpu.VMEM((12 * row_lanes + 32, LANE), f32),
        ],
        compiler_params=pltpu.CompilerParams(vmem_limit_bytes=VMEM_CAP),
        cost_estimate=LIGHT,
        name="byte_forward",
    )(
        seq,
        lead,
        both,
        table,
        conv_w,
        score_w,
        gain_one,
    )


def byte_backward_kernel(
    total_bytes,
    first_ref,
    ids_ref,
    tok_ref,
    dnorm_ref,
    dres_ref,
    conv_ref,
    mix_ref,
    table_ref,
    conv_w_ref,
    score_ref,
    gain_ref,
    out_ref,
    dtok,
    dconv,
    onehot,
):
    groups = conv_ref.shape[1]
    width = conv_ref.shape[2]
    tiles = width // LANE
    token_count = dnorm_ref.shape[0]
    vocab_rows = onehot.shape[0]
    lanes = ids_ref.shape[1]
    gain = gain_ref[...]

    def norm_back(i, acc):
        rows = pl.ds(pl.multiple_of(i * 8, 8), 8)
        value = tok_ref[rows, :]
        grad = dnorm_ref[rows, :]
        scale = lax.rsqrt(jnp.mean(value * value, axis=1, keepdims=True) + 1e-06)
        grad_gain = grad * gain
        inner = jnp.mean(value * grad_gain, axis=1, keepdims=True)
        total = 0.5 * scale * grad_gain - value * (0.5 * scale * scale * scale * inner)
        for tile in range(tiles):
            dtok[tile, rows, :] = total[:, tile * LANE : (tile + 1) * LANE]
        return acc + grad * value * scale

    gain_acc = lax.fori_loop(0, token_count // 8, norm_back, jnp.zeros((8, width), f32))
    rest = dtok.shape[1] - token_count
    dtok[:, token_count:, :] = jnp.zeros((tiles, rest, LANE), f32)
    for slot in range(dres_ref.shape[0]):
        start = pl.multiple_of(first_ref[slot] * BLK, BLK)

        def add(i, carry, slot=slot, start=start):
            r = pl.multiple_of(i * 8, 8)
            rows = pl.ds(start + r, 8)
            more = 0.5 * dres_ref[slot, pl.ds(r, 8), :]
            for tile in range(tiles):
                dtok[tile, rows, :] = (
                    dtok[tile, rows, :] + more[:, tile * LANE : (tile + 1) * LANE]
                )
            return carry

        lax.fori_loop(0, BLK // 8, add, 0)
    vocab = lax.broadcasted_iota(jnp.int32, (vocab_rows, lanes), 0).astype(f32)
    for r in range(15):
        onehot[:, r * lanes : (r + 1) * lanes] = (vocab == ids_ref[r : r + 1, :]).astype(bf16)
    for r in range(12):
        dconv[r * lanes + groups : (r + 1) * lanes, :] = jnp.zeros((lanes - groups, width), bf16)
    lane = lane_iota(8)

    def scalars(r0):
        rows = pl.ds(r0, 8)
        one = [jnp.zeros((8, LANE), f32) for _ in range(12)]
        cross = [jnp.zeros((8, LANE), f32) for _ in range(6)]
        tri = [jnp.zeros((8, LANE), f32) for _ in range(8)]
        for tile in range(tiles):
            cols = slice(tile * LANE, (tile + 1) * LANE)
            conv = [conv_ref[r, rows, cols] for r in range(12)]
            grad = [dtok[tile, pl.ds(6 * r0 + j, 8, stride=6), :] for j in range(6)]
            two = [conv[2 * j] + conv[2 * j + 1] for j in range(6)]
            three = [conv[3 * q] + conv[3 * q + 1] + conv[3 * q + 2] for q in range(4)]
            for r in range(12):
                one[r] = one[r] + conv[r] * grad[r // 2]
            slot = 0
            for j in range(6):
                cross[j] = cross[j] + two[j ^ 1] * grad[j]
                for q in sorted({(2 * j) // 3, (2 * j + 1) // 3}):
                    tri[slot] = tri[slot] + three[q] * grad[j]
                    slot += 1
        inner_one = jnp.zeros((8, LANE), f32)
        for r in range(12):
            inner_one = jnp.where(lane == r, jnp.sum(one[r], axis=1, keepdims=True), inner_one)
        inner_cross = jnp.zeros((8, LANE), f32)
        for j in range(6):
            inner_cross = jnp.where(
                lane // 2 == j, jnp.sum(cross[j], axis=1, keepdims=True), inner_cross
            )
        inner_three = jnp.zeros((8, LANE), f32)
        slot = 0
        for j in range(6):
            for q in sorted({(2 * j) // 3, (2 * j + 1) // 3}):
                here = (lane // 2 == j) & (lane // 3 == q)
                inner_three = jnp.where(
                    here, jnp.sum(tri[slot], axis=1, keepdims=True), inner_three
                )
                slot += 1
        inner_two = block_sum(inner_one, 2, lane)
        mix = [mix_ref[b, rows, :] for b in range(4)]
        d_mix = [
            inner_one,
            inner_two * 0.5,
            inner_three * (1.0 / 3.0),
            (inner_two + inner_cross) * 0.25,
        ]
        mean = mix[0] * d_mix[0] + mix[1] * d_mix[1] + mix[2] * d_mix[2] + mix[3] * d_mix[3]
        d_logit = [mix[b] * (d_mix[b] - mean) for b in range(4)]
        d_logit = [jnp.where(lane < 12, value, 0.0) for value in d_logit]
        slope = d_logit[0]
        for b in range(2, 5):
            slope = slope + block_sum(d_logit[b - 1], b, lane) * (1.0 / b)
        pair_two = block_sum(mix[1], 2, lane) * 0.5
        single_three = mix[2] * (1.0 / 3.0)
        pair_three = block_sum(mix[2], 2, lane) * (1.0 / 3.0)
        pair_four = block_sum(mix[3], 2, lane) * 0.25
        return mix[0], pair_two, single_three, pair_three, pair_four, slope

    def spread(r0, coefs, tile, masked, score_acc):
        one, pair_two, single_three, pair_three, pair_four, slope = coefs
        rows = pl.ds(r0, 8)
        cols = slice(tile * LANE, (tile + 1) * LANE)
        grad = [dtok[tile, pl.ds(6 * r0 + j, 8, stride=6), :] for j in range(6)]
        score = score_ref[0:1, cols]
        four = [
            pick(pair_four, 4 * q) * grad[2 * q] + pick(pair_four, 4 * q + 2) * grad[2 * q + 1]
            for q in range(3)
        ]
        three = []
        for q in range(4):
            a = 3 * q
            if a % 2 == 0:
                three.append(
                    pick(pair_three, a) * grad[a // 2]
                    + pick(single_three, a + 2) * grad[a // 2 + 1]
                )
            else:
                three.append(
                    pick(single_three, a) * grad[a // 2]
                    + pick(pair_three, a + 1) * grad[a // 2 + 1]
                )
        result = []
        for r in range(12):
            weight = pick(slope, r)
            own = (pick(one, r) + pick(pair_two, r)) * grad[r // 2]
            value = own + three[r // 3] + four[r // 4] + weight * score
            score_acc = score_acc + weight * conv_ref[r, rows, cols]
            if masked:
                group = r0 + lax.broadcasted_iota(jnp.int32, (8, LANE), 0)
                value = jnp.where(group * 12 + r < total_bytes, value, 0.0)
            result.append(value)
        return result, score_acc

    def chunk(i, accs, masked):
        r0 = pl.multiple_of(i * 16, 16)
        r1 = pl.multiple_of(i * 16 + 8, 8)
        low_coefs = scalars(r0)
        high_coefs = scalars(r1)
        new = []
        for tile in range(tiles):
            cols = slice(tile * LANE, (tile + 1) * LANE)
            low, acc = spread(r0, low_coefs, tile, masked, accs[tile])
            high, acc = spread(r1, high_coefs, tile, masked, acc)
            new.append(acc)
            for r in range(12):
                both = jnp.concatenate([low[r], high[r]], axis=0).astype(bf16)
                dconv[pl.ds(pl.multiple_of(r * lanes + r0, 16), 16), cols] = both
        return tuple(new)

    accs = tuple(jnp.zeros((8, LANE), f32) for _ in range(tiles))
    whole = (total_bytes // 12) // 16
    accs = lax.fori_loop(0, whole, lambda i, a: chunk(i, a, False), accs)
    for i in range(whole, groups // 16):
        accs = chunk(i, accs, True)
    tail = [jnp.zeros((1, width), f32) for _ in range(8)]
    for k in range(4):
        part = jnp.dot(
            onehot[:, k * lanes : (k + 12) * lanes], dconv[...], preferred_element_type=f32
        )
        if k == 0:
            out_ref[0:vocab_rows, :] = part * conv_w_ref[k : k + 1, :]
        else:
            out_ref[0:vocab_rows, :] = out_ref[0:vocab_rows, :] + part * conv_w_ref[k : k + 1, :]
        tail[k] = jnp.sum(part * table_ref[0:vocab_rows, :], axis=0, keepdims=True)
    tail[4] = jnp.sum(jnp.concatenate(accs, axis=1), axis=0, keepdims=True)
    tail[5] = jnp.sum(gain_acc, axis=0, keepdims=True)
    out_ref[vocab_rows:, :] = jnp.concatenate(tail, axis=0)


def byte_backward(
    first,
    ids,
    tokens,
    d_norm,
    d_resid,
    conv,
    mix,
    table,
    vocab_rows,
    conv_w,
    score_w,
    gain_one,
    total_bytes,
):
    width = conv.shape[2]
    groups = conv.shape[1]
    lanes = ids.shape[1]
    return pl.pallas_call(
        functools.partial(byte_backward_kernel, total_bytes),
        out_shape=jax.ShapeDtypeStruct((vocab_rows + 8, width), f32),
        in_specs=[pl.BlockSpec(memory_space=pltpu.SMEM)]
        + [pl.BlockSpec(memory_space=pltpu.VMEM)] * 10,
        scratch_shapes=[
            pltpu.VMEM((width // LANE, 6 * groups, LANE), f32),
            pltpu.VMEM((12 * lanes, width), bf16),
            pltpu.VMEM((vocab_rows, 15 * lanes), bf16),
        ],
        compiler_params=pltpu.CompilerParams(vmem_limit_bytes=VMEM_CAP),
        cost_estimate=LIGHT,
        name="byte_backward",
    )(
        first,
        ids,
        tokens,
        d_norm,
        d_resid,
        conv,
        mix,
        table,
        conv_w,
        score_w,
        gain_one,
    )


def head_mask(value, head):
    half = value.shape[1] // 2
    lane = lax.broadcasted_iota(jnp.int32, value.shape, 1)
    keep = lane < half if head == 0 else lane >= half
    return jnp.where(keep, value, jnp.zeros_like(value))


def two_heads(value):
    return jnp.concatenate([head_mask(value, 0), head_mask(value, 1)], axis=0)


def bucket_row(buckets_ref, n, reach):
    row = buckets_ref.shape[0] // 2 - 1 - (n - reach)
    return jnp.concatenate([buckets_ref[row : row + 1, :], buckets_ref[row + 1 : row + 2, :]], axis=1)


def bias_tiles(buckets_ref, rel, tiles):
    count = tiles.shape[1]
    levels = rel.shape[1]
    level = lax.broadcasted_iota(jnp.int32, (levels, 2 * BLK), 0)
    for n in range(count):
        onehot = (level == bucket_row(buckets_ref, n, count // 2)).astype(f32)
        values = lax.dot_general(rel, onehot, NN, precision=HIGH, preferred_element_type=f32)
        for head in range(2 * tiles.shape[0]):
            spread = jnp.broadcast_to(values[head : head + 1, :], (BLK, 2 * BLK))
            rolled = pltpu.roll(spread, BLK + 1, 1, stride=1, stride_axis=0)
            half = slice(head % 2 * BLK, head % 2 * BLK + BLK)
            tiles[head // 2, n, :, half] = rolled[:, :BLK]


def fold_rows(value, op):
    return op(value.reshape(BLK // 8, 8, value.shape[1]), axis=0)


def attend_kernel(
    lead_ref,
    low_ref,
    high_ref,
    q_ref,
    k_ref,
    v_ref,
    known,
    barred,
    buckets_ref,
    rel_ref,
    out_ref,
    low_out_ref,
    log_ref,
    tiles,
    v_turned,
    *scratch,
):
    pairs = tiles.shape[0]
    held, accum = scratch[:pairs], scratch[pairs:]
    reach = tiles.shape[1] // 2
    slots = q_ref.shape[0] // BLK
    half = BLK // 2
    bias_tiles(buckets_ref, rel_ref[0], tiles)
    v_turned[...] = jnp.transpose(v_ref[...])
    cols = [slice(p * BLK, (p + 1) * BLK) for p in range(pairs)]
    for slot in range(slots):
        block = lead_ref[slot]
        first = low_ref[slot]
        last = high_ref[slot]
        base = pl.multiple_of(block * BLK, BLK)
        own = slice(slot * BLK, (slot + 1) * BLK)
        bar = barred[pl.ds(base, BLK), :]
        bar = jnp.concatenate([bar, bar], axis=0)
        q_full = [jnp.concatenate([two_heads(q_ref[own, c]), bar], axis=1) for c in cols]

        def score(kb, best):
            rows = pl.ds(pl.multiple_of(kb * BLK, BLK), BLK)
            mark = known[rows, :]
            values = [
                lax.dot_general(
                    jnp.concatenate([k_ref[rows, c], mark], axis=1),
                    q_full[p],
                    NT,
                    preferred_element_type=f32,
                )
                + tiles[p, kb - block + reach]
                for p, c in enumerate(cols)
            ]
            for p in range(pairs):
                held[p][kb - first] = values[p]
            return tuple(jnp.maximum(best[p], fold_rows(values[p], jnp.max)) for p in range(pairs))

        lowest = jnp.full((8, 2 * BLK), -3e38, f32)
        best = lax.fori_loop(first, last, score, (lowest,) * pairs)
        best = [jnp.max(value, axis=0, keepdims=True) for value in best]
        for p in range(pairs):
            accum[p][...] = jnp.zeros((BLK, 2 * BLK), f32)

        def gather(kb, total):
            keys = pl.ds(pl.multiple_of(kb * BLK, BLK), BLK)
            weights = [jnp.exp(held[p][kb - first] - best[p]) for p in range(pairs)]
            products = [
                jnp.dot(v_turned[c, keys], weights[p].astype(bf16), preferred_element_type=f32)
                for p, c in enumerate(cols)
            ]
            for p in range(pairs):
                accum[p][...] += products[p]
            return tuple(total[p] + fold_rows(weights[p], jnp.sum) for p in range(pairs))

        none = jnp.zeros((8, 2 * BLK), f32)
        total = lax.fori_loop(first, last, gather, (none,) * pairs)
        for p in range(pairs):
            row_total = jnp.sum(total[p], axis=0, keepdims=True)
            value = accum[p][...] / row_total
            both = jnp.concatenate([value[:half, :BLK], value[half:, BLK:]], axis=0)
            both = jnp.transpose(both)
            out_ref[own, cols[p]] = both
            low_out_ref[own, cols[p]] = both.astype(bf16)
            log_ref[0, slot, p : p + 1, :] = best[p] + jnp.log(row_total)


def attend(lead, low, high, q, k, v, known, barred, buckets, rel):
    rows, width = q.shape
    keys = k.shape[0]
    groups = rel.shape[0]
    pairs = rel.shape[1] // 2
    blocks = keys // BLK
    slots = rows // BLK
    count = 2 * (blocks // 2) + 1
    smem = pl.BlockSpec(memory_space=pltpu.SMEM)

    def cols(size):
        return pl.BlockSpec((size, pairs * BLK), lambda i: (0, i))

    def whole(array):
        return pl.BlockSpec(array.shape, lambda i: (0,) * array.ndim)

    return pl.pallas_call(
        attend_kernel,
        grid=(groups,),
        out_shape=(
            jax.ShapeDtypeStruct((rows, width), f32),
            jax.ShapeDtypeStruct((rows, width), bf16),
            jax.ShapeDtypeStruct((groups, slots, pairs, 2 * BLK), f32),
            jax.ShapeDtypeStruct((groups * pairs, count, BLK, 2 * BLK), f32),
        ),
        in_specs=[
            smem,
            smem,
            smem,
            cols(rows),
            cols(keys),
            cols(keys),
            whole(known),
            whole(barred),
            whole(buckets),
            pl.BlockSpec((1,) + rel.shape[1:], lambda i: (i, 0, 0)),
        ],
        out_specs=(
            cols(rows),
            cols(rows),
            pl.BlockSpec((1, slots, pairs, 2 * BLK), lambda i: (i, 0, 0, 0)),
            pl.BlockSpec((pairs, count, BLK, 2 * BLK), lambda i: (i, 0, 0, 0)),
        ),
        scratch_shapes=[pltpu.VMEM((pairs * BLK, keys), bf16)]
        + [pltpu.VMEM((blocks, BLK, 2 * BLK), f32)] * pairs
        + [pltpu.VMEM((BLK, 2 * BLK), f32)] * pairs,
        compiler_params=pltpu.CompilerParams(vmem_limit_bytes=VMEM_CAP),
        cost_estimate=LIGHT,
        name="attend",
    )(lead, low, high, q, k, v, known, barred, buckets, rel)


def attend_back_kernel(
    lead_ref,
    low_ref,
    high_ref,
    q_ref,
    k_ref,
    v_ref,
    g_ref,
    out_ref,
    log_ref,
    tiles,
    known,
    barred,
    buckets_ref,
    dq_ref,
    dk_ref,
    dv_ref,
    dbias_ref,
    k_turned,
    *scratch,
):
    pairs, count = tiles.shape[:2]
    dk_acc, dv_acc, d_tiles, dq_acc = (scratch[n * pairs : (n + 1) * pairs] for n in range(4))
    reach = count // 2
    slots = q_ref.shape[0] // BLK
    half = BLK // 2
    k_turned[...] = jnp.transpose(k_ref[...])
    for p in range(pairs):
        dk_acc[p][...] = jnp.zeros(dk_acc[p].shape, f32)
        dv_acc[p][...] = jnp.zeros(dv_acc[p].shape, f32)
        d_tiles[p][...] = jnp.zeros(d_tiles[p].shape, f32)
    sub = lax.broadcasted_iota(jnp.int32, (8, BLK), 0)
    chooser = jnp.where((lane_iota(8) // half) == sub, 1.0, 0.0)
    cols = [slice(p * BLK, (p + 1) * BLK) for p in range(pairs)]
    for slot in range(slots):
        block = lead_ref[slot]
        first = low_ref[slot]
        last = high_ref[slot]
        base = pl.multiple_of(block * BLK, BLK)
        own = slice(slot * BLK, (slot + 1) * BLK)
        bar = barred[pl.ds(base, BLK), :]
        bar = jnp.concatenate([bar, bar], axis=0)
        q_two = [two_heads(q_ref[own, c]) for c in cols]
        q_full = [jnp.concatenate([value, bar], axis=1) for value in q_two]
        g_two = [two_heads(g_ref[own, c]) for c in cols]
        deltas = []
        for p, c in enumerate(cols):
            product = g_ref[own, c].astype(f32) * out_ref[own, c]
            delta = lax.dot_general(
                chooser, product, NT, precision=HIGH, preferred_element_type=f32
            )
            deltas.append(jnp.concatenate([delta[0:1, :], delta[1:2, :]], axis=1))
            dq_acc[p][...] = jnp.zeros((BLK, 2 * BLK), f32)
        logs = [log_ref[0, slot, p : p + 1, :] for p in range(pairs)]

        def step(kb, carry):
            rows = pl.ds(pl.multiple_of(kb * BLK, BLK), BLK)
            at = kb - block + reach
            mark = known[rows, :]
            values = [
                lax.dot_general(
                    jnp.concatenate([k_ref[rows, c], mark], axis=1),
                    q_full[p],
                    NT,
                    preferred_element_type=f32,
                )
                for p, c in enumerate(cols)
            ]
            d_probs = [
                lax.dot_general(v_ref[rows, c], g_two[p], NT, preferred_element_type=f32)
                for p, c in enumerate(cols)
            ]
            probs = [jnp.exp(values[p] + (tiles[p, at] - logs[p])) for p in range(pairs)]
            d_scores = [probs[p] * (d_probs[p] - deltas[p]) for p in range(pairs)]
            lows = [value.astype(bf16) for value in d_scores]
            dvs = [
                jnp.dot(probs[p].astype(bf16), g_two[p], preferred_element_type=f32)
                for p in range(pairs)
            ]
            dks = [jnp.dot(lows[p], q_two[p], preferred_element_type=f32) for p in range(pairs)]
            dqs = [
                jnp.dot(k_turned[c, rows], lows[p], preferred_element_type=f32)
                for p, c in enumerate(cols)
            ]
            for p in range(pairs):
                d_tiles[p][at] += d_scores[p]
                dv_acc[p][rows, :] += dvs[p]
                dk_acc[p][rows, :] += dks[p]
                dq_acc[p][...] += dqs[p]
            return carry

        lax.fori_loop(first, last, step, 0)
        for p in range(pairs):
            dq = dq_acc[p][...]
            both = jnp.concatenate([dq[:half, :BLK], dq[half:, BLK:]], axis=0)
            dq_ref[own, cols[p]] = jnp.transpose(both).astype(bf16)
    for p in range(pairs):
        dk_ref[:, cols[p]] = dk_acc[p][...].astype(bf16)
        dv_ref[:, cols[p]] = dv_acc[p][...].astype(bf16)
    levels = dbias_ref.shape[2]
    level = lax.broadcasted_iota(jnp.int32, (levels, 2 * BLK), 0)
    pad = jnp.zeros((BLK, BLK), f32)
    mirror = (
        lax.broadcasted_iota(jnp.int32, (BLK, BLK), 0)
        + lax.broadcasted_iota(jnp.int32, (BLK, BLK), 1)
        == BLK - 1
    ).astype(bf16)
    total = jnp.zeros((8, levels), f32)
    for n in range(count):
        onehot = (level == bucket_row(buckets_ref, n, reach)).astype(f32)
        sums = []
        for p in range(pairs):
            flipped = jnp.dot(mirror, d_tiles[p][n].astype(bf16), preferred_element_type=f32)
            for head in range(2):
                wide = jnp.concatenate([flipped[:, head * BLK : (head + 1) * BLK], pad], axis=1)
                rolled = pltpu.roll(wide, 0, 1, stride=1, stride_axis=0)
                sums.append(jnp.sum(rolled, axis=0, keepdims=True))
        rest = jnp.zeros((8 - 2 * pairs, 2 * BLK), f32)
        total = total + lax.dot_general(
            jnp.concatenate(sums + [rest], axis=0),
            onehot,
            NT,
            precision=HIGH,
            preferred_element_type=f32,
        )
    dbias_ref[0] = total


def attend_back(
    group, levels, lead, low, high, q, k, v, g, out, log, tiles, known, barred, buckets
):
    rows = q.shape[0]
    keys = k.shape[0]
    slots, pairs = log.shape[1:3]
    count = tiles.shape[1]
    width = pairs * BLK
    smem = pl.BlockSpec(memory_space=pltpu.SMEM)

    def cols(size):
        return pl.BlockSpec((size, width), lambda i: (0, group))

    def whole(array):
        return pl.BlockSpec(array.shape, lambda i: (0,) * array.ndim)

    def fresh(*shape):
        return pl.BlockSpec(shape, lambda i: (0,) * len(shape))

    return pl.pallas_call(
        attend_back_kernel,
        grid=(1,),
        out_shape=(
            jax.ShapeDtypeStruct((rows, width), bf16),
            jax.ShapeDtypeStruct((keys, width), bf16),
            jax.ShapeDtypeStruct((keys, width), bf16),
            jax.ShapeDtypeStruct((1, 8, levels), f32),
        ),
        in_specs=[
            smem,
            smem,
            smem,
            cols(rows),
            cols(keys),
            cols(keys),
            cols(rows),
            cols(rows),
            pl.BlockSpec((1, slots, pairs, 2 * BLK), lambda i: (group, 0, 0, 0)),
            pl.BlockSpec((pairs, count, BLK, 2 * BLK), lambda i: (group, 0, 0, 0)),
            whole(known),
            whole(barred),
            whole(buckets),
        ],
        out_specs=(
            fresh(rows, width),
            fresh(keys, width),
            fresh(keys, width),
            fresh(1, 8, levels),
        ),
        scratch_shapes=[pltpu.VMEM((width, keys), bf16)]
        + [pltpu.VMEM((keys, BLK), f32)] * (2 * pairs)
        + [pltpu.VMEM((count, BLK, 2 * BLK), f32)] * pairs
        + [pltpu.VMEM((BLK, 2 * BLK), f32)] * pairs,
        compiler_params=pltpu.CompilerParams(vmem_limit_bytes=VMEM_CAP),
        cost_estimate=LIGHT,
        name="attend_back",
    )(lead, low, high, q, k, v, g, out, log, tiles, known, barred, buckets)


GROUPS = 2


def attention_tables(starts, ends, rel_bucket, rel_bias, lead):
    blocks = starts.shape[0]
    mine = (lead[:, None] == jnp.arange(blocks)[None, :]).astype(jnp.int32)
    own_start = jnp.sum(mine * starts[None, :], axis=1)
    own_end = jnp.sum(mine * ends[None, :], axis=1)
    low = jnp.sum((ends[None, :] < own_start[:, None]).astype(jnp.int32), axis=1)
    high = jnp.sum((starts[None, :] <= own_end[:, None]).astype(jnp.int32), axis=1)
    buckets = jnp.pad(jnp.flip(rel_bucket), (0, 1)).reshape(2 * blocks, BLK)
    levels, heads = rel_bias.shape
    rel = jnp.transpose(rel_bias).reshape(GROUPS, heads // GROUPS, levels)
    return low, high, buckets, rel


def pack_kernel(*refs):
    outs = [ref for ref in refs if ref.dtype == bf16]
    masters = [ref for ref in refs if ref.dtype == f32]
    at = 0
    for out in outs:
        col = 0
        while col < out.shape[1]:
            wide = masters[at].shape[1]
            out[:, col : col + wide] = masters[at][...].astype(bf16)
            col += wide
            at += 1


def pack(groups):
    steps = 1
    while all(group[0].shape[0] % (32 * steps) == 0 for group in groups) and steps < 4:
        steps *= 2

    def spec(array):
        return pl.BlockSpec((array.shape[0] // steps, array.shape[1]), lambda i: (i, 0))

    outs = tuple(
        jax.ShapeDtypeStruct((group[0].shape[0], sum(a.shape[1] for a in group)), bf16)
        for group in groups
    )
    arrays = [array for group in groups for array in group]
    return pl.pallas_call(
        pack_kernel,
        grid=(steps,),
        out_shape=outs,
        in_specs=[spec(array) for array in arrays],
        out_specs=tuple(spec(out) for out in outs),
        compiler_params=pltpu.CompilerParams(vmem_limit_bytes=VMEM_CAP),
        cost_estimate=LIGHT,
        name="pack",
    )(*arrays)


TN = (((0,), (0,)), ((), ()))


def fetch_rows(index, parts, whole, sems):
    rows = parts[0].shape[0]
    copies = []
    for j, part in enumerate(parts):
        start = pl.multiple_of((index ^ j) * rows, rows)
        copies.append(pltpu.make_async_copy(part, whole.at[pl.ds(start, rows), :], sems.at[j]))
    return copies


def project_kernel(count, index_ref, *refs):
    parts = refs[:count]
    norm_ref, own_ref, q_ref, k_ref, v_ref, whole_ref, whole, sems, done = refs[count:]
    width = norm_ref.shape[1]
    copies = fetch_rows(index_ref[0], parts, whole, sems)
    for copy in copies:
        copy.start()
    for copy in copies:
        copy.wait()
    keep = pltpu.make_async_copy(whole, whole_ref, done)
    keep.start()
    for out, rows, col in ((q_ref, own_ref, 0), (k_ref, norm_ref, 1), (v_ref, norm_ref, 2)):
        weight = whole[:, col * width : (col + 1) * width]
        for block in range(rows.shape[0] // 256):
            part = slice(block * 256, (block + 1) * 256)
            out[part, :] = jnp.dot(rows[part, :], weight, preferred_element_type=f32).astype(bf16)
    keep.wait()


def project(index, parts, norm, own):
    count = len(parts)
    width = norm.shape[1]
    full = (parts[0].shape[0] * count, parts[0].shape[1])
    vmem = pl.BlockSpec(memory_space=pltpu.VMEM)
    anywhere = pl.BlockSpec(memory_space=pl.ANY)
    return pl.pallas_call(
        functools.partial(project_kernel, count),
        out_shape=(
            jax.ShapeDtypeStruct(own.shape, bf16),
            jax.ShapeDtypeStruct(norm.shape, bf16),
            jax.ShapeDtypeStruct(norm.shape, bf16),
            jax.ShapeDtypeStruct(full, bf16),
        ),
        in_specs=[pl.BlockSpec(memory_space=pltpu.SMEM)] + [anywhere] * count + [vmem] * 2,
        out_specs=(vmem, vmem, vmem, anywhere),
        scratch_shapes=[
            pltpu.VMEM(full, bf16),
            pltpu.SemaphoreType.DMA((count,)),
            pltpu.SemaphoreType.DMA,
        ],
        compiler_params=pltpu.CompilerParams(vmem_limit_bytes=VMEM_CAP),
        cost_estimate=LIGHT,
        name="project",
    )(index, *parts, norm, own)


def project_back_kernel(count, halves, index_ref, lead_ref, norm_ref, own_ref, whole_ref, *refs):
    keep_ref, send_ref, dnorm_ref, grad_ref, sems = refs[3 * halves :]
    width = norm_ref.shape[1]
    part_width = width // halves
    for half in range(halves):
        for col in range(3):
            rows = own_ref if col == 0 else norm_ref
            here = slice(col * width + half * part_width, col * width + (half + 1) * part_width)
            grad_ref[:, here] = lax.dot_general(
                rows[...], refs[3 * half + col][...], TN, preferred_element_type=f32
            ).astype(bf16)
    for block in range(norm_ref.shape[0] // 256):
        part = slice(block * 256, (block + 1) * 256)
        total = None
        for half in range(halves):
            for col in (1, 2):
                here = slice(col * width + half * part_width, col * width + (half + 1) * part_width)
                term = lax.dot_general(
                    refs[3 * half + col][part, :],
                    whole_ref[:, here],
                    NT,
                    preferred_element_type=f32,
                )
                total = term if total is None else total + term
        dnorm_ref[part, :] = total
    for slot in range(own_ref.shape[0] // BLK):
        rows = pl.ds(pl.multiple_of(lead_ref[slot] * BLK, BLK), BLK)
        total = dnorm_ref[rows, :]
        for half in range(halves):
            total = total + lax.dot_general(
                refs[3 * half][slot * BLK : (slot + 1) * BLK, :],
                whole_ref[:, half * part_width : (half + 1) * part_width],
                NT,
                preferred_element_type=f32,
            )
        dnorm_ref[rows, :] = total
    scatter_rows(
        index_ref[0], count, ((grad_ref, 0, grad_ref.shape[1], keep_ref, send_ref),), sems
    )


def project_back(index, count, lead, norm, own, whole, halves):
    vmem = pl.BlockSpec(memory_space=pltpu.VMEM)
    anywhere = pl.BlockSpec(memory_space=pl.ANY)
    smem = pl.BlockSpec(memory_space=pltpu.SMEM)
    grads = [grad for half in halves for grad in half]
    part = jax.ShapeDtypeStruct((count // 2, whole.shape[0] // count, whole.shape[1]), bf16)
    return pl.pallas_call(
        functools.partial(project_back_kernel, count, len(halves)),
        out_shape=(part, part, jax.ShapeDtypeStruct(norm.shape, f32)),
        in_specs=[smem] * 2 + [vmem] * (3 + len(grads)),
        out_specs=(anywhere, anywhere, vmem),
        scratch_shapes=[pltpu.VMEM(whole.shape, bf16), pltpu.SemaphoreType.DMA((count,))],
        compiler_params=pltpu.CompilerParams(vmem_limit_bytes=VMEM_CAP),
        cost_estimate=LIGHT,
        name="project_back",
    )(index, lead, norm, own, whole, *grads)


ROOT = 0.7978845608028654
CUBE = 0.044715


def feed_kernel(count, index_ref, *refs):
    upper = refs[:count]
    lower = refs[count : 2 * count]
    (
        tok_ref,
        att_ref,
        cot_ref,
        gain_ref,
        out_ref,
        d_att_ref,
        d_resid_ref,
        gain_grad_ref,
        left_keep,
        left_send,
        right_keep,
        right_send,
        ogu,
        down,
        store,
        resid,
        norm,
        d_norm,
        total,
        hid,
        d_gate,
        d_up,
        sems_upper,
        sems_lower,
        sems_store,
    ) = refs[2 * count :]
    rows, width = tok_ref.shape
    hidden = down.shape[0]
    copies_upper = fetch_rows(index_ref[0], upper, ogu, sems_upper)
    copies_lower = fetch_rows(index_ref[0], lower, down, sems_lower)
    for copy in copies_upper + copies_lower:
        copy.start()
    for copy in copies_upper:
        copy.wait()
    gain = gain_ref[...]
    row_step = 128
    tile = 512
    for block in range(rows // row_step):
        part = slice(block * row_step, (block + 1) * row_step)
        value = tok_ref[part, :] + jnp.dot(
            att_ref[part, :], ogu[:, :width], preferred_element_type=f32
        )
        resid[part, :] = value
        scale = lax.rsqrt(jnp.mean(value * value, axis=1, keepdims=True) + 1e-06)
        norm[part, :] = (value * scale * gain).astype(bf16)
    for copy in copies_lower:
        copy.wait()
    for n in range(hidden // tile):
        here = slice(n * tile, (n + 1) * tile)
        gate_cols = slice(width + n * tile, width + (n + 1) * tile)
        up_cols = slice(width + hidden + n * tile, width + hidden + (n + 1) * tile)
        for block in range(rows // row_step):
            part = slice(block * row_step, (block + 1) * row_step)
            gate_pre = jnp.dot(norm[part, :], ogu[:, gate_cols], preferred_element_type=f32)
            up_pre = jnp.dot(norm[part, :], ogu[:, up_cols], preferred_element_type=f32)
            d_hidden = lax.dot_general(
                cot_ref[part, :], down[here, :], NT, preferred_element_type=f32
            )
            square = gate_pre * gate_pre
            bent = jnp.tanh(ROOT * gate_pre * (1.0 + CUBE * square))
            half = 0.5 + 0.5 * bent
            gelu = gate_pre * half
            slope = half + (0.5 * ROOT) * gate_pre * (1.0 - bent * bent) * (
                1.0 + (3.0 * CUBE) * square
            )
            low = (gelu * up_pre).astype(bf16)
            d_gate_low = (d_hidden * up_pre * slope).astype(bf16)
            d_up_low = (d_hidden * gelu).astype(bf16)
            hid[part, :] = low
            d_gate[part, :] = d_gate_low
            d_up[part, :] = d_up_low
            add = jnp.dot(low, down[here, :], preferred_element_type=f32)
            back = lax.dot_general(
                d_gate_low, ogu[:, gate_cols], NT, preferred_element_type=f32
            ) + lax.dot_general(d_up_low, ogu[:, up_cols], NT, preferred_element_type=f32)
            if n == 0:
                total[part, :] = resid[part, :] + add
                d_norm[part, :] = back
            else:
                total[part, :] = total[part, :] + add
                d_norm[part, :] = d_norm[part, :] + back
        store[:, gate_cols] = lax.dot_general(
            norm[...], d_gate[...], TN, preferred_element_type=f32
        ).astype(bf16)
        store[:, up_cols] = lax.dot_general(
            norm[...], d_up[...], TN, preferred_element_type=f32
        ).astype(bf16)
        part = lax.dot_general(
            hid[...], cot_ref[...], TN, preferred_element_type=f32
        ).astype(bf16)
        for low_row, low_col, row, size in down_pieces(width // count, hidden // count, width):
            for device in range(count):
                source = device * (hidden // count) + low_row
                if n * tile <= source < (n + 1) * tile:
                    source = source - n * tile
                    target = device * (width // count) + row
                    col = width + 2 * hidden + low_col[1]
                    store[target : target + size, col : col + LANE] = part[
                        source : source + size, low_col[0] : low_col[0] + LANE
                    ]
    gain_sum = jnp.zeros((1, width), f32)
    for block in range(rows // row_step):
        part = slice(block * row_step, (block + 1) * row_step)
        out_ref[part, :] = total[part, :].astype(bf16)
        value = resid[part, :]
        grad = d_norm[part, :]
        scale = lax.rsqrt(jnp.mean(value * value, axis=1, keepdims=True) + 1e-06)
        scaled = grad * gain
        inner = jnp.mean(value * scaled, axis=1, keepdims=True)
        d_value = (
            cot_ref[part, :].astype(f32)
            + scale * scaled
            - value * (scale * scale * scale * inner)
        )
        gain_sum = gain_sum + jnp.sum(grad * value * scale, axis=0, keepdims=True)
        d_resid_ref[part, :] = d_value
        d_low = d_value.astype(bf16)
        norm[part, :] = d_low
        d_att_ref[part, :] = lax.dot_general(
            d_low, ogu[:, :width], NT, preferred_element_type=f32
        ).astype(bf16)
    gain_grad_ref[...] = gain_sum
    store[:, :width] = lax.dot_general(
        att_ref[...], norm[...], TN, preferred_element_type=f32
    ).astype(bf16)
    half = store.shape[1] // 2
    scatter_rows(
        index_ref[0],
        count,
        ((store, 0, half, left_keep, left_send), (store, half, half, right_keep, right_send)),
        sems_store,
    )


def scatter_rows(index, count, jobs, sems):
    rows = jobs[0][0].shape[0] // count
    waits = []
    for n, (source, first, wide, keep, send) in enumerate(jobs):
        for device in range(count):
            other = index ^ device
            part = source.at[device * rows : (device + 1) * rows, first : first + wide]
            sem = sems.at[n * count + device]

            @pl.when(other % 2 == 0)
            def _():
                pltpu.make_async_copy(part, keep.at[other // 2], sem).start()

            @pl.when(other % 2 == 1)
            def _():
                pltpu.make_async_copy(part, send.at[other // 2], sem).start()

            waits.append(pltpu.make_async_copy(part, keep.at[0], sem))
    for wait in waits:
        wait.wait()


def down_pieces(rows, tall, width):
    size = 16
    while tall % (2 * size) == 0 and rows % (2 * size) == 0:
        size *= 2
    pieces = []
    for q in range(tall * (width // LANE) // size):
        there = (q % (tall // size)) * size
        here = (q % (rows // size)) * size
        pieces.append((there, (q // (tall // size) * LANE, q // (rows // size) * LANE), here, size))
    return pieces


def unpack_kernel(hidden, left_ref, right_ref, qkv_ref, *outs):
    rows = left_ref.shape[0]
    half = left_ref.shape[1]
    width = outs[0].shape[1]
    for n in range(3):
        outs[n][...] = qkv_ref[:, n * width : (n + 1) * width].astype(f32)

    def column(first, last):
        parts = []
        if first < half:
            parts.append((left_ref, first, min(last, half), 0))
        if last > half:
            begin = max(first, half)
            parts.append((right_ref, begin - half, last - half, begin - first))
        return parts

    spans = ((0, width), (width, width + hidden), (width + hidden, width + 2 * hidden))
    for out, (first, last) in zip(outs[3:6], spans):
        for ref, begin, end, at in column(first, last):
            out[:, at : at + end - begin] = ref[:, begin:end].astype(f32)
    base = width + 2 * hidden - half
    for there, (col_there, col_here), here, size in down_pieces(rows, outs[6].shape[0], width):
        outs[6][there : there + size, col_there : col_there + LANE] = right_ref[
            here : here + size, base + col_here : base + col_here + LANE
        ].astype(f32)


def unpack(left, right, qkv, hidden, tall):
    rows = left.shape[0]
    width = qkv.shape[1] // 3
    shapes = [(rows, width)] * 4 + [(rows, hidden)] * 2 + [(tall, width)]
    return pl.pallas_call(
        functools.partial(unpack_kernel, hidden),
        out_shape=tuple(jax.ShapeDtypeStruct(shape, f32) for shape in shapes),
        compiler_params=pltpu.CompilerParams(vmem_limit_bytes=VMEM_CAP),
        cost_estimate=LIGHT,
        name="unpack",
    )(left, right, qkv)


def feed(index, upper, lower, tokens, attended, cotangent, gain):
    count = len(upper)
    rows, width = tokens.shape
    full_upper = (upper[0].shape[0] * count, upper[0].shape[1])
    full_lower = (lower[0].shape[0] * count, width)
    hidden = full_lower[0]
    columns = width + 3 * hidden
    vmem = pl.BlockSpec(memory_space=pltpu.VMEM)
    anywhere = pl.BlockSpec(memory_space=pl.ANY)
    tile = 512
    return pl.pallas_call(
        functools.partial(feed_kernel, count),
        out_shape=(
            jax.ShapeDtypeStruct((rows, width), bf16),
            jax.ShapeDtypeStruct((rows, width), bf16),
            jax.ShapeDtypeStruct((rows, width), f32),
            jax.ShapeDtypeStruct((1, width), f32),
            *[jax.ShapeDtypeStruct((count // 2, width // count, columns // 2), bf16)] * 4,
        ),
        in_specs=[pl.BlockSpec(memory_space=pltpu.SMEM)]
        + [anywhere] * (2 * count)
        + [vmem] * 4,
        out_specs=(vmem,) * 4 + (anywhere,) * 4,
        scratch_shapes=[
            pltpu.VMEM(full_upper, bf16),
            pltpu.VMEM(full_lower, bf16),
            pltpu.VMEM((width, columns), bf16),
            pltpu.VMEM((rows, width), f32),
            pltpu.VMEM((rows, width), bf16),
            pltpu.VMEM((rows, width), f32),
            pltpu.VMEM((rows, width), f32),
            pltpu.VMEM((rows, tile), bf16),
            pltpu.VMEM((rows, tile), bf16),
            pltpu.VMEM((rows, tile), bf16),
            pltpu.SemaphoreType.DMA((count,)),
            pltpu.SemaphoreType.DMA((count,)),
            pltpu.SemaphoreType.DMA((2 * count,)),
        ],
        compiler_params=pltpu.CompilerParams(vmem_limit_bytes=VMEM_CAP),
        cost_estimate=LIGHT,
        name="feed",
    )(index, *upper, *lower, tokens, attended, cotangent, gain.reshape(1, width))


def bits_of(count):
    bits = count.bit_length() - 1
    assert 1 << bits == count
    return bits


def swap(value, axis, bit):
    count = lax.axis_size(axis)
    return lax.ppermute(value, axis, [(i, i ^ (1 << bit)) for i in range(count)])


def ordered(mine, other, index, bit, axis=0):
    upper = ((index >> bit) & 1) == 1
    return jnp.concatenate(
        [jnp.where(upper, other, mine), jnp.where(upper, mine, other)], axis=axis
    )


def gather_small(value, axis):
    index = lax.axis_index(axis)
    value = value[None]
    for bit in range(bits_of(lax.axis_size(axis))):
        value = ordered(value, swap(value, axis, bit), index, bit)
    return value


def first_swap(shard, axis):
    bit = bits_of(lax.axis_size(axis)) - 1
    return [(0, shard), (1 << bit, swap(shard, axis, bit))]


def other_swaps(parts, axis):
    for bit in reversed(range(bits_of(lax.axis_size(axis)) - 1)):
        parts = parts + [(j | (1 << bit), swap(part, axis, bit)) for j, part in parts]
    return [part for _, part in sorted(parts, key=lambda pair: pair[0])]


def after(anchor, part):
    j, array = part
    anchor, array = lax.optimization_barrier((anchor, array))
    return anchor, (j, array)


def add_low(left, right):
    return (left.astype(f32) + right.astype(f32)).astype(bf16)


def piece(value, index, dim=0):
    return lax.dynamic_index_in_dim(value, index, dim, keepdims=False)


def scatter_step(value, axis, bit, dim):
    own = (lax.axis_index(axis) >> bit) & 1
    other = swap(piece(value, 1 - own, dim), axis, bit)
    return add_low(piece(value, own, dim), other)


def rest_sum(value, axis):
    count = lax.axis_size(axis)
    index = lax.axis_index(axis)
    mine = index // 2
    total = piece(value, mine).astype(f32)
    for j in range(1, count // 2):
        pairs = [(i, ((i // 2) ^ j) * 2 + i % 2) for i in range(count)]
        total = total + lax.ppermute(piece(value, mine ^ j), axis, pairs).astype(f32)
    return total.astype(bf16)


def rest_gather(value, axis):
    count = lax.axis_size(axis)
    index = lax.axis_index(axis)
    whole = jnp.zeros((count // 2,) + value.shape, value.dtype)
    for j in range(count // 2):
        part = value
        if j:
            pairs = [(i, ((i // 2) ^ j) * 2 + i % 2) for i in range(count)]
            part = lax.ppermute(value, axis, pairs)
        whole = lax.dynamic_update_index_in_dim(whole, part, (index // 2) ^ j, 0)
    return whole


def pair_gather(whole, axis):
    other = swap(whole, axis, 0)
    upper = lax.axis_index(axis) % 2 == 1
    both = jnp.stack([jnp.where(upper, other, whole), jnp.where(upper, whole, other)], axis=1)
    return both.reshape((2 * whole.shape[0] * whole.shape[1],) + whole.shape[2:])


class Chain:
    def __init__(self, keep, send, whole_sum=False):
        self.whole_sum = whole_sum
        self.steps = self.run(keep, send)
        self.value = next(self.steps)

    def run(self, keep, send):
        bits = bits_of(lax.axis_size("fsdp"))
        for bit in range(bits):
            other = swap(send, "fsdp", bit)
            if bit == bits - 1:
                break
            left = keep.shape[0] // 2
            split = (left, 2) + keep.shape[1:]
            keep, other = keep.reshape(split), other.reshape(split)
            send = add_low(keep[:, 1], other[:, 1])
            keep = keep[:, 0].astype(f32) + other[:, 0].astype(f32)
            (keep, send) = yield (keep, send)
        total = yield add_low(keep, other)[0]
        if self.whole_sum:
            yield lax.psum(total, "ctx")
            return
        count = lax.axis_size("ctx")
        total = total.reshape((count // 2, 2, total.shape[0] // count) + total.shape[1:])
        total = yield scatter_step(total, "ctx", 0, 1)
        total = yield rest_sum(total, "ctx")
        total = yield rest_gather(total, "ctx")
        yield pair_gather(total, "ctx")

    def advance(self, value):
        self.value = self.steps.send(value)

    def finish(self):
        while True:
            try:
                self.advance(self.value)
            except StopIteration:
                return self.value


def gate(anchor, *chains):
    joined = lax.optimization_barrier((anchor,) + tuple(chain.value for chain in chains))
    for chain, value in zip(chains, joined[1:]):
        chain.advance(value)
    return joined[0]


def reduce_small(value, early):
    fsdp_bits = bits_of(lax.axis_size("fsdp"))
    count = lax.axis_size("ctx")
    rows, width = value.shape
    value = value.reshape(2, count // 2, 2 * rows // (2 * count), width)
    value = scatter_step(value, "fsdp", 0, 0)
    value = rest_sum(value, "ctx")
    value, early.value = lax.optimization_barrier((value, early.value))
    value = add_low(value, swap(value, "ctx", 0))
    for bit in range(1, fsdp_bits):
        value = add_low(value, swap(value, "fsdp", bit))
    whole = rest_gather(value, "ctx")
    whole = whole.reshape((rows // 2, width))
    return ordered(whole, swap(whole, "fsdp", 0), lax.axis_index("fsdp"), 0)


def local(
    byte_ids,
    doc_ids,
    rel_bucket,
    table,
    conv_w,
    score_w,
    gain_one,
    gain_two,
    rel_bias,
    query_master,
    key_master,
    value_master,
    out_master,
    gate_master,
    up_master,
    down_master,
    out_cotangent,
):
    ctx_count = lax.axis_size("ctx")
    ctx_index = lax.axis_index("ctx")
    seq_count, byte_count = byte_ids.shape
    total_bytes = byte_count * ctx_count
    width = table.shape[1]
    vocab = table.shape[0]
    hidden_width = gate_master.shape[1]
    levels, heads = rel_bias.shape
    share = ctx_count // seq_count
    assert share * seq_count == ctx_count and byte_count == 2 * BLK
    seq = ctx_index // share
    part = ctx_index % share
    near = [seq ^ slot for slot in range(seq_count)]
    lead = jnp.stack([share * other + part for other in near]).astype(jnp.int32)
    rows = seq_count * BLK

    qkv_low, down_low, ogu_low = pack(
        [[query_master, key_master, value_master], [down_master], [out_master, gate_master, up_master]]
    )
    both = jnp.stack([byte_ids, doc_ids], axis=1)
    both, qkv_low = lax.optimization_barrier((both, qkv_low))
    qkv_parts = first_swap(qkv_low, "fsdp")
    both = gather_small(both, "ctx")
    both, qkv_parts[1] = after(both, qkv_parts[1])
    both, down_low = lax.optimization_barrier((both, down_low))
    shard = lax.axis_index("fsdp")[None]
    shards = lax.axis_size("fsdp")

    def to_owner(block, slot):
        if slot == 0:
            return block
        pairs = []
        for c in range(ctx_count):
            pairs.append((c, ((c // share) ^ slot) * share + c % share))
        return lax.ppermute(block, "ctx", pairs)

    table_wide = jnp.pad(table, ((0, -vocab % LANE), (0, 0)))
    score_row = score_w.reshape(1, width)
    gain_row = gain_one.reshape(1, width)
    seq_row = seq[None]
    tokens, norm_one, norm_own, tokens_own, conv, mix, phases, known, barred = byte_forward(
        seq_row, lead, both, table_wide, conv_w, score_row, gain_row, total_bytes
    )
    down_parts = first_swap(down_low, "fsdp")
    qkv_parts = other_swaps(qkv_parts, "fsdp")
    queries, keys, values, qkv = project(shard, qkv_parts, norm_one, norm_own)
    blocks = [to_owner(piece(out_cotangent, near[s], 1), s) for s in range(seq_count)]
    queries, ogu_low, blocks, down_parts = lax.optimization_barrier(
        (queries, ogu_low, blocks, [part for _, part in down_parts])
    )
    down_parts = [(0, down_parts[0]), (shards // 2, down_parts[1])]
    docs = piece(both[:, :, 1], seq, 1)
    low, high, buckets, rel = attention_tables(
        docs[:, 0], docs[:, 2 * BLK - 2], rel_bucket, rel_bias, lead
    )
    ogu_parts = first_swap(ogu_low, "fsdp")
    down_parts = other_swaps(down_parts, "fsdp")
    attended, attended_low, log_total, tiles = attend(
        lead, low, high, queries, keys, values, known, barred, buckets, rel
    )
    cotangent = jnp.concatenate(blocks, axis=0)

    attended_low, ogu_parts[1] = after(attended_low, ogu_parts[1])
    output, d_attended, d_resid, grad_gain_two, *grads = feed(
        shard,
        other_swaps(ogu_parts, "fsdp"),
        down_parts,
        tokens_own,
        attended_low,
        cotangent,
        gain_two,
    )
    left = Chain(*grads[:2], whole_sum=True)
    right = Chain(*grads[2:])
    d_attended = gate(d_attended, left, right)

    output = output.reshape(seq_count, BLK, width)
    arrived = [to_owner(output[s], s) for s in range(seq_count)]

    halves = []
    for group in range(GROUPS):
        if group:
            d_attended = gate(d_attended, left)
            d_attended, arrived = lax.optimization_barrier((d_attended, arrived))
            arrived = jnp.stack(arrived)
            output = jnp.stack([piece(arrived, seq ^ s) for s in range(seq_count)], axis=1)
        *grads, d_bias = attend_back(
            group,
            levels,
            lead,
            low,
            high,
            queries,
            keys,
            values,
            d_attended,
            attended,
            log_total,
            tiles,
            known,
            barred,
            buckets,
        )
        halves.append((grads, d_bias))
        d_attended, _ = lax.optimization_barrier((d_attended, grads[0]))
    d_bias = jnp.concatenate([half[1] for half in halves], axis=0)
    norm_own, halves = gate((norm_own, [half[0] for half in halves]), right)
    keep, send, d_norm_one = project_back(shard, shards, lead, norm_one, norm_own, qkv, halves)
    qkv_chain = Chain(keep, send)
    d_norm_one = gate(d_norm_one, qkv_chain, right)

    vocab_rows = -(-vocab // 16) * 16
    d_resid = d_resid.reshape(seq_count, BLK, width)
    small = byte_backward(
        lead,
        phases,
        tokens,
        d_norm_one,
        d_resid,
        conv,
        mix,
        table_wide,
        vocab_rows,
        conv_w,
        score_row,
        gain_row,
        total_bytes,
    )
    bias_grad = jnp.transpose(d_bias[:, : heads // GROUPS].reshape(heads, levels)).reshape(1, levels * heads)
    bias_grad = jnp.pad(bias_grad, ((0, 0), (0, width - levels * heads)))
    small = jnp.concatenate([small[: vocab_rows + 6], grad_gain_two, bias_grad], axis=0)
    small = jnp.pad(small, ((0, -small.shape[0] % (8 * ctx_count)), (0, 0))).astype(bf16)
    small = gate(small, qkv_chain, right)
    small = reduce_small(small, left).astype(f32)
    grads = unpack(
        left.finish(), right.finish(), qkv_chain.finish(), hidden_width, down_master.shape[0]
    )
    top = vocab_rows
    return (
        output,
        small[:vocab],
        small[top : top + 4],
        small[top + 4],
        small[top + 5],
        small[top + 6],
        small[top + 7, : levels * heads].reshape(levels, heads),
        *grads,
    )


def solution(mesh):
    placed = (
        P("fsdp", "ctx"),
        P("fsdp", "ctx"),
        P(),
        P(),
        P(),
        P(),
        P(),
        P(),
        P(),
        P("fsdp", None),
        P("fsdp", None),
        P("fsdp", None),
        P("fsdp", None),
        P("fsdp", None),
        P("fsdp", None),
        P("fsdp", None),
        P("ctx", "fsdp", None),
    )
    return jax.shard_map(
        local,
        mesh=mesh,
        in_specs=placed,
        out_specs=(
            P("ctx", "fsdp", None),
            P(),
            P(),
            P(),
            P(),
            P(),
            P(),
            P("fsdp", None),
            P("fsdp", None),
            P("fsdp", None),
            P("fsdp", None),
            P("fsdp", None),
            P("fsdp", None),
            P("fsdp", None),
        ),
        check_vma=False,
    )
```

```python
import functools

import jax
import jax.numpy as jnp
from jax import lax
from jax.experimental import pallas as pl
from jax.experimental.pallas import tpu as pltpu
from jax.sharding import PartitionSpec as P

f32 = jnp.float32
bf16 = jnp.bfloat16
LANE = 128
BLK = 128
VMEM_CAP = 60 * 1024 * 1024
HIGH = lax.Precision.HIGHEST
NT = (((1,), (1,)), ((), ()))
NN = (((1,), (0,)), ((), ()))
LIGHT = pl.CostEstimate(flops=1, transcendentals=0, bytes_accessed=1)


def lane_iota(rows):
    return lax.broadcasted_iota(jnp.int32, (rows, LANE), 1)


def block_sum(value, width, lane):
    def ahead(v, n):
        return pltpu.roll(v, LANE - n, 1)

    def behind(v, n):
        return pltpu.roll(v, n, 1)

    if width == 1:
        return value
    if width == 3:
        lead = value + ahead(value, 1) + ahead(value, 2)
        phase = lane % 3
        return jnp.where(phase == 0, lead, jnp.where(phase == 1, behind(lead, 1), behind(lead, 2)))
    pair = value + jnp.where(lane % 2 == 0, ahead(value, 1), behind(value, 1))
    if width == 2:
        return pair
    return pair + jnp.where(lane % 4 < 2, ahead(pair, 2), behind(pair, 2))


def pick(value, lane_index):
    return value[:, lane_index : lane_index + 1]


def byte_forward_kernel(
    total_bytes,
    seq_ref,
    lead_ref,
    both_ref,
    table_ref,
    conv_w_ref,
    score_ref,
    gain_ref,
    tok_ref,
    norm_ref,
    norm_own_ref,
    tok_own_ref,
    conv_ref,
    mix_ref,
    ids_ref,
    known_ref,
    barred_ref,
    hi_ref,
    lo_ref,
    emb,
    flat,
    spread,
):
    groups = conv_ref.shape[1]
    width = conv_ref.shape[2]
    tiles = width // LANE
    token_count = norm_ref.shape[0]
    vocab_pad = table_ref.shape[0]
    row_lanes = ids_ref.shape[1]
    seq = seq_ref[0]
    high = table_ref[...].astype(bf16)
    hi_ref[...] = high
    lo_ref[...] = (table_ref[...] - high.astype(f32)).astype(bf16)
    lane_f = lane_iota(BLK).astype(f32)
    chunk_bytes = both_ref.shape[3]

    def lay(kind, first):
        for block in range(both_ref.shape[0]):
            row = both_ref[block, seq, kind : kind + 1, :].astype(f32)
            for half in range(chunk_bytes // LANE):
                part = jnp.broadcast_to(row[:, half * LANE : (half + 1) * LANE], (LANE, LANE))
                start = first + block * chunk_bytes + half * LANE
                spread[start : start + LANE, :] = jnp.transpose(part)

    lay(1, 0)
    for block in range(token_count // BLK):
        docs = spread[pl.ds(block * 2 * BLK, BLK, stride=2), :]
        same = docs == lane_f
        rows = slice(block * BLK, (block + 1) * BLK)
        known_ref[rows, :] = same.astype(bf16)
        barred_ref[rows, :] = jnp.where(same | (lane_f >= 16.0), 0.0, -1e30).astype(bf16)
    lay(0, 16)
    none = jnp.full((16, LANE), -1.0, f32)
    spread[0:16, :] = none
    tail = spread.shape[0] - total_bytes - 16
    spread[total_bytes + 16 :, :] = jnp.full((tail, LANE), -1.0, f32)
    lane_g = lane_iota(groups).astype(f32)
    for r in range(15):
        here = spread[pl.ds(13 + r, row_lanes, stride=12), :]
        turned = [
            jnp.transpose(here[n * LANE : (n + 1) * LANE, :])[0:1, :]
            for n in range(row_lanes // LANE)
        ]
        ids_ref[r : r + 1, :] = jnp.concatenate(turned, axis=1)
        onehot = jnp.concatenate(
            [
                (here[0:groups, :] == lane_g + n * LANE).astype(bf16)
                for n in range(vocab_pad // LANE)
            ],
            axis=1,
        )
        emb[r] = jnp.dot(onehot, hi_ref[...], preferred_element_type=f32) + jnp.dot(
            onehot, lo_ref[...], preferred_element_type=f32
        )
    ids_ref[15:16, :] = jnp.full((1, row_lanes), -1.0, f32)
    lane = lane_iota(8)

    def chunk(i, masked):
        r0 = pl.multiple_of(i * 8, 8)
        rows = pl.ds(r0, 8)
        sums = [jnp.zeros((8, LANE), f32) for _ in range(12)]
        for tile in range(tiles):
            cols = slice(tile * LANE, (tile + 1) * LANE)
            taps = [conv_w_ref[k : k + 1, cols] for k in range(4)]
            piece = [emb[r, rows, cols] for r in range(15)]
            score = score_ref[0:1, cols]
            for r in range(12):
                value = (
                    piece[r] * taps[0]
                    + piece[r + 1] * taps[1]
                    + piece[r + 2] * taps[2]
                    + piece[r + 3] * taps[3]
                )
                if masked:
                    group = r0 + lax.broadcasted_iota(jnp.int32, (8, LANE), 0)
                    value = jnp.where(group * 12 + r < total_bytes, value, 0.0)
                conv_ref[r, rows, cols] = value
                sums[r] = sums[r] + value * score
        packed = jnp.zeros((8, LANE), f32)
        for r in range(12):
            packed = jnp.where(lane == r, jnp.sum(sums[r], axis=1, keepdims=True), packed)
        logits = [block_sum(packed, b, lane) * (1.0 / b) for b in range(1, 5)]
        best = jnp.maximum(jnp.maximum(logits[0], logits[1]), jnp.maximum(logits[2], logits[3]))
        parts = [jnp.exp(value - best) for value in logits]
        total = parts[0] + parts[1] + parts[2] + parts[3]
        mix = [part / total for part in parts]
        for b in range(4):
            mix_ref[b, rows, :] = mix[b]
        half_one = mix[0] * 0.5
        pair_two = block_sum(mix[1], 2, lane) * 0.25
        single_three = mix[2] * (1.0 / 6.0)
        pair_three = block_sum(mix[2], 2, lane) * (1.0 / 6.0)
        pair_four = block_sum(mix[3], 2, lane) * 0.125
        coef_one = [pick(half_one, r) for r in range(12)]
        coef_two = [pick(pair_two, 2 * j) for j in range(6)]
        coef_four = [pick(pair_four, 2 * j) for j in range(6)]
        coef_three = []
        for j in range(6):
            if j % 3 == 1:
                coef_three.append((pick(single_three, 2 * j), pick(single_three, 2 * j + 1)))
            else:
                coef_three.append((pick(pair_three, 2 * j), None))
        for tile in range(tiles):
            cols = slice(tile * LANE, (tile + 1) * LANE)
            conv = [conv_ref[r, rows, cols] for r in range(12)]
            two = [conv[2 * j] + conv[2 * j + 1] for j in range(6)]
            three = [conv[3 * q] + conv[3 * q + 1] + conv[3 * q + 2] for q in range(4)]
            four = [two[2 * q] + two[2 * q + 1] for q in range(3)]
            for j in range(6):
                a, b = 2 * j, 2 * j + 1
                value = coef_one[a] * conv[a] + coef_one[b] * conv[b]
                value = value + coef_two[j] * two[j] + coef_four[j] * four[j // 2]
                value = value + coef_three[j][0] * three[a // 3]
                if j % 3 == 1:
                    value = value + coef_three[j][1] * three[b // 3]
                flat[tile, pl.ds(6 * r0 + j, 8, stride=6), :] = value

    whole = (total_bytes // 12) // 8

    def plain(i, carry):
        chunk(i, False)
        return carry

    lax.fori_loop(0, whole, plain, 0)
    for i in range(whole, groups // 8):
        chunk(i, True)

    def norm(i, carry):
        rows = pl.ds(pl.multiple_of(i * 16, 16), 16)
        value = jnp.concatenate([flat[tile, rows, :] for tile in range(tiles)], axis=1)
        tok_ref[rows, :] = value
        scale = lax.rsqrt(jnp.mean(value * value, axis=1, keepdims=True) + 1e-06)
        norm_ref[rows, :] = (value * scale * gain_ref[...]).astype(bf16)
        return carry

    lax.fori_loop(0, token_count // 16, norm, 0)
    for slot in range(norm_own_ref.shape[0] // BLK):
        start = pl.multiple_of(lead_ref[slot] * BLK, BLK)
        norm_own_ref[slot * BLK : (slot + 1) * BLK, :] = norm_ref[pl.ds(start, BLK), :]
        tok_own_ref[slot * BLK : (slot + 1) * BLK, :] = tok_ref[pl.ds(start, BLK), :]


def byte_forward(seq, lead, both, table, conv_w, score_w, gain_one, total_bytes):
    width = conv_w.shape[1]
    token_count = total_bytes // 2
    least = -(-total_bytes // 12)
    groups = -(-least // 16) * 16
    row_lanes = -(-least // LANE) * LANE
    smem = pl.BlockSpec(memory_space=pltpu.SMEM)
    vmem = pl.BlockSpec(memory_space=pltpu.VMEM)
    return pl.pallas_call(
        functools.partial(byte_forward_kernel, total_bytes),
        out_shape=(
            jax.ShapeDtypeStruct((token_count, width), f32),
            jax.ShapeDtypeStruct((token_count, width), bf16),
            jax.ShapeDtypeStruct((lead.shape[0] * BLK, width), bf16),
            jax.ShapeDtypeStruct((lead.shape[0] * BLK, width), f32),
            jax.ShapeDtypeStruct((12, groups, width), f32),
            jax.ShapeDtypeStruct((4, groups, LANE), f32),
            jax.ShapeDtypeStruct((16, row_lanes), f32),
            jax.ShapeDtypeStruct((token_count, LANE), bf16),
            jax.ShapeDtypeStruct((token_count, LANE), bf16),
        ),
        in_specs=[smem, smem] + [vmem] * 5,
        scratch_shapes=[
            pltpu.VMEM(table.shape, bf16),
            pltpu.VMEM(table.shape, bf16),
            pltpu.VMEM((15, groups, width), f32),
            pltpu.VMEM((width // LANE, 6 * groups, LANE), f32),
            pltpu.VMEM((12 * row_lanes + 32, LANE), f32),
        ],
        compiler_params=pltpu.CompilerParams(vmem_limit_bytes=VMEM_CAP),
        cost_estimate=LIGHT,
        name="byte_forward",
    )(
        seq,
        lead,
        both,
        table,
        conv_w,
        score_w,
        gain_one,
    )


def byte_backward_kernel(
    total_bytes,
    first_ref,
    ids_ref,
    tok_ref,
    dnorm_ref,
    dres_ref,
    conv_ref,
    mix_ref,
    table_ref,
    conv_w_ref,
    score_ref,
    gain_ref,
    out_ref,
    dtok,
    dconv,
    onehot,
):
    groups = conv_ref.shape[1]
    width = conv_ref.shape[2]
    tiles = width // LANE
    token_count = dnorm_ref.shape[0]
    vocab_rows = onehot.shape[0]
    lanes = ids_ref.shape[1]
    gain = gain_ref[...]

    def norm_back(i, acc):
        rows = pl.ds(pl.multiple_of(i * 8, 8), 8)
        value = tok_ref[rows, :]
        grad = dnorm_ref[rows, :]
        scale = lax.rsqrt(jnp.mean(value * value, axis=1, keepdims=True) + 1e-06)
        grad_gain = grad * gain
        inner = jnp.mean(value * grad_gain, axis=1, keepdims=True)
        total = 0.5 * scale * grad_gain - value * (0.5 * scale * scale * scale * inner)
        for tile in range(tiles):
            dtok[tile, rows, :] = total[:, tile * LANE : (tile + 1) * LANE]
        return acc + grad * value * scale

    gain_acc = lax.fori_loop(0, token_count // 8, norm_back, jnp.zeros((8, width), f32))
    rest = dtok.shape[1] - token_count
    dtok[:, token_count:, :] = jnp.zeros((tiles, rest, LANE), f32)
    for slot in range(dres_ref.shape[0]):
        start = pl.multiple_of(first_ref[slot] * BLK, BLK)

        def add(i, carry, slot=slot, start=start):
            r = pl.multiple_of(i * 8, 8)
            rows = pl.ds(start + r, 8)
            more = 0.5 * dres_ref[slot, pl.ds(r, 8), :]
            for tile in range(tiles):
                dtok[tile, rows, :] = (
                    dtok[tile, rows, :] + more[:, tile * LANE : (tile + 1) * LANE]
                )
            return carry

        lax.fori_loop(0, BLK // 8, add, 0)
    vocab = lax.broadcasted_iota(jnp.int32, (vocab_rows, lanes), 0).astype(f32)
    for r in range(15):
        onehot[:, r * lanes : (r + 1) * lanes] = (vocab == ids_ref[r : r + 1, :]).astype(bf16)
    for r in range(12):
        dconv[r * lanes + groups : (r + 1) * lanes, :] = jnp.zeros((lanes - groups, width), bf16)
    lane = lane_iota(8)

    def scalars(r0):
        rows = pl.ds(r0, 8)
        one = [jnp.zeros((8, LANE), f32) for _ in range(12)]
        cross = [jnp.zeros((8, LANE), f32) for _ in range(6)]
        tri = [jnp.zeros((8, LANE), f32) for _ in range(8)]
        for tile in range(tiles):
            cols = slice(tile * LANE, (tile + 1) * LANE)
            conv = [conv_ref[r, rows, cols] for r in range(12)]
            grad = [dtok[tile, pl.ds(6 * r0 + j, 8, stride=6), :] for j in range(6)]
            two = [conv[2 * j] + conv[2 * j + 1] for j in range(6)]
            three = [conv[3 * q] + conv[3 * q + 1] + conv[3 * q + 2] for q in range(4)]
            for r in range(12):
                one[r] = one[r] + conv[r] * grad[r // 2]
            slot = 0
            for j in range(6):
                cross[j] = cross[j] + two[j ^ 1] * grad[j]
                for q in sorted({(2 * j) // 3, (2 * j + 1) // 3}):
                    tri[slot] = tri[slot] + three[q] * grad[j]
                    slot += 1
        inner_one = jnp.zeros((8, LANE), f32)
        for r in range(12):
            inner_one = jnp.where(lane == r, jnp.sum(one[r], axis=1, keepdims=True), inner_one)
        inner_cross = jnp.zeros((8, LANE), f32)
        for j in range(6):
            inner_cross = jnp.where(
                lane // 2 == j, jnp.sum(cross[j], axis=1, keepdims=True), inner_cross
            )
        inner_three = jnp.zeros((8, LANE), f32)
        slot = 0
        for j in range(6):
            for q in sorted({(2 * j) // 3, (2 * j + 1) // 3}):
                here = (lane // 2 == j) & (lane // 3 == q)
                inner_three = jnp.where(
                    here, jnp.sum(tri[slot], axis=1, keepdims=True), inner_three
                )
                slot += 1
        inner_two = block_sum(inner_one, 2, lane)
        mix = [mix_ref[b, rows, :] for b in range(4)]
        d_mix = [
            inner_one,
            inner_two * 0.5,
            inner_three * (1.0 / 3.0),
            (inner_two + inner_cross) * 0.25,
        ]
        mean = mix[0] * d_mix[0] + mix[1] * d_mix[1] + mix[2] * d_mix[2] + mix[3] * d_mix[3]
        d_logit = [mix[b] * (d_mix[b] - mean) for b in range(4)]
        d_logit = [jnp.where(lane < 12, value, 0.0) for value in d_logit]
        slope = d_logit[0]
        for b in range(2, 5):
            slope = slope + block_sum(d_logit[b - 1], b, lane) * (1.0 / b)
        pair_two = block_sum(mix[1], 2, lane) * 0.5
        single_three = mix[2] * (1.0 / 3.0)
        pair_three = block_sum(mix[2], 2, lane) * (1.0 / 3.0)
        pair_four = block_sum(mix[3], 2, lane) * 0.25
        return mix[0], pair_two, single_three, pair_three, pair_four, slope

    def spread(r0, coefs, tile, masked, score_acc):
        one, pair_two, single_three, pair_three, pair_four, slope = coefs
        rows = pl.ds(r0, 8)
        cols = slice(tile * LANE, (tile + 1) * LANE)
        grad = [dtok[tile, pl.ds(6 * r0 + j, 8, stride=6), :] for j in range(6)]
        score = score_ref[0:1, cols]
        four = [
            pick(pair_four, 4 * q) * grad[2 * q] + pick(pair_four, 4 * q + 2) * grad[2 * q + 1]
            for q in range(3)
        ]
        three = []
        for q in range(4):
            a = 3 * q
            if a % 2 == 0:
                three.append(
                    pick(pair_three, a) * grad[a // 2]
                    + pick(single_three, a + 2) * grad[a // 2 + 1]
                )
            else:
                three.append(
                    pick(single_three, a) * grad[a // 2]
                    + pick(pair_three, a + 1) * grad[a // 2 + 1]
                )
        result = []
        for r in range(12):
            weight = pick(slope, r)
            own = (pick(one, r) + pick(pair_two, r)) * grad[r // 2]
            value = own + three[r // 3] + four[r // 4] + weight * score
            score_acc = score_acc + weight * conv_ref[r, rows, cols]
            if masked:
                group = r0 + lax.broadcasted_iota(jnp.int32, (8, LANE), 0)
                value = jnp.where(group * 12 + r < total_bytes, value, 0.0)
            result.append(value)
        return result, score_acc

    def chunk(i, accs, masked):
        r0 = pl.multiple_of(i * 16, 16)
        r1 = pl.multiple_of(i * 16 + 8, 8)
        low_coefs = scalars(r0)
        high_coefs = scalars(r1)
        new = []
        for tile in range(tiles):
            cols = slice(tile * LANE, (tile + 1) * LANE)
            low, acc = spread(r0, low_coefs, tile, masked, accs[tile])
            high, acc = spread(r1, high_coefs, tile, masked, acc)
            new.append(acc)
            for r in range(12):
                both = jnp.concatenate([low[r], high[r]], axis=0).astype(bf16)
                dconv[pl.ds(pl.multiple_of(r * lanes + r0, 16), 16), cols] = both
        return tuple(new)

    accs = tuple(jnp.zeros((8, LANE), f32) for _ in range(tiles))
    whole = (total_bytes // 12) // 16
    accs = lax.fori_loop(0, whole, lambda i, a: chunk(i, a, False), accs)
    for i in range(whole, groups // 16):
        accs = chunk(i, accs, True)
    tail = [jnp.zeros((1, width), f32) for _ in range(8)]
    for k in range(4):
        part = jnp.dot(
            onehot[:, k * lanes : (k + 12) * lanes], dconv[...], preferred_element_type=f32
        )
        if k == 0:
            out_ref[0:vocab_rows, :] = part * conv_w_ref[k : k + 1, :]
        else:
            out_ref[0:vocab_rows, :] = out_ref[0:vocab_rows, :] + part * conv_w_ref[k : k + 1, :]
        tail[k] = jnp.sum(part * table_ref[0:vocab_rows, :], axis=0, keepdims=True)
    tail[4] = jnp.sum(jnp.concatenate(accs, axis=1), axis=0, keepdims=True)
    tail[5] = jnp.sum(gain_acc, axis=0, keepdims=True)
    out_ref[vocab_rows:, :] = jnp.concatenate(tail, axis=0)


def byte_backward(
    first,
    ids,
    tokens,
    d_norm,
    d_resid,
    conv,
    mix,
    table,
    vocab_rows,
    conv_w,
    score_w,
    gain_one,
    total_bytes,
):
    width = conv.shape[2]
    groups = conv.shape[1]
    lanes = ids.shape[1]
    return pl.pallas_call(
        functools.partial(byte_backward_kernel, total_bytes),
        out_shape=jax.ShapeDtypeStruct((vocab_rows + 8, width), f32),
        in_specs=[pl.BlockSpec(memory_space=pltpu.SMEM)]
        + [pl.BlockSpec(memory_space=pltpu.VMEM)] * 10,
        scratch_shapes=[
            pltpu.VMEM((width // LANE, 6 * groups, LANE), f32),
            pltpu.VMEM((12 * lanes, width), bf16),
            pltpu.VMEM((vocab_rows, 15 * lanes), bf16),
        ],
        compiler_params=pltpu.CompilerParams(vmem_limit_bytes=VMEM_CAP),
        cost_estimate=LIGHT,
        name="byte_backward",
    )(
        first,
        ids,
        tokens,
        d_norm,
        d_resid,
        conv,
        mix,
        table,
        conv_w,
        score_w,
        gain_one,
    )


def head_mask(value, head):
    half = value.shape[1] // 2
    lane = lax.broadcasted_iota(jnp.int32, value.shape, 1)
    keep = lane < half if head == 0 else lane >= half
    return jnp.where(keep, value, jnp.zeros_like(value))


def two_heads(value):
    return jnp.concatenate([head_mask(value, 0), head_mask(value, 1)], axis=0)


def bucket_row(buckets_ref, n, reach):
    row = buckets_ref.shape[0] // 2 - 1 - (n - reach)
    return jnp.concatenate([buckets_ref[row : row + 1, :], buckets_ref[row + 1 : row + 2, :]], axis=1)


def bias_tiles(buckets_ref, rel, tiles):
    count = tiles.shape[1]
    levels = rel.shape[1]
    level = lax.broadcasted_iota(jnp.int32, (levels, 2 * BLK), 0)
    for n in range(count):
        onehot = (level == bucket_row(buckets_ref, n, count // 2)).astype(f32)
        values = lax.dot_general(rel, onehot, NN, precision=HIGH, preferred_element_type=f32)
        for head in range(2 * tiles.shape[0]):
            spread = jnp.broadcast_to(values[head : head + 1, :], (BLK, 2 * BLK))
            rolled = pltpu.roll(spread, BLK + 1, 1, stride=1, stride_axis=0)
            half = slice(head % 2 * BLK, head % 2 * BLK + BLK)
            tiles[head // 2, n, :, half] = rolled[:, :BLK]


def fold_rows(value, op):
    return op(value.reshape(BLK // 8, 8, value.shape[1]), axis=0)


def attend_kernel(
    lead_ref,
    low_ref,
    high_ref,
    q_ref,
    k_ref,
    v_ref,
    known,
    barred,
    buckets_ref,
    rel_ref,
    out_ref,
    low_out_ref,
    log_ref,
    tiles,
    v_turned,
    *scratch,
):
    pairs = tiles.shape[0]
    held, accum = scratch[:pairs], scratch[pairs:]
    reach = tiles.shape[1] // 2
    slots = q_ref.shape[0] // BLK
    half = BLK // 2
    bias_tiles(buckets_ref, rel_ref[0], tiles)
    v_turned[...] = jnp.transpose(v_ref[...])
    cols = [slice(p * BLK, (p + 1) * BLK) for p in range(pairs)]
    for slot in range(slots):
        block = lead_ref[slot]
        first = low_ref[slot]
        last = high_ref[slot]
        base = pl.multiple_of(block * BLK, BLK)
        own = slice(slot * BLK, (slot + 1) * BLK)
        bar = barred[pl.ds(base, BLK), :]
        bar = jnp.concatenate([bar, bar], axis=0)
        q_full = [jnp.concatenate([two_heads(q_ref[own, c]), bar], axis=1) for c in cols]

        def score(kb, best):
            rows = pl.ds(pl.multiple_of(kb * BLK, BLK), BLK)
            mark = known[rows, :]
            values = [
                lax.dot_general(
                    jnp.concatenate([k_ref[rows, c], mark], axis=1),
                    q_full[p],
                    NT,
                    preferred_element_type=f32,
                )
                + tiles[p, kb - block + reach]
                for p, c in enumerate(cols)
            ]
            for p in range(pairs):
                held[p][kb - first] = values[p]
            return tuple(jnp.maximum(best[p], fold_rows(values[p], jnp.max)) for p in range(pairs))

        lowest = jnp.full((8, 2 * BLK), -3e38, f32)
        best = lax.fori_loop(first, last, score, (lowest,) * pairs)
        best = [jnp.max(value, axis=0, keepdims=True) for value in best]
        for p in range(pairs):
            accum[p][...] = jnp.zeros((BLK, 2 * BLK), f32)

        def gather(kb, total):
            keys = pl.ds(pl.multiple_of(kb * BLK, BLK), BLK)
            weights = [jnp.exp(held[p][kb - first] - best[p]) for p in range(pairs)]
            products = [
                jnp.dot(v_turned[c, keys], weights[p].astype(bf16), preferred_element_type=f32)
                for p, c in enumerate(cols)
            ]
            for p in range(pairs):
                accum[p][...] += products[p]
            return tuple(total[p] + fold_rows(weights[p], jnp.sum) for p in range(pairs))

        none = jnp.zeros((8, 2 * BLK), f32)
        total = lax.fori_loop(first, last, gather, (none,) * pairs)
        for p in range(pairs):
            row_total = jnp.sum(total[p], axis=0, keepdims=True)
            value = accum[p][...] / row_total
            both = jnp.concatenate([value[:half, :BLK], value[half:, BLK:]], axis=0)
            both = jnp.transpose(both)
            out_ref[own, cols[p]] = both
            low_out_ref[own, cols[p]] = both.astype(bf16)
            log_ref[0, slot, p : p + 1, :] = best[p] + jnp.log(row_total)


def attend(lead, low, high, q, k, v, known, barred, buckets, rel):
    rows, width = q.shape
    keys = k.shape[0]
    groups = rel.shape[0]
    pairs = rel.shape[1] // 2
    blocks = keys // BLK
    slots = rows // BLK
    count = 2 * (blocks // 2) + 1
    smem = pl.BlockSpec(memory_space=pltpu.SMEM)

    def cols(size):
        return pl.BlockSpec((size, pairs * BLK), lambda i: (0, i))

    def whole(array):
        return pl.BlockSpec(array.shape, lambda i: (0,) * array.ndim)

    return pl.pallas_call(
        attend_kernel,
        grid=(groups,),
        out_shape=(
            jax.ShapeDtypeStruct((rows, width), f32),
            jax.ShapeDtypeStruct((rows, width), bf16),
            jax.ShapeDtypeStruct((groups, slots, pairs, 2 * BLK), f32),
            jax.ShapeDtypeStruct((groups * pairs, count, BLK, 2 * BLK), f32),
        ),
        in_specs=[
            smem,
            smem,
            smem,
            cols(rows),
            cols(keys),
            cols(keys),
            whole(known),
            whole(barred),
            whole(buckets),
            pl.BlockSpec((1,) + rel.shape[1:], lambda i: (i, 0, 0)),
        ],
        out_specs=(
            cols(rows),
            cols(rows),
            pl.BlockSpec((1, slots, pairs, 2 * BLK), lambda i: (i, 0, 0, 0)),
            pl.BlockSpec((pairs, count, BLK, 2 * BLK), lambda i: (i, 0, 0, 0)),
        ),
        scratch_shapes=[pltpu.VMEM((pairs * BLK, keys), bf16)]
        + [pltpu.VMEM((blocks, BLK, 2 * BLK), f32)] * pairs
        + [pltpu.VMEM((BLK, 2 * BLK), f32)] * pairs,
        compiler_params=pltpu.CompilerParams(vmem_limit_bytes=VMEM_CAP),
        cost_estimate=LIGHT,
        name="attend",
    )(lead, low, high, q, k, v, known, barred, buckets, rel)


def attend_back_kernel(
    lead_ref,
    low_ref,
    high_ref,
    q_ref,
    k_ref,
    v_ref,
    g_ref,
    out_ref,
    log_ref,
    tiles,
    known,
    barred,
    buckets_ref,
    dq_ref,
    dk_ref,
    dv_ref,
    dbias_ref,
    k_turned,
    *scratch,
):
    pairs, count = tiles.shape[:2]
    dk_acc, dv_acc, d_tiles, dq_acc = (scratch[n * pairs : (n + 1) * pairs] for n in range(4))
    reach = count // 2
    slots = q_ref.shape[0] // BLK
    half = BLK // 2
    k_turned[...] = jnp.transpose(k_ref[...])
    for p in range(pairs):
        dk_acc[p][...] = jnp.zeros(dk_acc[p].shape, f32)
        dv_acc[p][...] = jnp.zeros(dv_acc[p].shape, f32)
        d_tiles[p][...] = jnp.zeros(d_tiles[p].shape, f32)
    sub = lax.broadcasted_iota(jnp.int32, (8, BLK), 0)
    chooser = jnp.where((lane_iota(8) // half) == sub, 1.0, 0.0)
    cols = [slice(p * BLK, (p + 1) * BLK) for p in range(pairs)]
    for slot in range(slots):
        block = lead_ref[slot]
        first = low_ref[slot]
        last = high_ref[slot]
        base = pl.multiple_of(block * BLK, BLK)
        own = slice(slot * BLK, (slot + 1) * BLK)
        bar = barred[pl.ds(base, BLK), :]
        bar = jnp.concatenate([bar, bar], axis=0)
        q_two = [two_heads(q_ref[own, c]) for c in cols]
        q_full = [jnp.concatenate([value, bar], axis=1) for value in q_two]
        g_two = [two_heads(g_ref[own, c]) for c in cols]
        deltas = []
        for p, c in enumerate(cols):
            product = g_ref[own, c].astype(f32) * out_ref[own, c]
            delta = lax.dot_general(
                chooser, product, NT, precision=HIGH, preferred_element_type=f32
            )
            deltas.append(jnp.concatenate([delta[0:1, :], delta[1:2, :]], axis=1))
            dq_acc[p][...] = jnp.zeros((BLK, 2 * BLK), f32)
        logs = [log_ref[0, slot, p : p + 1, :] for p in range(pairs)]

        def step(kb, carry):
            rows = pl.ds(pl.multiple_of(kb * BLK, BLK), BLK)
            at = kb - block + reach
            mark = known[rows, :]
            values = [
                lax.dot_general(
                    jnp.concatenate([k_ref[rows, c], mark], axis=1),
                    q_full[p],
                    NT,
                    preferred_element_type=f32,
                )
                for p, c in enumerate(cols)
            ]
            d_probs = [
                lax.dot_general(v_ref[rows, c], g_two[p], NT, preferred_element_type=f32)
                for p, c in enumerate(cols)
            ]
            probs = [jnp.exp(values[p] + (tiles[p, at] - logs[p])) for p in range(pairs)]
            d_scores = [probs[p] * (d_probs[p] - deltas[p]) for p in range(pairs)]
            lows = [value.astype(bf16) for value in d_scores]
            dvs = [
                jnp.dot(probs[p].astype(bf16), g_two[p], preferred_element_type=f32)
                for p in range(pairs)
            ]
            dks = [jnp.dot(lows[p], q_two[p], preferred_element_type=f32) for p in range(pairs)]
            dqs = [
                jnp.dot(k_turned[c, rows], lows[p], preferred_element_type=f32)
                for p, c in enumerate(cols)
            ]
            for p in range(pairs):
                d_tiles[p][at] += d_scores[p]
                dv_acc[p][rows, :] += dvs[p]
                dk_acc[p][rows, :] += dks[p]
                dq_acc[p][...] += dqs[p]
            return carry

        lax.fori_loop(first, last, step, 0)
        for p in range(pairs):
            dq = dq_acc[p][...]
            both = jnp.concatenate([dq[:half, :BLK], dq[half:, BLK:]], axis=0)
            dq_ref[own, cols[p]] = jnp.transpose(both).astype(bf16)
    for p in range(pairs):
        dk_ref[:, cols[p]] = dk_acc[p][...].astype(bf16)
        dv_ref[:, cols[p]] = dv_acc[p][...].astype(bf16)
    levels = dbias_ref.shape[2]
    level = lax.broadcasted_iota(jnp.int32, (levels, 2 * BLK), 0)
    pad = jnp.zeros((BLK, BLK), f32)
    mirror = (
        lax.broadcasted_iota(jnp.int32, (BLK, BLK), 0)
        + lax.broadcasted_iota(jnp.int32, (BLK, BLK), 1)
        == BLK - 1
    ).astype(bf16)
    total = jnp.zeros((8, levels), f32)
    for n in range(count):
        onehot = (level == bucket_row(buckets_ref, n, reach)).astype(f32)
        sums = []
        for p in range(pairs):
            flipped = jnp.dot(mirror, d_tiles[p][n].astype(bf16), preferred_element_type=f32)
            for head in range(2):
                wide = jnp.concatenate([flipped[:, head * BLK : (head + 1) * BLK], pad], axis=1)
                rolled = pltpu.roll(wide, 0, 1, stride=1, stride_axis=0)
                sums.append(jnp.sum(rolled, axis=0, keepdims=True))
        rest = jnp.zeros((8 - 2 * pairs, 2 * BLK), f32)
        total = total + lax.dot_general(
            jnp.concatenate(sums + [rest], axis=0),
            onehot,
            NT,
            precision=HIGH,
            preferred_element_type=f32,
        )
    dbias_ref[0] = total


def attend_back(
    group, levels, lead, low, high, q, k, v, g, out, log, tiles, known, barred, buckets
):
    rows = q.shape[0]
    keys = k.shape[0]
    slots, pairs = log.shape[1:3]
    count = tiles.shape[1]
    width = pairs * BLK
    smem = pl.BlockSpec(memory_space=pltpu.SMEM)

    def cols(size):
        return pl.BlockSpec((size, width), lambda i: (0, group))

    def whole(array):
        return pl.BlockSpec(array.shape, lambda i: (0,) * array.ndim)

    def fresh(*shape):
        return pl.BlockSpec(shape, lambda i: (0,) * len(shape))

    return pl.pallas_call(
        attend_back_kernel,
        grid=(1,),
        out_shape=(
            jax.ShapeDtypeStruct((rows, width), bf16),
            jax.ShapeDtypeStruct((keys, width), bf16),
            jax.ShapeDtypeStruct((keys, width), bf16),
            jax.ShapeDtypeStruct((1, 8, levels), f32),
        ),
        in_specs=[
            smem,
            smem,
            smem,
            cols(rows),
            cols(keys),
            cols(keys),
            cols(rows),
            cols(rows),
            pl.BlockSpec((1, slots, pairs, 2 * BLK), lambda i: (group, 0, 0, 0)),
            pl.BlockSpec((pairs, count, BLK, 2 * BLK), lambda i: (group, 0, 0, 0)),
            whole(known),
            whole(barred),
            whole(buckets),
        ],
        out_specs=(
            fresh(rows, width),
            fresh(keys, width),
            fresh(keys, width),
            fresh(1, 8, levels),
        ),
        scratch_shapes=[pltpu.VMEM((width, keys), bf16)]
        + [pltpu.VMEM((keys, BLK), f32)] * (2 * pairs)
        + [pltpu.VMEM((count, BLK, 2 * BLK), f32)] * pairs
        + [pltpu.VMEM((BLK, 2 * BLK), f32)] * pairs,
        compiler_params=pltpu.CompilerParams(vmem_limit_bytes=VMEM_CAP),
        cost_estimate=LIGHT,
        name="attend_back",
    )(lead, low, high, q, k, v, g, out, log, tiles, known, barred, buckets)


GROUPS = 2


def attention_tables(starts, ends, rel_bucket, rel_bias, lead):
    blocks = starts.shape[0]
    mine = (lead[:, None] == jnp.arange(blocks)[None, :]).astype(jnp.int32)
    own_start = jnp.sum(mine * starts[None, :], axis=1)
    own_end = jnp.sum(mine * ends[None, :], axis=1)
    low = jnp.sum((ends[None, :] < own_start[:, None]).astype(jnp.int32), axis=1)
    high = jnp.sum((starts[None, :] <= own_end[:, None]).astype(jnp.int32), axis=1)
    buckets = jnp.pad(jnp.flip(rel_bucket), (0, 1)).reshape(2 * blocks, BLK)
    levels, heads = rel_bias.shape
    rel = jnp.transpose(rel_bias).reshape(GROUPS, heads // GROUPS, levels)
    return low, high, buckets, rel


def pack_kernel(*refs):
    outs = [ref for ref in refs if ref.dtype == bf16]
    masters = [ref for ref in refs if ref.dtype == f32]
    at = 0
    for out in outs:
        col = 0
        while col < out.shape[1]:
            wide = masters[at].shape[1]
            out[:, col : col + wide] = masters[at][...].astype(bf16)
            col += wide
            at += 1


def pack(groups):
    steps = 1
    while all(group[0].shape[0] % (32 * steps) == 0 for group in groups) and steps < 4:
        steps *= 2

    def spec(array):
        return pl.BlockSpec((array.shape[0] // steps, array.shape[1]), lambda i: (i, 0))

    outs = tuple(
        jax.ShapeDtypeStruct((group[0].shape[0], sum(a.shape[1] for a in group)), bf16)
        for group in groups
    )
    arrays = [array for group in groups for array in group]
    return pl.pallas_call(
        pack_kernel,
        grid=(steps,),
        out_shape=outs,
        in_specs=[spec(array) for array in arrays],
        out_specs=tuple(spec(out) for out in outs),
        compiler_params=pltpu.CompilerParams(vmem_limit_bytes=VMEM_CAP),
        cost_estimate=LIGHT,
        name="pack",
    )(*arrays)


TN = (((0,), (0,)), ((), ()))


def fetch_rows(index, parts, whole, sems):
    rows = parts[0].shape[0]
    copies = []
    for j, part in enumerate(parts):
        start = pl.multiple_of((index ^ j) * rows, rows)
        copies.append(pltpu.make_async_copy(part, whole.at[pl.ds(start, rows), :], sems.at[j]))
    return copies


def project_kernel(count, index_ref, *refs):
    parts = refs[:count]
    norm_ref, own_ref, q_ref, k_ref, v_ref, whole_ref, whole, sems, done = refs[count:]
    width = norm_ref.shape[1]
    copies = fetch_rows(index_ref[0], parts, whole, sems)
    for copy in copies:
        copy.start()
    for copy in copies:
        copy.wait()
    keep = pltpu.make_async_copy(whole, whole_ref, done)
    keep.start()
    for out, rows, col in ((q_ref, own_ref, 0), (k_ref, norm_ref, 1), (v_ref, norm_ref, 2)):
        weight = whole[:, col * width : (col + 1) * width]
        for block in range(rows.shape[0] // 256):
            part = slice(block * 256, (block + 1) * 256)
            out[part, :] = jnp.dot(rows[part, :], weight, preferred_element_type=f32).astype(bf16)
    keep.wait()


def project(index, parts, norm, own):
    count = len(parts)
    width = norm.shape[1]
    full = (parts[0].shape[0] * count, parts[0].shape[1])
    vmem = pl.BlockSpec(memory_space=pltpu.VMEM)
    anywhere = pl.BlockSpec(memory_space=pl.ANY)
    return pl.pallas_call(
        functools.partial(project_kernel, count),
        out_shape=(
            jax.ShapeDtypeStruct(own.shape, bf16),
            jax.ShapeDtypeStruct(norm.shape, bf16),
            jax.ShapeDtypeStruct(norm.shape, bf16),
            jax.ShapeDtypeStruct(full, bf16),
        ),
        in_specs=[pl.BlockSpec(memory_space=pltpu.SMEM)] + [anywhere] * count + [vmem] * 2,
        out_specs=(vmem, vmem, vmem, anywhere),
        scratch_shapes=[
            pltpu.VMEM(full, bf16),
            pltpu.SemaphoreType.DMA((count,)),
            pltpu.SemaphoreType.DMA,
        ],
        compiler_params=pltpu.CompilerParams(vmem_limit_bytes=VMEM_CAP),
        cost_estimate=LIGHT,
        name="project",
    )(index, *parts, norm, own)


def project_back_kernel(count, halves, index_ref, lead_ref, norm_ref, own_ref, whole_ref, *refs):
    keep_ref, send_ref, dnorm_ref, grad_ref, sems = refs[3 * halves :]
    width = norm_ref.shape[1]
    part_width = width // halves
    for half in range(halves):
        for col in range(3):
            rows = own_ref if col == 0 else norm_ref
            here = slice(col * width + half * part_width, col * width + (half + 1) * part_width)
            grad_ref[:, here] = lax.dot_general(
                rows[...], refs[3 * half + col][...], TN, preferred_element_type=f32
            ).astype(bf16)
    for block in range(norm_ref.shape[0] // 256):
        part = slice(block * 256, (block + 1) * 256)
        total = None
        for half in range(halves):
            for col in (1, 2):
                here = slice(col * width + half * part_width, col * width + (half + 1) * part_width)
                term = lax.dot_general(
                    refs[3 * half + col][part, :],
                    whole_ref[:, here],
                    NT,
                    preferred_element_type=f32,
                )
                total = term if total is None else total + term
        dnorm_ref[part, :] = total
    for slot in range(own_ref.shape[0] // BLK):
        rows = pl.ds(pl.multiple_of(lead_ref[slot] * BLK, BLK), BLK)
        total = dnorm_ref[rows, :]
        for half in range(halves):
            total = total + lax.dot_general(
                refs[3 * half][slot * BLK : (slot + 1) * BLK, :],
                whole_ref[:, half * part_width : (half + 1) * part_width],
                NT,
                preferred_element_type=f32,
            )
        dnorm_ref[rows, :] = total
    scatter_rows(
        index_ref[0], count, ((grad_ref, 0, grad_ref.shape[1], keep_ref, send_ref),), sems
    )


def project_back(index, count, lead, norm, own, whole, halves):
    vmem = pl.BlockSpec(memory_space=pltpu.VMEM)
    anywhere = pl.BlockSpec(memory_space=pl.ANY)
    smem = pl.BlockSpec(memory_space=pltpu.SMEM)
    grads = [grad for half in halves for grad in half]
    part = jax.ShapeDtypeStruct((count // 2, whole.shape[0] // count, whole.shape[1]), bf16)
    return pl.pallas_call(
        functools.partial(project_back_kernel, count, len(halves)),
        out_shape=(part, part, jax.ShapeDtypeStruct(norm.shape, f32)),
        in_specs=[smem] * 2 + [vmem] * (3 + len(grads)),
        out_specs=(anywhere, anywhere, vmem),
        scratch_shapes=[pltpu.VMEM(whole.shape, bf16), pltpu.SemaphoreType.DMA((count,))],
        compiler_params=pltpu.CompilerParams(vmem_limit_bytes=VMEM_CAP),
        cost_estimate=LIGHT,
        name="project_back",
    )(index, lead, norm, own, whole, *grads)


ROOT = 0.7978845608028654
CUBE = 0.044715


def feed_kernel(count, index_ref, *refs):
    upper = refs[:count]
    lower = refs[count : 2 * count]
    (
        tok_ref,
        att_ref,
        cot_ref,
        gain_ref,
        out_ref,
        d_att_ref,
        d_resid_ref,
        gain_grad_ref,
        keep_ref,
        send_ref,
        ogu,
        down,
        store,
        resid,
        norm,
        d_norm,
        total,
        hid,
        d_gate,
        d_up,
        sems_upper,
        sems_lower,
        sems_store,
    ) = refs[2 * count :]
    rows, width = tok_ref.shape
    hidden = down.shape[0]
    copies_upper = fetch_rows(index_ref[0], upper, ogu, sems_upper)
    copies_lower = fetch_rows(index_ref[0], lower, down, sems_lower)
    for copy in copies_upper + copies_lower:
        copy.start()
    for copy in copies_upper:
        copy.wait()
    gain = gain_ref[...]
    row_step = 128
    tile = 512
    for block in range(rows // row_step):
        part = slice(block * row_step, (block + 1) * row_step)
        value = tok_ref[part, :] + jnp.dot(
            att_ref[part, :], ogu[:, :width], preferred_element_type=f32
        )
        resid[part, :] = value
        scale = lax.rsqrt(jnp.mean(value * value, axis=1, keepdims=True) + 1e-06)
        norm[part, :] = (value * scale * gain).astype(bf16)
    for copy in copies_lower:
        copy.wait()
    for n in range(hidden // tile):
        here = slice(n * tile, (n + 1) * tile)
        gate_cols = slice(width + n * tile, width + (n + 1) * tile)
        up_cols = slice(width + hidden + n * tile, width + hidden + (n + 1) * tile)
        for block in range(rows // row_step):
            part = slice(block * row_step, (block + 1) * row_step)
            gate_pre = jnp.dot(norm[part, :], ogu[:, gate_cols], preferred_element_type=f32)
            up_pre = jnp.dot(norm[part, :], ogu[:, up_cols], preferred_element_type=f32)
            d_hidden = lax.dot_general(
                cot_ref[part, :], down[here, :], NT, preferred_element_type=f32
            )
            square = gate_pre * gate_pre
            bent = jnp.tanh(ROOT * gate_pre * (1.0 + CUBE * square))
            half = 0.5 + 0.5 * bent
            gelu = gate_pre * half
            slope = half + (0.5 * ROOT) * gate_pre * (1.0 - bent * bent) * (
                1.0 + (3.0 * CUBE) * square
            )
            low = (gelu * up_pre).astype(bf16)
            d_gate_low = (d_hidden * up_pre * slope).astype(bf16)
            d_up_low = (d_hidden * gelu).astype(bf16)
            hid[part, :] = low
            d_gate[part, :] = d_gate_low
            d_up[part, :] = d_up_low
            add = jnp.dot(low, down[here, :], preferred_element_type=f32)
            back = lax.dot_general(
                d_gate_low, ogu[:, gate_cols], NT, preferred_element_type=f32
            ) + lax.dot_general(d_up_low, ogu[:, up_cols], NT, preferred_element_type=f32)
            if n == 0:
                total[part, :] = resid[part, :] + add
                d_norm[part, :] = back
            else:
                total[part, :] = total[part, :] + add
                d_norm[part, :] = d_norm[part, :] + back
        store[:, gate_cols] = lax.dot_general(
            norm[...], d_gate[...], TN, preferred_element_type=f32
        ).astype(bf16)
        store[:, up_cols] = lax.dot_general(
            norm[...], d_up[...], TN, preferred_element_type=f32
        ).astype(bf16)
        part = lax.dot_general(
            hid[...], cot_ref[...], TN, preferred_element_type=f32
        ).astype(bf16)
        for low_row, low_col, row, size in down_pieces(width // count, hidden // count, width):
            for device in range(count):
                source = device * (hidden // count) + low_row
                if n * tile <= source < (n + 1) * tile:
                    source = source - n * tile
                    target = device * (width // count) + row
                    col = width + 2 * hidden + low_col[1]
                    store[target : target + size, col : col + LANE] = part[
                        source : source + size, low_col[0] : low_col[0] + LANE
                    ]
    gain_sum = jnp.zeros((1, width), f32)
    for block in range(rows // row_step):
        part = slice(block * row_step, (block + 1) * row_step)
        out_ref[part, :] = total[part, :].astype(bf16)
        value = resid[part, :]
        grad = d_norm[part, :]
        scale = lax.rsqrt(jnp.mean(value * value, axis=1, keepdims=True) + 1e-06)
        scaled = grad * gain
        inner = jnp.mean(value * scaled, axis=1, keepdims=True)
        d_value = (
            cot_ref[part, :].astype(f32)
            + scale * scaled
            - value * (scale * scale * scale * inner)
        )
        gain_sum = gain_sum + jnp.sum(grad * value * scale, axis=0, keepdims=True)
        d_resid_ref[part, :] = d_value
        d_low = d_value.astype(bf16)
        norm[part, :] = d_low
        d_att_ref[part, :] = lax.dot_general(
            d_low, ogu[:, :width], NT, preferred_element_type=f32
        ).astype(bf16)
    gain_grad_ref[...] = gain_sum
    store[:, :width] = lax.dot_general(
        att_ref[...], norm[...], TN, preferred_element_type=f32
    ).astype(bf16)
    half = store.shape[1] // 2
    scatter_rows(
        index_ref[0],
        count,
        (
            (store, 0, half, keep_ref.at[0], send_ref.at[0]),
            (store, half, half, keep_ref.at[1], send_ref.at[1]),
        ),
        sems_store,
    )


def scatter_rows(index, count, jobs, sems):
    rows = jobs[0][0].shape[0] // count
    waits = []
    for n, (source, first, wide, keep, send) in enumerate(jobs):
        for device in range(count):
            other = index ^ device
            part = source.at[device * rows : (device + 1) * rows, first : first + wide]
            sem = sems.at[n * count + device]

            @pl.when(other % 2 == 0)
            def _():
                pltpu.make_async_copy(part, keep.at[other // 2], sem).start()

            @pl.when(other % 2 == 1)
            def _():
                pltpu.make_async_copy(part, send.at[other // 2], sem).start()

            waits.append(pltpu.make_async_copy(part, keep.at[0], sem))
    for wait in waits:
        wait.wait()


def down_pieces(rows, tall, width):
    size = 16
    while tall % (2 * size) == 0 and rows % (2 * size) == 0:
        size *= 2
    pieces = []
    for q in range(tall * (width // LANE) // size):
        there = (q % (tall // size)) * size
        here = (q % (rows // size)) * size
        pieces.append((there, (q // (tall // size) * LANE, q // (rows // size) * LANE), here, size))
    return pieces


def unpack_kernel(hidden, joined_ref, qkv_ref, *outs):
    rows = joined_ref.shape[0]
    width = outs[0].shape[1]
    for n in range(3):
        outs[n][...] = qkv_ref[:, n * width : (n + 1) * width].astype(f32)
    spans = ((0, width), (width, width + hidden), (width + hidden, width + 2 * hidden))
    for out, (first, last) in zip(outs[3:6], spans):
        out[...] = joined_ref[:, first:last].astype(f32)
    base = width + 2 * hidden
    for there, (col_there, col_here), here, size in down_pieces(rows, outs[6].shape[0], width):
        outs[6][there : there + size, col_there : col_there + LANE] = joined_ref[
            here : here + size, base + col_here : base + col_here + LANE
        ].astype(f32)


def unpack(joined, qkv, hidden, tall):
    rows = joined.shape[0]
    width = qkv.shape[1] // 3
    shapes = [(rows, width)] * 4 + [(rows, hidden)] * 2 + [(tall, width)]
    return pl.pallas_call(
        functools.partial(unpack_kernel, hidden),
        out_shape=tuple(jax.ShapeDtypeStruct(shape, f32) for shape in shapes),
        compiler_params=pltpu.CompilerParams(vmem_limit_bytes=VMEM_CAP),
        cost_estimate=LIGHT,
        name="unpack",
    )(joined, qkv)


def feed(index, upper, lower, tokens, attended, cotangent, gain):
    count = len(upper)
    rows, width = tokens.shape
    full_upper = (upper[0].shape[0] * count, upper[0].shape[1])
    full_lower = (lower[0].shape[0] * count, width)
    hidden = full_lower[0]
    columns = width + 3 * hidden
    vmem = pl.BlockSpec(memory_space=pltpu.VMEM)
    anywhere = pl.BlockSpec(memory_space=pl.ANY)
    tile = 512
    return pl.pallas_call(
        functools.partial(feed_kernel, count),
        out_shape=(
            jax.ShapeDtypeStruct((rows, width), bf16),
            jax.ShapeDtypeStruct((rows, width), bf16),
            jax.ShapeDtypeStruct((rows, width), f32),
            jax.ShapeDtypeStruct((1, width), f32),
            *[jax.ShapeDtypeStruct((2, count // 2, width // count, columns // 2), bf16)] * 2,
        ),
        in_specs=[pl.BlockSpec(memory_space=pltpu.SMEM)]
        + [anywhere] * (2 * count)
        + [vmem] * 4,
        out_specs=(vmem,) * 4 + (anywhere,) * 2,
        scratch_shapes=[
            pltpu.VMEM(full_upper, bf16),
            pltpu.VMEM(full_lower, bf16),
            pltpu.VMEM((width, columns), bf16),
            pltpu.VMEM((rows, width), f32),
            pltpu.VMEM((rows, width), bf16),
            pltpu.VMEM((rows, width), f32),
            pltpu.VMEM((rows, width), f32),
            pltpu.VMEM((rows, tile), bf16),
            pltpu.VMEM((rows, tile), bf16),
            pltpu.VMEM((rows, tile), bf16),
            pltpu.SemaphoreType.DMA((count,)),
            pltpu.SemaphoreType.DMA((count,)),
            pltpu.SemaphoreType.DMA((2 * count,)),
        ],
        compiler_params=pltpu.CompilerParams(vmem_limit_bytes=VMEM_CAP),
        cost_estimate=LIGHT,
        name="feed",
    )(index, *upper, *lower, tokens, attended, cotangent, gain.reshape(1, width))


def bits_of(count):
    bits = count.bit_length() - 1
    assert 1 << bits == count
    return bits


def swap(value, axis, bit):
    count = lax.axis_size(axis)
    return lax.ppermute(value, axis, [(i, i ^ (1 << bit)) for i in range(count)])


def ordered(mine, other, index, bit, axis=0):
    upper = ((index >> bit) & 1) == 1
    return jnp.concatenate(
        [jnp.where(upper, other, mine), jnp.where(upper, mine, other)], axis=axis
    )


def gather_small(value, axis):
    index = lax.axis_index(axis)
    value = value[None]
    for bit in range(bits_of(lax.axis_size(axis))):
        value = ordered(value, swap(value, axis, bit), index, bit)
    return value


def first_swap(shard, axis):
    bit = bits_of(lax.axis_size(axis)) - 1
    return [(0, shard), (1 << bit, swap(shard, axis, bit))]


def other_swaps(parts, axis):
    for bit in reversed(range(bits_of(lax.axis_size(axis)) - 1)):
        parts = parts + [(j | (1 << bit), swap(part, axis, bit)) for j, part in parts]
    return [part for _, part in sorted(parts, key=lambda pair: pair[0])]


def after(anchor, part):
    j, array = part
    anchor, array = lax.optimization_barrier((anchor, array))
    return anchor, (j, array)


def add_low(left, right):
    return (left.astype(f32) + right.astype(f32)).astype(bf16)


def piece(value, index, dim=0):
    return lax.dynamic_index_in_dim(value, index, dim, keepdims=False)


def scatter_step(value, axis, bit, dim):
    own = (lax.axis_index(axis) >> bit) & 1
    other = swap(piece(value, 1 - own, dim), axis, bit)
    return add_low(piece(value, own, dim), other)


def rest_sum(value, axis):
    count = lax.axis_size(axis)
    index = lax.axis_index(axis)
    mine = index // 2
    total = piece(value, mine).astype(f32)
    for j in range(1, count // 2):
        pairs = [(i, ((i // 2) ^ j) * 2 + i % 2) for i in range(count)]
        total = total + lax.ppermute(piece(value, mine ^ j), axis, pairs).astype(f32)
    return total.astype(bf16)


def rest_gather(value, axis):
    count = lax.axis_size(axis)
    index = lax.axis_index(axis)
    whole = jnp.zeros((count // 2,) + value.shape, value.dtype)
    for j in range(count // 2):
        part = value
        if j:
            pairs = [(i, ((i // 2) ^ j) * 2 + i % 2) for i in range(count)]
            part = lax.ppermute(value, axis, pairs)
        whole = lax.dynamic_update_index_in_dim(whole, part, (index // 2) ^ j, 0)
    return whole


def pair_gather(whole, axis):
    other = swap(whole, axis, 0)
    upper = lax.axis_index(axis) % 2 == 1
    both = jnp.stack([jnp.where(upper, other, whole), jnp.where(upper, whole, other)], axis=1)
    return both.reshape((2 * whole.shape[0] * whole.shape[1],) + whole.shape[2:])


def fsdp_step(keep, send, bit):
    return add_low(keep, swap(send, "fsdp", bit))


def split_bit(value):
    value = value.reshape((value.shape[0] // 2, 2) + value.shape[1:])
    return value[:, 0], value[:, 1]


def parity_step(value, dim):
    count = lax.axis_size("ctx")
    shape = value.shape
    value = value.reshape(shape[:dim] + (count // 2, 2, shape[dim] // count) + shape[dim + 1 :])
    return scatter_step(value, "ctx", 0, dim + 1)


def rest_of_chain(total):
    total = yield rest_sum(total, "ctx")
    total = yield rest_gather(total, "ctx")
    yield pair_gather(total, "ctx")


def single_chain(keep, send):
    bits = bits_of(lax.axis_size("fsdp"))
    total = yield fsdp_step(keep, send, 0)
    for bit in range(1, bits):
        keep, send = split_bit(total)
        total = yield fsdp_step(keep, send, bit)
    total = yield parity_step(total[0], 0)
    yield from rest_of_chain(total)


def double_chain(keep, send):
    bits = bits_of(lax.axis_size("fsdp"))
    other = swap(send, "fsdp", 0)
    left, right = yield (add_low(keep[0], other[0]), add_low(keep[1], other[1]))
    for bit in range(bits):
        if bit < bits - 1:
            left = fsdp_step(*split_bit(left), bit + 1)
        else:
            left = parity_step(left[0], 0)
        if bit == 0:
            right = parity_step(right, 1)
        else:
            right = fsdp_step(*split_bit(right), bit)
        left, right = yield (left, right)
    joined = jnp.concatenate([left, right[0]], axis=-1)
    yield from rest_of_chain(joined)


class Chain:
    def __init__(self, steps):
        self.steps = steps
        self.value = next(steps)

    def advance(self, value):
        self.value = self.steps.send(value)

    def finish(self):
        while True:
            try:
                self.advance(self.value)
            except StopIteration:
                return self.value


def gate(anchor, *chains):
    joined = lax.optimization_barrier((anchor,) + tuple(chain.value for chain in chains))
    for chain, value in zip(chains, joined[1:]):
        chain.advance(value)
    return joined[0]


def reduce_small(value):
    fsdp_bits = bits_of(lax.axis_size("fsdp"))
    count = lax.axis_size("ctx")
    rows, width = value.shape
    value = value.reshape(2, count // 2, 2 * rows // (2 * count), width)
    value = scatter_step(value, "fsdp", 0, 0)
    value = rest_sum(value, "ctx")
    value = add_low(value, swap(value, "ctx", 0))
    for bit in range(1, fsdp_bits):
        value = add_low(value, swap(value, "fsdp", bit))
    whole = rest_gather(value, "ctx")
    whole = whole.reshape((rows // 2, width))
    return ordered(whole, swap(whole, "fsdp", 0), lax.axis_index("fsdp"), 0)


def local(
    byte_ids,
    doc_ids,
    rel_bucket,
    table,
    conv_w,
    score_w,
    gain_one,
    gain_two,
    rel_bias,
    query_master,
    key_master,
    value_master,
    out_master,
    gate_master,
    up_master,
    down_master,
    out_cotangent,
):
    ctx_count = lax.axis_size("ctx")
    ctx_index = lax.axis_index("ctx")
    seq_count, byte_count = byte_ids.shape
    total_bytes = byte_count * ctx_count
    width = table.shape[1]
    vocab = table.shape[0]
    hidden_width = gate_master.shape[1]
    levels, heads = rel_bias.shape
    share = ctx_count // seq_count
    assert share * seq_count == ctx_count and byte_count == 2 * BLK
    seq = ctx_index // share
    part = ctx_index % share
    near = [seq ^ slot for slot in range(seq_count)]
    lead = jnp.stack([share * other + part for other in near]).astype(jnp.int32)
    rows = seq_count * BLK

    qkv_low, down_low, ogu_low = pack(
        [[query_master, key_master, value_master], [down_master], [out_master, gate_master, up_master]]
    )
    both = jnp.stack([byte_ids, doc_ids], axis=1)
    both = gather_small(both, "ctx")
    both, qkv_low, down_low = lax.optimization_barrier((both, qkv_low, down_low))
    qkv_parts = first_swap(qkv_low, "fsdp")
    shard = lax.axis_index("fsdp")[None]
    shards = lax.axis_size("fsdp")

    def to_owner(block, slot):
        if slot == 0:
            return block
        pairs = []
        for c in range(ctx_count):
            pairs.append((c, ((c // share) ^ slot) * share + c % share))
        return lax.ppermute(block, "ctx", pairs)

    table_wide = jnp.pad(table, ((0, -vocab % LANE), (0, 0)))
    score_row = score_w.reshape(1, width)
    gain_row = gain_one.reshape(1, width)
    seq_row = seq[None]
    tokens, norm_one, norm_own, tokens_own, conv, mix, phases, known, barred = byte_forward(
        seq_row, lead, both, table_wide, conv_w, score_row, gain_row, total_bytes
    )
    down_parts = first_swap(down_low, "fsdp")
    blocks = [to_owner(piece(out_cotangent, near[s], 1), s) for s in range(seq_count)]
    norm_one, crossed, down_crossed, blocks, ogu_low = lax.optimization_barrier(
        (norm_one, qkv_parts[1][1], down_parts[1][1], blocks, ogu_low)
    )
    qkv_parts[1] = (qkv_parts[1][0], crossed)
    down_parts[1] = (down_parts[1][0], down_crossed)
    qkv_parts = other_swaps(qkv_parts, "fsdp")
    queries, keys, values, qkv = project(shard, qkv_parts, norm_one, norm_own)
    ogu_parts = first_swap(ogu_low, "fsdp")
    down_parts = other_swaps(down_parts, "fsdp")
    docs = piece(both[:, :, 1], seq, 1)
    low, high, buckets, rel = attention_tables(
        docs[:, 0], docs[:, 2 * BLK - 2], rel_bucket, rel_bias, lead
    )
    attended, attended_low, log_total, tiles = attend(
        lead, low, high, queries, keys, values, known, barred, buckets, rel
    )
    cotangent = jnp.concatenate(blocks, axis=0)

    attended_low, ogu_parts[1] = after(attended_low, ogu_parts[1])
    output, d_attended, d_resid, grad_gain_two, *grads = feed(
        shard,
        other_swaps(ogu_parts, "fsdp"),
        down_parts,
        tokens_own,
        attended_low,
        cotangent,
        gain_two,
    )
    chain = Chain(double_chain(*grads))
    d_attended = gate(d_attended, chain)

    output = output.reshape(seq_count, BLK, width)
    arrived = [to_owner(output[s], s) for s in range(seq_count)]

    halves = []
    for group in range(GROUPS):
        if group:
            d_attended, arrived = gate((d_attended, arrived), chain)
            arrived = jnp.stack(arrived)
            output = jnp.stack([piece(arrived, seq ^ s) for s in range(seq_count)], axis=1)
        *grads, d_bias = attend_back(
            group,
            levels,
            lead,
            low,
            high,
            queries,
            keys,
            values,
            d_attended,
            attended,
            log_total,
            tiles,
            known,
            barred,
            buckets,
        )
        halves.append((grads, d_bias))
        d_attended, _ = lax.optimization_barrier((d_attended, grads[0]))
    d_bias = jnp.concatenate([half[1] for half in halves], axis=0)
    norm_own, halves = gate((norm_own, [half[0] for half in halves]), chain)
    keep, send, d_norm_one = project_back(shard, shards, lead, norm_one, norm_own, qkv, halves)
    qkv_chain = Chain(single_chain(keep, send))
    d_norm_one = gate(d_norm_one, qkv_chain, chain)

    vocab_rows = -(-vocab // 16) * 16
    d_resid = d_resid.reshape(seq_count, BLK, width)
    small = byte_backward(
        lead,
        phases,
        tokens,
        d_norm_one,
        d_resid,
        conv,
        mix,
        table_wide,
        vocab_rows,
        conv_w,
        score_row,
        gain_row,
        total_bytes,
    )
    bias_grad = jnp.transpose(d_bias[:, : heads // GROUPS].reshape(heads, levels)).reshape(1, levels * heads)
    bias_grad = jnp.pad(bias_grad, ((0, 0), (0, width - levels * heads)))
    small = jnp.concatenate([small[: vocab_rows + 6], grad_gain_two, bias_grad], axis=0)
    small = jnp.pad(small, ((0, -small.shape[0] % (8 * ctx_count)), (0, 0))).astype(bf16)
    small = gate(small, qkv_chain, chain)
    small = reduce_small(small).astype(f32)
    grads = unpack(chain.finish(), qkv_chain.finish(), hidden_width, down_master.shape[0])
    top = vocab_rows
    return (
        output,
        small[:vocab],
        small[top : top + 4],
        small[top + 4],
        small[top + 5],
        small[top + 6],
        small[top + 7, : levels * heads].reshape(levels, heads),
        *grads,
    )


def solution(mesh):
    placed = (
        P("fsdp", "ctx"),
        P("fsdp", "ctx"),
        P(),
        P(),
        P(),
        P(),
        P(),
        P(),
        P(),
        P("fsdp", None),
        P("fsdp", None),
        P("fsdp", None),
        P("fsdp", None),
        P("fsdp", None),
        P("fsdp", None),
        P("fsdp", None),
        P("ctx", "fsdp", None),
    )
    return jax.shard_map(
        local,
        mesh=mesh,
        in_specs=placed,
        out_specs=(
            P("ctx", "fsdp", None),
            P(),
            P(),
            P(),
            P(),
            P(),
            P(),
            P("fsdp", None),
            P("fsdp", None),
            P("fsdp", None),
            P("fsdp", None),
            P("fsdp", None),
            P("fsdp", None),
            P("fsdp", None),
        ),
        check_vma=False,
    )
```

```python
import functools

import jax
import jax.numpy as jnp
from jax import lax
from jax.experimental import pallas as pl
from jax.experimental.pallas import tpu as pltpu
from jax.sharding import PartitionSpec as P

f32 = jnp.float32
bf16 = jnp.bfloat16
LANE = 128
BLK = 128
VMEM_CAP = 60 * 1024 * 1024
HIGH = lax.Precision.HIGHEST
NT = (((1,), (1,)), ((), ()))
NN = (((1,), (0,)), ((), ()))
LIGHT = pl.CostEstimate(flops=1, transcendentals=0, bytes_accessed=1)


STEP = 16
NORM_ROWS = 128


def lane_iota(rows):
    return lax.broadcasted_iota(jnp.int32, (rows, LANE), 1)


def block_sum(value, width, lane):
    def ahead(v, n):
        return pltpu.roll(v, LANE - n, 1)

    def behind(v, n):
        return pltpu.roll(v, n, 1)

    if width == 1:
        return value
    if width == 3:
        lead = value + ahead(value, 1) + ahead(value, 2)
        phase = lane % 3
        return jnp.where(phase == 0, lead, jnp.where(phase == 1, behind(lead, 1), behind(lead, 2)))
    pair = value + jnp.where(lane % 2 == 0, ahead(value, 1), behind(value, 1))
    if width == 2:
        return pair
    return pair + jnp.where(lane % 4 < 2, ahead(pair, 2), behind(pair, 2))


def pick(value, lane_index):
    return value[:, lane_index : lane_index + 1]


def byte_forward_kernel(
    total_bytes,
    seq_ref,
    lead_ref,
    both_ref,
    table_ref,
    conv_w_ref,
    score_ref,
    gain_ref,
    tok_ref,
    norm_ref,
    norm_own_ref,
    tok_own_ref,
    conv_ref,
    mix_ref,
    ids_ref,
    known_ref,
    barred_ref,
    hi_ref,
    lo_ref,
    emb,
    flat,
    spread,
):
    groups = conv_ref.shape[1]
    width = conv_ref.shape[2]
    tiles = width // LANE
    token_count = norm_ref.shape[0]
    vocab_pad = hi_ref.shape[0]
    row_lanes = ids_ref.shape[1]
    seq = seq_ref[0]
    vocab = table_ref.shape[0]
    whole_rows = vocab // 128 * 128
    rest = jnp.zeros((vocab_pad - whole_rows, width), f32)
    rest_row = lax.broadcasted_iota(jnp.int32, rest.shape, 0)
    for row in range(whole_rows, vocab):
        rest = jnp.where(rest_row == row - whole_rows, table_ref[row : row + 1, :], rest)
    for here, value in ((0, table_ref[0:whole_rows, :]), (whole_rows, rest)):
        high = value.astype(bf16)
        hi_ref[here : here + value.shape[0], :] = high
        lo_ref[here : here + value.shape[0], :] = (value - high.astype(f32)).astype(bf16)
    lane_f = lane_iota(BLK).astype(f32)
    chunk_bytes = both_ref.shape[3]

    def lay(kind, first):
        for block in range(both_ref.shape[0]):
            row = both_ref[block, seq, kind : kind + 1, :].astype(f32)
            for half in range(chunk_bytes // LANE):
                part = jnp.broadcast_to(row[:, half * LANE : (half + 1) * LANE], (LANE, LANE))
                start = first + block * chunk_bytes + half * LANE
                spread[start : start + LANE, :] = jnp.transpose(part)

    lay(1, 0)
    for block in range(token_count // BLK):
        docs = spread[pl.ds(block * 2 * BLK, BLK, stride=2), :]
        same = docs == lane_f
        rows = slice(block * BLK, (block + 1) * BLK)
        known_ref[rows, :] = same.astype(bf16)
        barred_ref[rows, :] = jnp.where(same | (lane_f >= 16.0), 0.0, -1e30).astype(bf16)
    lay(0, 16)
    none = jnp.full((16, LANE), -1.0, f32)
    spread[0:16, :] = none
    tail = spread.shape[0] - total_bytes - 16
    spread[total_bytes + 16 :, :] = jnp.full((tail, LANE), -1.0, f32)
    lane_g = lane_iota(groups).astype(f32)
    for r in range(15):
        here = spread[pl.ds(13 + r, row_lanes, stride=12), :]
        turned = [
            jnp.transpose(here[n * LANE : (n + 1) * LANE, :])[0:1, :]
            for n in range(row_lanes // LANE)
        ]
        ids_ref[r : r + 1, :] = jnp.concatenate(turned, axis=1)
        onehot = jnp.concatenate(
            [
                (here[0:groups, :] == lane_g + n * LANE).astype(bf16)
                for n in range(vocab_pad // LANE)
            ],
            axis=1,
        )
        emb[r] = jnp.dot(onehot, hi_ref[...], preferred_element_type=f32) + jnp.dot(
            onehot, lo_ref[...], preferred_element_type=f32
        )
    ids_ref[15:16, :] = jnp.full((1, row_lanes), -1.0, f32)
    lane = lane_iota(STEP)

    def chunk(i, masked):
        r0 = pl.multiple_of(i * STEP, STEP)
        rows = pl.ds(r0, STEP)
        sums = [jnp.zeros((STEP, LANE), f32) for _ in range(12)]
        for tile in range(tiles):
            cols = slice(tile * LANE, (tile + 1) * LANE)
            taps = [conv_w_ref[k : k + 1, cols] for k in range(4)]
            piece = [emb[r, rows, cols] for r in range(15)]
            score = score_ref[0:1, cols]
            for r in range(12):
                value = (
                    piece[r] * taps[0]
                    + piece[r + 1] * taps[1]
                    + piece[r + 2] * taps[2]
                    + piece[r + 3] * taps[3]
                )
                if masked:
                    group = r0 + lax.broadcasted_iota(jnp.int32, (STEP, LANE), 0)
                    value = jnp.where(group * 12 + r < total_bytes, value, 0.0)
                conv_ref[r, rows, cols] = value
                sums[r] = sums[r] + value * score
        packed = jnp.zeros((STEP, LANE), f32)
        for r in range(12):
            packed = jnp.where(lane == r, jnp.sum(sums[r], axis=1, keepdims=True), packed)
        logits = [block_sum(packed, b, lane) * (1.0 / b) for b in range(1, 5)]
        best = jnp.maximum(jnp.maximum(logits[0], logits[1]), jnp.maximum(logits[2], logits[3]))
        parts = [jnp.exp(value - best) for value in logits]
        total = parts[0] + parts[1] + parts[2] + parts[3]
        mix = [part / total for part in parts]
        for b in range(4):
            mix_ref[b, rows, :] = mix[b]
        half_one = mix[0] * 0.5
        pair_two = block_sum(mix[1], 2, lane) * 0.25
        single_three = mix[2] * (1.0 / 6.0)
        pair_three = block_sum(mix[2], 2, lane) * (1.0 / 6.0)
        pair_four = block_sum(mix[3], 2, lane) * 0.125
        coef_one = [pick(half_one, r) for r in range(12)]
        coef_two = [pick(pair_two, 2 * j) for j in range(6)]
        coef_four = [pick(pair_four, 2 * j) for j in range(6)]
        coef_three = []
        for j in range(6):
            if j % 3 == 1:
                coef_three.append((pick(single_three, 2 * j), pick(single_three, 2 * j + 1)))
            else:
                coef_three.append((pick(pair_three, 2 * j), None))
        for tile in range(tiles):
            cols = slice(tile * LANE, (tile + 1) * LANE)
            conv = [conv_ref[r, rows, cols] for r in range(12)]
            two = [conv[2 * j] + conv[2 * j + 1] for j in range(6)]
            three = [conv[3 * q] + conv[3 * q + 1] + conv[3 * q + 2] for q in range(4)]
            four = [two[2 * q] + two[2 * q + 1] for q in range(3)]
            for j in range(6):
                a, b = 2 * j, 2 * j + 1
                value = coef_one[a] * conv[a] + coef_one[b] * conv[b]
                value = value + coef_two[j] * two[j] + coef_four[j] * four[j // 2]
                value = value + coef_three[j][0] * three[a // 3]
                if j % 3 == 1:
                    value = value + coef_three[j][1] * three[b // 3]
                flat[tile, pl.ds(6 * r0 + j, STEP, stride=6), :] = value

    whole = (total_bytes // 12) // STEP

    def plain(i, carry):
        chunk(i, False)
        return carry

    lax.fori_loop(0, whole, plain, 0)
    for i in range(whole, groups // STEP):
        chunk(i, True)

    def norm(i, carry):
        rows = pl.ds(pl.multiple_of(i * NORM_ROWS, NORM_ROWS), NORM_ROWS)
        value = jnp.concatenate([flat[tile, rows, :] for tile in range(tiles)], axis=1)
        tok_ref[rows, :] = value
        scale = lax.rsqrt(jnp.mean(value * value, axis=1, keepdims=True) + 1e-06)
        norm_ref[rows, :] = (value * scale * gain_ref[...]).astype(bf16)
        return carry

    lax.fori_loop(0, token_count // NORM_ROWS, norm, 0)
    for slot in range(norm_own_ref.shape[0] // BLK):
        start = pl.multiple_of(lead_ref[slot] * BLK, BLK)
        norm_own_ref[slot * BLK : (slot + 1) * BLK, :] = norm_ref[pl.ds(start, BLK), :]
        tok_own_ref[slot * BLK : (slot + 1) * BLK, :] = tok_ref[pl.ds(start, BLK), :]


def byte_forward(seq, lead, both, table, conv_w, score_w, gain_one, total_bytes):
    width = conv_w.shape[1]
    token_count = total_bytes // 2
    least = -(-total_bytes // 12)
    groups = -(-least // 16) * 16
    row_lanes = -(-least // LANE) * LANE
    vocab_pad = -(-table.shape[0] // LANE) * LANE
    smem = pl.BlockSpec(memory_space=pltpu.SMEM)
    vmem = pl.BlockSpec(memory_space=pltpu.VMEM)
    return pl.pallas_call(
        functools.partial(byte_forward_kernel, total_bytes),
        out_shape=(
            jax.ShapeDtypeStruct((token_count, width), f32),
            jax.ShapeDtypeStruct((token_count, width), bf16),
            jax.ShapeDtypeStruct((lead.shape[0] * BLK, width), bf16),
            jax.ShapeDtypeStruct((lead.shape[0] * BLK, width), f32),
            jax.ShapeDtypeStruct((12, groups, width), f32),
            jax.ShapeDtypeStruct((4, groups, LANE), f32),
            jax.ShapeDtypeStruct((16, row_lanes), f32),
            jax.ShapeDtypeStruct((token_count, LANE), bf16),
            jax.ShapeDtypeStruct((token_count, LANE), bf16),
        ),
        in_specs=[smem, smem] + [vmem] * 5,
        scratch_shapes=[
            pltpu.VMEM((vocab_pad, width), bf16),
            pltpu.VMEM((vocab_pad, width), bf16),
            pltpu.VMEM((15, groups, width), f32),
            pltpu.VMEM((width // LANE, 6 * groups, LANE), f32),
            pltpu.VMEM((12 * row_lanes + 32, LANE), f32),
        ],
        compiler_params=pltpu.CompilerParams(vmem_limit_bytes=VMEM_CAP),
        cost_estimate=LIGHT,
        name="byte_forward",
    )(
        seq,
        lead,
        both,
        table,
        conv_w,
        score_w,
        gain_one,
    )


def byte_backward_kernel(
    total_bytes,
    first_ref,
    ids_ref,
    tok_ref,
    dnorm_ref,
    dres_ref,
    conv_ref,
    mix_ref,
    table_ref,
    conv_w_ref,
    score_ref,
    gain_ref,
    out_ref,
    dtok,
    dconv,
    onehot,
):
    groups = conv_ref.shape[1]
    width = conv_ref.shape[2]
    tiles = width // LANE
    token_count = dnorm_ref.shape[0]
    vocab_rows = onehot.shape[0]
    lanes = ids_ref.shape[1]
    gain = gain_ref[...]

    def norm_back(i, acc):
        rows = pl.ds(pl.multiple_of(i * NORM_ROWS, NORM_ROWS), NORM_ROWS)
        value = tok_ref[rows, :]
        grad = dnorm_ref[rows, :]
        scale = lax.rsqrt(jnp.mean(value * value, axis=1, keepdims=True) + 1e-06)
        grad_gain = grad * gain
        inner = jnp.mean(value * grad_gain, axis=1, keepdims=True)
        total = 0.5 * scale * grad_gain - value * (0.5 * scale * scale * scale * inner)
        for tile in range(tiles):
            dtok[tile, rows, :] = total[:, tile * LANE : (tile + 1) * LANE]
        product = (grad * value * scale).reshape(NORM_ROWS // 8, 8, width)
        return acc + jnp.sum(product, axis=0)

    gain_acc = lax.fori_loop(0, token_count // NORM_ROWS, norm_back, jnp.zeros((8, width), f32))
    rest = dtok.shape[1] - token_count
    dtok[:, token_count:, :] = jnp.zeros((tiles, rest, LANE), f32)
    for slot in range(dres_ref.shape[0]):
        start = pl.multiple_of(first_ref[slot] * BLK, BLK)

        def add(i, carry, slot=slot, start=start):
            r = pl.multiple_of(i * 32, 32)
            rows = pl.ds(pl.multiple_of(start + r, 32), 32)
            more = 0.5 * dres_ref[slot, pl.ds(r, 32), :]
            for tile in range(tiles):
                dtok[tile, rows, :] = (
                    dtok[tile, rows, :] + more[:, tile * LANE : (tile + 1) * LANE]
                )
            return carry

        lax.fori_loop(0, BLK // 32, add, 0)
    vocab = lax.broadcasted_iota(jnp.int32, (vocab_rows, lanes), 0).astype(f32)
    for r in range(15):
        onehot[:, r * lanes : (r + 1) * lanes] = (vocab == ids_ref[r : r + 1, :]).astype(bf16)
    for r in range(12):
        dconv[r * lanes + groups : (r + 1) * lanes, :] = jnp.zeros((lanes - groups, width), bf16)
    lane = lane_iota(8)

    def scalars(r0):
        rows = pl.ds(r0, 8)
        one = [jnp.zeros((8, LANE), f32) for _ in range(12)]
        cross = [jnp.zeros((8, LANE), f32) for _ in range(6)]
        tri = [jnp.zeros((8, LANE), f32) for _ in range(8)]
        for tile in range(tiles):
            cols = slice(tile * LANE, (tile + 1) * LANE)
            conv = [conv_ref[r, rows, cols] for r in range(12)]
            grad = [dtok[tile, pl.ds(6 * r0 + j, 8, stride=6), :] for j in range(6)]
            two = [conv[2 * j] + conv[2 * j + 1] for j in range(6)]
            three = [conv[3 * q] + conv[3 * q + 1] + conv[3 * q + 2] for q in range(4)]
            for r in range(12):
                one[r] = one[r] + conv[r] * grad[r // 2]
            slot = 0
            for j in range(6):
                cross[j] = cross[j] + two[j ^ 1] * grad[j]
                for q in sorted({(2 * j) // 3, (2 * j + 1) // 3}):
                    tri[slot] = tri[slot] + three[q] * grad[j]
                    slot += 1
        inner_one = jnp.zeros((8, LANE), f32)
        for r in range(12):
            inner_one = jnp.where(lane == r, jnp.sum(one[r], axis=1, keepdims=True), inner_one)
        inner_cross = jnp.zeros((8, LANE), f32)
        for j in range(6):
            inner_cross = jnp.where(
                lane // 2 == j, jnp.sum(cross[j], axis=1, keepdims=True), inner_cross
            )
        inner_three = jnp.zeros((8, LANE), f32)
        slot = 0
        for j in range(6):
            for q in sorted({(2 * j) // 3, (2 * j + 1) // 3}):
                here = (lane // 2 == j) & (lane // 3 == q)
                inner_three = jnp.where(
                    here, jnp.sum(tri[slot], axis=1, keepdims=True), inner_three
                )
                slot += 1
        inner_two = block_sum(inner_one, 2, lane)
        mix = [mix_ref[b, rows, :] for b in range(4)]
        d_mix = [
            inner_one,
            inner_two * 0.5,
            inner_three * (1.0 / 3.0),
            (inner_two + inner_cross) * 0.25,
        ]
        mean = mix[0] * d_mix[0] + mix[1] * d_mix[1] + mix[2] * d_mix[2] + mix[3] * d_mix[3]
        d_logit = [mix[b] * (d_mix[b] - mean) for b in range(4)]
        d_logit = [jnp.where(lane < 12, value, 0.0) for value in d_logit]
        slope = d_logit[0]
        for b in range(2, 5):
            slope = slope + block_sum(d_logit[b - 1], b, lane) * (1.0 / b)
        pair_two = block_sum(mix[1], 2, lane) * 0.5
        single_three = mix[2] * (1.0 / 3.0)
        pair_three = block_sum(mix[2], 2, lane) * (1.0 / 3.0)
        pair_four = block_sum(mix[3], 2, lane) * 0.25
        return mix[0], pair_two, single_three, pair_three, pair_four, slope

    def spread(r0, coefs, tile, masked, score_acc):
        one, pair_two, single_three, pair_three, pair_four, slope = coefs
        rows = pl.ds(r0, 8)
        cols = slice(tile * LANE, (tile + 1) * LANE)
        grad = [dtok[tile, pl.ds(6 * r0 + j, 8, stride=6), :] for j in range(6)]
        score = score_ref[0:1, cols]
        four = [
            pick(pair_four, 4 * q) * grad[2 * q] + pick(pair_four, 4 * q + 2) * grad[2 * q + 1]
            for q in range(3)
        ]
        three = []
        for q in range(4):
            a = 3 * q
            if a % 2 == 0:
                three.append(
                    pick(pair_three, a) * grad[a // 2]
                    + pick(single_three, a + 2) * grad[a // 2 + 1]
                )
            else:
                three.append(
                    pick(single_three, a) * grad[a // 2]
                    + pick(pair_three, a + 1) * grad[a // 2 + 1]
                )
        result = []
        for r in range(12):
            weight = pick(slope, r)
            own = (pick(one, r) + pick(pair_two, r)) * grad[r // 2]
            value = own + three[r // 3] + four[r // 4] + weight * score
            score_acc = score_acc + weight * conv_ref[r, rows, cols]
            if masked:
                group = r0 + lax.broadcasted_iota(jnp.int32, (8, LANE), 0)
                value = jnp.where(group * 12 + r < total_bytes, value, 0.0)
            result.append(value)
        return result, score_acc

    def chunk(i, accs, masked):
        r0 = pl.multiple_of(i * 16, 16)
        r1 = pl.multiple_of(i * 16 + 8, 8)
        low_coefs = scalars(r0)
        high_coefs = scalars(r1)
        new = []
        for tile in range(tiles):
            cols = slice(tile * LANE, (tile + 1) * LANE)
            low, acc = spread(r0, low_coefs, tile, masked, accs[tile])
            high, acc = spread(r1, high_coefs, tile, masked, acc)
            new.append(acc)
            for r in range(12):
                both = jnp.concatenate([low[r], high[r]], axis=0).astype(bf16)
                dconv[pl.ds(pl.multiple_of(r * lanes + r0, 16), 16), cols] = both
        return tuple(new)

    accs = tuple(jnp.zeros((8, LANE), f32) for _ in range(tiles))
    whole = (total_bytes // 12) // 16
    accs = lax.fori_loop(0, whole, lambda i, a: chunk(i, a, False), accs)
    for i in range(whole, groups // 16):
        accs = chunk(i, accs, True)
    tail = [jnp.zeros((1, width), f32) for _ in range(8)]
    for k in range(4):
        part = jnp.dot(
            onehot[:, k * lanes : (k + 12) * lanes], dconv[...], preferred_element_type=f32
        )
        if k == 0:
            out_ref[0:vocab_rows, :] = part * conv_w_ref[k : k + 1, :]
        else:
            out_ref[0:vocab_rows, :] = out_ref[0:vocab_rows, :] + part * conv_w_ref[k : k + 1, :]
        vocab = table_ref.shape[0]
        whole_rows = vocab // 8 * 8
        tail[k] = jnp.sum(part[:whole_rows] * table_ref[0:whole_rows, :], axis=0, keepdims=True)
        for row in range(whole_rows, vocab):
            tail[k] = tail[k] + part[row : row + 1] * table_ref[row : row + 1, :]
    tail[4] = jnp.sum(jnp.concatenate(accs, axis=1), axis=0, keepdims=True)
    tail[5] = jnp.sum(gain_acc, axis=0, keepdims=True)
    out_ref[vocab_rows:, :] = jnp.concatenate(tail, axis=0)


def byte_backward(
    first,
    ids,
    tokens,
    d_norm,
    d_resid,
    conv,
    mix,
    table,
    vocab_rows,
    conv_w,
    score_w,
    gain_one,
    total_bytes,
):
    width = conv.shape[2]
    groups = conv.shape[1]
    lanes = ids.shape[1]
    return pl.pallas_call(
        functools.partial(byte_backward_kernel, total_bytes),
        out_shape=jax.ShapeDtypeStruct((vocab_rows + 8, width), f32),
        in_specs=[pl.BlockSpec(memory_space=pltpu.SMEM)]
        + [pl.BlockSpec(memory_space=pltpu.VMEM)] * 10,
        scratch_shapes=[
            pltpu.VMEM((width // LANE, 6 * groups, LANE), f32),
            pltpu.VMEM((12 * lanes, width), bf16),
            pltpu.VMEM((vocab_rows, 15 * lanes), bf16),
        ],
        compiler_params=pltpu.CompilerParams(vmem_limit_bytes=VMEM_CAP),
        cost_estimate=LIGHT,
        name="byte_backward",
    )(
        first,
        ids,
        tokens,
        d_norm,
        d_resid,
        conv,
        mix,
        table,
        conv_w,
        score_w,
        gain_one,
    )


def head_mask(value, head):
    half = value.shape[1] // 2
    lane = lax.broadcasted_iota(jnp.int32, value.shape, 1)
    keep = lane < half if head == 0 else lane >= half
    return jnp.where(keep, value, jnp.zeros_like(value))


def two_heads(value):
    return jnp.concatenate([head_mask(value, 0), head_mask(value, 1)], axis=0)


def bucket_row(buckets_ref, n, reach):
    row = buckets_ref.shape[0] // 2 - 1 - (n - reach)
    return jnp.concatenate([buckets_ref[row : row + 1, :], buckets_ref[row + 1 : row + 2, :]], axis=1)


def bias_tiles(buckets_ref, rel, tiles):
    count = tiles.shape[1]
    levels = rel.shape[1]
    level = lax.broadcasted_iota(jnp.int32, (levels, 2 * BLK), 0)
    for n in range(count):
        onehot = (level == bucket_row(buckets_ref, n, count // 2)).astype(f32)
        values = lax.dot_general(rel, onehot, NN, precision=HIGH, preferred_element_type=f32)
        for head in range(2 * tiles.shape[0]):
            spread = jnp.broadcast_to(values[head : head + 1, :], (BLK, 2 * BLK))
            rolled = pltpu.roll(spread, BLK + 1, 1, stride=1, stride_axis=0)
            half = slice(head % 2 * BLK, head % 2 * BLK + BLK)
            tiles[head // 2, n, :, half] = rolled[:, :BLK]


def fold_rows(value, op):
    return op(value.reshape(BLK // 8, 8, value.shape[1]), axis=0)


def attend_kernel(
    lead_ref,
    low_ref,
    high_ref,
    q_ref,
    k_ref,
    v_ref,
    known,
    barred,
    buckets_ref,
    rel_ref,
    out_ref,
    low_out_ref,
    log_ref,
    tiles,
    v_turned,
    *scratch,
):
    pairs = tiles.shape[0]
    held, accum = scratch[:pairs], scratch[pairs:]
    reach = tiles.shape[1] // 2
    slots = q_ref.shape[0] // BLK
    half = BLK // 2
    bias_tiles(buckets_ref, rel_ref[0], tiles)
    v_turned[...] = jnp.transpose(v_ref[...])
    cols = [slice(p * BLK, (p + 1) * BLK) for p in range(pairs)]
    for slot in range(slots):
        block = lead_ref[slot]
        first = low_ref[slot]
        last = high_ref[slot]
        base = pl.multiple_of(block * BLK, BLK)
        own = slice(slot * BLK, (slot + 1) * BLK)
        bar = barred[pl.ds(base, BLK), :]
        bar = jnp.concatenate([bar, bar], axis=0)
        q_full = [jnp.concatenate([two_heads(q_ref[own, c]), bar], axis=1) for c in cols]

        def score(kb, best):
            rows = pl.ds(pl.multiple_of(kb * BLK, BLK), BLK)
            mark = known[rows, :]
            values = [
                lax.dot_general(
                    jnp.concatenate([k_ref[rows, c], mark], axis=1),
                    q_full[p],
                    NT,
                    preferred_element_type=f32,
                )
                + tiles[p, kb - block + reach]
                for p, c in enumerate(cols)
            ]
            for p in range(pairs):
                held[p][kb - first] = values[p]
            return tuple(jnp.maximum(best[p], fold_rows(values[p], jnp.max)) for p in range(pairs))

        lowest = jnp.full((8, 2 * BLK), -3e38, f32)
        best = lax.fori_loop(first, last, score, (lowest,) * pairs)
        best = [jnp.max(value, axis=0, keepdims=True) for value in best]
        for p in range(pairs):
            accum[p][...] = jnp.zeros((BLK, 2 * BLK), f32)

        def gather(kb, total):
            keys = pl.ds(pl.multiple_of(kb * BLK, BLK), BLK)
            weights = [jnp.exp(held[p][kb - first] - best[p]) for p in range(pairs)]
            products = [
                jnp.dot(v_turned[c, keys], weights[p].astype(bf16), preferred_element_type=f32)
                for p, c in enumerate(cols)
            ]
            for p in range(pairs):
                accum[p][...] += products[p]
            return tuple(total[p] + fold_rows(weights[p], jnp.sum) for p in range(pairs))

        none = jnp.zeros((8, 2 * BLK), f32)
        total = lax.fori_loop(first, last, gather, (none,) * pairs)
        for p in range(pairs):
            row_total = jnp.sum(total[p], axis=0, keepdims=True)
            value = accum[p][...] / row_total
            both = jnp.concatenate([value[:half, :BLK], value[half:, BLK:]], axis=0)
            both = jnp.transpose(both)
            out_ref[own, cols[p]] = both
            low_out_ref[own, cols[p]] = both.astype(bf16)
            log_ref[0, slot, p : p + 1, :] = best[p] + jnp.log(row_total)


def attend(lead, low, high, q, k, v, known, barred, buckets, rel):
    rows, width = q.shape
    keys = k.shape[0]
    groups = rel.shape[0]
    pairs = rel.shape[1] // 2
    blocks = keys // BLK
    slots = rows // BLK
    count = 2 * (blocks // 2) + 1
    smem = pl.BlockSpec(memory_space=pltpu.SMEM)

    def cols(size):
        return pl.BlockSpec((size, pairs * BLK), lambda i: (0, i))

    def whole(array):
        return pl.BlockSpec(array.shape, lambda i: (0,) * array.ndim)

    return pl.pallas_call(
        attend_kernel,
        grid=(groups,),
        out_shape=(
            jax.ShapeDtypeStruct((rows, width), f32),
            jax.ShapeDtypeStruct((rows, width), bf16),
            jax.ShapeDtypeStruct((groups, slots, pairs, 2 * BLK), f32),
            jax.ShapeDtypeStruct((groups * pairs, count, BLK, 2 * BLK), f32),
        ),
        in_specs=[
            smem,
            smem,
            smem,
            cols(rows),
            cols(keys),
            cols(keys),
            whole(known),
            whole(barred),
            whole(buckets),
            pl.BlockSpec((1,) + rel.shape[1:], lambda i: (i, 0, 0)),
        ],
        out_specs=(
            cols(rows),
            cols(rows),
            pl.BlockSpec((1, slots, pairs, 2 * BLK), lambda i: (i, 0, 0, 0)),
            pl.BlockSpec((pairs, count, BLK, 2 * BLK), lambda i: (i, 0, 0, 0)),
        ),
        scratch_shapes=[pltpu.VMEM((pairs * BLK, keys), bf16)]
        + [pltpu.VMEM((blocks, BLK, 2 * BLK), f32)] * pairs
        + [pltpu.VMEM((BLK, 2 * BLK), f32)] * pairs,
        compiler_params=pltpu.CompilerParams(vmem_limit_bytes=VMEM_CAP),
        cost_estimate=LIGHT,
        name="attend",
    )(lead, low, high, q, k, v, known, barred, buckets, rel)


def attend_back_kernel(
    lead_ref,
    low_ref,
    high_ref,
    q_ref,
    k_ref,
    v_ref,
    g_ref,
    out_ref,
    log_ref,
    tiles,
    known,
    barred,
    buckets_ref,
    dq_ref,
    dk_ref,
    dv_ref,
    dbias_ref,
    k_turned,
    *scratch,
):
    pairs, count = tiles.shape[:2]
    dk_acc, dv_acc, d_tiles, dq_acc = (scratch[n * pairs : (n + 1) * pairs] for n in range(4))
    reach = count // 2
    slots = q_ref.shape[0] // BLK
    half = BLK // 2
    k_turned[...] = jnp.transpose(k_ref[...])
    for p in range(pairs):
        dk_acc[p][...] = jnp.zeros(dk_acc[p].shape, f32)
        dv_acc[p][...] = jnp.zeros(dv_acc[p].shape, f32)
        d_tiles[p][...] = jnp.zeros(d_tiles[p].shape, f32)
    sub = lax.broadcasted_iota(jnp.int32, (8, BLK), 0)
    chooser = jnp.where((lane_iota(8) // half) == sub, 1.0, 0.0).astype(bf16)
    cols = [slice(p * BLK, (p + 1) * BLK) for p in range(pairs)]
    for slot in range(slots):
        block = lead_ref[slot]
        first = low_ref[slot]
        last = high_ref[slot]
        base = pl.multiple_of(block * BLK, BLK)
        own = slice(slot * BLK, (slot + 1) * BLK)
        bar = barred[pl.ds(base, BLK), :]
        bar = jnp.concatenate([bar, bar], axis=0)
        q_two = [two_heads(q_ref[own, c]) for c in cols]
        q_full = [jnp.concatenate([value, bar], axis=1) for value in q_two]
        g_two = [two_heads(g_ref[own, c]) for c in cols]
        deltas = []
        for p, c in enumerate(cols):
            product = g_ref[own, c].astype(f32) * out_ref[own, c]
            high_part = product.astype(bf16)
            low_part = (product - high_part.astype(f32)).astype(bf16)
            delta = lax.dot_general(
                chooser, high_part, NT, preferred_element_type=f32
            ) + lax.dot_general(chooser, low_part, NT, preferred_element_type=f32)
            deltas.append(jnp.concatenate([delta[0:1, :], delta[1:2, :]], axis=1))
            dq_acc[p][...] = jnp.zeros((BLK, 2 * BLK), f32)
        logs = [log_ref[0, slot, p : p + 1, :] for p in range(pairs)]

        def step(kb, carry):
            rows = pl.ds(pl.multiple_of(kb * BLK, BLK), BLK)
            at = kb - block + reach
            mark = known[rows, :]
            values = [
                lax.dot_general(
                    jnp.concatenate([k_ref[rows, c], mark], axis=1),
                    q_full[p],
                    NT,
                    preferred_element_type=f32,
                )
                for p, c in enumerate(cols)
            ]
            d_probs = [
                lax.dot_general(v_ref[rows, c], g_two[p], NT, preferred_element_type=f32)
                for p, c in enumerate(cols)
            ]
            probs = [jnp.exp(values[p] + (tiles[p, at] - logs[p])) for p in range(pairs)]
            d_scores = [probs[p] * (d_probs[p] - deltas[p]) for p in range(pairs)]
            lows = [value.astype(bf16) for value in d_scores]
            dvs = [
                jnp.dot(probs[p].astype(bf16), g_two[p], preferred_element_type=f32)
                for p in range(pairs)
            ]
            dks = [jnp.dot(lows[p], q_two[p], preferred_element_type=f32) for p in range(pairs)]
            dqs = [
                jnp.dot(k_turned[c, rows], lows[p], preferred_element_type=f32)
                for p, c in enumerate(cols)
            ]
            for p in range(pairs):
                d_tiles[p][at] += d_scores[p]
                dv_acc[p][rows, :] += dvs[p]
                dk_acc[p][rows, :] += dks[p]
                dq_acc[p][...] += dqs[p]
            return carry

        lax.fori_loop(first, last, step, 0)
        for p in range(pairs):
            dq = dq_acc[p][...]
            both = jnp.concatenate([dq[:half, :BLK], dq[half:, BLK:]], axis=0)
            dq_ref[own, cols[p]] = jnp.transpose(both).astype(bf16)
    for p in range(pairs):
        dk_ref[:, cols[p]] = dk_acc[p][...].astype(bf16)
        dv_ref[:, cols[p]] = dv_acc[p][...].astype(bf16)
    levels = dbias_ref.shape[2]
    level = lax.broadcasted_iota(jnp.int32, (levels, 2 * BLK), 0)
    pad = jnp.zeros((BLK, BLK), f32)
    mirror = (
        lax.broadcasted_iota(jnp.int32, (BLK, BLK), 0)
        + lax.broadcasted_iota(jnp.int32, (BLK, BLK), 1)
        == BLK - 1
    ).astype(bf16)
    total = jnp.zeros((8, levels), f32)
    for n in range(count):
        onehot = (level == bucket_row(buckets_ref, n, reach)).astype(f32)
        sums = []
        for p in range(pairs):
            flipped = jnp.dot(mirror, d_tiles[p][n].astype(bf16), preferred_element_type=f32)
            for head in range(2):
                wide = jnp.concatenate([flipped[:, head * BLK : (head + 1) * BLK], pad], axis=1)
                rolled = pltpu.roll(wide, 0, 1, stride=1, stride_axis=0)
                sums.append(jnp.sum(rolled, axis=0, keepdims=True))
        rest = jnp.zeros((8 - 2 * pairs, 2 * BLK), f32)
        total = total + lax.dot_general(
            jnp.concatenate(sums + [rest], axis=0),
            onehot,
            NT,
            precision=HIGH,
            preferred_element_type=f32,
        )
    dbias_ref[0] = total


def attend_back(
    group, levels, lead, low, high, q, k, v, g, out, log, tiles, known, barred, buckets
):
    rows = q.shape[0]
    keys = k.shape[0]
    slots, pairs = log.shape[1:3]
    count = tiles.shape[1]
    width = pairs * BLK
    smem = pl.BlockSpec(memory_space=pltpu.SMEM)

    def cols(size):
        return pl.BlockSpec((size, width), lambda i: (0, group))

    def whole(array):
        return pl.BlockSpec(array.shape, lambda i: (0,) * array.ndim)

    def fresh(*shape):
        return pl.BlockSpec(shape, lambda i: (0,) * len(shape))

    return pl.pallas_call(
        attend_back_kernel,
        grid=(1,),
        out_shape=(
            jax.ShapeDtypeStruct((rows, width), bf16),
            jax.ShapeDtypeStruct((keys, width), bf16),
            jax.ShapeDtypeStruct((keys, width), bf16),
            jax.ShapeDtypeStruct((1, 8, levels), f32),
        ),
        in_specs=[
            smem,
            smem,
            smem,
            cols(rows),
            cols(keys),
            cols(keys),
            cols(rows),
            cols(rows),
            pl.BlockSpec((1, slots, pairs, 2 * BLK), lambda i: (group, 0, 0, 0)),
            pl.BlockSpec((pairs, count, BLK, 2 * BLK), lambda i: (group, 0, 0, 0)),
            whole(known),
            whole(barred),
            whole(buckets),
        ],
        out_specs=(
            fresh(rows, width),
            fresh(keys, width),
            fresh(keys, width),
            fresh(1, 8, levels),
        ),
        scratch_shapes=[pltpu.VMEM((width, keys), bf16)]
        + [pltpu.VMEM((keys, BLK), f32)] * (2 * pairs)
        + [pltpu.VMEM((count, BLK, 2 * BLK), f32)] * pairs
        + [pltpu.VMEM((BLK, 2 * BLK), f32)] * pairs,
        compiler_params=pltpu.CompilerParams(vmem_limit_bytes=VMEM_CAP),
        cost_estimate=LIGHT,
        name="attend_back",
    )(lead, low, high, q, k, v, g, out, log, tiles, known, barred, buckets)


GROUPS = 2


def attention_tables(starts, ends, rel_bucket, rel_bias, lead):
    blocks = starts.shape[0]
    mine = (lead[:, None] == jnp.arange(blocks)[None, :]).astype(jnp.int32)
    own_start = jnp.sum(mine * starts[None, :], axis=1)
    own_end = jnp.sum(mine * ends[None, :], axis=1)
    low = jnp.sum((ends[None, :] < own_start[:, None]).astype(jnp.int32), axis=1)
    high = jnp.sum((starts[None, :] <= own_end[:, None]).astype(jnp.int32), axis=1)
    buckets = jnp.pad(jnp.flip(rel_bucket), (0, 1)).reshape(2 * blocks, BLK)
    levels, heads = rel_bias.shape
    rel = jnp.transpose(rel_bias).reshape(GROUPS, heads // GROUPS, levels)
    return low, high, buckets, rel


def pack_kernel(*refs):
    outs = [ref for ref in refs if ref.dtype == bf16]
    masters = [ref for ref in refs if ref.dtype == f32]
    at = 0
    for out in outs:
        col = 0
        while col < out.shape[1]:
            wide = masters[at].shape[1]
            out[:, col : col + wide] = masters[at][...].astype(bf16)
            col += wide
            at += 1


def pack(groups):
    steps = 1
    while all(group[0].shape[0] % (32 * steps) == 0 for group in groups) and steps < 4:
        steps *= 2

    def spec(array):
        return pl.BlockSpec((array.shape[0] // steps, array.shape[1]), lambda i: (i, 0))

    outs = tuple(
        jax.ShapeDtypeStruct((group[0].shape[0], sum(a.shape[1] for a in group)), bf16)
        for group in groups
    )
    arrays = [array for group in groups for array in group]
    return pl.pallas_call(
        pack_kernel,
        grid=(steps,),
        out_shape=outs,
        in_specs=[spec(array) for array in arrays],
        out_specs=tuple(spec(out) for out in outs),
        compiler_params=pltpu.CompilerParams(vmem_limit_bytes=VMEM_CAP),
        cost_estimate=LIGHT,
        name="pack",
    )(*arrays)


TN = (((0,), (0,)), ((), ()))


def fetch_rows(index, parts, whole, sems):
    rows = parts[0].shape[0]
    copies = []
    for j, part in enumerate(parts):
        start = pl.multiple_of((index ^ j) * rows, rows)
        copies.append(pltpu.make_async_copy(part, whole.at[pl.ds(start, rows), :], sems.at[j]))
    return copies


def project_kernel(count, index_ref, *refs):
    parts = refs[:count]
    norm_ref, own_ref, q_ref, k_ref, v_ref, whole_ref, whole, sems, done = refs[count:]
    width = norm_ref.shape[1]
    copies = fetch_rows(index_ref[0], parts, whole, sems)
    for copy in copies:
        copy.start()
    for copy in copies:
        copy.wait()
    keep = pltpu.make_async_copy(whole, whole_ref, done)
    keep.start()
    for out, rows, col in ((q_ref, own_ref, 0), (k_ref, norm_ref, 1), (v_ref, norm_ref, 2)):
        weight = whole[:, col * width : (col + 1) * width]
        for block in range(rows.shape[0] // 256):
            part = slice(block * 256, (block + 1) * 256)
            out[part, :] = jnp.dot(rows[part, :], weight, preferred_element_type=f32).astype(bf16)
    keep.wait()


def project(index, parts, norm, own):
    count = len(parts)
    width = norm.shape[1]
    full = (parts[0].shape[0] * count, parts[0].shape[1])
    vmem = pl.BlockSpec(memory_space=pltpu.VMEM)
    anywhere = pl.BlockSpec(memory_space=pl.ANY)
    return pl.pallas_call(
        functools.partial(project_kernel, count),
        out_shape=(
            jax.ShapeDtypeStruct(own.shape, bf16),
            jax.ShapeDtypeStruct(norm.shape, bf16),
            jax.ShapeDtypeStruct(norm.shape, bf16),
            jax.ShapeDtypeStruct(full, bf16),
        ),
        in_specs=[pl.BlockSpec(memory_space=pltpu.SMEM)] + [anywhere] * count + [vmem] * 2,
        out_specs=(vmem, vmem, vmem, anywhere),
        scratch_shapes=[
            pltpu.VMEM(full, bf16),
            pltpu.SemaphoreType.DMA((count,)),
            pltpu.SemaphoreType.DMA,
        ],
        compiler_params=pltpu.CompilerParams(vmem_limit_bytes=VMEM_CAP),
        cost_estimate=LIGHT,
        name="project",
    )(index, *parts, norm, own)


def project_back_kernel(count, halves, index_ref, lead_ref, norm_ref, own_ref, whole_ref, *refs):
    keep_ref, send_ref, dnorm_ref, grad_ref, sems = refs[3 * halves :]
    width = norm_ref.shape[1]
    part_width = width // halves
    for half in range(halves):
        for col in range(3):
            rows = own_ref if col == 0 else norm_ref
            here = slice(col * width + half * part_width, col * width + (half + 1) * part_width)
            grad_ref[:, here] = lax.dot_general(
                rows[...], refs[3 * half + col][...], TN, preferred_element_type=f32
            ).astype(bf16)
    for block in range(norm_ref.shape[0] // 256):
        part = slice(block * 256, (block + 1) * 256)
        total = None
        for half in range(halves):
            for col in (1, 2):
                here = slice(col * width + half * part_width, col * width + (half + 1) * part_width)
                term = lax.dot_general(
                    refs[3 * half + col][part, :],
                    whole_ref[:, here],
                    NT,
                    preferred_element_type=f32,
                )
                total = term if total is None else total + term
        dnorm_ref[part, :] = total
    for slot in range(own_ref.shape[0] // BLK):
        rows = pl.ds(pl.multiple_of(lead_ref[slot] * BLK, BLK), BLK)
        total = dnorm_ref[rows, :]
        for half in range(halves):
            total = total + lax.dot_general(
                refs[3 * half][slot * BLK : (slot + 1) * BLK, :],
                whole_ref[:, half * part_width : (half + 1) * part_width],
                NT,
                preferred_element_type=f32,
            )
        dnorm_ref[rows, :] = total
    scatter_rows(
        index_ref[0], count, ((grad_ref, 0, grad_ref.shape[1], keep_ref, send_ref),), sems
    )


def project_back(index, count, lead, norm, own, whole, halves):
    vmem = pl.BlockSpec(memory_space=pltpu.VMEM)
    anywhere = pl.BlockSpec(memory_space=pl.ANY)
    smem = pl.BlockSpec(memory_space=pltpu.SMEM)
    grads = [grad for half in halves for grad in half]
    part = jax.ShapeDtypeStruct((count // 2, whole.shape[0] // count, whole.shape[1]), bf16)
    return pl.pallas_call(
        functools.partial(project_back_kernel, count, len(halves)),
        out_shape=(part, part, jax.ShapeDtypeStruct(norm.shape, f32)),
        in_specs=[smem] * 2 + [vmem] * (3 + len(grads)),
        out_specs=(anywhere, anywhere, vmem),
        scratch_shapes=[pltpu.VMEM(whole.shape, bf16), pltpu.SemaphoreType.DMA((count,))],
        compiler_params=pltpu.CompilerParams(vmem_limit_bytes=VMEM_CAP),
        cost_estimate=LIGHT,
        name="project_back",
    )(index, lead, norm, own, whole, *grads)


ROOT = 0.7978845608028654
CUBE = 0.044715


def feed_kernel(count, index_ref, *refs):
    upper = refs[:count]
    lower = refs[count : 2 * count]
    blocks = refs[2 * count].shape[0] // BLK
    cot_blocks = refs[2 * count + 3 : 2 * count + 3 + blocks]
    refs = refs[: 2 * count + 3] + refs[2 * count + 3 + blocks :]
    (
        tok_ref,
        att_ref,
        gain_ref,
        out_ref,
        d_att_ref,
        d_resid_ref,
        gain_grad_ref,
        keep_ref,
        send_ref,
        ogu,
        down,
        store,
        cot_ref,
        resid,
        norm,
        d_norm,
        total,
        hid,
        d_gate,
        d_up,
        sems_upper,
        sems_lower,
        sems_store,
    ) = refs[2 * count :]
    rows, width = tok_ref.shape
    hidden = down.shape[0]
    copies_upper = fetch_rows(index_ref[0], upper, ogu, sems_upper)
    copies_lower = fetch_rows(index_ref[0], lower, down, sems_lower)
    for copy in copies_upper + copies_lower:
        copy.start()
    for n, block in enumerate(cot_blocks):
        cot_ref[n * BLK : (n + 1) * BLK, :] = block[...]
    for copy in copies_upper:
        copy.wait()
    gain = gain_ref[...]
    row_step = 128
    tile = 512
    for block in range(rows // row_step):
        part = slice(block * row_step, (block + 1) * row_step)
        value = tok_ref[part, :] + jnp.dot(
            att_ref[part, :], ogu[:, :width], preferred_element_type=f32
        )
        resid[part, :] = value
        scale = lax.rsqrt(jnp.mean(value * value, axis=1, keepdims=True) + 1e-06)
        norm[part, :] = (value * scale * gain).astype(bf16)
    for copy in copies_lower:
        copy.wait()
    for n in range(hidden // tile):
        here = slice(n * tile, (n + 1) * tile)
        gate_cols = slice(width + n * tile, width + (n + 1) * tile)
        up_cols = slice(width + hidden + n * tile, width + hidden + (n + 1) * tile)
        for block in range(rows // row_step):
            part = slice(block * row_step, (block + 1) * row_step)
            gate_pre = jnp.dot(norm[part, :], ogu[:, gate_cols], preferred_element_type=f32)
            up_pre = jnp.dot(norm[part, :], ogu[:, up_cols], preferred_element_type=f32)
            d_hidden = lax.dot_general(
                cot_ref[part, :], down[here, :], NT, preferred_element_type=f32
            )
            square = gate_pre * gate_pre
            bent = jnp.tanh(ROOT * gate_pre * (1.0 + CUBE * square))
            half = 0.5 + 0.5 * bent
            gelu = gate_pre * half
            slope = half + (0.5 * ROOT) * gate_pre * (1.0 - bent * bent) * (
                1.0 + (3.0 * CUBE) * square
            )
            low = (gelu * up_pre).astype(bf16)
            d_gate_low = (d_hidden * up_pre * slope).astype(bf16)
            d_up_low = (d_hidden * gelu).astype(bf16)
            hid[part, :] = low
            d_gate[part, :] = d_gate_low
            d_up[part, :] = d_up_low
            add = jnp.dot(low, down[here, :], preferred_element_type=f32)
            back = lax.dot_general(
                d_gate_low, ogu[:, gate_cols], NT, preferred_element_type=f32
            ) + lax.dot_general(d_up_low, ogu[:, up_cols], NT, preferred_element_type=f32)
            if n == 0:
                total[part, :] = resid[part, :] + add
                d_norm[part, :] = back
            else:
                total[part, :] = total[part, :] + add
                d_norm[part, :] = d_norm[part, :] + back
        store[:, gate_cols] = lax.dot_general(
            norm[...], d_gate[...], TN, preferred_element_type=f32
        ).astype(bf16)
        store[:, up_cols] = lax.dot_general(
            norm[...], d_up[...], TN, preferred_element_type=f32
        ).astype(bf16)
        part = lax.dot_general(
            hid[...], cot_ref[...], TN, preferred_element_type=f32
        ).astype(bf16)
        for low_row, low_col, row, size in down_pieces(width // count, hidden // count, width):
            for device in range(count):
                source = device * (hidden // count) + low_row
                if n * tile <= source < (n + 1) * tile:
                    source = source - n * tile
                    target = device * (width // count) + row
                    col = width + 2 * hidden + low_col[1]
                    store[target : target + size, col : col + LANE] = part[
                        source : source + size, low_col[0] : low_col[0] + LANE
                    ]
    gain_sum = jnp.zeros((1, width), f32)
    for block in range(rows // row_step):
        part = slice(block * row_step, (block + 1) * row_step)
        out_ref[part, :] = total[part, :].astype(bf16)
        value = resid[part, :]
        grad = d_norm[part, :]
        scale = lax.rsqrt(jnp.mean(value * value, axis=1, keepdims=True) + 1e-06)
        scaled = grad * gain
        inner = jnp.mean(value * scaled, axis=1, keepdims=True)
        d_value = (
            cot_ref[part, :].astype(f32)
            + scale * scaled
            - value * (scale * scale * scale * inner)
        )
        gain_sum = gain_sum + jnp.sum(grad * value * scale, axis=0, keepdims=True)
        d_resid_ref[part, :] = d_value
        d_low = d_value.astype(bf16)
        norm[part, :] = d_low
        d_att_ref[part, :] = lax.dot_general(
            d_low, ogu[:, :width], NT, preferred_element_type=f32
        ).astype(bf16)
    gain_grad_ref[...] = gain_sum
    store[:, :width] = lax.dot_general(
        att_ref[...], norm[...], TN, preferred_element_type=f32
    ).astype(bf16)
    half = store.shape[1] // 2
    scatter_rows(
        index_ref[0],
        count,
        (
            (store, 0, half, keep_ref.at[0], send_ref.at[0]),
            (store, half, half, keep_ref.at[1], send_ref.at[1]),
        ),
        sems_store,
    )


def scatter_rows(index, count, jobs, sems):
    rows = jobs[0][0].shape[0] // count
    waits = []
    for n, (source, first, wide, keep, send) in enumerate(jobs):
        for device in range(count):
            other = index ^ device
            part = source.at[device * rows : (device + 1) * rows, first : first + wide]
            sem = sems.at[n * count + device]

            @pl.when(other % 2 == 0)
            def _():
                pltpu.make_async_copy(part, keep.at[other // 2], sem).start()

            @pl.when(other % 2 == 1)
            def _():
                pltpu.make_async_copy(part, send.at[other // 2], sem).start()

            waits.append(pltpu.make_async_copy(part, keep.at[0], sem))
    for wait in waits:
        wait.wait()


def down_pieces(rows, tall, width):
    size = 16
    while tall % (2 * size) == 0 and rows % (2 * size) == 0:
        size *= 2
    pieces = []
    for q in range(tall * (width // LANE) // size):
        there = (q % (tall // size)) * size
        here = (q % (rows // size)) * size
        pieces.append((there, (q // (tall // size) * LANE, q // (rows // size) * LANE), here, size))
    return pieces


def by_parity(index, mine, other, put):
    rows = mine.shape[1]
    for parity in range(2):

        @pl.when(index % 2 == parity)
        def _():
            for k in range(mine.shape[0]):
                put((2 * k + parity) * rows, mine, k)
                put((2 * k + 1 - parity) * rows, other, k)


def unpack_three_kernel(index_ref, mine, other, *outs):
    rows, width = mine.shape[1], outs[0].shape[1]

    def put(row, array, k):
        for n in range(3):
            outs[n][row : row + rows, :] = array[k, :, n * width : (n + 1) * width].astype(f32)

    by_parity(index_ref[0], mine, other, put)


def unpack_joined_kernel(hidden, index_ref, mine, other, *refs):
    outs, spread = refs[:4], refs[4]
    rows, width = mine.shape[1], outs[0].shape[1]
    spans = ((0, width), (width, width + hidden), (width + hidden, width + 2 * hidden))
    base = width + 2 * hidden

    def put(row, array, k):
        for out, (first, last) in zip(outs[:3], spans):
            out[row : row + rows, :] = array[k, :, first:last].astype(f32)
        spread[row : row + rows, :] = array[k, :, base:].astype(f32)

    by_parity(index_ref[0], mine, other, put)
    tall = outs[3].shape[0]
    for there, (col_there, col_here), here, size in down_pieces(spread.shape[0], tall, width):
        outs[3][there : there + size, col_there : col_there + LANE] = spread[
            here : here + size, col_here : col_here + LANE
        ]


def unpack(kernel, index, mine, other, shapes, scratch, name):
    vmem = pl.BlockSpec(memory_space=pltpu.VMEM)
    return pl.pallas_call(
        kernel,
        out_shape=tuple(jax.ShapeDtypeStruct(shape, f32) for shape in shapes),
        in_specs=[pl.BlockSpec(memory_space=pltpu.SMEM), vmem, vmem],
        scratch_shapes=scratch,
        compiler_params=pltpu.CompilerParams(vmem_limit_bytes=VMEM_CAP),
        cost_estimate=LIGHT,
        name=name,
    )(index, mine, other)


def feed(index, upper, lower, tokens, attended, cotangent, gain):
    count = len(upper)
    rows, width = tokens.shape
    full_upper = (upper[0].shape[0] * count, upper[0].shape[1])
    full_lower = (lower[0].shape[0] * count, width)
    hidden = full_lower[0]
    columns = width + 3 * hidden
    vmem = pl.BlockSpec(memory_space=pltpu.VMEM)
    anywhere = pl.BlockSpec(memory_space=pl.ANY)
    tile = 512
    return pl.pallas_call(
        functools.partial(feed_kernel, count),
        out_shape=(
            jax.ShapeDtypeStruct((rows, width), bf16),
            jax.ShapeDtypeStruct((rows, width), bf16),
            jax.ShapeDtypeStruct((rows, width), f32),
            jax.ShapeDtypeStruct((1, width), f32),
            *[jax.ShapeDtypeStruct((2, count // 2, width // count, columns // 2), bf16)] * 2,
        ),
        in_specs=[pl.BlockSpec(memory_space=pltpu.SMEM)]
        + [anywhere] * (2 * count)
        + [vmem] * (3 + len(cotangent)),
        out_specs=(vmem,) * 4 + (anywhere,) * 2,
        scratch_shapes=[
            pltpu.VMEM(full_upper, bf16),
            pltpu.VMEM(full_lower, bf16),
            pltpu.VMEM((width, columns), bf16),
            pltpu.VMEM((rows, width), bf16),
            pltpu.VMEM((rows, width), f32),
            pltpu.VMEM((rows, width), bf16),
            pltpu.VMEM((rows, width), f32),
            pltpu.VMEM((rows, width), f32),
            pltpu.VMEM((rows, tile), bf16),
            pltpu.VMEM((rows, tile), bf16),
            pltpu.VMEM((rows, tile), bf16),
            pltpu.SemaphoreType.DMA((count,)),
            pltpu.SemaphoreType.DMA((count,)),
            pltpu.SemaphoreType.DMA((2 * count,)),
        ],
        compiler_params=pltpu.CompilerParams(vmem_limit_bytes=VMEM_CAP),
        cost_estimate=LIGHT,
        name="feed",
    )(index, *upper, *lower, tokens, attended, gain.reshape(1, width), *cotangent)


def bits_of(count):
    bits = count.bit_length() - 1
    assert 1 << bits == count
    return bits


def swap(value, axis, bit):
    count = lax.axis_size(axis)
    return lax.ppermute(value, axis, [(i, i ^ (1 << bit)) for i in range(count)])


def ordered(mine, other, index, bit, axis=0):
    upper = ((index >> bit) & 1) == 1
    return jnp.concatenate(
        [jnp.where(upper, other, mine), jnp.where(upper, mine, other)], axis=axis
    )


def gather_small(value, axis):
    index = lax.axis_index(axis)
    value = value[None]
    for bit in range(bits_of(lax.axis_size(axis))):
        value = ordered(value, swap(value, axis, bit), index, bit)
    return value


def first_swap(shard, axis):
    bit = bits_of(lax.axis_size(axis)) - 1
    return [(0, shard), (1 << bit, swap(shard, axis, bit))]


def other_swaps(parts, axis):
    for bit in reversed(range(bits_of(lax.axis_size(axis)) - 1)):
        parts = parts + [(j | (1 << bit), swap(part, axis, bit)) for j, part in parts]
    return [part for _, part in sorted(parts, key=lambda pair: pair[0])]


def after(anchor, part):
    j, array = part
    anchor, array = lax.optimization_barrier((anchor, array))
    return anchor, (j, array)


def add_low(left, right):
    return (left.astype(f32) + right.astype(f32)).astype(bf16)


def piece(value, index, dim=0):
    return lax.dynamic_index_in_dim(value, index, dim, keepdims=False)


def scatter_step(value, axis, bit, dim):
    own = (lax.axis_index(axis) >> bit) & 1
    other = swap(piece(value, 1 - own, dim), axis, bit)
    return add_low(piece(value, own, dim), other)


def rest_sum(value, axis):
    count = lax.axis_size(axis)
    index = lax.axis_index(axis)
    mine = index // 2
    total = piece(value, mine).astype(f32)
    for j in range(1, count // 2):
        pairs = [(i, ((i // 2) ^ j) * 2 + i % 2) for i in range(count)]
        total = total + lax.ppermute(piece(value, mine ^ j), axis, pairs).astype(f32)
    return total.astype(bf16)


def rest_gather(value, axis):
    count = lax.axis_size(axis)
    index = lax.axis_index(axis)
    whole = jnp.zeros((count // 2,) + value.shape, value.dtype)
    for j in range(count // 2):
        part = value
        if j:
            pairs = [(i, ((i // 2) ^ j) * 2 + i % 2) for i in range(count)]
            part = lax.ppermute(value, axis, pairs)
        whole = lax.dynamic_update_index_in_dim(whole, part, (index // 2) ^ j, 0)
    return whole


def fsdp_step(keep, send, bit):
    return add_low(keep, swap(send, "fsdp", bit))


def split_bit(value):
    value = value.reshape((value.shape[0] // 2, 2) + value.shape[1:])
    return value[:, 0], value[:, 1]


def parity_step(value, dim):
    count = lax.axis_size("ctx")
    shape = value.shape
    value = value.reshape(shape[:dim] + (count // 2, 2, shape[dim] // count) + shape[dim + 1 :])
    return scatter_step(value, "ctx", 0, dim + 1)


def rest_of_chain(total):
    total = yield rest_sum(total, "ctx")
    total = yield rest_gather(total, "ctx")
    yield (total, swap(total, "ctx", 0))


def single_chain(keep, send):
    bits = bits_of(lax.axis_size("fsdp"))
    total = yield fsdp_step(keep, send, 0)
    for bit in range(1, bits):
        keep, send = split_bit(total)
        total = yield fsdp_step(keep, send, bit)
    total = yield parity_step(total[0], 0)
    yield from rest_of_chain(total)


def double_chain(keep, send):
    bits = bits_of(lax.axis_size("fsdp"))
    other = swap(send, "fsdp", 0)
    left, right = yield (add_low(keep[0], other[0]), add_low(keep[1], other[1]))
    for bit in range(bits):
        if bit < bits - 1:
            left = fsdp_step(*split_bit(left), bit + 1)
        else:
            left = parity_step(left[0], 0)
        if bit == 0:
            right = parity_step(right, 1)
        else:
            right = fsdp_step(*split_bit(right), bit)
        left, right = yield (left, right)
    joined = jnp.concatenate([left, right[0]], axis=-1)
    yield from rest_of_chain(joined)


class Chain:
    def __init__(self, steps):
        self.steps = steps
        self.value = next(steps)

    def advance(self, value):
        self.value = self.steps.send(value)

    def finish(self):
        while True:
            try:
                self.advance(self.value)
            except StopIteration:
                return self.value


def gate(anchor, *chains):
    joined = lax.optimization_barrier((anchor,) + tuple(chain.value for chain in chains))
    for chain, value in zip(chains, joined[1:]):
        chain.advance(value)
    return joined[0]


def reduce_small(value, chain):
    fsdp_bits = bits_of(lax.axis_size("fsdp"))
    count = lax.axis_size("ctx")
    rows, width = value.shape
    value = value.reshape(2, count // 2, 2 * rows // (2 * count), width)
    value = gate(scatter_step(value, "fsdp", 0, 0), chain)
    value = gate(rest_sum(value, "ctx"), chain)
    value = add_low(value, swap(value, "ctx", 0))
    for bit in range(1, fsdp_bits):
        value = add_low(value, swap(value, "fsdp", bit))
    value = gate(value, chain)
    whole = rest_gather(value, "ctx")
    whole = whole.reshape((rows // 2, width))
    return ordered(whole, swap(whole, "fsdp", 0), lax.axis_index("fsdp"), 0)


def local(
    byte_ids,
    doc_ids,
    rel_bucket,
    table,
    conv_w,
    score_w,
    gain_one,
    gain_two,
    rel_bias,
    query_master,
    key_master,
    value_master,
    out_master,
    gate_master,
    up_master,
    down_master,
    out_cotangent,
):
    ctx_count = lax.axis_size("ctx")
    ctx_index = lax.axis_index("ctx")
    seq_count, byte_count = byte_ids.shape
    total_bytes = byte_count * ctx_count
    width = table.shape[1]
    vocab = table.shape[0]
    hidden_width = gate_master.shape[1]
    levels, heads = rel_bias.shape
    share = ctx_count // seq_count
    assert share * seq_count == ctx_count and byte_count == 2 * BLK
    seq = ctx_index // share
    part = ctx_index % share
    near = [seq ^ slot for slot in range(seq_count)]
    lead = jnp.stack([share * other + part for other in near]).astype(jnp.int32)
    rows = seq_count * BLK

    qkv_low, down_low, ogu_low = pack(
        [[query_master, key_master, value_master], [down_master], [out_master, gate_master, up_master]]
    )
    both = jnp.stack([byte_ids, doc_ids], axis=1)
    both = gather_small(both, "ctx")
    both, qkv_low, down_low = lax.optimization_barrier((both, qkv_low, down_low))
    qkv_parts = first_swap(qkv_low, "fsdp")
    shard = lax.axis_index("fsdp")[None]
    shards = lax.axis_size("fsdp")

    def to_owner(block, slot):
        if slot == 0:
            return block
        pairs = []
        for c in range(ctx_count):
            pairs.append((c, ((c // share) ^ slot) * share + c % share))
        return lax.ppermute(block, "ctx", pairs)

    score_row = score_w.reshape(1, width)
    gain_row = gain_one.reshape(1, width)
    seq_row = seq[None]
    tokens, norm_one, norm_own, tokens_own, conv, mix, phases, known, barred = byte_forward(
        seq_row, lead, both, table, conv_w, score_row, gain_row, total_bytes
    )
    down_parts = first_swap(down_low, "fsdp")
    blocks = [to_owner(piece(out_cotangent, near[s], 1), s) for s in range(seq_count)]
    norm_one, crossed, down_crossed, blocks, ogu_low = lax.optimization_barrier(
        (norm_one, qkv_parts[1][1], down_parts[1][1], blocks, ogu_low)
    )
    qkv_parts[1] = (qkv_parts[1][0], crossed)
    down_parts[1] = (down_parts[1][0], down_crossed)
    qkv_parts = other_swaps(qkv_parts, "fsdp")
    queries, keys, values, qkv = project(shard, qkv_parts, norm_one, norm_own)
    ogu_parts = first_swap(ogu_low, "fsdp")
    down_parts = other_swaps(down_parts, "fsdp")
    docs = piece(both[:, :, 1], seq, 1)
    low, high, buckets, rel = attention_tables(
        docs[:, 0], docs[:, 2 * BLK - 2], rel_bucket, rel_bias, lead
    )
    attended, attended_low, log_total, tiles = attend(
        lead, low, high, queries, keys, values, known, barred, buckets, rel
    )

    attended_low, ogu_parts[1] = after(attended_low, ogu_parts[1])
    output, d_attended, d_resid, grad_gain_two, *grads = feed(
        shard,
        other_swaps(ogu_parts, "fsdp"),
        down_parts,
        tokens_own,
        attended_low,
        blocks,
        gain_two,
    )
    chain = Chain(double_chain(*grads))
    d_attended = gate(d_attended, chain)

    output = output.reshape(seq_count, BLK, width)
    arrived = [to_owner(output[s], s) for s in range(seq_count)]

    halves = []
    for group in range(GROUPS):
        if group:
            d_attended, arrived = gate((d_attended, arrived), chain)
            arrived = jnp.stack(arrived)
            output = jnp.stack([piece(arrived, seq ^ s) for s in range(seq_count)], axis=1)
        *grads, d_bias = attend_back(
            group,
            levels,
            lead,
            low,
            high,
            queries,
            keys,
            values,
            d_attended,
            attended,
            log_total,
            tiles,
            known,
            barred,
            buckets,
        )
        halves.append((grads, d_bias))
        d_attended, _ = lax.optimization_barrier((d_attended, grads[0]))
    d_bias = jnp.concatenate([half[1] for half in halves], axis=0)
    norm_own, halves = gate((norm_own, [half[0] for half in halves]), chain)
    keep, send, d_norm_one = project_back(shard, shards, lead, norm_one, norm_own, qkv, halves)
    qkv_chain = Chain(single_chain(keep, send))
    d_norm_one = gate(d_norm_one, qkv_chain, chain)

    vocab_rows = -(-vocab // 16) * 16
    d_resid = d_resid.reshape(seq_count, BLK, width)
    small = byte_backward(
        lead,
        phases,
        tokens,
        d_norm_one,
        d_resid,
        conv,
        mix,
        table,
        vocab_rows,
        conv_w,
        score_row,
        gain_row,
        total_bytes,
    )
    bias_grad = jnp.transpose(d_bias[:, : heads // GROUPS].reshape(heads, levels)).reshape(1, levels * heads)
    bias_grad = jnp.pad(bias_grad, ((0, 0), (0, width - levels * heads)))
    small = jnp.concatenate([small[: vocab_rows + 6], grad_gain_two, bias_grad], axis=0)
    small = jnp.pad(small, ((0, -small.shape[0] % (8 * ctx_count)), (0, 0))).astype(bf16)
    small = gate(small, qkv_chain, chain)
    small = reduce_small(small, qkv_chain).astype(f32)
    shard_rows, tall = query_master.shape[0], down_master.shape[0]
    ctx_row = ctx_index[None]
    ffn_grads = unpack(
        functools.partial(unpack_joined_kernel, hidden_width),
        ctx_row,
        *chain.finish(),
        [(shard_rows, width)] + [(shard_rows, hidden_width)] * 2 + [(tall, width)],
        [pltpu.VMEM((shard_rows, hidden_width), f32)],
        "unpack_joined",
    )
    qkv_grads = unpack(
        unpack_three_kernel,
        ctx_row,
        *qkv_chain.finish(),
        [(shard_rows, width)] * 3,
        [],
        "unpack_three",
    )
    top = vocab_rows
    return (
        output,
        small[:vocab],
        small[top : top + 4],
        small[top + 4],
        small[top + 5],
        small[top + 6],
        small[top + 7, : levels * heads].reshape(levels, heads),
        *qkv_grads,
        *ffn_grads,
    )


def solution(mesh):
    placed = (
        P("fsdp", "ctx"),
        P("fsdp", "ctx"),
        P(),
        P(),
        P(),
        P(),
        P(),
        P(),
        P(),
        P("fsdp", None),
        P("fsdp", None),
        P("fsdp", None),
        P("fsdp", None),
        P("fsdp", None),
        P("fsdp", None),
        P("fsdp", None),
        P("ctx", "fsdp", None),
    )
    return jax.shard_map(
        local,
        mesh=mesh,
        in_specs=placed,
        out_specs=(
            P("ctx", "fsdp", None),
            P(),
            P(),
            P(),
            P(),
            P(),
            P(),
            P("fsdp", None),
            P("fsdp", None),
            P("fsdp", None),
            P("fsdp", None),
            P("fsdp", None),
            P("fsdp", None),
            P("fsdp", None),
        ),
        check_vma=False,
    )
```

```python
import functools

import jax
import jax.numpy as jnp
from jax import lax
from jax.experimental import pallas as pl
from jax.experimental.pallas import tpu as pltpu
from jax.sharding import PartitionSpec as P

f32 = jnp.float32
bf16 = jnp.bfloat16
LANE = 128
BLK = 128
VMEM_CAP = 60 * 1024 * 1024
HIGH = lax.Precision.HIGHEST
NT = (((1,), (1,)), ((), ()))
NN = (((1,), (0,)), ((), ()))
LIGHT = pl.CostEstimate(flops=1, transcendentals=0, bytes_accessed=1)


STEP = 16
NORM_ROWS = 128


def lane_iota(rows):
    return lax.broadcasted_iota(jnp.int32, (rows, LANE), 1)


def block_sum(value, width, lane):
    def ahead(v, n):
        return pltpu.roll(v, LANE - n, 1)

    def behind(v, n):
        return pltpu.roll(v, n, 1)

    if width == 1:
        return value
    if width == 3:
        lead = value + ahead(value, 1) + ahead(value, 2)
        phase = lane % 3
        return jnp.where(phase == 0, lead, jnp.where(phase == 1, behind(lead, 1), behind(lead, 2)))
    pair = value + jnp.where(lane % 2 == 0, ahead(value, 1), behind(value, 1))
    if width == 2:
        return pair
    return pair + jnp.where(lane % 4 < 2, ahead(pair, 2), behind(pair, 2))


def pick(value, lane_index):
    return value[:, lane_index : lane_index + 1]


def byte_forward_kernel(
    total_bytes,
    seq_ref,
    lead_ref,
    both_ref,
    table_ref,
    conv_w_ref,
    score_ref,
    gain_ref,
    tok_ref,
    norm_ref,
    norm_own_ref,
    tok_own_ref,
    conv_ref,
    mix_ref,
    ids_ref,
    known_ref,
    barred_ref,
    hi_ref,
    lo_ref,
    emb,
    flat,
    spread,
):
    groups = conv_ref.shape[1]
    width = conv_ref.shape[2]
    tiles = width // LANE
    token_count = norm_ref.shape[0]
    vocab_pad = hi_ref.shape[0]
    row_lanes = ids_ref.shape[1]
    seq = seq_ref[0]
    vocab = table_ref.shape[0]
    whole_rows = vocab // 128 * 128
    rest = jnp.zeros((vocab_pad - whole_rows, width), f32)
    rest_row = lax.broadcasted_iota(jnp.int32, rest.shape, 0)
    for row in range(whole_rows, vocab):
        rest = jnp.where(rest_row == row - whole_rows, table_ref[row : row + 1, :], rest)
    for here, value in ((0, table_ref[0:whole_rows, :]), (whole_rows, rest)):
        high = value.astype(bf16)
        hi_ref[here : here + value.shape[0], :] = high
        lo_ref[here : here + value.shape[0], :] = (value - high.astype(f32)).astype(bf16)
    lane_f = lane_iota(BLK).astype(f32)
    chunk_bytes = both_ref.shape[3]

    def lay(kind, first):
        for block in range(both_ref.shape[0]):
            row = both_ref[block, seq, kind : kind + 1, :].astype(f32)
            for half in range(chunk_bytes // LANE):
                part = jnp.broadcast_to(row[:, half * LANE : (half + 1) * LANE], (LANE, LANE))
                start = first + block * chunk_bytes + half * LANE
                spread[start : start + LANE, :] = jnp.transpose(part)

    lay(1, 0)
    for block in range(token_count // BLK):
        docs = spread[pl.ds(block * 2 * BLK, BLK, stride=2), :]
        same = docs == lane_f
        rows = slice(block * BLK, (block + 1) * BLK)
        known_ref[rows, :] = same.astype(bf16)
        barred_ref[rows, :] = jnp.where(same | (lane_f >= 16.0), 0.0, -1e30).astype(bf16)
    lay(0, 16)
    none = jnp.full((16, LANE), -1.0, f32)
    spread[0:16, :] = none
    tail = spread.shape[0] - total_bytes - 16
    spread[total_bytes + 16 :, :] = jnp.full((tail, LANE), -1.0, f32)
    lane_g = lane_iota(groups).astype(f32)
    for r in range(15):
        here = spread[pl.ds(13 + r, row_lanes, stride=12), :]
        turned = [
            jnp.transpose(here[n * LANE : (n + 1) * LANE, :])[0:1, :]
            for n in range(row_lanes // LANE)
        ]
        ids_ref[r : r + 1, :] = jnp.concatenate(turned, axis=1)
        onehot = jnp.concatenate(
            [
                (here[0:groups, :] == lane_g + n * LANE).astype(bf16)
                for n in range(vocab_pad // LANE)
            ],
            axis=1,
        )
        emb[r] = jnp.dot(onehot, hi_ref[...], preferred_element_type=f32) + jnp.dot(
            onehot, lo_ref[...], preferred_element_type=f32
        )
    ids_ref[15:16, :] = jnp.full((1, row_lanes), -1.0, f32)
    lane = lane_iota(STEP)

    def chunk(i, masked):
        r0 = pl.multiple_of(i * STEP, STEP)
        rows = pl.ds(r0, STEP)
        sums = [jnp.zeros((STEP, LANE), f32) for _ in range(12)]
        for tile in range(tiles):
            cols = slice(tile * LANE, (tile + 1) * LANE)
            taps = [conv_w_ref[k : k + 1, cols] for k in range(4)]
            piece = [emb[r, rows, cols] for r in range(15)]
            score = score_ref[0:1, cols]
            for r in range(12):
                value = (
                    piece[r] * taps[0]
                    + piece[r + 1] * taps[1]
                    + piece[r + 2] * taps[2]
                    + piece[r + 3] * taps[3]
                )
                if masked:
                    group = r0 + lax.broadcasted_iota(jnp.int32, (STEP, LANE), 0)
                    value = jnp.where(group * 12 + r < total_bytes, value, 0.0)
                conv_ref[r, rows, cols] = value
                sums[r] = sums[r] + value * score
        packed = jnp.zeros((STEP, LANE), f32)
        for r in range(12):
            packed = jnp.where(lane == r, jnp.sum(sums[r], axis=1, keepdims=True), packed)
        logits = [block_sum(packed, b, lane) * (1.0 / b) for b in range(1, 5)]
        best = jnp.maximum(jnp.maximum(logits[0], logits[1]), jnp.maximum(logits[2], logits[3]))
        parts = [jnp.exp(value - best) for value in logits]
        total = parts[0] + parts[1] + parts[2] + parts[3]
        mix = [part / total for part in parts]
        for b in range(4):
            mix_ref[b, rows, :] = mix[b]
        half_one = mix[0] * 0.5
        pair_two = block_sum(mix[1], 2, lane) * 0.25
        single_three = mix[2] * (1.0 / 6.0)
        pair_three = block_sum(mix[2], 2, lane) * (1.0 / 6.0)
        pair_four = block_sum(mix[3], 2, lane) * 0.125
        coef_one = [pick(half_one, r) for r in range(12)]
        coef_two = [pick(pair_two, 2 * j) for j in range(6)]
        coef_four = [pick(pair_four, 2 * j) for j in range(6)]
        coef_three = []
        for j in range(6):
            if j % 3 == 1:
                coef_three.append((pick(single_three, 2 * j), pick(single_three, 2 * j + 1)))
            else:
                coef_three.append((pick(pair_three, 2 * j), None))
        for tile in range(tiles):
            cols = slice(tile * LANE, (tile + 1) * LANE)
            conv = [conv_ref[r, rows, cols] for r in range(12)]
            two = [conv[2 * j] + conv[2 * j + 1] for j in range(6)]
            three = [conv[3 * q] + conv[3 * q + 1] + conv[3 * q + 2] for q in range(4)]
            four = [two[2 * q] + two[2 * q + 1] for q in range(3)]
            for j in range(6):
                a, b = 2 * j, 2 * j + 1
                value = coef_one[a] * conv[a] + coef_one[b] * conv[b]
                value = value + coef_two[j] * two[j] + coef_four[j] * four[j // 2]
                value = value + coef_three[j][0] * three[a // 3]
                if j % 3 == 1:
                    value = value + coef_three[j][1] * three[b // 3]
                flat[tile, pl.ds(6 * r0 + j, STEP, stride=6), :] = value

    whole = (total_bytes // 12) // STEP

    def plain(i, carry):
        chunk(i, False)
        return carry

    lax.fori_loop(0, whole, plain, 0)
    for i in range(whole, groups // STEP):
        chunk(i, True)

    def norm(i, carry):
        rows = pl.ds(pl.multiple_of(i * NORM_ROWS, NORM_ROWS), NORM_ROWS)
        value = jnp.concatenate([flat[tile, rows, :] for tile in range(tiles)], axis=1)
        tok_ref[rows, :] = value
        scale = lax.rsqrt(jnp.mean(value * value, axis=1, keepdims=True) + 1e-06)
        norm_ref[rows, :] = (value * scale * gain_ref[...]).astype(bf16)
        return carry

    lax.fori_loop(0, token_count // NORM_ROWS, norm, 0)
    for slot in range(norm_own_ref.shape[0] // BLK):
        start = pl.multiple_of(lead_ref[slot] * BLK, BLK)
        norm_own_ref[slot * BLK : (slot + 1) * BLK, :] = norm_ref[pl.ds(start, BLK), :]
        tok_own_ref[slot * BLK : (slot + 1) * BLK, :] = tok_ref[pl.ds(start, BLK), :]


def byte_forward(seq, lead, both, table, conv_w, score_w, gain_one, total_bytes):
    width = conv_w.shape[1]
    token_count = total_bytes // 2
    least = -(-total_bytes // 12)
    groups = -(-least // 16) * 16
    row_lanes = -(-least // LANE) * LANE
    vocab_pad = -(-table.shape[0] // LANE) * LANE
    smem = pl.BlockSpec(memory_space=pltpu.SMEM)
    vmem = pl.BlockSpec(memory_space=pltpu.VMEM)
    return pl.pallas_call(
        functools.partial(byte_forward_kernel, total_bytes),
        out_shape=(
            jax.ShapeDtypeStruct((token_count, width), f32),
            jax.ShapeDtypeStruct((token_count, width), bf16),
            jax.ShapeDtypeStruct((lead.shape[0] * BLK, width), bf16),
            jax.ShapeDtypeStruct((lead.shape[0] * BLK, width), f32),
            jax.ShapeDtypeStruct((12, groups, width), f32),
            jax.ShapeDtypeStruct((4, groups, LANE), f32),
            jax.ShapeDtypeStruct((16, row_lanes), f32),
            jax.ShapeDtypeStruct((token_count, LANE), bf16),
            jax.ShapeDtypeStruct((token_count, LANE), bf16),
        ),
        in_specs=[smem, smem] + [vmem] * 5,
        scratch_shapes=[
            pltpu.VMEM((vocab_pad, width), bf16),
            pltpu.VMEM((vocab_pad, width), bf16),
            pltpu.VMEM((15, groups, width), f32),
            pltpu.VMEM((width // LANE, 6 * groups, LANE), f32),
            pltpu.VMEM((12 * row_lanes + 32, LANE), f32),
        ],
        compiler_params=pltpu.CompilerParams(vmem_limit_bytes=VMEM_CAP),
        cost_estimate=LIGHT,
        name="byte_forward",
    )(
        seq,
        lead,
        both,
        table,
        conv_w,
        score_w,
        gain_one,
    )


def byte_backward_kernel(
    total_bytes,
    first_ref,
    ids_ref,
    tok_ref,
    dnorm_ref,
    dres_ref,
    conv_ref,
    mix_ref,
    table_ref,
    conv_w_ref,
    score_ref,
    gain_ref,
    out_ref,
    dtok,
    dconv,
    onehot,
):
    groups = conv_ref.shape[1]
    width = conv_ref.shape[2]
    tiles = width // LANE
    token_count = dnorm_ref.shape[0]
    vocab_rows = onehot.shape[0]
    lanes = ids_ref.shape[1]
    gain = gain_ref[...]

    def norm_back(i, acc):
        rows = pl.ds(pl.multiple_of(i * NORM_ROWS, NORM_ROWS), NORM_ROWS)
        value = tok_ref[rows, :]
        grad = dnorm_ref[rows, :]
        scale = lax.rsqrt(jnp.mean(value * value, axis=1, keepdims=True) + 1e-06)
        grad_gain = grad * gain
        inner = jnp.mean(value * grad_gain, axis=1, keepdims=True)
        total = 0.5 * scale * grad_gain - value * (0.5 * scale * scale * scale * inner)
        for tile in range(tiles):
            dtok[tile, rows, :] = total[:, tile * LANE : (tile + 1) * LANE]
        product = (grad * value * scale).reshape(NORM_ROWS // 8, 8, width)
        return acc + jnp.sum(product, axis=0)

    gain_acc = lax.fori_loop(0, token_count // NORM_ROWS, norm_back, jnp.zeros((8, width), f32))
    rest = dtok.shape[1] - token_count
    dtok[:, token_count:, :] = jnp.zeros((tiles, rest, LANE), f32)
    for slot in range(dres_ref.shape[0]):
        start = pl.multiple_of(first_ref[slot] * BLK, BLK)

        def add(i, carry, slot=slot, start=start):
            r = pl.multiple_of(i * 32, 32)
            rows = pl.ds(pl.multiple_of(start + r, 32), 32)
            more = 0.5 * dres_ref[slot, pl.ds(r, 32), :]
            for tile in range(tiles):
                dtok[tile, rows, :] = (
                    dtok[tile, rows, :] + more[:, tile * LANE : (tile + 1) * LANE]
                )
            return carry

        lax.fori_loop(0, BLK // 32, add, 0)
    vocab = lax.broadcasted_iota(jnp.int32, (vocab_rows, lanes), 0).astype(f32)
    for r in range(15):
        onehot[:, r * lanes : (r + 1) * lanes] = (vocab == ids_ref[r : r + 1, :]).astype(bf16)
    for r in range(12):
        dconv[r * lanes + groups : (r + 1) * lanes, :] = jnp.zeros((lanes - groups, width), bf16)
    lane = lane_iota(8)

    def scalars(r0):
        rows = pl.ds(r0, 8)
        one = [jnp.zeros((8, LANE), f32) for _ in range(12)]
        cross = [jnp.zeros((8, LANE), f32) for _ in range(6)]
        tri = [jnp.zeros((8, LANE), f32) for _ in range(8)]
        for tile in range(tiles):
            cols = slice(tile * LANE, (tile + 1) * LANE)
            conv = [conv_ref[r, rows, cols] for r in range(12)]
            grad = [dtok[tile, pl.ds(6 * r0 + j, 8, stride=6), :] for j in range(6)]
            two = [conv[2 * j] + conv[2 * j + 1] for j in range(6)]
            three = [conv[3 * q] + conv[3 * q + 1] + conv[3 * q + 2] for q in range(4)]
            for r in range(12):
                one[r] = one[r] + conv[r] * grad[r // 2]
            slot = 0
            for j in range(6):
                cross[j] = cross[j] + two[j ^ 1] * grad[j]
                for q in sorted({(2 * j) // 3, (2 * j + 1) // 3}):
                    tri[slot] = tri[slot] + three[q] * grad[j]
                    slot += 1
        inner_one = jnp.zeros((8, LANE), f32)
        for r in range(12):
            inner_one = jnp.where(lane == r, jnp.sum(one[r], axis=1, keepdims=True), inner_one)
        inner_cross = jnp.zeros((8, LANE), f32)
        for j in range(6):
            inner_cross = jnp.where(
                lane // 2 == j, jnp.sum(cross[j], axis=1, keepdims=True), inner_cross
            )
        inner_three = jnp.zeros((8, LANE), f32)
        slot = 0
        for j in range(6):
            for q in sorted({(2 * j) // 3, (2 * j + 1) // 3}):
                here = (lane // 2 == j) & (lane // 3 == q)
                inner_three = jnp.where(
                    here, jnp.sum(tri[slot], axis=1, keepdims=True), inner_three
                )
                slot += 1
        inner_two = block_sum(inner_one, 2, lane)
        mix = [mix_ref[b, rows, :] for b in range(4)]
        d_mix = [
            inner_one,
            inner_two * 0.5,
            inner_three * (1.0 / 3.0),
            (inner_two + inner_cross) * 0.25,
        ]
        mean = mix[0] * d_mix[0] + mix[1] * d_mix[1] + mix[2] * d_mix[2] + mix[3] * d_mix[3]
        d_logit = [mix[b] * (d_mix[b] - mean) for b in range(4)]
        d_logit = [jnp.where(lane < 12, value, 0.0) for value in d_logit]
        slope = d_logit[0]
        for b in range(2, 5):
            slope = slope + block_sum(d_logit[b - 1], b, lane) * (1.0 / b)
        pair_two = block_sum(mix[1], 2, lane) * 0.5
        single_three = mix[2] * (1.0 / 3.0)
        pair_three = block_sum(mix[2], 2, lane) * (1.0 / 3.0)
        pair_four = block_sum(mix[3], 2, lane) * 0.25
        return mix[0], pair_two, single_three, pair_three, pair_four, slope

    def spread(r0, coefs, tile, masked, score_acc):
        one, pair_two, single_three, pair_three, pair_four, slope = coefs
        rows = pl.ds(r0, 8)
        cols = slice(tile * LANE, (tile + 1) * LANE)
        grad = [dtok[tile, pl.ds(6 * r0 + j, 8, stride=6), :] for j in range(6)]
        score = score_ref[0:1, cols]
        four = [
            pick(pair_four, 4 * q) * grad[2 * q] + pick(pair_four, 4 * q + 2) * grad[2 * q + 1]
            for q in range(3)
        ]
        three = []
        for q in range(4):
            a = 3 * q
            if a % 2 == 0:
                three.append(
                    pick(pair_three, a) * grad[a // 2]
                    + pick(single_three, a + 2) * grad[a // 2 + 1]
                )
            else:
                three.append(
                    pick(single_three, a) * grad[a // 2]
                    + pick(pair_three, a + 1) * grad[a // 2 + 1]
                )
        result = []
        for r in range(12):
            weight = pick(slope, r)
            own = (pick(one, r) + pick(pair_two, r)) * grad[r // 2]
            value = own + three[r // 3] + four[r // 4] + weight * score
            score_acc = score_acc + weight * conv_ref[r, rows, cols]
            if masked:
                group = r0 + lax.broadcasted_iota(jnp.int32, (8, LANE), 0)
                value = jnp.where(group * 12 + r < total_bytes, value, 0.0)
            result.append(value)
        return result, score_acc

    def chunk(i, accs, masked):
        r0 = pl.multiple_of(i * 16, 16)
        r1 = pl.multiple_of(i * 16 + 8, 8)
        low_coefs = scalars(r0)
        high_coefs = scalars(r1)
        new = []
        for tile in range(tiles):
            cols = slice(tile * LANE, (tile + 1) * LANE)
            low, acc = spread(r0, low_coefs, tile, masked, accs[tile])
            high, acc = spread(r1, high_coefs, tile, masked, acc)
            new.append(acc)
            for r in range(12):
                both = jnp.concatenate([low[r], high[r]], axis=0).astype(bf16)
                dconv[pl.ds(pl.multiple_of(r * lanes + r0, 16), 16), cols] = both
        return tuple(new)

    accs = tuple(jnp.zeros((8, LANE), f32) for _ in range(tiles))
    whole = (total_bytes // 12) // 16
    accs = lax.fori_loop(0, whole, lambda i, a: chunk(i, a, False), accs)
    for i in range(whole, groups // 16):
        accs = chunk(i, accs, True)
    tail = [jnp.zeros((1, width), f32) for _ in range(8)]
    for k in range(4):
        part = jnp.dot(
            onehot[:, k * lanes : (k + 12) * lanes], dconv[...], preferred_element_type=f32
        )
        if k == 0:
            out_ref[0:vocab_rows, :] = part * conv_w_ref[k : k + 1, :]
        else:
            out_ref[0:vocab_rows, :] = out_ref[0:vocab_rows, :] + part * conv_w_ref[k : k + 1, :]
        vocab = table_ref.shape[0]
        whole_rows = vocab // 8 * 8
        tail[k] = jnp.sum(part[:whole_rows] * table_ref[0:whole_rows, :], axis=0, keepdims=True)
        for row in range(whole_rows, vocab):
            tail[k] = tail[k] + part[row : row + 1] * table_ref[row : row + 1, :]
    tail[4] = jnp.sum(jnp.concatenate(accs, axis=1), axis=0, keepdims=True)
    tail[5] = jnp.sum(gain_acc, axis=0, keepdims=True)
    out_ref[vocab_rows:, :] = jnp.concatenate(tail, axis=0)


def byte_backward(
    first,
    ids,
    tokens,
    d_norm,
    d_resid,
    conv,
    mix,
    table,
    vocab_rows,
    conv_w,
    score_w,
    gain_one,
    total_bytes,
):
    width = conv.shape[2]
    groups = conv.shape[1]
    lanes = ids.shape[1]
    return pl.pallas_call(
        functools.partial(byte_backward_kernel, total_bytes),
        out_shape=jax.ShapeDtypeStruct((vocab_rows + 8, width), f32),
        in_specs=[pl.BlockSpec(memory_space=pltpu.SMEM)]
        + [pl.BlockSpec(memory_space=pltpu.VMEM)] * 10,
        scratch_shapes=[
            pltpu.VMEM((width // LANE, 6 * groups, LANE), f32),
            pltpu.VMEM((12 * lanes, width), bf16),
            pltpu.VMEM((vocab_rows, 15 * lanes), bf16),
        ],
        compiler_params=pltpu.CompilerParams(vmem_limit_bytes=VMEM_CAP),
        cost_estimate=LIGHT,
        name="byte_backward",
    )(
        first,
        ids,
        tokens,
        d_norm,
        d_resid,
        conv,
        mix,
        table,
        conv_w,
        score_w,
        gain_one,
    )


def head_mask(value, head):
    half = value.shape[1] // 2
    lane = lax.broadcasted_iota(jnp.int32, value.shape, 1)
    keep = lane < half if head == 0 else lane >= half
    return jnp.where(keep, value, jnp.zeros_like(value))


def two_heads(value):
    return jnp.concatenate([head_mask(value, 0), head_mask(value, 1)], axis=0)


def bucket_row(buckets_ref, n, reach):
    row = buckets_ref.shape[0] // 2 - 1 - (n - reach)
    return jnp.concatenate([buckets_ref[row : row + 1, :], buckets_ref[row + 1 : row + 2, :]], axis=1)


def bias_tiles(buckets_ref, rel, tiles):
    count = tiles.shape[1]
    levels = rel.shape[1]
    level = lax.broadcasted_iota(jnp.int32, (levels, 2 * BLK), 0)
    for n in range(count):
        onehot = (level == bucket_row(buckets_ref, n, count // 2)).astype(f32)
        values = lax.dot_general(rel, onehot, NN, precision=HIGH, preferred_element_type=f32)
        for head in range(2 * tiles.shape[0]):
            spread = jnp.broadcast_to(values[head : head + 1, :], (BLK, 2 * BLK))
            rolled = pltpu.roll(spread, BLK + 1, 1, stride=1, stride_axis=0)
            half = slice(head % 2 * BLK, head % 2 * BLK + BLK)
            tiles[head // 2, n, :, half] = rolled[:, :BLK]


def fold_rows(value, op):
    return op(value.reshape(BLK // 8, 8, value.shape[1]), axis=0)


def attend_kernel(
    lead_ref,
    low_ref,
    high_ref,
    q_ref,
    k_ref,
    v_ref,
    known,
    barred,
    buckets_ref,
    rel_ref,
    out_ref,
    low_out_ref,
    log_ref,
    tiles,
    v_turned,
    *scratch,
):
    pairs = tiles.shape[0]
    held, accum = scratch[:pairs], scratch[pairs:]
    reach = tiles.shape[1] // 2
    slots = q_ref.shape[0] // BLK
    half = BLK // 2
    bias_tiles(buckets_ref, rel_ref[0], tiles)
    v_turned[...] = jnp.transpose(v_ref[...])
    cols = [slice(p * BLK, (p + 1) * BLK) for p in range(pairs)]
    for slot in range(slots):
        block = lead_ref[slot]
        first = low_ref[slot]
        last = high_ref[slot]
        base = pl.multiple_of(block * BLK, BLK)
        own = slice(slot * BLK, (slot + 1) * BLK)
        bar = barred[pl.ds(base, BLK), :]
        bar = jnp.concatenate([bar, bar], axis=0)
        q_full = [jnp.concatenate([two_heads(q_ref[own, c]), bar], axis=1) for c in cols]

        def score(kb, best):
            rows = pl.ds(pl.multiple_of(kb * BLK, BLK), BLK)
            mark = known[rows, :]
            values = [
                lax.dot_general(
                    jnp.concatenate([k_ref[rows, c], mark], axis=1),
                    q_full[p],
                    NT,
                    preferred_element_type=f32,
                )
                + tiles[p, kb - block + reach]
                for p, c in enumerate(cols)
            ]
            for p in range(pairs):
                held[p][kb - first] = values[p]
            return tuple(jnp.maximum(best[p], fold_rows(values[p], jnp.max)) for p in range(pairs))

        lowest = jnp.full((8, 2 * BLK), -3e38, f32)
        best = lax.fori_loop(first, last, score, (lowest,) * pairs)
        best = [jnp.max(value, axis=0, keepdims=True) for value in best]
        for p in range(pairs):
            accum[p][...] = jnp.zeros((BLK, 2 * BLK), f32)

        def gather(kb, total):
            keys = pl.ds(pl.multiple_of(kb * BLK, BLK), BLK)
            weights = [jnp.exp(held[p][kb - first] - best[p]) for p in range(pairs)]
            products = [
                jnp.dot(v_turned[c, keys], weights[p].astype(bf16), preferred_element_type=f32)
                for p, c in enumerate(cols)
            ]
            for p in range(pairs):
                accum[p][...] += products[p]
            return tuple(total[p] + fold_rows(weights[p], jnp.sum) for p in range(pairs))

        none = jnp.zeros((8, 2 * BLK), f32)
        total = lax.fori_loop(first, last, gather, (none,) * pairs)
        for p in range(pairs):
            row_total = jnp.sum(total[p], axis=0, keepdims=True)
            value = accum[p][...] / row_total
            both = jnp.concatenate([value[:half, :BLK], value[half:, BLK:]], axis=0)
            both = jnp.transpose(both)
            out_ref[own, cols[p]] = both
            low_out_ref[own, cols[p]] = both.astype(bf16)
            log_ref[0, slot, p : p + 1, :] = best[p] + jnp.log(row_total)


def attend(lead, low, high, q, k, v, known, barred, buckets, rel):
    rows, width = q.shape
    keys = k.shape[0]
    groups = rel.shape[0]
    pairs = rel.shape[1] // 2
    blocks = keys // BLK
    slots = rows // BLK
    count = 2 * (blocks // 2) + 1
    smem = pl.BlockSpec(memory_space=pltpu.SMEM)

    def cols(size):
        return pl.BlockSpec((size, pairs * BLK), lambda i: (0, i))

    def whole(array):
        return pl.BlockSpec(array.shape, lambda i: (0,) * array.ndim)

    return pl.pallas_call(
        attend_kernel,
        grid=(groups,),
        out_shape=(
            jax.ShapeDtypeStruct((rows, width), f32),
            jax.ShapeDtypeStruct((rows, width), bf16),
            jax.ShapeDtypeStruct((groups, slots, pairs, 2 * BLK), f32),
            jax.ShapeDtypeStruct((groups * pairs, count, BLK, 2 * BLK), f32),
        ),
        in_specs=[
            smem,
            smem,
            smem,
            cols(rows),
            cols(keys),
            cols(keys),
            whole(known),
            whole(barred),
            whole(buckets),
            pl.BlockSpec((1,) + rel.shape[1:], lambda i: (i, 0, 0)),
        ],
        out_specs=(
            cols(rows),
            cols(rows),
            pl.BlockSpec((1, slots, pairs, 2 * BLK), lambda i: (i, 0, 0, 0)),
            pl.BlockSpec((pairs, count, BLK, 2 * BLK), lambda i: (i, 0, 0, 0)),
        ),
        scratch_shapes=[pltpu.VMEM((pairs * BLK, keys), bf16)]
        + [pltpu.VMEM((blocks, BLK, 2 * BLK), f32)] * pairs
        + [pltpu.VMEM((BLK, 2 * BLK), f32)] * pairs,
        compiler_params=pltpu.CompilerParams(vmem_limit_bytes=VMEM_CAP),
        cost_estimate=LIGHT,
        name="attend",
    )(lead, low, high, q, k, v, known, barred, buckets, rel)


def attend_back_kernel(
    lead_ref,
    low_ref,
    high_ref,
    q_ref,
    k_ref,
    v_ref,
    g_ref,
    out_ref,
    log_ref,
    tiles,
    known,
    barred,
    buckets_ref,
    dq_ref,
    dk_ref,
    dv_ref,
    dbias_ref,
    k_turned,
    *scratch,
):
    pairs, count = tiles.shape[:2]
    dk_acc, dv_acc, d_tiles, dq_acc = (scratch[n * pairs : (n + 1) * pairs] for n in range(4))
    reach = count // 2
    slots = q_ref.shape[0] // BLK
    half = BLK // 2
    k_turned[...] = jnp.transpose(k_ref[...])
    for p in range(pairs):
        dk_acc[p][...] = jnp.zeros(dk_acc[p].shape, f32)
        dv_acc[p][...] = jnp.zeros(dv_acc[p].shape, f32)
        d_tiles[p][...] = jnp.zeros(d_tiles[p].shape, f32)
    sub = lax.broadcasted_iota(jnp.int32, (8, BLK), 0)
    chooser = jnp.where((lane_iota(8) // half) == sub, 1.0, 0.0).astype(bf16)
    cols = [slice(p * BLK, (p + 1) * BLK) for p in range(pairs)]
    for slot in range(slots):
        block = lead_ref[slot]
        first = low_ref[slot]
        last = high_ref[slot]
        base = pl.multiple_of(block * BLK, BLK)
        own = slice(slot * BLK, (slot + 1) * BLK)
        bar = barred[pl.ds(base, BLK), :]
        bar = jnp.concatenate([bar, bar], axis=0)
        q_two = [two_heads(q_ref[own, c]) for c in cols]
        q_full = [jnp.concatenate([value, bar], axis=1) for value in q_two]
        g_two = [two_heads(g_ref[own, c]) for c in cols]
        deltas = []
        for p, c in enumerate(cols):
            product = g_ref[own, c].astype(f32) * out_ref[own, c]
            high_part = product.astype(bf16)
            low_part = (product - high_part.astype(f32)).astype(bf16)
            delta = lax.dot_general(
                chooser, high_part, NT, preferred_element_type=f32
            ) + lax.dot_general(chooser, low_part, NT, preferred_element_type=f32)
            deltas.append(jnp.concatenate([delta[0:1, :], delta[1:2, :]], axis=1))
            dq_acc[p][...] = jnp.zeros((BLK, 2 * BLK), f32)
        logs = [log_ref[0, slot, p : p + 1, :] for p in range(pairs)]

        def step(kb, carry):
            rows = pl.ds(pl.multiple_of(kb * BLK, BLK), BLK)
            at = kb - block + reach
            mark = known[rows, :]
            values = [
                lax.dot_general(
                    jnp.concatenate([k_ref[rows, c], mark], axis=1),
                    q_full[p],
                    NT,
                    preferred_element_type=f32,
                )
                for p, c in enumerate(cols)
            ]
            d_probs = [
                lax.dot_general(v_ref[rows, c], g_two[p], NT, preferred_element_type=f32)
                for p, c in enumerate(cols)
            ]
            probs = [jnp.exp(values[p] + (tiles[p, at] - logs[p])) for p in range(pairs)]
            d_scores = [probs[p] * (d_probs[p] - deltas[p]) for p in range(pairs)]
            lows = [value.astype(bf16) for value in d_scores]
            dvs = [
                jnp.dot(probs[p].astype(bf16), g_two[p], preferred_element_type=f32)
                for p in range(pairs)
            ]
            dks = [jnp.dot(lows[p], q_two[p], preferred_element_type=f32) for p in range(pairs)]
            dqs = [
                jnp.dot(k_turned[c, rows], lows[p], preferred_element_type=f32)
                for p, c in enumerate(cols)
            ]
            for p in range(pairs):
                d_tiles[p][at] += d_scores[p]
                dv_acc[p][rows, :] += dvs[p]
                dk_acc[p][rows, :] += dks[p]
                dq_acc[p][...] += dqs[p]
            return carry

        lax.fori_loop(first, last, step, 0)
        for p in range(pairs):
            dq = dq_acc[p][...]
            both = jnp.concatenate([dq[:half, :BLK], dq[half:, BLK:]], axis=0)
            dq_ref[own, cols[p]] = jnp.transpose(both).astype(bf16)
    for p in range(pairs):
        dk_ref[:, cols[p]] = dk_acc[p][...].astype(bf16)
        dv_ref[:, cols[p]] = dv_acc[p][...].astype(bf16)
    levels = dbias_ref.shape[2]
    level = lax.broadcasted_iota(jnp.int32, (levels, 2 * BLK), 0)
    pad = jnp.zeros((BLK, BLK), f32)
    mirror = (
        lax.broadcasted_iota(jnp.int32, (BLK, BLK), 0)
        + lax.broadcasted_iota(jnp.int32, (BLK, BLK), 1)
        == BLK - 1
    ).astype(bf16)
    total = jnp.zeros((8, levels), f32)
    for n in range(count):
        onehot = (level == bucket_row(buckets_ref, n, reach)).astype(f32)
        sums = []
        for p in range(pairs):
            flipped = jnp.dot(mirror, d_tiles[p][n].astype(bf16), preferred_element_type=f32)
            for head in range(2):
                wide = jnp.concatenate([flipped[:, head * BLK : (head + 1) * BLK], pad], axis=1)
                rolled = pltpu.roll(wide, 0, 1, stride=1, stride_axis=0)
                sums.append(jnp.sum(rolled, axis=0, keepdims=True))
        rest = jnp.zeros((8 - 2 * pairs, 2 * BLK), f32)
        total = total + lax.dot_general(
            jnp.concatenate(sums + [rest], axis=0),
            onehot,
            NT,
            precision=HIGH,
            preferred_element_type=f32,
        )
    dbias_ref[0] = total


def attend_back(
    group, levels, lead, low, high, q, k, v, g, out, log, tiles, known, barred, buckets
):
    rows = q.shape[0]
    keys = k.shape[0]
    slots, pairs = log.shape[1:3]
    count = tiles.shape[1]
    width = pairs * BLK
    smem = pl.BlockSpec(memory_space=pltpu.SMEM)

    def cols(size):
        return pl.BlockSpec((size, width), lambda i: (0, group))

    def whole(array):
        return pl.BlockSpec(array.shape, lambda i: (0,) * array.ndim)

    def fresh(*shape):
        return pl.BlockSpec(shape, lambda i: (0,) * len(shape))

    return pl.pallas_call(
        attend_back_kernel,
        grid=(1,),
        out_shape=(
            jax.ShapeDtypeStruct((rows, width), bf16),
            jax.ShapeDtypeStruct((keys, width), bf16),
            jax.ShapeDtypeStruct((keys, width), bf16),
            jax.ShapeDtypeStruct((1, 8, levels), f32),
        ),
        in_specs=[
            smem,
            smem,
            smem,
            cols(rows),
            cols(keys),
            cols(keys),
            cols(rows),
            cols(rows),
            pl.BlockSpec((1, slots, pairs, 2 * BLK), lambda i: (group, 0, 0, 0)),
            pl.BlockSpec((pairs, count, BLK, 2 * BLK), lambda i: (group, 0, 0, 0)),
            whole(known),
            whole(barred),
            whole(buckets),
        ],
        out_specs=(
            fresh(rows, width),
            fresh(keys, width),
            fresh(keys, width),
            fresh(1, 8, levels),
        ),
        scratch_shapes=[pltpu.VMEM((width, keys), bf16)]
        + [pltpu.VMEM((keys, BLK), f32)] * (2 * pairs)
        + [pltpu.VMEM((count, BLK, 2 * BLK), f32)] * pairs
        + [pltpu.VMEM((BLK, 2 * BLK), f32)] * pairs,
        compiler_params=pltpu.CompilerParams(vmem_limit_bytes=VMEM_CAP),
        cost_estimate=LIGHT,
        name="attend_back",
    )(lead, low, high, q, k, v, g, out, log, tiles, known, barred, buckets)


GROUPS = 2


def attention_tables(starts, ends, rel_bucket, rel_bias, lead):
    blocks = starts.shape[0]
    mine = (lead[:, None] == jnp.arange(blocks)[None, :]).astype(jnp.int32)
    own_start = jnp.sum(mine * starts[None, :], axis=1)
    own_end = jnp.sum(mine * ends[None, :], axis=1)
    low = jnp.sum((ends[None, :] < own_start[:, None]).astype(jnp.int32), axis=1)
    high = jnp.sum((starts[None, :] <= own_end[:, None]).astype(jnp.int32), axis=1)
    buckets = jnp.pad(jnp.flip(rel_bucket), (0, 1)).reshape(2 * blocks, BLK)
    levels, heads = rel_bias.shape
    rel = jnp.transpose(rel_bias).reshape(GROUPS, heads // GROUPS, levels)
    return low, high, buckets, rel


def pack_kernel(*refs):
    outs = [ref for ref in refs if ref.dtype == bf16]
    masters = [ref for ref in refs if ref.dtype == f32]
    at = 0
    for out in outs:
        col = 0
        while col < out.shape[1]:
            wide = masters[at].shape[1]
            out[:, col : col + wide] = masters[at][...].astype(bf16)
            col += wide
            at += 1


def pack(groups):
    steps = 1
    while all(group[0].shape[0] % (32 * steps) == 0 for group in groups) and steps < 4:
        steps *= 2

    def spec(array):
        return pl.BlockSpec((array.shape[0] // steps, array.shape[1]), lambda i: (i, 0))

    outs = tuple(
        jax.ShapeDtypeStruct((group[0].shape[0], sum(a.shape[1] for a in group)), bf16)
        for group in groups
    )
    arrays = [array for group in groups for array in group]
    return pl.pallas_call(
        pack_kernel,
        grid=(steps,),
        out_shape=outs,
        in_specs=[spec(array) for array in arrays],
        out_specs=tuple(spec(out) for out in outs),
        compiler_params=pltpu.CompilerParams(vmem_limit_bytes=VMEM_CAP),
        cost_estimate=LIGHT,
        name="pack",
    )(*arrays)


TN = (((0,), (0,)), ((), ()))


def fetch_rows(index, parts, whole, sems):
    rows = parts[0].shape[0]
    copies = []
    for j, part in enumerate(parts):
        start = pl.multiple_of((index ^ j) * rows, rows)
        copies.append(pltpu.make_async_copy(part, whole.at[pl.ds(start, rows), :], sems.at[j]))
    return copies


def project_kernel(count, index_ref, *refs):
    parts = refs[:count]
    norm_ref, own_ref, q_ref, k_ref, v_ref, whole_ref, whole, sems, done = refs[count:]
    width = norm_ref.shape[1]
    copies = fetch_rows(index_ref[0], parts, whole, sems)
    for copy in copies:
        copy.start()
    for copy in copies:
        copy.wait()
    keep = pltpu.make_async_copy(whole, whole_ref, done)
    keep.start()
    for out, rows, col in ((q_ref, own_ref, 0), (k_ref, norm_ref, 1), (v_ref, norm_ref, 2)):
        weight = whole[:, col * width : (col + 1) * width]
        for block in range(rows.shape[0] // 256):
            part = slice(block * 256, (block + 1) * 256)
            out[part, :] = jnp.dot(rows[part, :], weight, preferred_element_type=f32).astype(bf16)
    keep.wait()


def project(index, parts, norm, own):
    count = len(parts)
    width = norm.shape[1]
    full = (parts[0].shape[0] * count, parts[0].shape[1])
    vmem = pl.BlockSpec(memory_space=pltpu.VMEM)
    anywhere = pl.BlockSpec(memory_space=pl.ANY)
    return pl.pallas_call(
        functools.partial(project_kernel, count),
        out_shape=(
            jax.ShapeDtypeStruct(own.shape, bf16),
            jax.ShapeDtypeStruct(norm.shape, bf16),
            jax.ShapeDtypeStruct(norm.shape, bf16),
            jax.ShapeDtypeStruct(full, bf16),
        ),
        in_specs=[pl.BlockSpec(memory_space=pltpu.SMEM)] + [anywhere] * count + [vmem] * 2,
        out_specs=(vmem, vmem, vmem, anywhere),
        scratch_shapes=[
            pltpu.VMEM(full, bf16),
            pltpu.SemaphoreType.DMA((count,)),
            pltpu.SemaphoreType.DMA,
        ],
        compiler_params=pltpu.CompilerParams(vmem_limit_bytes=VMEM_CAP),
        cost_estimate=LIGHT,
        name="project",
    )(index, *parts, norm, own)


def project_back_kernel(count, halves, index_ref, lead_ref, norm_ref, own_ref, whole_ref, *refs):
    keep_ref, send_ref, dnorm_ref, grad_ref, sems = refs[3 * halves :]
    width = norm_ref.shape[1]
    part_width = width // halves
    for half in range(halves):
        for col in range(3):
            rows = own_ref if col == 0 else norm_ref
            here = slice(col * width + half * part_width, col * width + (half + 1) * part_width)
            grad_ref[:, here] = lax.dot_general(
                rows[...], refs[3 * half + col][...], TN, preferred_element_type=f32
            ).astype(bf16)
    waits = scatter_rows(
        index_ref[0], count, (grad_ref, 0, grad_ref.shape[1]), (keep_ref, send_ref, 0), sems, 0
    )
    for block in range(norm_ref.shape[0] // 256):
        part = slice(block * 256, (block + 1) * 256)
        total = None
        for half in range(halves):
            for col in (1, 2):
                here = slice(col * width + half * part_width, col * width + (half + 1) * part_width)
                term = lax.dot_general(
                    refs[3 * half + col][part, :],
                    whole_ref[:, here],
                    NT,
                    preferred_element_type=f32,
                )
                total = term if total is None else total + term
        dnorm_ref[part, :] = total
    for slot in range(own_ref.shape[0] // BLK):
        rows = pl.ds(pl.multiple_of(lead_ref[slot] * BLK, BLK), BLK)
        total = dnorm_ref[rows, :]
        for half in range(halves):
            total = total + lax.dot_general(
                refs[3 * half][slot * BLK : (slot + 1) * BLK, :],
                whole_ref[:, half * part_width : (half + 1) * part_width],
                NT,
                preferred_element_type=f32,
            )
        dnorm_ref[rows, :] = total
    for wait in waits:
        wait.wait()


def project_back(index, count, lead, norm, own, whole, halves):
    vmem = pl.BlockSpec(memory_space=pltpu.VMEM)
    anywhere = pl.BlockSpec(memory_space=pl.ANY)
    smem = pl.BlockSpec(memory_space=pltpu.SMEM)
    grads = [grad for half in halves for grad in half]
    part = jax.ShapeDtypeStruct((count // 2, whole.shape[0] // count, whole.shape[1]), bf16)
    return pl.pallas_call(
        functools.partial(project_back_kernel, count, len(halves)),
        out_shape=(part, part, jax.ShapeDtypeStruct(norm.shape, f32)),
        in_specs=[smem] * 2 + [vmem] * (3 + len(grads)),
        out_specs=(anywhere, anywhere, vmem),
        scratch_shapes=[pltpu.VMEM(whole.shape, bf16), pltpu.SemaphoreType.DMA((count,))],
        compiler_params=pltpu.CompilerParams(vmem_limit_bytes=VMEM_CAP),
        cost_estimate=LIGHT,
        name="project_back",
    )(index, lead, norm, own, whole, *grads)


ROOT = 0.7978845608028654
CUBE = 0.044715


def feed_kernel(count, index_ref, *refs):
    upper = refs[:count]
    lower = refs[count : 2 * count]
    blocks = refs[2 * count].shape[0] // BLK
    cot_blocks = refs[2 * count + 3 : 2 * count + 3 + blocks]
    refs = refs[: 2 * count + 3] + refs[2 * count + 3 + blocks :]
    (
        tok_ref,
        att_ref,
        gain_ref,
        out_ref,
        d_att_ref,
        d_resid_ref,
        gain_grad_ref,
        keep_ref,
        send_ref,
        ogu,
        down,
        store,
        cot_ref,
        resid,
        norm,
        d_norm,
        total,
        hid,
        d_gate,
        d_up,
        sems_upper,
        sems_lower,
        sems_store,
    ) = refs[2 * count :]
    rows, width = tok_ref.shape
    hidden = down.shape[0]
    copies_upper = fetch_rows(index_ref[0], upper, ogu, sems_upper)
    copies_lower = fetch_rows(index_ref[0], lower, down, sems_lower)
    for copy in copies_upper + copies_lower:
        copy.start()
    for n, block in enumerate(cot_blocks):
        cot_ref[n * BLK : (n + 1) * BLK, :] = block[...]
    for copy in copies_upper:
        copy.wait()
    gain = gain_ref[...]
    row_step = 128
    tile = 512
    for block in range(rows // row_step):
        part = slice(block * row_step, (block + 1) * row_step)
        value = tok_ref[part, :] + jnp.dot(
            att_ref[part, :], ogu[:, :width], preferred_element_type=f32
        )
        resid[part, :] = value
        scale = lax.rsqrt(jnp.mean(value * value, axis=1, keepdims=True) + 1e-06)
        norm[part, :] = (value * scale * gain).astype(bf16)
    for copy in copies_lower:
        copy.wait()
    waits = []

    def put(first, last):
        half = store.shape[1] // 2
        for side, begin, end in ((0, first, min(last, half)), (1, max(first, half), last)):
            if begin < end:
                waits.extend(
                    scatter_rows(
                        index_ref[0],
                        count,
                        (store, begin, end),
                        (keep_ref.at[side], send_ref.at[side], begin - side * half),
                        sems_store,
                        len(waits),
                    )
                )

    for n in range(hidden // tile):
        here = slice(n * tile, (n + 1) * tile)
        gate_cols = slice(width + n * tile, width + (n + 1) * tile)
        up_cols = slice(width + hidden + n * tile, width + hidden + (n + 1) * tile)
        for block in range(rows // row_step):
            part = slice(block * row_step, (block + 1) * row_step)
            gate_pre = jnp.dot(norm[part, :], ogu[:, gate_cols], preferred_element_type=f32)
            up_pre = jnp.dot(norm[part, :], ogu[:, up_cols], preferred_element_type=f32)
            d_hidden = lax.dot_general(
                cot_ref[part, :], down[here, :], NT, preferred_element_type=f32
            )
            square = gate_pre * gate_pre
            bent = jnp.tanh(ROOT * gate_pre * (1.0 + CUBE * square))
            half = 0.5 + 0.5 * bent
            gelu = gate_pre * half
            slope = half + (0.5 * ROOT) * gate_pre * (1.0 - bent * bent) * (
                1.0 + (3.0 * CUBE) * square
            )
            low = (gelu * up_pre).astype(bf16)
            d_gate_low = (d_hidden * up_pre * slope).astype(bf16)
            d_up_low = (d_hidden * gelu).astype(bf16)
            hid[part, :] = low
            d_gate[part, :] = d_gate_low
            d_up[part, :] = d_up_low
            add = jnp.dot(low, down[here, :], preferred_element_type=f32)
            back = lax.dot_general(
                d_gate_low, ogu[:, gate_cols], NT, preferred_element_type=f32
            ) + lax.dot_general(d_up_low, ogu[:, up_cols], NT, preferred_element_type=f32)
            if n == 0:
                total[part, :] = resid[part, :] + add
                d_norm[part, :] = back
            else:
                total[part, :] = total[part, :] + add
                d_norm[part, :] = d_norm[part, :] + back
        store[:, gate_cols] = lax.dot_general(
            norm[...], d_gate[...], TN, preferred_element_type=f32
        ).astype(bf16)
        store[:, up_cols] = lax.dot_general(
            norm[...], d_up[...], TN, preferred_element_type=f32
        ).astype(bf16)
        put(width + n * tile, width + (n + 1) * tile)
        put(width + hidden + n * tile, width + hidden + (n + 1) * tile)
        part = lax.dot_general(
            hid[...], cot_ref[...], TN, preferred_element_type=f32
        ).astype(bf16)
        for low_row, low_col, row, size in down_pieces(width // count, hidden // count, width):
            for device in range(count):
                source = device * (hidden // count) + low_row
                if n * tile <= source < (n + 1) * tile:
                    source = source - n * tile
                    target = device * (width // count) + row
                    col = width + 2 * hidden + low_col[1]
                    store[target : target + size, col : col + LANE] = part[
                        source : source + size, low_col[0] : low_col[0] + LANE
                    ]
    gain_sum = jnp.zeros((1, width), f32)
    for block in range(rows // row_step):
        part = slice(block * row_step, (block + 1) * row_step)
        out_ref[part, :] = total[part, :].astype(bf16)
        value = resid[part, :]
        grad = d_norm[part, :]
        scale = lax.rsqrt(jnp.mean(value * value, axis=1, keepdims=True) + 1e-06)
        scaled = grad * gain
        inner = jnp.mean(value * scaled, axis=1, keepdims=True)
        d_value = (
            cot_ref[part, :].astype(f32)
            + scale * scaled
            - value * (scale * scale * scale * inner)
        )
        gain_sum = gain_sum + jnp.sum(grad * value * scale, axis=0, keepdims=True)
        d_resid_ref[part, :] = d_value
        d_low = d_value.astype(bf16)
        norm[part, :] = d_low
        d_att_ref[part, :] = lax.dot_general(
            d_low, ogu[:, :width], NT, preferred_element_type=f32
        ).astype(bf16)
    gain_grad_ref[...] = gain_sum
    store[:, :width] = lax.dot_general(
        att_ref[...], norm[...], TN, preferred_element_type=f32
    ).astype(bf16)
    put(0, width)
    put(width + 2 * hidden, store.shape[1])
    for wait in waits:
        wait.wait()


def scatter_rows(index, count, source, target, sems, at):
    store, begin, end = source
    keep, send, col = target
    rows = store.shape[0] // count
    cols = slice(col, col + end - begin)
    waits = []
    for device in range(count):
        other = index ^ device
        part = store.at[device * rows : (device + 1) * rows, begin:end]
        sem = sems.at[at + device]

        @pl.when(other % 2 == 0)
        def _():
            pltpu.make_async_copy(part, keep.at[other // 2, :, cols], sem).start()

        @pl.when(other % 2 == 1)
        def _():
            pltpu.make_async_copy(part, send.at[other // 2, :, cols], sem).start()

        waits.append(pltpu.make_async_copy(part, keep.at[0, :, cols], sem))
    return waits


def down_pieces(rows, tall, width):
    size = 16
    while tall % (2 * size) == 0 and rows % (2 * size) == 0:
        size *= 2
    pieces = []
    for q in range(tall * (width // LANE) // size):
        there = (q % (tall // size)) * size
        here = (q % (rows // size)) * size
        pieces.append((there, (q // (tall // size) * LANE, q // (rows // size) * LANE), here, size))
    return pieces


def by_parity(index, mine, other, put):
    rows = mine.shape[1]
    for parity in range(2):

        @pl.when(index % 2 == parity)
        def _():
            for k in range(mine.shape[0]):
                put((2 * k + parity) * rows, mine, k)
                put((2 * k + 1 - parity) * rows, other, k)


def unpack_three_kernel(index_ref, mine, other, *outs):
    rows, width = mine.shape[1], outs[0].shape[1]

    def put(row, array, k):
        for n in range(3):
            outs[n][row : row + rows, :] = array[k, :, n * width : (n + 1) * width].astype(f32)

    by_parity(index_ref[0], mine, other, put)


def unpack_joined_kernel(hidden, index_ref, mine, other, *refs):
    outs, spread = refs[:4], refs[4]
    rows, width = mine.shape[1], outs[0].shape[1]
    spans = ((0, width), (width, width + hidden), (width + hidden, width + 2 * hidden))
    base = width + 2 * hidden

    def put(row, array, k):
        for out, (first, last) in zip(outs[:3], spans):
            out[row : row + rows, :] = array[k, :, first:last].astype(f32)
        spread[row : row + rows, :] = array[k, :, base:].astype(f32)

    by_parity(index_ref[0], mine, other, put)
    tall = outs[3].shape[0]
    for there, (col_there, col_here), here, size in down_pieces(spread.shape[0], tall, width):
        outs[3][there : there + size, col_there : col_there + LANE] = spread[
            here : here + size, col_here : col_here + LANE
        ]


def unpack(kernel, index, mine, other, shapes, scratch, name):
    vmem = pl.BlockSpec(memory_space=pltpu.VMEM)
    return pl.pallas_call(
        kernel,
        out_shape=tuple(jax.ShapeDtypeStruct(shape, f32) for shape in shapes),
        in_specs=[pl.BlockSpec(memory_space=pltpu.SMEM), vmem, vmem],
        scratch_shapes=scratch,
        compiler_params=pltpu.CompilerParams(vmem_limit_bytes=VMEM_CAP),
        cost_estimate=LIGHT,
        name=name,
    )(index, mine, other)


def feed(index, upper, lower, tokens, attended, cotangent, gain):
    count = len(upper)
    rows, width = tokens.shape
    full_upper = (upper[0].shape[0] * count, upper[0].shape[1])
    full_lower = (lower[0].shape[0] * count, width)
    hidden = full_lower[0]
    columns = width + 3 * hidden
    vmem = pl.BlockSpec(memory_space=pltpu.VMEM)
    anywhere = pl.BlockSpec(memory_space=pl.ANY)
    tile = 512
    return pl.pallas_call(
        functools.partial(feed_kernel, count),
        out_shape=(
            jax.ShapeDtypeStruct((rows, width), bf16),
            jax.ShapeDtypeStruct((rows, width), bf16),
            jax.ShapeDtypeStruct((rows, width), f32),
            jax.ShapeDtypeStruct((1, width), f32),
            *[jax.ShapeDtypeStruct((2, count // 2, width // count, columns // 2), bf16)] * 2,
        ),
        in_specs=[pl.BlockSpec(memory_space=pltpu.SMEM)]
        + [anywhere] * (2 * count)
        + [vmem] * (3 + len(cotangent)),
        out_specs=(vmem,) * 4 + (anywhere,) * 2,
        scratch_shapes=[
            pltpu.VMEM(full_upper, bf16),
            pltpu.VMEM(full_lower, bf16),
            pltpu.VMEM((width, columns), bf16),
            pltpu.VMEM((rows, width), bf16),
            pltpu.VMEM((rows, width), f32),
            pltpu.VMEM((rows, width), bf16),
            pltpu.VMEM((rows, width), f32),
            pltpu.VMEM((rows, width), f32),
            pltpu.VMEM((rows, tile), bf16),
            pltpu.VMEM((rows, tile), bf16),
            pltpu.VMEM((rows, tile), bf16),
            pltpu.SemaphoreType.DMA((count,)),
            pltpu.SemaphoreType.DMA((count,)),
            pltpu.SemaphoreType.DMA(((2 * hidden // tile + 4) * count,)),
        ],
        compiler_params=pltpu.CompilerParams(vmem_limit_bytes=VMEM_CAP),
        cost_estimate=LIGHT,
        name="feed",
    )(index, *upper, *lower, tokens, attended, gain.reshape(1, width), *cotangent)


def bits_of(count):
    bits = count.bit_length() - 1
    assert 1 << bits == count
    return bits


def swap(value, axis, bit):
    count = lax.axis_size(axis)
    return lax.ppermute(value, axis, [(i, i ^ (1 << bit)) for i in range(count)])


def ordered(mine, other, index, bit, axis=0):
    upper = ((index >> bit) & 1) == 1
    return jnp.concatenate(
        [jnp.where(upper, other, mine), jnp.where(upper, mine, other)], axis=axis
    )


def gather_small(value, axis):
    index = lax.axis_index(axis)
    value = value[None]
    for bit in range(bits_of(lax.axis_size(axis))):
        value = ordered(value, swap(value, axis, bit), index, bit)
    return value


def first_swap(shard, axis):
    bit = bits_of(lax.axis_size(axis)) - 1
    return [(0, shard), (1 << bit, swap(shard, axis, bit))]


def other_swaps(parts, axis):
    for bit in reversed(range(bits_of(lax.axis_size(axis)) - 1)):
        parts = parts + [(j | (1 << bit), swap(part, axis, bit)) for j, part in parts]
    return [part for _, part in sorted(parts, key=lambda pair: pair[0])]


def after(anchor, part):
    j, array = part
    anchor, array = lax.optimization_barrier((anchor, array))
    return anchor, (j, array)


def add_low(left, right):
    return (left.astype(f32) + right.astype(f32)).astype(bf16)


def piece(value, index, dim=0):
    return lax.dynamic_index_in_dim(value, index, dim, keepdims=False)


def scatter_step(value, axis, bit, dim):
    own = (lax.axis_index(axis) >> bit) & 1
    other = swap(piece(value, 1 - own, dim), axis, bit)
    return add_low(piece(value, own, dim), other)


def rest_sum(value, axis):
    count = lax.axis_size(axis)
    index = lax.axis_index(axis)
    mine = index // 2
    total = piece(value, mine).astype(f32)
    for j in range(1, count // 2):
        pairs = [(i, ((i // 2) ^ j) * 2 + i % 2) for i in range(count)]
        total = total + lax.ppermute(piece(value, mine ^ j), axis, pairs).astype(f32)
    return total.astype(bf16)


def rest_gather(value, axis):
    count = lax.axis_size(axis)
    index = lax.axis_index(axis)
    whole = jnp.zeros((count // 2,) + value.shape, value.dtype)
    for j in range(count // 2):
        part = value
        if j:
            pairs = [(i, ((i // 2) ^ j) * 2 + i % 2) for i in range(count)]
            part = lax.ppermute(value, axis, pairs)
        whole = lax.dynamic_update_index_in_dim(whole, part, (index // 2) ^ j, 0)
    return whole


def fsdp_step(keep, send, bit):
    return add_low(keep, swap(send, "fsdp", bit))


def split_bit(value):
    value = value.reshape((value.shape[0] // 2, 2) + value.shape[1:])
    return value[:, 0], value[:, 1]


def parity_step(value, dim):
    count = lax.axis_size("ctx")
    shape = value.shape
    value = value.reshape(shape[:dim] + (count // 2, 2, shape[dim] // count) + shape[dim + 1 :])
    return scatter_step(value, "ctx", 0, dim + 1)


def rest_of_chain(total):
    total = yield rest_sum(total, "ctx")
    total = yield rest_gather(total, "ctx")
    yield (total, swap(total, "ctx", 0))


def single_chain(keep, send):
    bits = bits_of(lax.axis_size("fsdp"))
    total = yield fsdp_step(keep, send, 0)
    for bit in range(1, bits):
        keep, send = split_bit(total)
        total = yield fsdp_step(keep, send, bit)
    total = yield parity_step(total[0], 0)
    yield from rest_of_chain(total)


def double_chain(keep, send):
    bits = bits_of(lax.axis_size("fsdp"))
    other = swap(send, "fsdp", 0)
    left, right = yield (add_low(keep[0], other[0]), add_low(keep[1], other[1]))
    for bit in range(bits):
        if bit < bits - 1:
            left = fsdp_step(*split_bit(left), bit + 1)
        else:
            left = parity_step(left[0], 0)
        if bit == 0:
            right = parity_step(right, 1)
        else:
            right = fsdp_step(*split_bit(right), bit)
        left, right = yield (left, right)
    joined = jnp.concatenate([left, right[0]], axis=-1)
    yield from rest_of_chain(joined)


class Chain:
    def __init__(self, steps):
        self.steps = steps
        self.value = next(steps)

    def advance(self, value):
        self.value = self.steps.send(value)

    def finish(self):
        while True:
            try:
                self.advance(self.value)
            except StopIteration:
                return self.value


def gate(anchor, *chains):
    joined = lax.optimization_barrier((anchor,) + tuple(chain.value for chain in chains))
    for chain, value in zip(chains, joined[1:]):
        chain.advance(value)
    return joined[0]


def reduce_small(value, chain, joined, finish):
    fsdp_bits = bits_of(lax.axis_size("fsdp"))
    count = lax.axis_size("ctx")
    rows, width = value.shape
    value = value.reshape(2, count // 2, 2 * rows // (2 * count), width)
    value = gate(scatter_step(value, "fsdp", 0, 0), chain)
    value = gate(rest_sum(value, "ctx"), chain)
    value = add_low(value, swap(value, "ctx", 0))
    for bit in range(1, fsdp_bits):
        value = add_low(value, swap(value, "fsdp", bit))
    value, pieces = gate((value, joined.finish()), chain)
    done = finish(*pieces)
    whole = rest_gather(value, "ctx")
    whole = whole.reshape((rows // 2, width))
    whole, chain.value, done = lax.optimization_barrier((whole, chain.value, done))
    return ordered(whole, swap(whole, "fsdp", 0), lax.axis_index("fsdp"), 0), done


def local(
    byte_ids,
    doc_ids,
    rel_bucket,
    table,
    conv_w,
    score_w,
    gain_one,
    gain_two,
    rel_bias,
    query_master,
    key_master,
    value_master,
    out_master,
    gate_master,
    up_master,
    down_master,
    out_cotangent,
):
    ctx_count = lax.axis_size("ctx")
    ctx_index = lax.axis_index("ctx")
    seq_count, byte_count = byte_ids.shape
    total_bytes = byte_count * ctx_count
    width = table.shape[1]
    vocab = table.shape[0]
    hidden_width = gate_master.shape[1]
    levels, heads = rel_bias.shape
    share = ctx_count // seq_count
    assert share * seq_count == ctx_count and byte_count == 2 * BLK
    seq = ctx_index // share
    part = ctx_index % share
    near = [seq ^ slot for slot in range(seq_count)]
    lead = jnp.stack([share * other + part for other in near]).astype(jnp.int32)
    rows = seq_count * BLK

    qkv_low, down_low, ogu_low = pack(
        [[query_master, key_master, value_master], [down_master], [out_master, gate_master, up_master]]
    )
    both = jnp.stack([byte_ids, doc_ids], axis=1)
    both = gather_small(both, "ctx")
    both, qkv_low, down_low = lax.optimization_barrier((both, qkv_low, down_low))
    qkv_parts = first_swap(qkv_low, "fsdp")
    shard = lax.axis_index("fsdp")[None]
    shards = lax.axis_size("fsdp")

    def to_owner(block, slot):
        if slot == 0:
            return block
        pairs = []
        for c in range(ctx_count):
            pairs.append((c, ((c // share) ^ slot) * share + c % share))
        return lax.ppermute(block, "ctx", pairs)

    score_row = score_w.reshape(1, width)
    gain_row = gain_one.reshape(1, width)
    seq_row = seq[None]
    tokens, norm_one, norm_own, tokens_own, conv, mix, phases, known, barred = byte_forward(
        seq_row, lead, both, table, conv_w, score_row, gain_row, total_bytes
    )
    down_parts = first_swap(down_low, "fsdp")
    blocks = [to_owner(piece(out_cotangent, near[s], 1), s) for s in range(seq_count)]
    norm_one, crossed, down_crossed, blocks, ogu_low = lax.optimization_barrier(
        (norm_one, qkv_parts[1][1], down_parts[1][1], blocks, ogu_low)
    )
    qkv_parts[1] = (qkv_parts[1][0], crossed)
    down_parts[1] = (down_parts[1][0], down_crossed)
    qkv_parts = other_swaps(qkv_parts, "fsdp")
    queries, keys, values, qkv = project(shard, qkv_parts, norm_one, norm_own)
    ogu_parts = first_swap(ogu_low, "fsdp")
    down_parts = other_swaps(down_parts, "fsdp")
    docs = piece(both[:, :, 1], seq, 1)
    low, high, buckets, rel = attention_tables(
        docs[:, 0], docs[:, 2 * BLK - 2], rel_bucket, rel_bias, lead
    )
    attended, attended_low, log_total, tiles = attend(
        lead, low, high, queries, keys, values, known, barred, buckets, rel
    )

    attended_low, ogu_parts[1] = after(attended_low, ogu_parts[1])
    output, d_attended, d_resid, grad_gain_two, *grads = feed(
        shard,
        other_swaps(ogu_parts, "fsdp"),
        down_parts,
        tokens_own,
        attended_low,
        blocks,
        gain_two,
    )
    chain = Chain(double_chain(*grads))
    d_attended = gate(d_attended, chain)

    output = output.reshape(seq_count, BLK, width)
    arrived = [to_owner(output[s], s) for s in range(seq_count)]

    halves = []
    for group in range(GROUPS):
        if group:
            d_attended, arrived = gate((d_attended, arrived), chain)
            arrived = jnp.stack(arrived)
            output = jnp.stack([piece(arrived, seq ^ s) for s in range(seq_count)], axis=1)
        *grads, d_bias = attend_back(
            group,
            levels,
            lead,
            low,
            high,
            queries,
            keys,
            values,
            d_attended,
            attended,
            log_total,
            tiles,
            known,
            barred,
            buckets,
        )
        halves.append((grads, d_bias))
        d_attended, _ = lax.optimization_barrier((d_attended, grads[0]))
    d_bias = jnp.concatenate([half[1] for half in halves], axis=0)
    norm_own, halves = gate((norm_own, [half[0] for half in halves]), chain)
    keep, send, d_norm_one = project_back(shard, shards, lead, norm_one, norm_own, qkv, halves)
    qkv_chain = Chain(single_chain(keep, send))
    d_norm_one = gate(d_norm_one, qkv_chain, chain)

    vocab_rows = -(-vocab // 16) * 16
    d_resid = d_resid.reshape(seq_count, BLK, width)
    small = byte_backward(
        lead,
        phases,
        tokens,
        d_norm_one,
        d_resid,
        conv,
        mix,
        table,
        vocab_rows,
        conv_w,
        score_row,
        gain_row,
        total_bytes,
    )
    bias_grad = jnp.transpose(d_bias[:, : heads // GROUPS].reshape(heads, levels)).reshape(1, levels * heads)
    bias_grad = jnp.pad(bias_grad, ((0, 0), (0, width - levels * heads)))
    small = jnp.concatenate([small[: vocab_rows + 6], grad_gain_two, bias_grad], axis=0)
    small = jnp.pad(small, ((0, -small.shape[0] % (8 * ctx_count)), (0, 0))).astype(bf16)
    small = gate(small, qkv_chain, chain)
    shard_rows, tall = query_master.shape[0], down_master.shape[0]
    ctx_row = ctx_index[None]

    def finish(mine, other):
        return unpack(
            functools.partial(unpack_joined_kernel, hidden_width),
            ctx_row,
            mine,
            other,
            [(shard_rows, width)] + [(shard_rows, hidden_width)] * 2 + [(tall, width)],
            [pltpu.VMEM((shard_rows, hidden_width), f32)],
            "unpack_joined",
        )

    small, ffn_grads = reduce_small(small, qkv_chain, chain, finish)
    small = small.astype(f32)
    qkv_grads = unpack(
        unpack_three_kernel,
        ctx_row,
        *qkv_chain.finish(),
        [(shard_rows, width)] * 3,
        [],
        "unpack_three",
    )
    top = vocab_rows
    return (
        output,
        small[:vocab],
        small[top : top + 4],
        small[top + 4],
        small[top + 5],
        small[top + 6],
        small[top + 7, : levels * heads].reshape(levels, heads),
        *qkv_grads,
        *ffn_grads,
    )


def solution(mesh):
    placed = (
        P("fsdp", "ctx"),
        P("fsdp", "ctx"),
        P(),
        P(),
        P(),
        P(),
        P(),
        P(),
        P(),
        P("fsdp", None),
        P("fsdp", None),
        P("fsdp", None),
        P("fsdp", None),
        P("fsdp", None),
        P("fsdp", None),
        P("fsdp", None),
        P("ctx", "fsdp", None),
    )
    return jax.shard_map(
        local,
        mesh=mesh,
        in_specs=placed,
        out_specs=(
            P("ctx", "fsdp", None),
            P(),
            P(),
            P(),
            P(),
            P(),
            P(),
            P("fsdp", None),
            P("fsdp", None),
            P("fsdp", None),
            P("fsdp", None),
            P("fsdp", None),
            P("fsdp", None),
            P("fsdp", None),
        ),
        check_vma=False,
    )
```

```python
import functools

import jax
import jax.numpy as jnp
from jax import lax
from jax.experimental import pallas as pl
from jax.experimental.pallas import tpu as pltpu
from jax.sharding import PartitionSpec as P

f32 = jnp.float32
bf16 = jnp.bfloat16
LANE = 128
BLK = 128
VMEM_CAP = 60 * 1024 * 1024
HIGH = lax.Precision.HIGHEST
NT = (((1,), (1,)), ((), ()))
NN = (((1,), (0,)), ((), ()))
LIGHT = pl.CostEstimate(flops=1, transcendentals=0, bytes_accessed=1)


STEP = 16
NORM_ROWS = 128


def lane_iota(rows):
    return lax.broadcasted_iota(jnp.int32, (rows, LANE), 1)


def block_sum(value, width, lane):
    def ahead(v, n):
        return pltpu.roll(v, LANE - n, 1)

    def behind(v, n):
        return pltpu.roll(v, n, 1)

    if width == 1:
        return value
    if width == 3:
        lead = value + ahead(value, 1) + ahead(value, 2)
        phase = lane % 3
        return jnp.where(phase == 0, lead, jnp.where(phase == 1, behind(lead, 1), behind(lead, 2)))
    pair = value + jnp.where(lane % 2 == 0, ahead(value, 1), behind(value, 1))
    if width == 2:
        return pair
    return pair + jnp.where(lane % 4 < 2, ahead(pair, 2), behind(pair, 2))


def pick(value, lane_index):
    return value[:, lane_index : lane_index + 1]


def byte_forward_kernel(
    total_bytes,
    seq_ref,
    lead_ref,
    both_ref,
    table_ref,
    conv_w_ref,
    score_ref,
    gain_ref,
    tok_ref,
    norm_ref,
    norm_own_ref,
    tok_own_ref,
    conv_ref,
    mix_ref,
    ids_ref,
    known_ref,
    barred_ref,
    hi_ref,
    lo_ref,
    emb,
    flat,
    spread,
):
    groups = conv_ref.shape[1]
    width = conv_ref.shape[2]
    tiles = width // LANE
    token_count = norm_ref.shape[0]
    vocab_pad = hi_ref.shape[0]
    row_lanes = ids_ref.shape[1]
    seq = seq_ref[0]
    vocab = table_ref.shape[0]
    whole_rows = vocab // 128 * 128
    rest = jnp.zeros((vocab_pad - whole_rows, width), f32)
    rest_row = lax.broadcasted_iota(jnp.int32, rest.shape, 0)
    for row in range(whole_rows, vocab):
        rest = jnp.where(rest_row == row - whole_rows, table_ref[row : row + 1, :], rest)
    for here, value in ((0, table_ref[0:whole_rows, :]), (whole_rows, rest)):
        high = value.astype(bf16)
        hi_ref[here : here + value.shape[0], :] = high
        lo_ref[here : here + value.shape[0], :] = (value - high.astype(f32)).astype(bf16)
    lane_f = lane_iota(BLK).astype(f32)
    chunk_bytes = both_ref.shape[3]

    def lay(kind, first):
        for block in range(both_ref.shape[0]):
            row = both_ref[block, seq, kind : kind + 1, :].astype(f32)
            for half in range(chunk_bytes // LANE):
                part = jnp.broadcast_to(row[:, half * LANE : (half + 1) * LANE], (LANE, LANE))
                start = first + block * chunk_bytes + half * LANE
                spread[start : start + LANE, :] = jnp.transpose(part)

    lay(1, 0)
    for block in range(token_count // BLK):
        docs = spread[pl.ds(block * 2 * BLK, BLK, stride=2), :]
        same = docs == lane_f
        rows = slice(block * BLK, (block + 1) * BLK)
        known_ref[rows, :] = same.astype(bf16)
        barred_ref[rows, :] = jnp.where(same | (lane_f >= 16.0), 0.0, -1e30).astype(bf16)
    lay(0, 16)
    none = jnp.full((16, LANE), -1.0, f32)
    spread[0:16, :] = none
    tail = spread.shape[0] - total_bytes - 16
    spread[total_bytes + 16 :, :] = jnp.full((tail, LANE), -1.0, f32)
    lane_g = lane_iota(groups).astype(f32)
    for r in range(15):
        here = spread[pl.ds(13 + r, row_lanes, stride=12), :]
        turned = [
            jnp.transpose(here[n * LANE : (n + 1) * LANE, :])[0:1, :]
            for n in range(row_lanes // LANE)
        ]
        ids_ref[r : r + 1, :] = jnp.concatenate(turned, axis=1)
        onehot = jnp.concatenate(
            [
                (here[0:groups, :] == lane_g + n * LANE).astype(bf16)
                for n in range(vocab_pad // LANE)
            ],
            axis=1,
        )
        emb[r] = jnp.dot(onehot, hi_ref[...], preferred_element_type=f32) + jnp.dot(
            onehot, lo_ref[...], preferred_element_type=f32
        )
    ids_ref[15:16, :] = jnp.full((1, row_lanes), -1.0, f32)
    lane = lane_iota(STEP)

    def chunk(i, masked):
        r0 = pl.multiple_of(i * STEP, STEP)
        rows = pl.ds(r0, STEP)
        sums = [jnp.zeros((STEP, LANE), f32) for _ in range(12)]
        for tile in range(tiles):
            cols = slice(tile * LANE, (tile + 1) * LANE)
            taps = [conv_w_ref[k : k + 1, cols] for k in range(4)]
            piece = [emb[r, rows, cols] for r in range(15)]
            score = score_ref[0:1, cols]
            for r in range(12):
                value = (
                    piece[r] * taps[0]
                    + piece[r + 1] * taps[1]
                    + piece[r + 2] * taps[2]
                    + piece[r + 3] * taps[3]
                )
                if masked:
                    group = r0 + lax.broadcasted_iota(jnp.int32, (STEP, LANE), 0)
                    value = jnp.where(group * 12 + r < total_bytes, value, 0.0)
                conv_ref[r, rows, cols] = value
                sums[r] = sums[r] + value * score
        packed = jnp.zeros((STEP, LANE), f32)
        for r in range(12):
            packed = jnp.where(lane == r, jnp.sum(sums[r], axis=1, keepdims=True), packed)
        logits = [block_sum(packed, b, lane) * (1.0 / b) for b in range(1, 5)]
        best = jnp.maximum(jnp.maximum(logits[0], logits[1]), jnp.maximum(logits[2], logits[3]))
        parts = [jnp.exp(value - best) for value in logits]
        total = parts[0] + parts[1] + parts[2] + parts[3]
        mix = [part / total for part in parts]
        for b in range(4):
            mix_ref[b, rows, :] = mix[b]
        half_one = mix[0] * 0.5
        pair_two = block_sum(mix[1], 2, lane) * 0.25
        single_three = mix[2] * (1.0 / 6.0)
        pair_three = block_sum(mix[2], 2, lane) * (1.0 / 6.0)
        pair_four = block_sum(mix[3], 2, lane) * 0.125
        coef_one = [pick(half_one, r) for r in range(12)]
        coef_two = [pick(pair_two, 2 * j) for j in range(6)]
        coef_four = [pick(pair_four, 2 * j) for j in range(6)]
        coef_three = []
        for j in range(6):
            if j % 3 == 1:
                coef_three.append((pick(single_three, 2 * j), pick(single_three, 2 * j + 1)))
            else:
                coef_three.append((pick(pair_three, 2 * j), None))
        for tile in range(tiles):
            cols = slice(tile * LANE, (tile + 1) * LANE)
            conv = [conv_ref[r, rows, cols] for r in range(12)]
            two = [conv[2 * j] + conv[2 * j + 1] for j in range(6)]
            three = [conv[3 * q] + conv[3 * q + 1] + conv[3 * q + 2] for q in range(4)]
            four = [two[2 * q] + two[2 * q + 1] for q in range(3)]
            for j in range(6):
                a, b = 2 * j, 2 * j + 1
                value = coef_one[a] * conv[a] + coef_one[b] * conv[b]
                value = value + coef_two[j] * two[j] + coef_four[j] * four[j // 2]
                value = value + coef_three[j][0] * three[a // 3]
                if j % 3 == 1:
                    value = value + coef_three[j][1] * three[b // 3]
                flat[tile, pl.ds(6 * r0 + j, STEP, stride=6), :] = value

    whole = (total_bytes // 12) // STEP

    def plain(i, carry):
        chunk(i, False)
        return carry

    lax.fori_loop(0, whole, plain, 0)
    for i in range(whole, groups // STEP):
        chunk(i, True)

    def norm(i, carry):
        rows = pl.ds(pl.multiple_of(i * NORM_ROWS, NORM_ROWS), NORM_ROWS)
        value = jnp.concatenate([flat[tile, rows, :] for tile in range(tiles)], axis=1)
        tok_ref[rows, :] = value
        scale = lax.rsqrt(jnp.mean(value * value, axis=1, keepdims=True) + 1e-06)
        norm_ref[rows, :] = (value * scale * gain_ref[...]).astype(bf16)
        return carry

    lax.fori_loop(0, token_count // NORM_ROWS, norm, 0)
    for slot in range(norm_own_ref.shape[0] // BLK):
        start = pl.multiple_of(lead_ref[slot] * BLK, BLK)
        norm_own_ref[slot * BLK : (slot + 1) * BLK, :] = norm_ref[pl.ds(start, BLK), :]
        tok_own_ref[slot * BLK : (slot + 1) * BLK, :] = tok_ref[pl.ds(start, BLK), :]


def byte_forward(seq, lead, both, table, conv_w, score_w, gain_one, total_bytes):
    width = conv_w.shape[1]
    token_count = total_bytes // 2
    least = -(-total_bytes // 12)
    groups = -(-least // 16) * 16
    row_lanes = -(-least // LANE) * LANE
    vocab_pad = -(-table.shape[0] // LANE) * LANE
    smem = pl.BlockSpec(memory_space=pltpu.SMEM)
    vmem = pl.BlockSpec(memory_space=pltpu.VMEM)
    return pl.pallas_call(
        functools.partial(byte_forward_kernel, total_bytes),
        out_shape=(
            jax.ShapeDtypeStruct((token_count, width), f32),
            jax.ShapeDtypeStruct((token_count, width), bf16),
            jax.ShapeDtypeStruct((lead.shape[0] * BLK, width), bf16),
            jax.ShapeDtypeStruct((lead.shape[0] * BLK, width), f32),
            jax.ShapeDtypeStruct((12, groups, width), f32),
            jax.ShapeDtypeStruct((4, groups, LANE), f32),
            jax.ShapeDtypeStruct((16, row_lanes), f32),
            jax.ShapeDtypeStruct((token_count, LANE), bf16),
            jax.ShapeDtypeStruct((token_count, LANE), bf16),
        ),
        in_specs=[smem, smem] + [vmem] * 5,
        scratch_shapes=[
            pltpu.VMEM((vocab_pad, width), bf16),
            pltpu.VMEM((vocab_pad, width), bf16),
            pltpu.VMEM((15, groups, width), f32),
            pltpu.VMEM((width // LANE, 6 * groups, LANE), f32),
            pltpu.VMEM((12 * row_lanes + 32, LANE), f32),
        ],
        compiler_params=pltpu.CompilerParams(vmem_limit_bytes=VMEM_CAP),
        cost_estimate=LIGHT,
        name="byte_forward",
    )(
        seq,
        lead,
        both,
        table,
        conv_w,
        score_w,
        gain_one,
    )


def byte_backward_kernel(
    total_bytes,
    first_ref,
    ids_ref,
    tok_ref,
    dnorm_ref,
    dres_ref,
    conv_ref,
    mix_ref,
    table_ref,
    conv_w_ref,
    score_ref,
    gain_ref,
    out_ref,
    dtok,
    dconv,
    onehot,
):
    groups = conv_ref.shape[1]
    width = conv_ref.shape[2]
    tiles = width // LANE
    token_count = dnorm_ref.shape[0]
    vocab_rows = onehot.shape[0]
    lanes = ids_ref.shape[1]
    gain = gain_ref[...]

    def norm_back(i, acc):
        rows = pl.ds(pl.multiple_of(i * NORM_ROWS, NORM_ROWS), NORM_ROWS)
        value = tok_ref[rows, :]
        grad = dnorm_ref[rows, :]
        scale = lax.rsqrt(jnp.mean(value * value, axis=1, keepdims=True) + 1e-06)
        grad_gain = grad * gain
        inner = jnp.mean(value * grad_gain, axis=1, keepdims=True)
        total = 0.5 * scale * grad_gain - value * (0.5 * scale * scale * scale * inner)
        for tile in range(tiles):
            dtok[tile, rows, :] = total[:, tile * LANE : (tile + 1) * LANE]
        product = (grad * value * scale).reshape(NORM_ROWS // 8, 8, width)
        return acc + jnp.sum(product, axis=0)

    gain_acc = lax.fori_loop(0, token_count // NORM_ROWS, norm_back, jnp.zeros((8, width), f32))
    rest = dtok.shape[1] - token_count
    dtok[:, token_count:, :] = jnp.zeros((tiles, rest, LANE), f32)
    for slot in range(dres_ref.shape[0]):
        start = pl.multiple_of(first_ref[slot] * BLK, BLK)

        def add(i, carry, slot=slot, start=start):
            r = pl.multiple_of(i * 32, 32)
            rows = pl.ds(pl.multiple_of(start + r, 32), 32)
            more = 0.5 * dres_ref[slot, pl.ds(r, 32), :]
            for tile in range(tiles):
                dtok[tile, rows, :] = (
                    dtok[tile, rows, :] + more[:, tile * LANE : (tile + 1) * LANE]
                )
            return carry

        lax.fori_loop(0, BLK // 32, add, 0)
    vocab = lax.broadcasted_iota(jnp.int32, (vocab_rows, lanes), 0).astype(f32)
    for r in range(15):
        onehot[:, r * lanes : (r + 1) * lanes] = (vocab == ids_ref[r : r + 1, :]).astype(bf16)
    for r in range(12):
        dconv[r * lanes + groups : (r + 1) * lanes, :] = jnp.zeros((lanes - groups, width), bf16)
    lane = lane_iota(8)

    def scalars(r0):
        rows = pl.ds(r0, 8)
        one = [jnp.zeros((8, LANE), f32) for _ in range(12)]
        cross = [jnp.zeros((8, LANE), f32) for _ in range(6)]
        tri = [jnp.zeros((8, LANE), f32) for _ in range(8)]
        for tile in range(tiles):
            cols = slice(tile * LANE, (tile + 1) * LANE)
            conv = [conv_ref[r, rows, cols] for r in range(12)]
            grad = [dtok[tile, pl.ds(6 * r0 + j, 8, stride=6), :] for j in range(6)]
            two = [conv[2 * j] + conv[2 * j + 1] for j in range(6)]
            three = [conv[3 * q] + conv[3 * q + 1] + conv[3 * q + 2] for q in range(4)]
            for r in range(12):
                one[r] = one[r] + conv[r] * grad[r // 2]
            slot = 0
            for j in range(6):
                cross[j] = cross[j] + two[j ^ 1] * grad[j]
                for q in sorted({(2 * j) // 3, (2 * j + 1) // 3}):
                    tri[slot] = tri[slot] + three[q] * grad[j]
                    slot += 1
        inner_one = jnp.zeros((8, LANE), f32)
        for r in range(12):
            inner_one = jnp.where(lane == r, jnp.sum(one[r], axis=1, keepdims=True), inner_one)
        inner_cross = jnp.zeros((8, LANE), f32)
        for j in range(6):
            inner_cross = jnp.where(
                lane // 2 == j, jnp.sum(cross[j], axis=1, keepdims=True), inner_cross
            )
        inner_three = jnp.zeros((8, LANE), f32)
        slot = 0
        for j in range(6):
            for q in sorted({(2 * j) // 3, (2 * j + 1) // 3}):
                here = (lane // 2 == j) & (lane // 3 == q)
                inner_three = jnp.where(
                    here, jnp.sum(tri[slot], axis=1, keepdims=True), inner_three
                )
                slot += 1
        inner_two = block_sum(inner_one, 2, lane)
        mix = [mix_ref[b, rows, :] for b in range(4)]
        d_mix = [
            inner_one,
            inner_two * 0.5,
            inner_three * (1.0 / 3.0),
            (inner_two + inner_cross) * 0.25,
        ]
        mean = mix[0] * d_mix[0] + mix[1] * d_mix[1] + mix[2] * d_mix[2] + mix[3] * d_mix[3]
        d_logit = [mix[b] * (d_mix[b] - mean) for b in range(4)]
        d_logit = [jnp.where(lane < 12, value, 0.0) for value in d_logit]
        slope = d_logit[0]
        for b in range(2, 5):
            slope = slope + block_sum(d_logit[b - 1], b, lane) * (1.0 / b)
        pair_two = block_sum(mix[1], 2, lane) * 0.5
        single_three = mix[2] * (1.0 / 3.0)
        pair_three = block_sum(mix[2], 2, lane) * (1.0 / 3.0)
        pair_four = block_sum(mix[3], 2, lane) * 0.25
        return mix[0], pair_two, single_three, pair_three, pair_four, slope

    def spread(r0, coefs, tile, masked, score_acc):
        one, pair_two, single_three, pair_three, pair_four, slope = coefs
        rows = pl.ds(r0, 8)
        cols = slice(tile * LANE, (tile + 1) * LANE)
        grad = [dtok[tile, pl.ds(6 * r0 + j, 8, stride=6), :] for j in range(6)]
        score = score_ref[0:1, cols]
        four = [
            pick(pair_four, 4 * q) * grad[2 * q] + pick(pair_four, 4 * q + 2) * grad[2 * q + 1]
            for q in range(3)
        ]
        three = []
        for q in range(4):
            a = 3 * q
            if a % 2 == 0:
                three.append(
                    pick(pair_three, a) * grad[a // 2]
                    + pick(single_three, a + 2) * grad[a // 2 + 1]
                )
            else:
                three.append(
                    pick(single_three, a) * grad[a // 2]
                    + pick(pair_three, a + 1) * grad[a // 2 + 1]
                )
        result = []
        for r in range(12):
            weight = pick(slope, r)
            own = (pick(one, r) + pick(pair_two, r)) * grad[r // 2]
            value = own + three[r // 3] + four[r // 4] + weight * score
            score_acc = score_acc + weight * conv_ref[r, rows, cols]
            if masked:
                group = r0 + lax.broadcasted_iota(jnp.int32, (8, LANE), 0)
                value = jnp.where(group * 12 + r < total_bytes, value, 0.0)
            result.append(value)
        return result, score_acc

    def chunk(i, accs, masked):
        r0 = pl.multiple_of(i * 16, 16)
        r1 = pl.multiple_of(i * 16 + 8, 8)
        low_coefs = scalars(r0)
        high_coefs = scalars(r1)
        new = []
        for tile in range(tiles):
            cols = slice(tile * LANE, (tile + 1) * LANE)
            low, acc = spread(r0, low_coefs, tile, masked, accs[tile])
            high, acc = spread(r1, high_coefs, tile, masked, acc)
            new.append(acc)
            for r in range(12):
                both = jnp.concatenate([low[r], high[r]], axis=0).astype(bf16)
                dconv[pl.ds(pl.multiple_of(r * lanes + r0, 16), 16), cols] = both
        return tuple(new)

    accs = tuple(jnp.zeros((8, LANE), f32) for _ in range(tiles))
    whole = (total_bytes // 12) // 16
    accs = lax.fori_loop(0, whole, lambda i, a: chunk(i, a, False), accs)
    for i in range(whole, groups // 16):
        accs = chunk(i, accs, True)
    tail = [jnp.zeros((1, width), f32) for _ in range(8)]
    for k in range(4):
        part = jnp.dot(
            onehot[:, k * lanes : (k + 12) * lanes], dconv[...], preferred_element_type=f32
        )
        if k == 0:
            out_ref[0:vocab_rows, :] = part * conv_w_ref[k : k + 1, :]
        else:
            out_ref[0:vocab_rows, :] = out_ref[0:vocab_rows, :] + part * conv_w_ref[k : k + 1, :]
        vocab = table_ref.shape[0]
        whole_rows = vocab // 8 * 8
        tail[k] = jnp.sum(part[:whole_rows] * table_ref[0:whole_rows, :], axis=0, keepdims=True)
        for row in range(whole_rows, vocab):
            tail[k] = tail[k] + part[row : row + 1] * table_ref[row : row + 1, :]
    tail[4] = jnp.sum(jnp.concatenate(accs, axis=1), axis=0, keepdims=True)
    tail[5] = jnp.sum(gain_acc, axis=0, keepdims=True)
    out_ref[vocab_rows:, :] = jnp.concatenate(tail, axis=0)


def byte_backward(
    first,
    ids,
    tokens,
    d_norm,
    d_resid,
    conv,
    mix,
    table,
    vocab_rows,
    conv_w,
    score_w,
    gain_one,
    total_bytes,
):
    width = conv.shape[2]
    groups = conv.shape[1]
    lanes = ids.shape[1]
    return pl.pallas_call(
        functools.partial(byte_backward_kernel, total_bytes),
        out_shape=jax.ShapeDtypeStruct((vocab_rows + 8, width), f32),
        in_specs=[pl.BlockSpec(memory_space=pltpu.SMEM)]
        + [pl.BlockSpec(memory_space=pltpu.VMEM)] * 10,
        scratch_shapes=[
            pltpu.VMEM((width // LANE, 6 * groups, LANE), f32),
            pltpu.VMEM((12 * lanes, width), bf16),
            pltpu.VMEM((vocab_rows, 15 * lanes), bf16),
        ],
        compiler_params=pltpu.CompilerParams(vmem_limit_bytes=VMEM_CAP),
        cost_estimate=LIGHT,
        name="byte_backward",
    )(
        first,
        ids,
        tokens,
        d_norm,
        d_resid,
        conv,
        mix,
        table,
        conv_w,
        score_w,
        gain_one,
    )


def head_mask(value, head):
    half = value.shape[1] // 2
    lane = lax.broadcasted_iota(jnp.int32, value.shape, 1)
    keep = lane < half if head == 0 else lane >= half
    return jnp.where(keep, value, jnp.zeros_like(value))


def two_heads(value):
    return jnp.concatenate([head_mask(value, 0), head_mask(value, 1)], axis=0)


def bucket_row(buckets_ref, n, reach):
    row = buckets_ref.shape[0] // 2 - 1 - (n - reach)
    return jnp.concatenate([buckets_ref[row : row + 1, :], buckets_ref[row + 1 : row + 2, :]], axis=1)


def bias_tiles(buckets_ref, rel, tiles):
    count = tiles.shape[1]
    levels = rel.shape[1]
    level = lax.broadcasted_iota(jnp.int32, (levels, 2 * BLK), 0)
    for n in range(count):
        onehot = (level == bucket_row(buckets_ref, n, count // 2)).astype(f32)
        values = lax.dot_general(rel, onehot, NN, precision=HIGH, preferred_element_type=f32)
        for head in range(2 * tiles.shape[0]):
            spread = jnp.broadcast_to(values[head : head + 1, :], (BLK, 2 * BLK))
            rolled = pltpu.roll(spread, BLK + 1, 1, stride=1, stride_axis=0)
            half = slice(head % 2 * BLK, head % 2 * BLK + BLK)
            tiles[head // 2, n, :, half] = rolled[:, :BLK]


def fold_rows(value, op):
    return op(value.reshape(BLK // 8, 8, value.shape[1]), axis=0)


def attend_kernel(
    lead_ref,
    low_ref,
    high_ref,
    q_ref,
    k_ref,
    v_ref,
    known,
    barred,
    tiles,
    out_ref,
    low_out_ref,
    log_ref,
    v_turned,
    *scratch,
):
    pairs = tiles.shape[0]
    held, accum = scratch[:pairs], scratch[pairs:]
    reach = tiles.shape[1] // 2
    slots = q_ref.shape[0] // BLK
    half = BLK // 2
    v_turned[...] = jnp.transpose(v_ref[...])
    cols = [slice(p * BLK, (p + 1) * BLK) for p in range(pairs)]
    for slot in range(slots):
        block = lead_ref[slot]
        first = low_ref[slot]
        last = high_ref[slot]
        base = pl.multiple_of(block * BLK, BLK)
        own = slice(slot * BLK, (slot + 1) * BLK)
        bar = barred[pl.ds(base, BLK), :]
        bar = jnp.concatenate([bar, bar], axis=0)
        q_full = [jnp.concatenate([two_heads(q_ref[own, c]), bar], axis=1) for c in cols]

        def score(kb, best):
            rows = pl.ds(pl.multiple_of(kb * BLK, BLK), BLK)
            mark = known[rows, :]
            values = [
                lax.dot_general(
                    jnp.concatenate([k_ref[rows, c], mark], axis=1),
                    q_full[p],
                    NT,
                    preferred_element_type=f32,
                )
                + tiles[p, kb - block + reach]
                for p, c in enumerate(cols)
            ]
            for p in range(pairs):
                held[p][kb - first] = values[p]
            return tuple(jnp.maximum(best[p], fold_rows(values[p], jnp.max)) for p in range(pairs))

        lowest = jnp.full((8, 2 * BLK), -3e38, f32)
        best = lax.fori_loop(first, last, score, (lowest,) * pairs)
        best = [jnp.max(value, axis=0, keepdims=True) for value in best]
        for p in range(pairs):
            accum[p][...] = jnp.zeros((BLK, 2 * BLK), f32)

        def gather(kb, total):
            keys = pl.ds(pl.multiple_of(kb * BLK, BLK), BLK)
            weights = [jnp.exp(held[p][kb - first] - best[p]) for p in range(pairs)]
            products = [
                jnp.dot(v_turned[c, keys], weights[p].astype(bf16), preferred_element_type=f32)
                for p, c in enumerate(cols)
            ]
            for p in range(pairs):
                accum[p][...] += products[p]
            return tuple(total[p] + fold_rows(weights[p], jnp.sum) for p in range(pairs))

        none = jnp.zeros((8, 2 * BLK), f32)
        total = lax.fori_loop(first, last, gather, (none,) * pairs)
        for p in range(pairs):
            row_total = jnp.sum(total[p], axis=0, keepdims=True)
            value = accum[p][...] / row_total
            both = jnp.concatenate([value[:half, :BLK], value[half:, BLK:]], axis=0)
            both = jnp.transpose(both)
            out_ref[own, cols[p]] = both
            low_out_ref[own, cols[p]] = both.astype(bf16)
            log_ref[0, slot, p : p + 1, :] = best[p] + jnp.log(row_total)


def tiles_kernel(buckets_ref, rel_ref, tiles):
    bias_tiles(buckets_ref, rel_ref[0], tiles)


def make_tiles(buckets, rel):
    groups, heads, levels = rel.shape
    shape = (heads // 2, 2 * (buckets.shape[0] // 4) + 1, BLK, 2 * BLK)
    return pl.pallas_call(
        tiles_kernel,
        grid=(groups,),
        out_shape=jax.ShapeDtypeStruct((groups * shape[0],) + shape[1:], f32),
        in_specs=[
            pl.BlockSpec(buckets.shape, lambda i: (0, 0)),
            pl.BlockSpec((1, heads, levels), lambda i: (i, 0, 0)),
        ],
        out_specs=pl.BlockSpec(shape, lambda i: (i, 0, 0, 0)),
        compiler_params=pltpu.CompilerParams(vmem_limit_bytes=VMEM_CAP),
        cost_estimate=LIGHT,
        name="bias_tiles",
    )(buckets, rel)


def attend(lead, low, high, q, k, v, known, barred, tiles):
    rows, width = q.shape
    keys = k.shape[0]
    pairs = tiles.shape[0] // GROUPS
    groups = GROUPS
    blocks = keys // BLK
    slots = rows // BLK
    count = tiles.shape[1]
    smem = pl.BlockSpec(memory_space=pltpu.SMEM)

    def cols(size):
        return pl.BlockSpec((size, pairs * BLK), lambda i: (0, i))

    def whole(array):
        return pl.BlockSpec(array.shape, lambda i: (0,) * array.ndim)

    return pl.pallas_call(
        attend_kernel,
        grid=(groups,),
        out_shape=(
            jax.ShapeDtypeStruct((rows, width), f32),
            jax.ShapeDtypeStruct((rows, width), bf16),
            jax.ShapeDtypeStruct((groups, slots, pairs, 2 * BLK), f32),
        ),
        in_specs=[
            smem,
            smem,
            smem,
            cols(rows),
            cols(keys),
            cols(keys),
            whole(known),
            whole(barred),
            pl.BlockSpec((pairs, count, BLK, 2 * BLK), lambda i: (i, 0, 0, 0)),
        ],
        out_specs=(
            cols(rows),
            cols(rows),
            pl.BlockSpec((1, slots, pairs, 2 * BLK), lambda i: (i, 0, 0, 0)),
        ),
        scratch_shapes=[pltpu.VMEM((pairs * BLK, keys), bf16)]
        + [pltpu.VMEM((blocks, BLK, 2 * BLK), f32)] * pairs
        + [pltpu.VMEM((BLK, 2 * BLK), f32)] * pairs,
        compiler_params=pltpu.CompilerParams(vmem_limit_bytes=VMEM_CAP),
        cost_estimate=LIGHT,
        name="attend",
    )(lead, low, high, q, k, v, known, barred, tiles)


def attend_back_kernel(
    lead_ref,
    low_ref,
    high_ref,
    q_ref,
    k_ref,
    v_ref,
    g_ref,
    out_ref,
    log_ref,
    tiles,
    known,
    barred,
    buckets_ref,
    dq_ref,
    dk_ref,
    dv_ref,
    dbias_ref,
    k_turned,
    *scratch,
):
    pairs, count = tiles.shape[:2]
    dk_acc, dv_acc, d_tiles, dq_acc = (scratch[n * pairs : (n + 1) * pairs] for n in range(4))
    reach = count // 2
    slots = q_ref.shape[0] // BLK
    half = BLK // 2
    k_turned[...] = jnp.transpose(k_ref[...])
    for p in range(pairs):
        dk_acc[p][...] = jnp.zeros(dk_acc[p].shape, f32)
        dv_acc[p][...] = jnp.zeros(dv_acc[p].shape, f32)
        d_tiles[p][...] = jnp.zeros(d_tiles[p].shape, f32)
    sub = lax.broadcasted_iota(jnp.int32, (8, BLK), 0)
    chooser = jnp.where((lane_iota(8) // half) == sub, 1.0, 0.0).astype(bf16)
    cols = [slice(p * BLK, (p + 1) * BLK) for p in range(pairs)]
    for slot in range(slots):
        block = lead_ref[slot]
        first = low_ref[slot]
        last = high_ref[slot]
        base = pl.multiple_of(block * BLK, BLK)
        own = slice(slot * BLK, (slot + 1) * BLK)
        bar = barred[pl.ds(base, BLK), :]
        bar = jnp.concatenate([bar, bar], axis=0)
        q_two = [two_heads(q_ref[own, c]) for c in cols]
        q_full = [jnp.concatenate([value, bar], axis=1) for value in q_two]
        g_two = [two_heads(g_ref[own, c]) for c in cols]
        deltas = []
        for p, c in enumerate(cols):
            product = g_ref[own, c].astype(f32) * out_ref[own, c]
            high_part = product.astype(bf16)
            low_part = (product - high_part.astype(f32)).astype(bf16)
            delta = lax.dot_general(
                chooser, high_part, NT, preferred_element_type=f32
            ) + lax.dot_general(chooser, low_part, NT, preferred_element_type=f32)
            deltas.append(jnp.concatenate([delta[0:1, :], delta[1:2, :]], axis=1))
            dq_acc[p][...] = jnp.zeros((BLK, 2 * BLK), f32)
        logs = [log_ref[0, slot, p : p + 1, :] for p in range(pairs)]

        def step(kb, carry):
            rows = pl.ds(pl.multiple_of(kb * BLK, BLK), BLK)
            at = kb - block + reach
            mark = known[rows, :]
            values = [
                lax.dot_general(
                    jnp.concatenate([k_ref[rows, c], mark], axis=1),
                    q_full[p],
                    NT,
                    preferred_element_type=f32,
                )
                for p, c in enumerate(cols)
            ]
            d_probs = [
                lax.dot_general(v_ref[rows, c], g_two[p], NT, preferred_element_type=f32)
                for p, c in enumerate(cols)
            ]
            probs = [jnp.exp(values[p] + (tiles[p, at] - logs[p])) for p in range(pairs)]
            d_scores = [probs[p] * (d_probs[p] - deltas[p]) for p in range(pairs)]
            lows = [value.astype(bf16) for value in d_scores]
            dvs = [
                jnp.dot(probs[p].astype(bf16), g_two[p], preferred_element_type=f32)
                for p in range(pairs)
            ]
            dks = [jnp.dot(lows[p], q_two[p], preferred_element_type=f32) for p in range(pairs)]
            dqs = [
                jnp.dot(k_turned[c, rows], lows[p], preferred_element_type=f32)
                for p, c in enumerate(cols)
            ]
            for p in range(pairs):
                d_tiles[p][at] += d_scores[p]
                dv_acc[p][rows, :] += dvs[p]
                dk_acc[p][rows, :] += dks[p]
                dq_acc[p][...] += dqs[p]
            return carry

        lax.fori_loop(first, last, step, 0)
        for p in range(pairs):
            dq = dq_acc[p][...]
            both = jnp.concatenate([dq[:half, :BLK], dq[half:, BLK:]], axis=0)
            dq_ref[own, cols[p]] = jnp.transpose(both).astype(bf16)
    for p in range(pairs):
        dk_ref[:, cols[p]] = dk_acc[p][...].astype(bf16)
        dv_ref[:, cols[p]] = dv_acc[p][...].astype(bf16)
    levels = dbias_ref.shape[2]
    level = lax.broadcasted_iota(jnp.int32, (levels, 2 * BLK), 0)
    pad = jnp.zeros((BLK, BLK), f32)
    mirror = (
        lax.broadcasted_iota(jnp.int32, (BLK, BLK), 0)
        + lax.broadcasted_iota(jnp.int32, (BLK, BLK), 1)
        == BLK - 1
    ).astype(bf16)
    total = jnp.zeros((8, levels), f32)
    for n in range(count):
        onehot = (level == bucket_row(buckets_ref, n, reach)).astype(f32)
        sums = []
        for p in range(pairs):
            flipped = jnp.dot(mirror, d_tiles[p][n].astype(bf16), preferred_element_type=f32)
            for head in range(2):
                wide = jnp.concatenate([flipped[:, head * BLK : (head + 1) * BLK], pad], axis=1)
                rolled = pltpu.roll(wide, 0, 1, stride=1, stride_axis=0)
                sums.append(jnp.sum(rolled, axis=0, keepdims=True))
        rest = jnp.zeros((8 - 2 * pairs, 2 * BLK), f32)
        total = total + lax.dot_general(
            jnp.concatenate(sums + [rest], axis=0),
            onehot,
            NT,
            precision=HIGH,
            preferred_element_type=f32,
        )
    dbias_ref[0] = total


def attend_back(
    group, levels, lead, low, high, q, k, v, g, out, log, tiles, known, barred, buckets
):
    rows = q.shape[0]
    keys = k.shape[0]
    slots, pairs = log.shape[1:3]
    count = tiles.shape[1]
    width = pairs * BLK
    smem = pl.BlockSpec(memory_space=pltpu.SMEM)

    def cols(size):
        return pl.BlockSpec((size, width), lambda i: (0, group))

    def whole(array):
        return pl.BlockSpec(array.shape, lambda i: (0,) * array.ndim)

    def fresh(*shape):
        return pl.BlockSpec(shape, lambda i: (0,) * len(shape))

    return pl.pallas_call(
        attend_back_kernel,
        grid=(1,),
        out_shape=(
            jax.ShapeDtypeStruct((rows, width), bf16),
            jax.ShapeDtypeStruct((keys, width), bf16),
            jax.ShapeDtypeStruct((keys, width), bf16),
            jax.ShapeDtypeStruct((1, 8, levels), f32),
        ),
        in_specs=[
            smem,
            smem,
            smem,
            cols(rows),
            cols(keys),
            cols(keys),
            cols(rows),
            cols(rows),
            pl.BlockSpec((1, slots, pairs, 2 * BLK), lambda i: (group, 0, 0, 0)),
            pl.BlockSpec((pairs, count, BLK, 2 * BLK), lambda i: (group, 0, 0, 0)),
            whole(known),
            whole(barred),
            whole(buckets),
        ],
        out_specs=(
            fresh(rows, width),
            fresh(keys, width),
            fresh(keys, width),
            fresh(1, 8, levels),
        ),
        scratch_shapes=[pltpu.VMEM((width, keys), bf16)]
        + [pltpu.VMEM((keys, BLK), f32)] * (2 * pairs)
        + [pltpu.VMEM((count, BLK, 2 * BLK), f32)] * pairs
        + [pltpu.VMEM((BLK, 2 * BLK), f32)] * pairs,
        compiler_params=pltpu.CompilerParams(vmem_limit_bytes=VMEM_CAP),
        cost_estimate=LIGHT,
        name="attend_back",
    )(lead, low, high, q, k, v, g, out, log, tiles, known, barred, buckets)


GROUPS = 2


def attention_tables(starts, ends, rel_bucket, rel_bias, lead):
    blocks = starts.shape[0]
    mine = (lead[:, None] == jnp.arange(blocks)[None, :]).astype(jnp.int32)
    own_start = jnp.sum(mine * starts[None, :], axis=1)
    own_end = jnp.sum(mine * ends[None, :], axis=1)
    low = jnp.sum((ends[None, :] < own_start[:, None]).astype(jnp.int32), axis=1)
    high = jnp.sum((starts[None, :] <= own_end[:, None]).astype(jnp.int32), axis=1)
    buckets = jnp.pad(jnp.flip(rel_bucket), (0, 1)).reshape(2 * blocks, BLK)
    levels, heads = rel_bias.shape
    rel = jnp.transpose(rel_bias).reshape(GROUPS, heads // GROUPS, levels)
    return low, high, buckets, rel


def pack_kernel(*refs):
    outs = [ref for ref in refs if ref.dtype == bf16]
    masters = [ref for ref in refs if ref.dtype == f32]
    at = 0
    for out in outs:
        col = 0
        while col < out.shape[1]:
            wide = masters[at].shape[1]
            out[:, col : col + wide] = masters[at][...].astype(bf16)
            col += wide
            at += 1


def pack(groups):
    steps = 1
    while all(group[0].shape[0] % (32 * steps) == 0 for group in groups) and steps < 4:
        steps *= 2

    def spec(array):
        return pl.BlockSpec((array.shape[0] // steps, array.shape[1]), lambda i: (i, 0))

    outs = tuple(
        jax.ShapeDtypeStruct((group[0].shape[0], sum(a.shape[1] for a in group)), bf16)
        for group in groups
    )
    arrays = [array for group in groups for array in group]
    return pl.pallas_call(
        pack_kernel,
        grid=(steps,),
        out_shape=outs,
        in_specs=[spec(array) for array in arrays],
        out_specs=tuple(spec(out) for out in outs),
        compiler_params=pltpu.CompilerParams(vmem_limit_bytes=VMEM_CAP),
        cost_estimate=LIGHT,
        name="pack",
    )(*arrays)


TN = (((0,), (0,)), ((), ()))


def fetch_rows(index, parts, whole, sems):
    rows = parts[0].shape[0]
    copies = []
    for j, part in enumerate(parts):
        start = pl.multiple_of((index ^ j) * rows, rows)
        copies.append(pltpu.make_async_copy(part, whole.at[pl.ds(start, rows), :], sems.at[j]))
    return copies


def project_kernel(count, index_ref, *refs):
    parts = refs[:count]
    norm_ref, own_ref, q_ref, k_ref, v_ref, whole_ref, whole, sems, done = refs[count:]
    width = norm_ref.shape[1]
    copies = fetch_rows(index_ref[0], parts, whole, sems)
    for copy in copies:
        copy.start()
    for copy in copies:
        copy.wait()
    keep = pltpu.make_async_copy(whole, whole_ref, done)
    keep.start()
    for out, rows, col in ((q_ref, own_ref, 0), (k_ref, norm_ref, 1), (v_ref, norm_ref, 2)):
        weight = whole[:, col * width : (col + 1) * width]
        for block in range(rows.shape[0] // 256):
            part = slice(block * 256, (block + 1) * 256)
            out[part, :] = jnp.dot(rows[part, :], weight, preferred_element_type=f32).astype(bf16)
    keep.wait()


def project(index, parts, norm, own):
    count = len(parts)
    width = norm.shape[1]
    full = (parts[0].shape[0] * count, parts[0].shape[1])
    vmem = pl.BlockSpec(memory_space=pltpu.VMEM)
    anywhere = pl.BlockSpec(memory_space=pl.ANY)
    return pl.pallas_call(
        functools.partial(project_kernel, count),
        out_shape=(
            jax.ShapeDtypeStruct(own.shape, bf16),
            jax.ShapeDtypeStruct(norm.shape, bf16),
            jax.ShapeDtypeStruct(norm.shape, bf16),
            jax.ShapeDtypeStruct(full, bf16),
        ),
        in_specs=[pl.BlockSpec(memory_space=pltpu.SMEM)] + [anywhere] * count + [vmem] * 2,
        out_specs=(vmem, vmem, vmem, anywhere),
        scratch_shapes=[
            pltpu.VMEM(full, bf16),
            pltpu.SemaphoreType.DMA((count,)),
            pltpu.SemaphoreType.DMA,
        ],
        compiler_params=pltpu.CompilerParams(vmem_limit_bytes=VMEM_CAP),
        cost_estimate=LIGHT,
        name="project",
    )(index, *parts, norm, own)


def project_back_kernel(count, halves, index_ref, lead_ref, norm_ref, own_ref, whole_ref, *refs):
    keep_ref, send_ref, dnorm_ref, grad_ref, sems = refs[3 * halves :]
    width = norm_ref.shape[1]
    part_width = width // halves
    for half in range(halves):
        for col in range(3):
            rows = own_ref if col == 0 else norm_ref
            here = slice(col * width + half * part_width, col * width + (half + 1) * part_width)
            grad_ref[:, here] = lax.dot_general(
                rows[...], refs[3 * half + col][...], TN, preferred_element_type=f32
            ).astype(bf16)
    waits = scatter_rows(
        index_ref[0], count, (grad_ref, 0, grad_ref.shape[1]), (keep_ref, send_ref, 0), sems, 0
    )
    for block in range(norm_ref.shape[0] // 256):
        part = slice(block * 256, (block + 1) * 256)
        total = None
        for half in range(halves):
            for col in (1, 2):
                here = slice(col * width + half * part_width, col * width + (half + 1) * part_width)
                term = lax.dot_general(
                    refs[3 * half + col][part, :],
                    whole_ref[:, here],
                    NT,
                    preferred_element_type=f32,
                )
                total = term if total is None else total + term
        dnorm_ref[part, :] = total
    for slot in range(own_ref.shape[0] // BLK):
        rows = pl.ds(pl.multiple_of(lead_ref[slot] * BLK, BLK), BLK)
        total = dnorm_ref[rows, :]
        for half in range(halves):
            total = total + lax.dot_general(
                refs[3 * half][slot * BLK : (slot + 1) * BLK, :],
                whole_ref[:, half * part_width : (half + 1) * part_width],
                NT,
                preferred_element_type=f32,
            )
        dnorm_ref[rows, :] = total
    for wait in waits:
        wait.wait()


def project_back(index, count, lead, norm, own, whole, halves):
    vmem = pl.BlockSpec(memory_space=pltpu.VMEM)
    anywhere = pl.BlockSpec(memory_space=pl.ANY)
    smem = pl.BlockSpec(memory_space=pltpu.SMEM)
    grads = [grad for half in halves for grad in half]
    part = jax.ShapeDtypeStruct((count // 2, whole.shape[0] // count, whole.shape[1]), bf16)
    return pl.pallas_call(
        functools.partial(project_back_kernel, count, len(halves)),
        out_shape=(part, part, jax.ShapeDtypeStruct(norm.shape, f32)),
        in_specs=[smem] * 2 + [vmem] * (3 + len(grads)),
        out_specs=(anywhere, anywhere, vmem),
        scratch_shapes=[pltpu.VMEM(whole.shape, bf16), pltpu.SemaphoreType.DMA((count,))],
        compiler_params=pltpu.CompilerParams(vmem_limit_bytes=VMEM_CAP),
        cost_estimate=LIGHT,
        name="project_back",
    )(index, lead, norm, own, whole, *grads)


ROOT = 0.7978845608028654
CUBE = 0.044715


def feed_kernel(count, index_ref, *refs):
    upper = refs[:count]
    lower = refs[count : 2 * count]
    blocks = refs[2 * count].shape[0] // BLK
    cot_blocks = refs[2 * count + 3 : 2 * count + 3 + blocks]
    refs = refs[: 2 * count + 3] + refs[2 * count + 3 + blocks :]
    (
        tok_ref,
        att_ref,
        gain_ref,
        out_ref,
        d_att_ref,
        d_resid_ref,
        gain_grad_ref,
        keep_ref,
        send_ref,
        ogu,
        down,
        store,
        cot_ref,
        resid,
        norm,
        d_norm,
        total,
        hid,
        d_gate,
        d_up,
        sems_upper,
        sems_lower,
        sems_store,
    ) = refs[2 * count :]
    rows, width = tok_ref.shape
    hidden = down.shape[0]
    copies_upper = fetch_rows(index_ref[0], upper, ogu, sems_upper)
    copies_lower = fetch_rows(index_ref[0], lower, down, sems_lower)
    for copy in copies_upper + copies_lower:
        copy.start()
    for n, block in enumerate(cot_blocks):
        cot_ref[n * BLK : (n + 1) * BLK, :] = block[...]
    for copy in copies_upper:
        copy.wait()
    gain = gain_ref[...]
    row_step = 128
    tile = 512
    for block in range(rows // row_step):
        part = slice(block * row_step, (block + 1) * row_step)
        value = tok_ref[part, :] + jnp.dot(
            att_ref[part, :], ogu[:, :width], preferred_element_type=f32
        )
        resid[part, :] = value
        scale = lax.rsqrt(jnp.mean(value * value, axis=1, keepdims=True) + 1e-06)
        norm[part, :] = (value * scale * gain).astype(bf16)
    for copy in copies_lower:
        copy.wait()
    waits = []

    def put(first, last):
        half = store.shape[1] // 2
        for side, begin, end in ((0, first, min(last, half)), (1, max(first, half), last)):
            if begin < end:
                waits.extend(
                    scatter_rows(
                        index_ref[0],
                        count,
                        (store, begin, end),
                        (keep_ref.at[side], send_ref.at[side], begin - side * half),
                        sems_store,
                        len(waits),
                    )
                )

    for n in range(hidden // tile):
        here = slice(n * tile, (n + 1) * tile)
        gate_cols = slice(width + n * tile, width + (n + 1) * tile)
        up_cols = slice(width + hidden + n * tile, width + hidden + (n + 1) * tile)
        for block in range(rows // row_step):
            part = slice(block * row_step, (block + 1) * row_step)
            gate_pre = jnp.dot(norm[part, :], ogu[:, gate_cols], preferred_element_type=f32)
            up_pre = jnp.dot(norm[part, :], ogu[:, up_cols], preferred_element_type=f32)
            d_hidden = lax.dot_general(
                cot_ref[part, :], down[here, :], NT, preferred_element_type=f32
            )
            square = gate_pre * gate_pre
            bent = jnp.tanh(ROOT * gate_pre * (1.0 + CUBE * square))
            half = 0.5 + 0.5 * bent
            gelu = gate_pre * half
            slope = half + (0.5 * ROOT) * gate_pre * (1.0 - bent * bent) * (
                1.0 + (3.0 * CUBE) * square
            )
            low = (gelu * up_pre).astype(bf16)
            d_gate_low = (d_hidden * up_pre * slope).astype(bf16)
            d_up_low = (d_hidden * gelu).astype(bf16)
            hid[part, :] = low
            d_gate[part, :] = d_gate_low
            d_up[part, :] = d_up_low
            add = jnp.dot(low, down[here, :], preferred_element_type=f32)
            back = lax.dot_general(
                d_gate_low, ogu[:, gate_cols], NT, preferred_element_type=f32
            ) + lax.dot_general(d_up_low, ogu[:, up_cols], NT, preferred_element_type=f32)
            if n == 0:
                total[part, :] = resid[part, :] + add
                d_norm[part, :] = back
            else:
                total[part, :] = total[part, :] + add
                d_norm[part, :] = d_norm[part, :] + back
        store[:, gate_cols] = lax.dot_general(
            norm[...], d_gate[...], TN, preferred_element_type=f32
        ).astype(bf16)
        store[:, up_cols] = lax.dot_general(
            norm[...], d_up[...], TN, preferred_element_type=f32
        ).astype(bf16)
        put(width + n * tile, width + (n + 1) * tile)
        put(width + hidden + n * tile, width + hidden + (n + 1) * tile)
        part = lax.dot_general(
            hid[...], cot_ref[...], TN, preferred_element_type=f32
        ).astype(bf16)
        for low_row, low_col, row, size in down_pieces(width // count, hidden // count, width):
            for device in range(count):
                source = device * (hidden // count) + low_row
                if n * tile <= source < (n + 1) * tile:
                    source = source - n * tile
                    target = device * (width // count) + row
                    col = width + 2 * hidden + low_col[1]
                    store[target : target + size, col : col + LANE] = part[
                        source : source + size, low_col[0] : low_col[0] + LANE
                    ]
    gain_sum = jnp.zeros((1, width), f32)
    for block in range(rows // row_step):
        part = slice(block * row_step, (block + 1) * row_step)
        out_ref[part, :] = total[part, :].astype(bf16)
        value = resid[part, :]
        grad = d_norm[part, :]
        scale = lax.rsqrt(jnp.mean(value * value, axis=1, keepdims=True) + 1e-06)
        scaled = grad * gain
        inner = jnp.mean(value * scaled, axis=1, keepdims=True)
        d_value = (
            cot_ref[part, :].astype(f32)
            + scale * scaled
            - value * (scale * scale * scale * inner)
        )
        gain_sum = gain_sum + jnp.sum(grad * value * scale, axis=0, keepdims=True)
        d_resid_ref[part, :] = d_value
        d_low = d_value.astype(bf16)
        norm[part, :] = d_low
        d_att_ref[part, :] = lax.dot_general(
            d_low, ogu[:, :width], NT, preferred_element_type=f32
        ).astype(bf16)
    gain_grad_ref[...] = gain_sum
    store[:, :width] = lax.dot_general(
        att_ref[...], norm[...], TN, preferred_element_type=f32
    ).astype(bf16)
    put(0, width)
    put(width + 2 * hidden, store.shape[1])
    for wait in waits:
        wait.wait()


def scatter_rows(index, count, source, target, sems, at):
    store, begin, end = source
    keep, send, col = target
    rows = store.shape[0] // count
    cols = slice(col, col + end - begin)
    waits = []
    for device in range(count):
        other = index ^ device
        part = store.at[device * rows : (device + 1) * rows, begin:end]
        sem = sems.at[at + device]

        @pl.when(other % 2 == 0)
        def _():
            pltpu.make_async_copy(part, keep.at[other // 2, :, cols], sem).start()

        @pl.when(other % 2 == 1)
        def _():
            pltpu.make_async_copy(part, send.at[other // 2, :, cols], sem).start()

        waits.append(pltpu.make_async_copy(part, keep.at[0, :, cols], sem))
    return waits


def down_pieces(rows, tall, width):
    size = 16
    while tall % (2 * size) == 0 and rows % (2 * size) == 0:
        size *= 2
    pieces = []
    for q in range(tall * (width // LANE) // size):
        there = (q % (tall // size)) * size
        here = (q % (rows // size)) * size
        pieces.append((there, (q // (tall // size) * LANE, q // (rows // size) * LANE), here, size))
    return pieces


def by_parity(index, mine, other, put):
    rows = mine.shape[1]
    for parity in range(2):

        @pl.when(index % 2 == parity)
        def _():
            for k in range(mine.shape[0]):
                put((2 * k + parity) * rows, mine, k)
                put((2 * k + 1 - parity) * rows, other, k)


def unpack_three_kernel(index_ref, mine, other, *outs):
    rows, width = mine.shape[1], outs[0].shape[1]

    def put(row, array, k):
        for n in range(3):
            outs[n][row : row + rows, :] = array[k, :, n * width : (n + 1) * width].astype(f32)

    by_parity(index_ref[0], mine, other, put)


def unpack_joined_kernel(hidden, index_ref, mine, other, *refs):
    outs, spread = refs[:4], refs[4]
    rows, width = mine.shape[1], outs[0].shape[1]
    spans = ((0, width), (width, width + hidden), (width + hidden, width + 2 * hidden))
    base = width + 2 * hidden

    def put(row, array, k):
        for out, (first, last) in zip(outs[:3], spans):
            out[row : row + rows, :] = array[k, :, first:last].astype(f32)
        spread[row : row + rows, :] = array[k, :, base:].astype(f32)

    by_parity(index_ref[0], mine, other, put)
    tall = outs[3].shape[0]
    for there, (col_there, col_here), here, size in down_pieces(spread.shape[0], tall, width):
        outs[3][there : there + size, col_there : col_there + LANE] = spread[
            here : here + size, col_here : col_here + LANE
        ]


def unpack(kernel, index, mine, other, shapes, scratch, name):
    vmem = pl.BlockSpec(memory_space=pltpu.VMEM)
    return pl.pallas_call(
        kernel,
        out_shape=tuple(jax.ShapeDtypeStruct(shape, f32) for shape in shapes),
        in_specs=[pl.BlockSpec(memory_space=pltpu.SMEM), vmem, vmem],
        scratch_shapes=scratch,
        compiler_params=pltpu.CompilerParams(vmem_limit_bytes=VMEM_CAP),
        cost_estimate=LIGHT,
        name=name,
    )(index, mine, other)


def feed(index, upper, lower, tokens, attended, cotangent, gain):
    count = len(upper)
    rows, width = tokens.shape
    full_upper = (upper[0].shape[0] * count, upper[0].shape[1])
    full_lower = (lower[0].shape[0] * count, width)
    hidden = full_lower[0]
    columns = width + 3 * hidden
    vmem = pl.BlockSpec(memory_space=pltpu.VMEM)
    anywhere = pl.BlockSpec(memory_space=pl.ANY)
    tile = 512
    return pl.pallas_call(
        functools.partial(feed_kernel, count),
        out_shape=(
            jax.ShapeDtypeStruct((rows, width), bf16),
            jax.ShapeDtypeStruct((rows, width), bf16),
            jax.ShapeDtypeStruct((rows, width), f32),
            jax.ShapeDtypeStruct((1, width), f32),
            *[jax.ShapeDtypeStruct((2, count // 2, width // count, columns // 2), bf16)] * 2,
        ),
        in_specs=[pl.BlockSpec(memory_space=pltpu.SMEM)]
        + [anywhere] * (2 * count)
        + [vmem] * (3 + len(cotangent)),
        out_specs=(vmem,) * 4 + (anywhere,) * 2,
        scratch_shapes=[
            pltpu.VMEM(full_upper, bf16),
            pltpu.VMEM(full_lower, bf16),
            pltpu.VMEM((width, columns), bf16),
            pltpu.VMEM((rows, width), bf16),
            pltpu.VMEM((rows, width), f32),
            pltpu.VMEM((rows, width), bf16),
            pltpu.VMEM((rows, width), f32),
            pltpu.VMEM((rows, width), f32),
            pltpu.VMEM((rows, tile), bf16),
            pltpu.VMEM((rows, tile), bf16),
            pltpu.VMEM((rows, tile), bf16),
            pltpu.SemaphoreType.DMA((count,)),
            pltpu.SemaphoreType.DMA((count,)),
            pltpu.SemaphoreType.DMA(((2 * hidden // tile + 4) * count,)),
        ],
        compiler_params=pltpu.CompilerParams(vmem_limit_bytes=VMEM_CAP),
        cost_estimate=LIGHT,
        name="feed",
    )(index, *upper, *lower, tokens, attended, gain.reshape(1, width), *cotangent)


def bits_of(count):
    bits = count.bit_length() - 1
    assert 1 << bits == count
    return bits


def swap(value, axis, bit):
    count = lax.axis_size(axis)
    return lax.ppermute(value, axis, [(i, i ^ (1 << bit)) for i in range(count)])


def ordered(mine, other, index, bit, axis=0):
    upper = ((index >> bit) & 1) == 1
    return jnp.concatenate(
        [jnp.where(upper, other, mine), jnp.where(upper, mine, other)], axis=axis
    )


def gather_small(value, axis):
    index = lax.axis_index(axis)
    value = value[None]
    for bit in range(bits_of(lax.axis_size(axis))):
        value = ordered(value, swap(value, axis, bit), index, bit)
    return value


def first_swap(shard, axis):
    bit = bits_of(lax.axis_size(axis)) - 1
    return [(0, shard), (1 << bit, swap(shard, axis, bit))]


def other_swaps(parts, axis):
    for bit in reversed(range(bits_of(lax.axis_size(axis)) - 1)):
        parts = parts + [(j | (1 << bit), swap(part, axis, bit)) for j, part in parts]
    return [part for _, part in sorted(parts, key=lambda pair: pair[0])]


def after(anchor, part):
    j, array = part
    anchor, array = lax.optimization_barrier((anchor, array))
    return anchor, (j, array)


def add_low(left, right):
    return (left.astype(f32) + right.astype(f32)).astype(bf16)


def piece(value, index, dim=0):
    return lax.dynamic_index_in_dim(value, index, dim, keepdims=False)


def scatter_step(value, axis, bit, dim):
    own = (lax.axis_index(axis) >> bit) & 1
    other = swap(piece(value, 1 - own, dim), axis, bit)
    return add_low(piece(value, own, dim), other)


def rest_sum(value, axis):
    count = lax.axis_size(axis)
    index = lax.axis_index(axis)
    mine = index // 2
    total = piece(value, mine).astype(f32)
    for j in range(1, count // 2):
        pairs = [(i, ((i // 2) ^ j) * 2 + i % 2) for i in range(count)]
        total = total + lax.ppermute(piece(value, mine ^ j), axis, pairs).astype(f32)
    return total.astype(bf16)


def rest_gather(value, axis):
    count = lax.axis_size(axis)
    index = lax.axis_index(axis)
    whole = jnp.zeros((count // 2,) + value.shape, value.dtype)
    for j in range(count // 2):
        part = value
        if j:
            pairs = [(i, ((i // 2) ^ j) * 2 + i % 2) for i in range(count)]
            part = lax.ppermute(value, axis, pairs)
        whole = lax.dynamic_update_index_in_dim(whole, part, (index // 2) ^ j, 0)
    return whole


def fsdp_step(keep, send, bit):
    return add_low(keep, swap(send, "fsdp", bit))


def split_bit(value):
    value = value.reshape((value.shape[0] // 2, 2) + value.shape[1:])
    return value[:, 0], value[:, 1]


def parity_step(value, dim):
    count = lax.axis_size("ctx")
    shape = value.shape
    value = value.reshape(shape[:dim] + (count // 2, 2, shape[dim] // count) + shape[dim + 1 :])
    return scatter_step(value, "ctx", 0, dim + 1)


def rest_of_chain(total):
    total = yield rest_sum(total, "ctx")
    total = yield rest_gather(total, "ctx")
    yield (total, swap(total, "ctx", 0))


def single_chain(keep, send):
    bits = bits_of(lax.axis_size("fsdp"))
    total = yield fsdp_step(keep, send, 0)
    for bit in range(1, bits):
        keep, send = split_bit(total)
        total = yield fsdp_step(keep, send, bit)
    total = yield parity_step(total[0], 0)
    yield from rest_of_chain(total)


def double_chain(keep, send):
    bits = bits_of(lax.axis_size("fsdp"))
    other = swap(send, "fsdp", 0)
    left, right = yield (add_low(keep[0], other[0]), add_low(keep[1], other[1]))
    for bit in range(bits):
        if bit < bits - 1:
            left = fsdp_step(*split_bit(left), bit + 1)
        else:
            left = parity_step(left[0], 0)
        if bit == 0:
            right = parity_step(right, 1)
        else:
            right = fsdp_step(*split_bit(right), bit)
        left, right = yield (left, right)
    joined = jnp.concatenate([left, right[0]], axis=-1)
    yield from rest_of_chain(joined)


class Chain:
    def __init__(self, steps):
        self.steps = steps
        self.value = next(steps)

    def advance(self, value):
        self.value = self.steps.send(value)

    def finish(self):
        while True:
            try:
                self.advance(self.value)
            except StopIteration:
                return self.value


def gate(anchor, *chains):
    joined = lax.optimization_barrier((anchor,) + tuple(chain.value for chain in chains))
    for chain, value in zip(chains, joined[1:]):
        chain.advance(value)
    return joined[0]


def reduce_small(value, chain, joined, finish):
    fsdp_bits = bits_of(lax.axis_size("fsdp"))
    count = lax.axis_size("ctx")
    rows, width = value.shape
    value = value.reshape(2, count // 2, 2 * rows // (2 * count), width)
    value = gate(scatter_step(value, "fsdp", 0, 0), chain)
    value = gate(rest_sum(value, "ctx"), chain)
    value = add_low(value, swap(value, "ctx", 0))
    for bit in range(1, fsdp_bits):
        value = add_low(value, swap(value, "fsdp", bit))
    value, pieces = gate((value, joined.finish()), chain)
    done = finish(*pieces)
    whole = rest_gather(value, "ctx")
    whole = whole.reshape((rows // 2, width))
    whole, chain.value, done = lax.optimization_barrier((whole, chain.value, done))
    return ordered(whole, swap(whole, "fsdp", 0), lax.axis_index("fsdp"), 0), done


def local(
    byte_ids,
    doc_ids,
    rel_bucket,
    table,
    conv_w,
    score_w,
    gain_one,
    gain_two,
    rel_bias,
    query_master,
    key_master,
    value_master,
    out_master,
    gate_master,
    up_master,
    down_master,
    out_cotangent,
):
    ctx_count = lax.axis_size("ctx")
    ctx_index = lax.axis_index("ctx")
    seq_count, byte_count = byte_ids.shape
    total_bytes = byte_count * ctx_count
    width = table.shape[1]
    vocab = table.shape[0]
    hidden_width = gate_master.shape[1]
    levels, heads = rel_bias.shape
    share = ctx_count // seq_count
    assert share * seq_count == ctx_count and byte_count == 2 * BLK
    seq = ctx_index // share
    part = ctx_index % share
    near = [seq ^ slot for slot in range(seq_count)]
    lead = jnp.stack([share * other + part for other in near]).astype(jnp.int32)
    rows = seq_count * BLK

    qkv_low, down_low, ogu_low = pack(
        [[query_master, key_master, value_master], [down_master], [out_master, gate_master, up_master]]
    )
    both = jnp.stack([byte_ids, doc_ids], axis=1)
    both = gather_small(both, "ctx")
    both, qkv_low, down_low = lax.optimization_barrier((both, qkv_low, down_low))
    qkv_parts = first_swap(qkv_low, "fsdp")
    shard = lax.axis_index("fsdp")[None]
    shards = lax.axis_size("fsdp")

    def to_owner(block, slot):
        if slot == 0:
            return block
        pairs = []
        for c in range(ctx_count):
            pairs.append((c, ((c // share) ^ slot) * share + c % share))
        return lax.ppermute(block, "ctx", pairs)

    score_row = score_w.reshape(1, width)
    gain_row = gain_one.reshape(1, width)
    seq_row = seq[None]
    tokens, norm_one, norm_own, tokens_own, conv, mix, phases, known, barred = byte_forward(
        seq_row, lead, both, table, conv_w, score_row, gain_row, total_bytes
    )
    down_parts = first_swap(down_low, "fsdp")
    docs = piece(both[:, :, 1], seq, 1)
    low, high, buckets, rel = attention_tables(
        docs[:, 0], docs[:, 2 * BLK - 2], rel_bucket, rel_bias, lead
    )
    tokens, buckets, rel, out_cotangent = lax.optimization_barrier(
        (tokens, buckets, rel, out_cotangent)
    )
    tiles = make_tiles(buckets, rel)
    blocks = [to_owner(piece(out_cotangent, near[s], 1), s) for s in range(seq_count)]
    norm_one, crossed, down_crossed, tiles, ogu_low = lax.optimization_barrier(
        (norm_one, qkv_parts[1][1], down_parts[1][1], tiles, ogu_low)
    )
    qkv_parts[1] = (qkv_parts[1][0], crossed)
    down_parts[1] = (down_parts[1][0], down_crossed)
    qkv_parts = other_swaps(qkv_parts, "fsdp")
    queries, keys, values, qkv = project(shard, qkv_parts, norm_one, norm_own)
    ogu_parts = first_swap(ogu_low, "fsdp")
    down_parts = other_swaps(down_parts, "fsdp")
    queries, blocks = lax.optimization_barrier((queries, blocks))
    attended, attended_low, log_total = attend(
        lead, low, high, queries, keys, values, known, barred, tiles
    )

    attended_low, ogu_parts[1] = after(attended_low, ogu_parts[1])
    output, d_attended, d_resid, grad_gain_two, *grads = feed(
        shard,
        other_swaps(ogu_parts, "fsdp"),
        down_parts,
        tokens_own,
        attended_low,
        blocks,
        gain_two,
    )
    chain = Chain(double_chain(*grads))
    d_attended = gate(d_attended, chain)

    output = output.reshape(seq_count, BLK, width)
    arrived = [to_owner(output[s], s) for s in range(seq_count)]

    halves = []
    for group in range(GROUPS):
        if group:
            d_attended, arrived = gate((d_attended, arrived), chain)
            arrived = jnp.stack(arrived)
            output = jnp.stack([piece(arrived, seq ^ s) for s in range(seq_count)], axis=1)
        *grads, d_bias = attend_back(
            group,
            levels,
            lead,
            low,
            high,
            queries,
            keys,
            values,
            d_attended,
            attended,
            log_total,
            tiles,
            known,
            barred,
            buckets,
        )
        halves.append((grads, d_bias))
        d_attended, _ = lax.optimization_barrier((d_attended, grads[0]))
    d_bias = jnp.concatenate([half[1] for half in halves], axis=0)
    norm_own, halves = gate((norm_own, [half[0] for half in halves]), chain)
    keep, send, d_norm_one = project_back(shard, shards, lead, norm_one, norm_own, qkv, halves)
    qkv_chain = Chain(single_chain(keep, send))
    d_norm_one = gate(d_norm_one, qkv_chain, chain)

    vocab_rows = -(-vocab // 16) * 16
    d_resid = d_resid.reshape(seq_count, BLK, width)
    small = byte_backward(
        lead,
        phases,
        tokens,
        d_norm_one,
        d_resid,
        conv,
        mix,
        table,
        vocab_rows,
        conv_w,
        score_row,
        gain_row,
        total_bytes,
    )
    bias_grad = jnp.transpose(d_bias[:, : heads // GROUPS].reshape(heads, levels)).reshape(1, levels * heads)
    bias_grad = jnp.pad(bias_grad, ((0, 0), (0, width - levels * heads)))
    small = jnp.concatenate([small[: vocab_rows + 6], grad_gain_two, bias_grad], axis=0)
    small = jnp.pad(small, ((0, -small.shape[0] % (8 * ctx_count)), (0, 0))).astype(bf16)
    small = gate(small, qkv_chain, chain)
    shard_rows, tall = query_master.shape[0], down_master.shape[0]
    ctx_row = ctx_index[None]

    def finish(mine, other):
        return unpack(
            functools.partial(unpack_joined_kernel, hidden_width),
            ctx_row,
            mine,
            other,
            [(shard_rows, width)] + [(shard_rows, hidden_width)] * 2 + [(tall, width)],
            [pltpu.VMEM((shard_rows, hidden_width), f32)],
            "unpack_joined",
        )

    small, ffn_grads = reduce_small(small, qkv_chain, chain, finish)
    small = small.astype(f32)
    qkv_grads = unpack(
        unpack_three_kernel,
        ctx_row,
        *qkv_chain.finish(),
        [(shard_rows, width)] * 3,
        [],
        "unpack_three",
    )
    top = vocab_rows
    return (
        output,
        small[:vocab],
        small[top : top + 4],
        small[top + 4],
        small[top + 5],
        small[top + 6],
        small[top + 7, : levels * heads].reshape(levels, heads),
        *qkv_grads,
        *ffn_grads,
    )


def solution(mesh):
    placed = (
        P("fsdp", "ctx"),
        P("fsdp", "ctx"),
        P(),
        P(),
        P(),
        P(),
        P(),
        P(),
        P(),
        P("fsdp", None),
        P("fsdp", None),
        P("fsdp", None),
        P("fsdp", None),
        P("fsdp", None),
        P("fsdp", None),
        P("fsdp", None),
        P("ctx", "fsdp", None),
    )
    return jax.shard_map(
        local,
        mesh=mesh,
        in_specs=placed,
        out_specs=(
            P("ctx", "fsdp", None),
            P(),
            P(),
            P(),
            P(),
            P(),
            P(),
            P("fsdp", None),
            P("fsdp", None),
            P("fsdp", None),
            P("fsdp", None),
            P("fsdp", None),
            P("fsdp", None),
            P("fsdp", None),
        ),
        check_vma=False,
    )
```

```python
import functools

import jax
import jax.numpy as jnp
from jax import lax
from jax.experimental import pallas as pl
from jax.experimental.pallas import tpu as pltpu
from jax.sharding import PartitionSpec as P

f32 = jnp.float32
bf16 = jnp.bfloat16
LANE = 128
BLK = 128
VMEM_CAP = 60 * 1024 * 1024
HIGH = lax.Precision.HIGHEST
NT = (((1,), (1,)), ((), ()))
NN = (((1,), (0,)), ((), ()))
LIGHT = pl.CostEstimate(flops=1, transcendentals=0, bytes_accessed=1)


STEP = 16
NORM_ROWS = 128


def lane_iota(rows):
    return lax.broadcasted_iota(jnp.int32, (rows, LANE), 1)


def block_sum(value, width, lane):
    def ahead(v, n):
        return pltpu.roll(v, LANE - n, 1)

    def behind(v, n):
        return pltpu.roll(v, n, 1)

    if width == 1:
        return value
    if width == 3:
        lead = value + ahead(value, 1) + ahead(value, 2)
        phase = lane % 3
        return jnp.where(phase == 0, lead, jnp.where(phase == 1, behind(lead, 1), behind(lead, 2)))
    pair = value + jnp.where(lane % 2 == 0, ahead(value, 1), behind(value, 1))
    if width == 2:
        return pair
    return pair + jnp.where(lane % 4 < 2, ahead(pair, 2), behind(pair, 2))


def pick(value, lane_index):
    return value[:, lane_index : lane_index + 1]


def byte_forward_kernel(
    total_bytes,
    seq_ref,
    lead_ref,
    both_ref,
    table_ref,
    conv_w_ref,
    score_ref,
    gain_ref,
    tok_ref,
    norm_ref,
    norm_own_ref,
    tok_own_ref,
    conv_ref,
    mix_ref,
    ids_ref,
    known_ref,
    barred_ref,
    hi_ref,
    lo_ref,
    emb,
    flat,
    spread,
):
    groups = conv_ref.shape[1]
    width = conv_ref.shape[2]
    tiles = width // LANE
    token_count = norm_ref.shape[0]
    vocab_pad = hi_ref.shape[0]
    row_lanes = ids_ref.shape[1]
    seq = seq_ref[0]
    vocab = table_ref.shape[0]
    whole_rows = vocab // 128 * 128
    rest = jnp.zeros((vocab_pad - whole_rows, width), f32)
    rest_row = lax.broadcasted_iota(jnp.int32, rest.shape, 0)
    for row in range(whole_rows, vocab):
        rest = jnp.where(rest_row == row - whole_rows, table_ref[row : row + 1, :], rest)
    for here, value in ((0, table_ref[0:whole_rows, :]), (whole_rows, rest)):
        high = value.astype(bf16)
        hi_ref[here : here + value.shape[0], :] = high
        lo_ref[here : here + value.shape[0], :] = (value - high.astype(f32)).astype(bf16)
    lane_f = lane_iota(BLK).astype(f32)
    chunk_bytes = both_ref.shape[3]

    def lay(kind, first):
        for block in range(both_ref.shape[0]):
            row = both_ref[block, seq, kind : kind + 1, :].astype(f32)
            for half in range(chunk_bytes // LANE):
                part = jnp.broadcast_to(row[:, half * LANE : (half + 1) * LANE], (LANE, LANE))
                start = first + block * chunk_bytes + half * LANE
                spread[start : start + LANE, :] = jnp.transpose(part)

    lay(1, 0)
    for block in range(token_count // BLK):
        docs = spread[pl.ds(block * 2 * BLK, BLK, stride=2), :]
        same = docs == lane_f
        rows = slice(block * BLK, (block + 1) * BLK)
        known_ref[rows, :] = same.astype(bf16)
        barred_ref[rows, :] = jnp.where(same | (lane_f >= 16.0), 0.0, -1e30).astype(bf16)
    lay(0, 16)
    none = jnp.full((16, LANE), -1.0, f32)
    spread[0:16, :] = none
    tail = spread.shape[0] - total_bytes - 16
    spread[total_bytes + 16 :, :] = jnp.full((tail, LANE), -1.0, f32)
    lane_g = lane_iota(groups).astype(f32)
    for r in range(15):
        here = spread[pl.ds(13 + r, row_lanes, stride=12), :]
        turned = [
            jnp.transpose(here[n * LANE : (n + 1) * LANE, :])[0:1, :]
            for n in range(row_lanes // LANE)
        ]
        ids_ref[r : r + 1, :] = jnp.concatenate(turned, axis=1)
        onehot = jnp.concatenate(
            [
                (here[0:groups, :] == lane_g + n * LANE).astype(bf16)
                for n in range(vocab_pad // LANE)
            ],
            axis=1,
        )
        emb[r] = jnp.dot(onehot, hi_ref[...], preferred_element_type=f32) + jnp.dot(
            onehot, lo_ref[...], preferred_element_type=f32
        )
    ids_ref[15:16, :] = jnp.full((1, row_lanes), -1.0, f32)
    lane = lane_iota(STEP)

    def chunk(i, masked):
        r0 = pl.multiple_of(i * STEP, STEP)
        rows = pl.ds(r0, STEP)
        sums = [jnp.zeros((STEP, LANE), f32) for _ in range(12)]
        for tile in range(tiles):
            cols = slice(tile * LANE, (tile + 1) * LANE)
            taps = [conv_w_ref[k : k + 1, cols] for k in range(4)]
            piece = [emb[r, rows, cols] for r in range(15)]
            score = score_ref[0:1, cols]
            for r in range(12):
                value = (
                    piece[r] * taps[0]
                    + piece[r + 1] * taps[1]
                    + piece[r + 2] * taps[2]
                    + piece[r + 3] * taps[3]
                )
                if masked:
                    group = r0 + lax.broadcasted_iota(jnp.int32, (STEP, LANE), 0)
                    value = jnp.where(group * 12 + r < total_bytes, value, 0.0)
                conv_ref[r, rows, cols] = value
                sums[r] = sums[r] + value * score
        packed = jnp.zeros((STEP, LANE), f32)
        for r in range(12):
            packed = jnp.where(lane == r, jnp.sum(sums[r], axis=1, keepdims=True), packed)
        logits = [block_sum(packed, b, lane) * (1.0 / b) for b in range(1, 5)]
        best = jnp.maximum(jnp.maximum(logits[0], logits[1]), jnp.maximum(logits[2], logits[3]))
        parts = [jnp.exp(value - best) for value in logits]
        total = parts[0] + parts[1] + parts[2] + parts[3]
        mix = [part / total for part in parts]
        for b in range(4):
            mix_ref[b, rows, :] = mix[b]
        half_one = mix[0] * 0.5
        pair_two = block_sum(mix[1], 2, lane) * 0.25
        single_three = mix[2] * (1.0 / 6.0)
        pair_three = block_sum(mix[2], 2, lane) * (1.0 / 6.0)
        pair_four = block_sum(mix[3], 2, lane) * 0.125
        coef_one = [pick(half_one, r) for r in range(12)]
        coef_two = [pick(pair_two, 2 * j) for j in range(6)]
        coef_four = [pick(pair_four, 2 * j) for j in range(6)]
        coef_three = []
        for j in range(6):
            if j % 3 == 1:
                coef_three.append((pick(single_three, 2 * j), pick(single_three, 2 * j + 1)))
            else:
                coef_three.append((pick(pair_three, 2 * j), None))
        for tile in range(tiles):
            cols = slice(tile * LANE, (tile + 1) * LANE)
            conv = [conv_ref[r, rows, cols] for r in range(12)]
            two = [conv[2 * j] + conv[2 * j + 1] for j in range(6)]
            three = [conv[3 * q] + conv[3 * q + 1] + conv[3 * q + 2] for q in range(4)]
            four = [two[2 * q] + two[2 * q + 1] for q in range(3)]
            for j in range(6):
                a, b = 2 * j, 2 * j + 1
                value = coef_one[a] * conv[a] + coef_one[b] * conv[b]
                value = value + coef_two[j] * two[j] + coef_four[j] * four[j // 2]
                value = value + coef_three[j][0] * three[a // 3]
                if j % 3 == 1:
                    value = value + coef_three[j][1] * three[b // 3]
                flat[tile, pl.ds(6 * r0 + j, STEP, stride=6), :] = value

    whole = (total_bytes // 12) // STEP

    def plain(i, carry):
        chunk(i, False)
        return carry

    lax.fori_loop(0, whole, plain, 0)
    for i in range(whole, groups // STEP):
        chunk(i, True)

    def norm(i, carry):
        rows = pl.ds(pl.multiple_of(i * NORM_ROWS, NORM_ROWS), NORM_ROWS)
        value = jnp.concatenate([flat[tile, rows, :] for tile in range(tiles)], axis=1)
        tok_ref[rows, :] = value
        scale = lax.rsqrt(jnp.mean(value * value, axis=1, keepdims=True) + 1e-06)
        norm_ref[rows, :] = (value * scale * gain_ref[...]).astype(bf16)
        return carry

    lax.fori_loop(0, token_count // NORM_ROWS, norm, 0)
    for slot in range(norm_own_ref.shape[0] // BLK):
        start = pl.multiple_of(lead_ref[slot] * BLK, BLK)
        norm_own_ref[slot * BLK : (slot + 1) * BLK, :] = norm_ref[pl.ds(start, BLK), :]
        tok_own_ref[slot * BLK : (slot + 1) * BLK, :] = tok_ref[pl.ds(start, BLK), :]


def byte_forward(seq, lead, both, table, conv_w, score_w, gain_one, total_bytes):
    width = conv_w.shape[1]
    token_count = total_bytes // 2
    least = -(-total_bytes // 12)
    groups = -(-least // 16) * 16
    row_lanes = -(-least // LANE) * LANE
    vocab_pad = -(-table.shape[0] // LANE) * LANE
    smem = pl.BlockSpec(memory_space=pltpu.SMEM)
    vmem = pl.BlockSpec(memory_space=pltpu.VMEM)
    return pl.pallas_call(
        functools.partial(byte_forward_kernel, total_bytes),
        out_shape=(
            jax.ShapeDtypeStruct((token_count, width), f32),
            jax.ShapeDtypeStruct((token_count, width), bf16),
            jax.ShapeDtypeStruct((lead.shape[0] * BLK, width), bf16),
            jax.ShapeDtypeStruct((lead.shape[0] * BLK, width), f32),
            jax.ShapeDtypeStruct((12, groups, width), f32),
            jax.ShapeDtypeStruct((4, groups, LANE), f32),
            jax.ShapeDtypeStruct((16, row_lanes), f32),
            jax.ShapeDtypeStruct((token_count, LANE), bf16),
            jax.ShapeDtypeStruct((token_count, LANE), bf16),
        ),
        in_specs=[smem, smem] + [vmem] * 5,
        scratch_shapes=[
            pltpu.VMEM((vocab_pad, width), bf16),
            pltpu.VMEM((vocab_pad, width), bf16),
            pltpu.VMEM((15, groups, width), f32),
            pltpu.VMEM((width // LANE, 6 * groups, LANE), f32),
            pltpu.VMEM((12 * row_lanes + 32, LANE), f32),
        ],
        compiler_params=pltpu.CompilerParams(vmem_limit_bytes=VMEM_CAP),
        cost_estimate=LIGHT,
        name="byte_forward",
    )(
        seq,
        lead,
        both,
        table,
        conv_w,
        score_w,
        gain_one,
    )


def byte_backward_kernel(
    total_bytes,
    first_ref,
    ids_ref,
    tok_ref,
    dnorm_ref,
    dres_ref,
    conv_ref,
    mix_ref,
    table_ref,
    conv_w_ref,
    score_ref,
    gain_ref,
    out_ref,
    dtok,
    dconv,
    onehot,
):
    groups = conv_ref.shape[1]
    width = conv_ref.shape[2]
    tiles = width // LANE
    token_count = dnorm_ref.shape[0]
    vocab_rows = onehot.shape[0]
    lanes = ids_ref.shape[1]
    gain = gain_ref[...]

    def norm_back(i, acc):
        rows = pl.ds(pl.multiple_of(i * NORM_ROWS, NORM_ROWS), NORM_ROWS)
        value = tok_ref[rows, :]
        grad = dnorm_ref[rows, :]
        scale = lax.rsqrt(jnp.mean(value * value, axis=1, keepdims=True) + 1e-06)
        grad_gain = grad * gain
        inner = jnp.mean(value * grad_gain, axis=1, keepdims=True)
        total = 0.5 * scale * grad_gain - value * (0.5 * scale * scale * scale * inner)
        for tile in range(tiles):
            dtok[tile, rows, :] = total[:, tile * LANE : (tile + 1) * LANE]
        product = (grad * value * scale).reshape(NORM_ROWS // 8, 8, width)
        return acc + jnp.sum(product, axis=0)

    gain_acc = lax.fori_loop(0, token_count // NORM_ROWS, norm_back, jnp.zeros((8, width), f32))
    rest = dtok.shape[1] - token_count
    dtok[:, token_count:, :] = jnp.zeros((tiles, rest, LANE), f32)
    for slot in range(dres_ref.shape[0]):
        start = pl.multiple_of(first_ref[slot] * BLK, BLK)

        def add(i, carry, slot=slot, start=start):
            r = pl.multiple_of(i * 32, 32)
            rows = pl.ds(pl.multiple_of(start + r, 32), 32)
            more = 0.5 * dres_ref[slot, pl.ds(r, 32), :]
            for tile in range(tiles):
                dtok[tile, rows, :] = (
                    dtok[tile, rows, :] + more[:, tile * LANE : (tile + 1) * LANE]
                )
            return carry

        lax.fori_loop(0, BLK // 32, add, 0)
    vocab = lax.broadcasted_iota(jnp.int32, (vocab_rows, lanes), 0).astype(f32)
    for r in range(15):
        onehot[:, r * lanes : (r + 1) * lanes] = (vocab == ids_ref[r : r + 1, :]).astype(bf16)
    for r in range(12):
        dconv[r * lanes + groups : (r + 1) * lanes, :] = jnp.zeros((lanes - groups, width), bf16)
    lane = lane_iota(8)

    def scalars(r0):
        rows = pl.ds(r0, 8)
        one = [jnp.zeros((8, LANE), f32) for _ in range(12)]
        cross = [jnp.zeros((8, LANE), f32) for _ in range(6)]
        tri = [jnp.zeros((8, LANE), f32) for _ in range(8)]
        for tile in range(tiles):
            cols = slice(tile * LANE, (tile + 1) * LANE)
            conv = [conv_ref[r, rows, cols] for r in range(12)]
            grad = [dtok[tile, pl.ds(6 * r0 + j, 8, stride=6), :] for j in range(6)]
            two = [conv[2 * j] + conv[2 * j + 1] for j in range(6)]
            three = [conv[3 * q] + conv[3 * q + 1] + conv[3 * q + 2] for q in range(4)]
            for r in range(12):
                one[r] = one[r] + conv[r] * grad[r // 2]
            slot = 0
            for j in range(6):
                cross[j] = cross[j] + two[j ^ 1] * grad[j]
                for q in sorted({(2 * j) // 3, (2 * j + 1) // 3}):
                    tri[slot] = tri[slot] + three[q] * grad[j]
                    slot += 1
        inner_one = jnp.zeros((8, LANE), f32)
        for r in range(12):
            inner_one = jnp.where(lane == r, jnp.sum(one[r], axis=1, keepdims=True), inner_one)
        inner_cross = jnp.zeros((8, LANE), f32)
        for j in range(6):
            inner_cross = jnp.where(
                lane // 2 == j, jnp.sum(cross[j], axis=1, keepdims=True), inner_cross
            )
        inner_three = jnp.zeros((8, LANE), f32)
        slot = 0
        for j in range(6):
            for q in sorted({(2 * j) // 3, (2 * j + 1) // 3}):
                here = (lane // 2 == j) & (lane // 3 == q)
                inner_three = jnp.where(
                    here, jnp.sum(tri[slot], axis=1, keepdims=True), inner_three
                )
                slot += 1
        inner_two = block_sum(inner_one, 2, lane)
        mix = [mix_ref[b, rows, :] for b in range(4)]
        d_mix = [
            inner_one,
            inner_two * 0.5,
            inner_three * (1.0 / 3.0),
            (inner_two + inner_cross) * 0.25,
        ]
        mean = mix[0] * d_mix[0] + mix[1] * d_mix[1] + mix[2] * d_mix[2] + mix[3] * d_mix[3]
        d_logit = [mix[b] * (d_mix[b] - mean) for b in range(4)]
        d_logit = [jnp.where(lane < 12, value, 0.0) for value in d_logit]
        slope = d_logit[0]
        for b in range(2, 5):
            slope = slope + block_sum(d_logit[b - 1], b, lane) * (1.0 / b)
        pair_two = block_sum(mix[1], 2, lane) * 0.5
        single_three = mix[2] * (1.0 / 3.0)
        pair_three = block_sum(mix[2], 2, lane) * (1.0 / 3.0)
        pair_four = block_sum(mix[3], 2, lane) * 0.25
        return mix[0], pair_two, single_three, pair_three, pair_four, slope

    def spread(r0, coefs, tile, masked, score_acc):
        one, pair_two, single_three, pair_three, pair_four, slope = coefs
        rows = pl.ds(r0, 8)
        cols = slice(tile * LANE, (tile + 1) * LANE)
        grad = [dtok[tile, pl.ds(6 * r0 + j, 8, stride=6), :] for j in range(6)]
        score = score_ref[0:1, cols]
        four = [
            pick(pair_four, 4 * q) * grad[2 * q] + pick(pair_four, 4 * q + 2) * grad[2 * q + 1]
            for q in range(3)
        ]
        three = []
        for q in range(4):
            a = 3 * q
            if a % 2 == 0:
                three.append(
                    pick(pair_three, a) * grad[a // 2]
                    + pick(single_three, a + 2) * grad[a // 2 + 1]
                )
            else:
                three.append(
                    pick(single_three, a) * grad[a // 2]
                    + pick(pair_three, a + 1) * grad[a // 2 + 1]
                )
        result = []
        for r in range(12):
            weight = pick(slope, r)
            own = (pick(one, r) + pick(pair_two, r)) * grad[r // 2]
            value = own + three[r // 3] + four[r // 4] + weight * score
            score_acc = score_acc + weight * conv_ref[r, rows, cols]
            if masked:
                group = r0 + lax.broadcasted_iota(jnp.int32, (8, LANE), 0)
                value = jnp.where(group * 12 + r < total_bytes, value, 0.0)
            result.append(value)
        return result, score_acc

    def chunk(i, accs, masked):
        r0 = pl.multiple_of(i * 16, 16)
        r1 = pl.multiple_of(i * 16 + 8, 8)
        low_coefs = scalars(r0)
        high_coefs = scalars(r1)
        new = []
        for tile in range(tiles):
            cols = slice(tile * LANE, (tile + 1) * LANE)
            low, acc = spread(r0, low_coefs, tile, masked, accs[tile])
            high, acc = spread(r1, high_coefs, tile, masked, acc)
            new.append(acc)
            for r in range(12):
                both = jnp.concatenate([low[r], high[r]], axis=0).astype(bf16)
                dconv[pl.ds(pl.multiple_of(r * lanes + r0, 16), 16), cols] = both
        return tuple(new)

    accs = tuple(jnp.zeros((8, LANE), f32) for _ in range(tiles))
    whole = (total_bytes // 12) // 16
    accs = lax.fori_loop(0, whole, lambda i, a: chunk(i, a, False), accs)
    for i in range(whole, groups // 16):
        accs = chunk(i, accs, True)
    tail = [jnp.zeros((1, width), f32) for _ in range(8)]
    for k in range(4):
        part = jnp.dot(
            onehot[:, k * lanes : (k + 12) * lanes], dconv[...], preferred_element_type=f32
        )
        if k == 0:
            out_ref[0:vocab_rows, :] = part * conv_w_ref[k : k + 1, :]
        else:
            out_ref[0:vocab_rows, :] = out_ref[0:vocab_rows, :] + part * conv_w_ref[k : k + 1, :]
        vocab = table_ref.shape[0]
        whole_rows = vocab // 8 * 8
        tail[k] = jnp.sum(part[:whole_rows] * table_ref[0:whole_rows, :], axis=0, keepdims=True)
        for row in range(whole_rows, vocab):
            tail[k] = tail[k] + part[row : row + 1] * table_ref[row : row + 1, :]
    tail[4] = jnp.sum(jnp.concatenate(accs, axis=1), axis=0, keepdims=True)
    tail[5] = jnp.sum(gain_acc, axis=0, keepdims=True)
    out_ref[vocab_rows:, :] = jnp.concatenate(tail, axis=0)


def byte_backward(
    first,
    ids,
    tokens,
    d_norm,
    d_resid,
    conv,
    mix,
    table,
    vocab_rows,
    conv_w,
    score_w,
    gain_one,
    total_bytes,
):
    width = conv.shape[2]
    groups = conv.shape[1]
    lanes = ids.shape[1]
    return pl.pallas_call(
        functools.partial(byte_backward_kernel, total_bytes),
        out_shape=jax.ShapeDtypeStruct((vocab_rows + 8, width), f32),
        in_specs=[pl.BlockSpec(memory_space=pltpu.SMEM)]
        + [pl.BlockSpec(memory_space=pltpu.VMEM)] * 10,
        scratch_shapes=[
            pltpu.VMEM((width // LANE, 6 * groups, LANE), f32),
            pltpu.VMEM((12 * lanes, width), bf16),
            pltpu.VMEM((vocab_rows, 15 * lanes), bf16),
        ],
        compiler_params=pltpu.CompilerParams(vmem_limit_bytes=VMEM_CAP),
        cost_estimate=LIGHT,
        name="byte_backward",
    )(
        first,
        ids,
        tokens,
        d_norm,
        d_resid,
        conv,
        mix,
        table,
        conv_w,
        score_w,
        gain_one,
    )


def head_mask(value, head):
    half = value.shape[1] // 2
    lane = lax.broadcasted_iota(jnp.int32, value.shape, 1)
    keep = lane < half if head == 0 else lane >= half
    return jnp.where(keep, value, jnp.zeros_like(value))


def two_heads(value):
    return jnp.concatenate([head_mask(value, 0), head_mask(value, 1)], axis=0)


def bucket_row(buckets_ref, n, reach):
    row = buckets_ref.shape[0] // 2 - 1 - (n - reach)
    return jnp.concatenate([buckets_ref[row : row + 1, :], buckets_ref[row + 1 : row + 2, :]], axis=1)


def bias_tiles(buckets_ref, rel, tiles):
    count = tiles.shape[1]
    levels = rel.shape[1]
    level = lax.broadcasted_iota(jnp.int32, (levels, 2 * BLK), 0)
    for n in range(count):
        onehot = (level == bucket_row(buckets_ref, n, count // 2)).astype(f32)
        values = lax.dot_general(rel, onehot, NN, precision=HIGH, preferred_element_type=f32)
        for head in range(2 * tiles.shape[0]):
            spread = jnp.broadcast_to(values[head : head + 1, :], (BLK, 2 * BLK))
            rolled = pltpu.roll(spread, BLK + 1, 1, stride=1, stride_axis=0)
            half = slice(head % 2 * BLK, head % 2 * BLK + BLK)
            tiles[head // 2, n, :, half] = rolled[:, :BLK]


def fold_rows(value, op):
    return op(value.reshape(BLK // 8, 8, value.shape[1]), axis=0)


def attend_kernel(
    lead_ref,
    low_ref,
    high_ref,
    q_ref,
    k_ref,
    v_ref,
    known,
    barred,
    tiles,
    out_ref,
    low_out_ref,
    log_ref,
    v_turned,
    *scratch,
):
    pairs = tiles.shape[0]
    held, accum = scratch[:pairs], scratch[pairs:]
    reach = tiles.shape[1] // 2
    slots = q_ref.shape[0] // BLK
    half = BLK // 2
    v_turned[...] = jnp.transpose(v_ref[...])
    cols = [slice(p * BLK, (p + 1) * BLK) for p in range(pairs)]
    for slot in range(slots):
        block = lead_ref[slot]
        first = low_ref[slot]
        last = high_ref[slot]
        base = pl.multiple_of(block * BLK, BLK)
        own = slice(slot * BLK, (slot + 1) * BLK)
        bar = barred[pl.ds(base, BLK), :]
        bar = jnp.concatenate([bar, bar], axis=0)
        q_full = [jnp.concatenate([two_heads(q_ref[own, c]), bar], axis=1) for c in cols]

        def score(kb, best):
            rows = pl.ds(pl.multiple_of(kb * BLK, BLK), BLK)
            mark = known[rows, :]
            values = [
                lax.dot_general(
                    jnp.concatenate([k_ref[rows, c], mark], axis=1),
                    q_full[p],
                    NT,
                    preferred_element_type=f32,
                )
                + tiles[p, kb - block + reach]
                for p, c in enumerate(cols)
            ]
            for p in range(pairs):
                held[p][kb - first] = values[p]
            return tuple(jnp.maximum(best[p], fold_rows(values[p], jnp.max)) for p in range(pairs))

        lowest = jnp.full((8, 2 * BLK), -3e38, f32)
        best = lax.fori_loop(first, last, score, (lowest,) * pairs)
        best = [jnp.max(value, axis=0, keepdims=True) for value in best]
        for p in range(pairs):
            accum[p][...] = jnp.zeros((BLK, 2 * BLK), f32)

        def gather(kb, total):
            keys = pl.ds(pl.multiple_of(kb * BLK, BLK), BLK)
            weights = [jnp.exp(held[p][kb - first] - best[p]) for p in range(pairs)]
            products = [
                jnp.dot(v_turned[c, keys], weights[p].astype(bf16), preferred_element_type=f32)
                for p, c in enumerate(cols)
            ]
            for p in range(pairs):
                accum[p][...] += products[p]
            return tuple(total[p] + fold_rows(weights[p], jnp.sum) for p in range(pairs))

        none = jnp.zeros((8, 2 * BLK), f32)
        total = lax.fori_loop(first, last, gather, (none,) * pairs)
        for p in range(pairs):
            row_total = jnp.sum(total[p], axis=0, keepdims=True)
            value = accum[p][...] / row_total
            both = jnp.concatenate([value[:half, :BLK], value[half:, BLK:]], axis=0)
            both = jnp.transpose(both)
            out_ref[own, cols[p]] = both
            low_out_ref[own, cols[p]] = both.astype(bf16)
            log_ref[0, slot, p : p + 1, :] = best[p] + jnp.log(row_total)


def tiles_kernel(buckets_ref, rel_ref, tiles):
    bias_tiles(buckets_ref, rel_ref[0], tiles)


def make_tiles(buckets, rel):
    groups, heads, levels = rel.shape
    shape = (heads // 2, 2 * (buckets.shape[0] // 4) + 1, BLK, 2 * BLK)
    return pl.pallas_call(
        tiles_kernel,
        grid=(groups,),
        out_shape=jax.ShapeDtypeStruct((groups * shape[0],) + shape[1:], f32),
        in_specs=[
            pl.BlockSpec(buckets.shape, lambda i: (0, 0)),
            pl.BlockSpec((1, heads, levels), lambda i: (i, 0, 0)),
        ],
        out_specs=pl.BlockSpec(shape, lambda i: (i, 0, 0, 0)),
        compiler_params=pltpu.CompilerParams(vmem_limit_bytes=VMEM_CAP),
        cost_estimate=LIGHT,
        name="bias_tiles",
    )(buckets, rel)


def attend(lead, low, high, q, k, v, known, barred, tiles):
    rows, width = q.shape
    keys = k.shape[0]
    pairs = tiles.shape[0] // GROUPS
    groups = GROUPS
    blocks = keys // BLK
    slots = rows // BLK
    count = tiles.shape[1]
    smem = pl.BlockSpec(memory_space=pltpu.SMEM)

    def cols(size):
        return pl.BlockSpec((size, pairs * BLK), lambda i: (0, i))

    def whole(array):
        return pl.BlockSpec(array.shape, lambda i: (0,) * array.ndim)

    return pl.pallas_call(
        attend_kernel,
        grid=(groups,),
        out_shape=(
            jax.ShapeDtypeStruct((rows, width), f32),
            jax.ShapeDtypeStruct((rows, width), bf16),
            jax.ShapeDtypeStruct((groups, slots, pairs, 2 * BLK), f32),
        ),
        in_specs=[
            smem,
            smem,
            smem,
            cols(rows),
            cols(keys),
            cols(keys),
            whole(known),
            whole(barred),
            pl.BlockSpec((pairs, count, BLK, 2 * BLK), lambda i: (i, 0, 0, 0)),
        ],
        out_specs=(
            cols(rows),
            cols(rows),
            pl.BlockSpec((1, slots, pairs, 2 * BLK), lambda i: (i, 0, 0, 0)),
        ),
        scratch_shapes=[pltpu.VMEM((pairs * BLK, keys), bf16)]
        + [pltpu.VMEM((blocks, BLK, 2 * BLK), f32)] * pairs
        + [pltpu.VMEM((BLK, 2 * BLK), f32)] * pairs,
        compiler_params=pltpu.CompilerParams(vmem_limit_bytes=VMEM_CAP),
        cost_estimate=LIGHT,
        name="attend",
    )(lead, low, high, q, k, v, known, barred, tiles)


def attend_back_kernel(
    lead_ref,
    low_ref,
    high_ref,
    q_ref,
    k_ref,
    v_ref,
    g_ref,
    out_ref,
    log_ref,
    tiles,
    known,
    barred,
    buckets_ref,
    dq_ref,
    dk_ref,
    dv_ref,
    dbias_ref,
    k_turned,
    *scratch,
):
    pairs, count = tiles.shape[:2]
    dk_acc, dv_acc, d_tiles, dq_acc = (scratch[n * pairs : (n + 1) * pairs] for n in range(4))
    reach = count // 2
    slots = q_ref.shape[0] // BLK
    half = BLK // 2
    k_turned[...] = jnp.transpose(k_ref[...])
    for p in range(pairs):
        dk_acc[p][...] = jnp.zeros(dk_acc[p].shape, f32)
        dv_acc[p][...] = jnp.zeros(dv_acc[p].shape, f32)
        d_tiles[p][...] = jnp.zeros(d_tiles[p].shape, f32)
    sub = lax.broadcasted_iota(jnp.int32, (8, BLK), 0)
    chooser = jnp.where((lane_iota(8) // half) == sub, 1.0, 0.0).astype(bf16)
    cols = [slice(p * BLK, (p + 1) * BLK) for p in range(pairs)]
    for slot in range(slots):
        block = lead_ref[slot]
        first = low_ref[slot]
        last = high_ref[slot]
        base = pl.multiple_of(block * BLK, BLK)
        own = slice(slot * BLK, (slot + 1) * BLK)
        bar = barred[pl.ds(base, BLK), :]
        bar = jnp.concatenate([bar, bar], axis=0)
        q_two = [two_heads(q_ref[own, c]) for c in cols]
        q_full = [jnp.concatenate([value, bar], axis=1) for value in q_two]
        g_two = [two_heads(g_ref[own, c]) for c in cols]
        deltas = []
        for p, c in enumerate(cols):
            product = g_ref[own, c].astype(f32) * out_ref[own, c]
            high_part = product.astype(bf16)
            low_part = (product - high_part.astype(f32)).astype(bf16)
            delta = lax.dot_general(
                chooser, high_part, NT, preferred_element_type=f32
            ) + lax.dot_general(chooser, low_part, NT, preferred_element_type=f32)
            deltas.append(jnp.concatenate([delta[0:1, :], delta[1:2, :]], axis=1))
            dq_acc[p][...] = jnp.zeros((BLK, 2 * BLK), f32)
        logs = [log_ref[0, slot, p : p + 1, :] for p in range(pairs)]

        def step(kb, carry):
            rows = pl.ds(pl.multiple_of(kb * BLK, BLK), BLK)
            at = kb - block + reach
            mark = known[rows, :]
            values = [
                lax.dot_general(
                    jnp.concatenate([k_ref[rows, c], mark], axis=1),
                    q_full[p],
                    NT,
                    preferred_element_type=f32,
                )
                for p, c in enumerate(cols)
            ]
            d_probs = [
                lax.dot_general(v_ref[rows, c], g_two[p], NT, preferred_element_type=f32)
                for p, c in enumerate(cols)
            ]
            probs = [jnp.exp(values[p] + (tiles[p, at] - logs[p])) for p in range(pairs)]
            d_scores = [probs[p] * (d_probs[p] - deltas[p]) for p in range(pairs)]
            lows = [value.astype(bf16) for value in d_scores]
            dvs = [
                jnp.dot(probs[p].astype(bf16), g_two[p], preferred_element_type=f32)
                for p in range(pairs)
            ]
            dks = [jnp.dot(lows[p], q_two[p], preferred_element_type=f32) for p in range(pairs)]
            dqs = [
                jnp.dot(k_turned[c, rows], lows[p], preferred_element_type=f32)
                for p, c in enumerate(cols)
            ]
            for p in range(pairs):
                d_tiles[p][at] += d_scores[p]
                dv_acc[p][rows, :] += dvs[p]
                dk_acc[p][rows, :] += dks[p]
                dq_acc[p][...] += dqs[p]
            return carry

        lax.fori_loop(first, last, step, 0)
        for p in range(pairs):
            dq = dq_acc[p][...]
            both = jnp.concatenate([dq[:half, :BLK], dq[half:, BLK:]], axis=0)
            dq_ref[own, cols[p]] = jnp.transpose(both).astype(bf16)
    for p in range(pairs):
        dk_ref[:, cols[p]] = dk_acc[p][...].astype(bf16)
        dv_ref[:, cols[p]] = dv_acc[p][...].astype(bf16)
    levels = dbias_ref.shape[2]
    level = lax.broadcasted_iota(jnp.int32, (levels, 2 * BLK), 0)
    pad = jnp.zeros((BLK, BLK), f32)
    mirror = (
        lax.broadcasted_iota(jnp.int32, (BLK, BLK), 0)
        + lax.broadcasted_iota(jnp.int32, (BLK, BLK), 1)
        == BLK - 1
    ).astype(bf16)
    total = jnp.zeros((8, levels), f32)
    for n in range(count):
        onehot = (level == bucket_row(buckets_ref, n, reach)).astype(f32)
        sums = []
        for p in range(pairs):
            flipped = jnp.dot(mirror, d_tiles[p][n].astype(bf16), preferred_element_type=f32)
            for head in range(2):
                wide = jnp.concatenate([flipped[:, head * BLK : (head + 1) * BLK], pad], axis=1)
                rolled = pltpu.roll(wide, 0, 1, stride=1, stride_axis=0)
                sums.append(jnp.sum(rolled, axis=0, keepdims=True))
        rest = jnp.zeros((8 - 2 * pairs, 2 * BLK), f32)
        total = total + lax.dot_general(
            jnp.concatenate(sums + [rest], axis=0),
            onehot,
            NT,
            precision=HIGH,
            preferred_element_type=f32,
        )
    dbias_ref[0] = total


def attend_back(
    group, levels, lead, low, high, q, k, v, g, out, log, tiles, known, barred, buckets
):
    rows = q.shape[0]
    keys = k.shape[0]
    slots, pairs = log.shape[1:3]
    count = tiles.shape[1]
    width = pairs * BLK
    smem = pl.BlockSpec(memory_space=pltpu.SMEM)

    def cols(size):
        return pl.BlockSpec((size, width), lambda i: (0, group))

    def whole(array):
        return pl.BlockSpec(array.shape, lambda i: (0,) * array.ndim)

    def fresh(*shape):
        return pl.BlockSpec(shape, lambda i: (0,) * len(shape))

    return pl.pallas_call(
        attend_back_kernel,
        grid=(1,),
        out_shape=(
            jax.ShapeDtypeStruct((rows, width), bf16),
            jax.ShapeDtypeStruct((keys, width), bf16),
            jax.ShapeDtypeStruct((keys, width), bf16),
            jax.ShapeDtypeStruct((1, 8, levels), f32),
        ),
        in_specs=[
            smem,
            smem,
            smem,
            cols(rows),
            cols(keys),
            cols(keys),
            cols(rows),
            cols(rows),
            pl.BlockSpec((1, slots, pairs, 2 * BLK), lambda i: (group, 0, 0, 0)),
            pl.BlockSpec((pairs, count, BLK, 2 * BLK), lambda i: (group, 0, 0, 0)),
            whole(known),
            whole(barred),
            whole(buckets),
        ],
        out_specs=(
            fresh(rows, width),
            fresh(keys, width),
            fresh(keys, width),
            fresh(1, 8, levels),
        ),
        scratch_shapes=[pltpu.VMEM((width, keys), bf16)]
        + [pltpu.VMEM((keys, BLK), f32)] * (2 * pairs)
        + [pltpu.VMEM((count, BLK, 2 * BLK), f32)] * pairs
        + [pltpu.VMEM((BLK, 2 * BLK), f32)] * pairs,
        compiler_params=pltpu.CompilerParams(vmem_limit_bytes=VMEM_CAP),
        cost_estimate=LIGHT,
        name="attend_back",
    )(lead, low, high, q, k, v, g, out, log, tiles, known, barred, buckets)


GROUPS = 2


def attention_tables(starts, ends, rel_bucket, rel_bias, lead):
    blocks = starts.shape[0]
    mine = (lead[:, None] == jnp.arange(blocks)[None, :]).astype(jnp.int32)
    own_start = jnp.sum(mine * starts[None, :], axis=1)
    own_end = jnp.sum(mine * ends[None, :], axis=1)
    low = jnp.sum((ends[None, :] < own_start[:, None]).astype(jnp.int32), axis=1)
    high = jnp.sum((starts[None, :] <= own_end[:, None]).astype(jnp.int32), axis=1)
    buckets = jnp.pad(jnp.flip(rel_bucket), (0, 1)).reshape(2 * blocks, BLK)
    levels, heads = rel_bias.shape
    rel = jnp.transpose(rel_bias).reshape(GROUPS, heads // GROUPS, levels)
    return low, high, buckets, rel


def pack_kernel(*refs):
    outs = [ref for ref in refs if ref.dtype == bf16]
    masters = [ref for ref in refs if ref.dtype == f32]
    at = 0
    for out in outs:
        col = 0
        while col < out.shape[1]:
            wide = masters[at].shape[1]
            out[:, col : col + wide] = masters[at][...].astype(bf16)
            col += wide
            at += 1


def pack(groups):
    steps = 1
    while all(group[0].shape[0] % (32 * steps) == 0 for group in groups) and steps < 4:
        steps *= 2

    def spec(array):
        return pl.BlockSpec((array.shape[0] // steps, array.shape[1]), lambda i: (i, 0))

    outs = tuple(
        jax.ShapeDtypeStruct((group[0].shape[0], sum(a.shape[1] for a in group)), bf16)
        for group in groups
    )
    arrays = [array for group in groups for array in group]
    return pl.pallas_call(
        pack_kernel,
        grid=(steps,),
        out_shape=outs,
        in_specs=[spec(array) for array in arrays],
        out_specs=tuple(spec(out) for out in outs),
        compiler_params=pltpu.CompilerParams(vmem_limit_bytes=VMEM_CAP),
        cost_estimate=LIGHT,
        name="pack",
    )(*arrays)


TN = (((0,), (0,)), ((), ()))


def fetch_rows(index, parts, whole, sems):
    rows = parts[0].shape[0]
    copies = []
    for j, part in enumerate(parts):
        start = pl.multiple_of((index ^ j) * rows, rows)
        copies.append(pltpu.make_async_copy(part, whole.at[pl.ds(start, rows), :], sems.at[j]))
    return copies


def project_kernel(count, index_ref, *refs):
    parts = refs[:count]
    norm_ref, own_ref, q_ref, k_ref, v_ref, whole_ref, whole, sems, done = refs[count:]
    width = norm_ref.shape[1]
    copies = fetch_rows(index_ref[0], parts, whole, sems)
    for copy in copies:
        copy.start()
    for copy in copies:
        copy.wait()
    keep = pltpu.make_async_copy(whole, whole_ref, done)
    keep.start()
    for out, rows, col in ((q_ref, own_ref, 0), (k_ref, norm_ref, 1), (v_ref, norm_ref, 2)):
        weight = whole[:, col * width : (col + 1) * width]
        for block in range(rows.shape[0] // 256):
            part = slice(block * 256, (block + 1) * 256)
            out[part, :] = jnp.dot(rows[part, :], weight, preferred_element_type=f32).astype(bf16)
    keep.wait()


def project(index, parts, norm, own):
    count = len(parts)
    width = norm.shape[1]
    full = (parts[0].shape[0] * count, parts[0].shape[1])
    vmem = pl.BlockSpec(memory_space=pltpu.VMEM)
    anywhere = pl.BlockSpec(memory_space=pl.ANY)
    return pl.pallas_call(
        functools.partial(project_kernel, count),
        out_shape=(
            jax.ShapeDtypeStruct(own.shape, bf16),
            jax.ShapeDtypeStruct(norm.shape, bf16),
            jax.ShapeDtypeStruct(norm.shape, bf16),
            jax.ShapeDtypeStruct(full, bf16),
        ),
        in_specs=[pl.BlockSpec(memory_space=pltpu.SMEM)] + [anywhere] * count + [vmem] * 2,
        out_specs=(vmem, vmem, vmem, anywhere),
        scratch_shapes=[
            pltpu.VMEM(full, bf16),
            pltpu.SemaphoreType.DMA((count,)),
            pltpu.SemaphoreType.DMA,
        ],
        compiler_params=pltpu.CompilerParams(vmem_limit_bytes=VMEM_CAP),
        cost_estimate=LIGHT,
        name="project",
    )(index, *parts, norm, own)


def project_back_kernel(count, halves, index_ref, lead_ref, norm_ref, own_ref, whole_ref, *refs):
    keep_ref, send_ref, dnorm_ref, grad_ref, sems = refs[3 * halves :]
    width = norm_ref.shape[1]
    part_width = width // halves
    for half in range(halves):
        for col in range(3):
            rows = own_ref if col == 0 else norm_ref
            here = slice(col * width + half * part_width, col * width + (half + 1) * part_width)
            grad_ref[:, here] = lax.dot_general(
                rows[...], refs[3 * half + col][...], TN, preferred_element_type=f32
            ).astype(bf16)
    waits = scatter_rows(
        index_ref[0], count, (grad_ref, 0, grad_ref.shape[1]), (keep_ref, send_ref, 0), sems, 0
    )
    for block in range(norm_ref.shape[0] // 256):
        part = slice(block * 256, (block + 1) * 256)
        total = None
        for half in range(halves):
            for col in (1, 2):
                here = slice(col * width + half * part_width, col * width + (half + 1) * part_width)
                term = lax.dot_general(
                    refs[3 * half + col][part, :],
                    whole_ref[:, here],
                    NT,
                    preferred_element_type=f32,
                )
                total = term if total is None else total + term
        dnorm_ref[part, :] = total
    for slot in range(own_ref.shape[0] // BLK):
        rows = pl.ds(pl.multiple_of(lead_ref[slot] * BLK, BLK), BLK)
        total = dnorm_ref[rows, :]
        for half in range(halves):
            total = total + lax.dot_general(
                refs[3 * half][slot * BLK : (slot + 1) * BLK, :],
                whole_ref[:, half * part_width : (half + 1) * part_width],
                NT,
                preferred_element_type=f32,
            )
        dnorm_ref[rows, :] = total
    for wait in waits:
        wait.wait()


def project_back(index, count, lead, norm, own, whole, halves):
    vmem = pl.BlockSpec(memory_space=pltpu.VMEM)
    anywhere = pl.BlockSpec(memory_space=pl.ANY)
    smem = pl.BlockSpec(memory_space=pltpu.SMEM)
    grads = [grad for half in halves for grad in half]
    part = jax.ShapeDtypeStruct((count // 2, whole.shape[0] // count, whole.shape[1]), bf16)
    return pl.pallas_call(
        functools.partial(project_back_kernel, count, len(halves)),
        out_shape=(part, part, jax.ShapeDtypeStruct(norm.shape, f32)),
        in_specs=[smem] * 2 + [vmem] * (3 + len(grads)),
        out_specs=(anywhere, anywhere, vmem),
        scratch_shapes=[pltpu.VMEM(whole.shape, bf16), pltpu.SemaphoreType.DMA((count,))],
        compiler_params=pltpu.CompilerParams(vmem_limit_bytes=VMEM_CAP),
        cost_estimate=LIGHT,
        name="project_back",
    )(index, lead, norm, own, whole, *grads)


ROOT = 0.7978845608028654
CUBE = 0.044715


def feed_kernel(count, index_ref, *refs):
    upper = refs[:count]
    lower = refs[count : 2 * count]
    blocks = refs[2 * count].shape[0] // BLK
    cot_blocks = refs[2 * count + 3 : 2 * count + 3 + blocks]
    refs = refs[: 2 * count + 3] + refs[2 * count + 3 + blocks :]
    (
        tok_ref,
        att_ref,
        gain_ref,
        out_ref,
        d_att_ref,
        d_resid_ref,
        gain_grad_ref,
        keep_ref,
        send_ref,
        ogu,
        down,
        store,
        cot_ref,
        resid,
        norm,
        d_norm,
        total,
        hid,
        d_gate,
        d_up,
        sems_upper,
        sems_lower,
        sems_store,
    ) = refs[2 * count :]
    rows, width = tok_ref.shape
    hidden = down.shape[0]
    copies_upper = fetch_rows(index_ref[0], upper, ogu, sems_upper)
    copies_lower = fetch_rows(index_ref[0], lower, down, sems_lower)
    for copy in copies_upper + copies_lower:
        copy.start()
    for n, block in enumerate(cot_blocks):
        cot_ref[n * BLK : (n + 1) * BLK, :] = block[...]
    for copy in copies_upper:
        copy.wait()
    gain = gain_ref[...]
    row_step = 128
    tile = 512
    for block in range(rows // row_step):
        part = slice(block * row_step, (block + 1) * row_step)
        value = tok_ref[part, :] + jnp.dot(
            att_ref[part, :], ogu[:, :width], preferred_element_type=f32
        )
        resid[part, :] = value
        scale = lax.rsqrt(jnp.mean(value * value, axis=1, keepdims=True) + 1e-06)
        norm[part, :] = (value * scale * gain).astype(bf16)
    for copy in copies_lower:
        copy.wait()
    waits = []

    def put(first, last):
        half = store.shape[1] // 2
        for side, begin, end in ((0, first, min(last, half)), (1, max(first, half), last)):
            if begin < end:
                waits.extend(
                    scatter_rows(
                        index_ref[0],
                        count,
                        (store, begin, end),
                        (keep_ref.at[side], send_ref.at[side], begin - side * half),
                        sems_store,
                        len(waits),
                    )
                )

    for n in range(hidden // tile):
        here = slice(n * tile, (n + 1) * tile)
        gate_cols = slice(width + n * tile, width + (n + 1) * tile)
        up_cols = slice(width + hidden + n * tile, width + hidden + (n + 1) * tile)
        for block in range(rows // row_step):
            part = slice(block * row_step, (block + 1) * row_step)
            gate_pre = jnp.dot(norm[part, :], ogu[:, gate_cols], preferred_element_type=f32)
            up_pre = jnp.dot(norm[part, :], ogu[:, up_cols], preferred_element_type=f32)
            d_hidden = lax.dot_general(
                cot_ref[part, :], down[here, :], NT, preferred_element_type=f32
            )
            square = gate_pre * gate_pre
            bent = jnp.tanh(ROOT * gate_pre * (1.0 + CUBE * square))
            half = 0.5 + 0.5 * bent
            gelu = gate_pre * half
            slope = half + (0.5 * ROOT) * gate_pre * (1.0 - bent * bent) * (
                1.0 + (3.0 * CUBE) * square
            )
            low = (gelu * up_pre).astype(bf16)
            d_gate_low = (d_hidden * up_pre * slope).astype(bf16)
            d_up_low = (d_hidden * gelu).astype(bf16)
            hid[part, :] = low
            d_gate[part, :] = d_gate_low
            d_up[part, :] = d_up_low
            add = jnp.dot(low, down[here, :], preferred_element_type=f32)
            back = lax.dot_general(
                d_gate_low, ogu[:, gate_cols], NT, preferred_element_type=f32
            ) + lax.dot_general(d_up_low, ogu[:, up_cols], NT, preferred_element_type=f32)
            if n == 0:
                total[part, :] = resid[part, :] + add
                d_norm[part, :] = back
            else:
                total[part, :] = total[part, :] + add
                d_norm[part, :] = d_norm[part, :] + back
        store[:, gate_cols] = lax.dot_general(
            norm[...], d_gate[...], TN, preferred_element_type=f32
        ).astype(bf16)
        store[:, up_cols] = lax.dot_general(
            norm[...], d_up[...], TN, preferred_element_type=f32
        ).astype(bf16)
        put(width + n * tile, width + (n + 1) * tile)
        put(width + hidden + n * tile, width + hidden + (n + 1) * tile)
        part = lax.dot_general(
            hid[...], cot_ref[...], TN, preferred_element_type=f32
        ).astype(bf16)
        for low_row, low_col, row, size in down_pieces(width // count, hidden // count, width):
            for device in range(count):
                source = device * (hidden // count) + low_row
                if n * tile <= source < (n + 1) * tile:
                    source = source - n * tile
                    target = device * (width // count) + row
                    col = width + 2 * hidden + low_col[1]
                    store[target : target + size, col : col + LANE] = part[
                        source : source + size, low_col[0] : low_col[0] + LANE
                    ]
    gain_sum = jnp.zeros((1, width), f32)
    for block in range(rows // row_step):
        part = slice(block * row_step, (block + 1) * row_step)
        out_ref[part, :] = total[part, :].astype(bf16)
        value = resid[part, :]
        grad = d_norm[part, :]
        scale = lax.rsqrt(jnp.mean(value * value, axis=1, keepdims=True) + 1e-06)
        scaled = grad * gain
        inner = jnp.mean(value * scaled, axis=1, keepdims=True)
        d_value = (
            cot_ref[part, :].astype(f32)
            + scale * scaled
            - value * (scale * scale * scale * inner)
        )
        gain_sum = gain_sum + jnp.sum(grad * value * scale, axis=0, keepdims=True)
        d_resid_ref[part, :] = d_value
        d_low = d_value.astype(bf16)
        norm[part, :] = d_low
        d_att_ref[part, :] = lax.dot_general(
            d_low, ogu[:, :width], NT, preferred_element_type=f32
        ).astype(bf16)
    gain_grad_ref[...] = gain_sum
    store[:, :width] = lax.dot_general(
        att_ref[...], norm[...], TN, preferred_element_type=f32
    ).astype(bf16)
    put(0, width)
    put(width + 2 * hidden, store.shape[1])
    for wait in waits:
        wait.wait()


def scatter_rows(index, count, source, target, sems, at):
    store, begin, end = source
    keep, send, col = target
    rows = store.shape[0] // count
    cols = slice(col, col + end - begin)
    waits = []
    for device in range(count):
        other = index ^ device
        part = store.at[device * rows : (device + 1) * rows, begin:end]
        sem = sems.at[at + device]

        @pl.when(other % 2 == 0)
        def _():
            pltpu.make_async_copy(part, keep.at[other // 2, :, cols], sem).start()

        @pl.when(other % 2 == 1)
        def _():
            pltpu.make_async_copy(part, send.at[other // 2, :, cols], sem).start()

        waits.append(pltpu.make_async_copy(part, keep.at[0, :, cols], sem))
    return waits


def down_pieces(rows, tall, width):
    size = 16
    while tall % (2 * size) == 0 and rows % (2 * size) == 0:
        size *= 2
    pieces = []
    for q in range(tall * (width // LANE) // size):
        there = (q % (tall // size)) * size
        here = (q % (rows // size)) * size
        pieces.append((there, (q // (tall // size) * LANE, q // (rows // size) * LANE), here, size))
    return pieces


def by_parity(index, mine, other, put):
    rows = mine.shape[1]
    for parity in range(2):

        @pl.when(index % 2 == parity)
        def _():
            for k in range(mine.shape[0]):
                put((2 * k + parity) * rows, mine, k)
                put((2 * k + 1 - parity) * rows, other, k)


def unpack_three_kernel(index_ref, mine, other, *outs):
    rows, width = mine.shape[1], outs[0].shape[1]

    def put(row, array, k):
        for n in range(3):
            outs[n][row : row + rows, :] = array[k, :, n * width : (n + 1) * width].astype(f32)

    by_parity(index_ref[0], mine, other, put)


def unpack_joined_kernel(hidden, index_ref, mine, other, *refs):
    outs, spread = refs[:4], refs[4]
    rows, width = mine.shape[1], outs[0].shape[1]
    spans = ((0, width), (width, width + hidden), (width + hidden, width + 2 * hidden))
    base = width + 2 * hidden

    def put(row, array, k):
        for out, (first, last) in zip(outs[:3], spans):
            out[row : row + rows, :] = array[k, :, first:last].astype(f32)
        spread[row : row + rows, :] = array[k, :, base:].astype(f32)

    by_parity(index_ref[0], mine, other, put)
    tall = outs[3].shape[0]
    for there, (col_there, col_here), here, size in down_pieces(spread.shape[0], tall, width):
        outs[3][there : there + size, col_there : col_there + LANE] = spread[
            here : here + size, col_here : col_here + LANE
        ]


def unpack(kernel, index, mine, other, shapes, scratch, name):
    vmem = pl.BlockSpec(memory_space=pltpu.VMEM)
    return pl.pallas_call(
        kernel,
        out_shape=tuple(jax.ShapeDtypeStruct(shape, f32) for shape in shapes),
        in_specs=[pl.BlockSpec(memory_space=pltpu.SMEM), vmem, vmem],
        scratch_shapes=scratch,
        compiler_params=pltpu.CompilerParams(vmem_limit_bytes=VMEM_CAP),
        cost_estimate=LIGHT,
        name=name,
    )(index, mine, other)


def feed(index, upper, lower, tokens, attended, cotangent, gain):
    count = len(upper)
    rows, width = tokens.shape
    full_upper = (upper[0].shape[0] * count, upper[0].shape[1])
    full_lower = (lower[0].shape[0] * count, width)
    hidden = full_lower[0]
    columns = width + 3 * hidden
    vmem = pl.BlockSpec(memory_space=pltpu.VMEM)
    anywhere = pl.BlockSpec(memory_space=pl.ANY)
    tile = 512
    return pl.pallas_call(
        functools.partial(feed_kernel, count),
        out_shape=(
            jax.ShapeDtypeStruct((rows, width), bf16),
            jax.ShapeDtypeStruct((rows, width), bf16),
            jax.ShapeDtypeStruct((rows, width), f32),
            jax.ShapeDtypeStruct((1, width), f32),
            *[jax.ShapeDtypeStruct((2, count // 2, width // count, columns // 2), bf16)] * 2,
        ),
        in_specs=[pl.BlockSpec(memory_space=pltpu.SMEM)]
        + [anywhere] * (2 * count)
        + [vmem] * (3 + len(cotangent)),
        out_specs=(vmem,) * 4 + (anywhere,) * 2,
        scratch_shapes=[
            pltpu.VMEM(full_upper, bf16),
            pltpu.VMEM(full_lower, bf16),
            pltpu.VMEM((width, columns), bf16),
            pltpu.VMEM((rows, width), bf16),
            pltpu.VMEM((rows, width), f32),
            pltpu.VMEM((rows, width), bf16),
            pltpu.VMEM((rows, width), f32),
            pltpu.VMEM((rows, width), f32),
            pltpu.VMEM((rows, tile), bf16),
            pltpu.VMEM((rows, tile), bf16),
            pltpu.VMEM((rows, tile), bf16),
            pltpu.SemaphoreType.DMA((count,)),
            pltpu.SemaphoreType.DMA((count,)),
            pltpu.SemaphoreType.DMA(((2 * hidden // tile + 4) * count,)),
        ],
        compiler_params=pltpu.CompilerParams(vmem_limit_bytes=VMEM_CAP),
        cost_estimate=LIGHT,
        name="feed",
    )(index, *upper, *lower, tokens, attended, gain.reshape(1, width), *cotangent)


def bits_of(count):
    bits = count.bit_length() - 1
    assert 1 << bits == count
    return bits


def swap(value, axis, bit):
    count = lax.axis_size(axis)
    return lax.ppermute(value, axis, [(i, i ^ (1 << bit)) for i in range(count)])


def ordered(mine, other, index, bit, axis=0):
    upper = ((index >> bit) & 1) == 1
    return jnp.concatenate(
        [jnp.where(upper, other, mine), jnp.where(upper, mine, other)], axis=axis
    )


def gather_small(value, axis):
    index = lax.axis_index(axis)
    value = value[None]
    for bit in range(bits_of(lax.axis_size(axis))):
        value = ordered(value, swap(value, axis, bit), index, bit)
    return value


def first_swap(shard, axis):
    bit = bits_of(lax.axis_size(axis)) - 1
    return [(0, shard), (1 << bit, swap(shard, axis, bit))]


def other_swaps(parts, axis):
    for bit in reversed(range(bits_of(lax.axis_size(axis)) - 1)):
        parts = parts + [(j | (1 << bit), swap(part, axis, bit)) for j, part in parts]
    return [part for _, part in sorted(parts, key=lambda pair: pair[0])]


def after(anchor, part):
    j, array = part
    anchor, array = lax.optimization_barrier((anchor, array))
    return anchor, (j, array)


def add_low(left, right):
    return (left.astype(f32) + right.astype(f32)).astype(bf16)


def piece(value, index, dim=0):
    return lax.dynamic_index_in_dim(value, index, dim, keepdims=False)


def scatter_step(value, axis, bit, dim):
    own = (lax.axis_index(axis) >> bit) & 1
    other = swap(piece(value, 1 - own, dim), axis, bit)
    return add_low(piece(value, own, dim), other)


def rest_sum(value, axis):
    count = lax.axis_size(axis)
    index = lax.axis_index(axis)
    mine = index // 2
    total = piece(value, mine).astype(f32)
    for j in range(1, count // 2):
        pairs = [(i, ((i // 2) ^ j) * 2 + i % 2) for i in range(count)]
        total = total + lax.ppermute(piece(value, mine ^ j), axis, pairs).astype(f32)
    return total.astype(bf16)


def rest_gather(value, axis):
    count = lax.axis_size(axis)
    index = lax.axis_index(axis)
    whole = jnp.zeros((count // 2,) + value.shape, value.dtype)
    for j in range(count // 2):
        part = value
        if j:
            pairs = [(i, ((i // 2) ^ j) * 2 + i % 2) for i in range(count)]
            part = lax.ppermute(value, axis, pairs)
        whole = lax.dynamic_update_index_in_dim(whole, part, (index // 2) ^ j, 0)
    return whole


def fsdp_step(keep, send, bit):
    return add_low(keep, swap(send, "fsdp", bit))


def split_bit(value):
    value = value.reshape((value.shape[0] // 2, 2) + value.shape[1:])
    return value[:, 0], value[:, 1]


def parity_step(value, dim):
    count = lax.axis_size("ctx")
    shape = value.shape
    value = value.reshape(shape[:dim] + (count // 2, 2, shape[dim] // count) + shape[dim + 1 :])
    return scatter_step(value, "ctx", 0, dim + 1)


def rest_of_chain(total):
    total = yield rest_sum(total, "ctx")
    total = yield rest_gather(total, "ctx")
    yield (total, swap(total, "ctx", 0))


def single_chain(keep, send):
    bits = bits_of(lax.axis_size("fsdp"))
    total = yield fsdp_step(keep, send, 0)
    for bit in range(1, bits):
        keep, send = split_bit(total)
        total = yield fsdp_step(keep, send, bit)
    total = yield parity_step(total[0], 0)
    yield from rest_of_chain(total)


def double_chain(keep, send):
    bits = bits_of(lax.axis_size("fsdp"))
    other = swap(send, "fsdp", 0)
    left, right = yield (add_low(keep[0], other[0]), add_low(keep[1], other[1]))
    for bit in range(bits):
        if bit < bits - 1:
            left = fsdp_step(*split_bit(left), bit + 1)
        else:
            left = parity_step(left[0], 0)
        if bit == 0:
            right = parity_step(right, 1)
        else:
            right = fsdp_step(*split_bit(right), bit)
        left, right = yield (left, right)
    joined = jnp.concatenate([left, right[0]], axis=-1)
    yield from rest_of_chain(joined)


class Chain:
    def __init__(self, steps):
        self.steps = steps
        self.value = next(steps)

    def advance(self, value):
        self.value = self.steps.send(value)

    def finish(self):
        while True:
            try:
                self.advance(self.value)
            except StopIteration:
                return self.value


def gate(anchor, *chains):
    joined = lax.optimization_barrier((anchor,) + tuple(chain.value for chain in chains))
    for chain, value in zip(chains, joined[1:]):
        chain.advance(value)
    return joined[0]


def reduce_small(value, chain, joined, finish):
    fsdp_bits = bits_of(lax.axis_size("fsdp"))
    count = lax.axis_size("ctx")
    rows, width = value.shape
    value = value.reshape(2, count // 2, 2 * rows // (2 * count), width)
    value = gate(scatter_step(value, "fsdp", 0, 0), chain)
    value = gate(rest_sum(value, "ctx"), chain)
    value = add_low(value, swap(value, "ctx", 0))
    for bit in range(1, fsdp_bits):
        value = add_low(value, swap(value, "fsdp", bit))
    value, pieces = gate((value, joined.finish()), chain)
    done = finish(*pieces)
    whole = rest_gather(value, "ctx")
    whole = whole.reshape((rows // 2, width))
    whole, chain.value, done = lax.optimization_barrier((whole, chain.value, done))
    return ordered(whole, swap(whole, "fsdp", 0), lax.axis_index("fsdp"), 0), done


def local(
    byte_ids,
    doc_ids,
    rel_bucket,
    table,
    conv_w,
    score_w,
    gain_one,
    gain_two,
    rel_bias,
    query_master,
    key_master,
    value_master,
    out_master,
    gate_master,
    up_master,
    down_master,
    out_cotangent,
):
    ctx_count = lax.axis_size("ctx")
    ctx_index = lax.axis_index("ctx")
    seq_count, byte_count = byte_ids.shape
    total_bytes = byte_count * ctx_count
    width = table.shape[1]
    vocab = table.shape[0]
    hidden_width = gate_master.shape[1]
    levels, heads = rel_bias.shape
    share = ctx_count // seq_count
    assert share * seq_count == ctx_count and byte_count == 2 * BLK
    seq = ctx_index // share
    part = ctx_index % share
    near = [seq ^ slot for slot in range(seq_count)]
    lead = jnp.stack([share * other + part for other in near]).astype(jnp.int32)
    rows = seq_count * BLK

    qkv_low, down_low, ogu_low = pack(
        [[query_master, key_master, value_master], [down_master], [out_master, gate_master, up_master]]
    )
    both = jnp.stack([byte_ids, doc_ids], axis=1)
    both = gather_small(both, "ctx")
    both, qkv_low, down_low = lax.optimization_barrier((both, qkv_low, down_low))
    qkv_parts = first_swap(qkv_low, "fsdp")
    shard = lax.axis_index("fsdp")[None]
    shards = lax.axis_size("fsdp")

    def to_owner(block, slot):
        if slot == 0:
            return block
        pairs = []
        for c in range(ctx_count):
            pairs.append((c, ((c // share) ^ slot) * share + c % share))
        return lax.ppermute(block, "ctx", pairs)

    score_row = score_w.reshape(1, width)
    gain_row = gain_one.reshape(1, width)
    seq_row = seq[None]
    tokens, norm_one, norm_own, tokens_own, conv, mix, phases, known, barred = byte_forward(
        seq_row, lead, both, table, conv_w, score_row, gain_row, total_bytes
    )
    down_parts = first_swap(down_low, "fsdp")
    docs = piece(both[:, :, 1], seq, 1)
    low, high, buckets, rel = attention_tables(
        docs[:, 0], docs[:, 2 * BLK - 2], rel_bucket, rel_bias, lead
    )
    blocks = [to_owner(piece(out_cotangent, near[s], 1), s) for s in range(seq_count)]
    tokens, buckets, rel = lax.optimization_barrier((tokens, buckets, rel))
    tiles = make_tiles(buckets, rel)
    norm_one, crossed, down_crossed, blocks, tiles, ogu_low = lax.optimization_barrier(
        (norm_one, qkv_parts[1][1], down_parts[1][1], blocks, tiles, ogu_low)
    )
    qkv_parts[1] = (qkv_parts[1][0], crossed)
    down_parts[1] = (down_parts[1][0], down_crossed)
    qkv_parts = other_swaps(qkv_parts, "fsdp")
    queries, keys, values, qkv = project(shard, qkv_parts, norm_one, norm_own)
    ogu_parts = first_swap(ogu_low, "fsdp")
    down_parts = other_swaps(down_parts, "fsdp")
    attended, attended_low, log_total = attend(
        lead, low, high, queries, keys, values, known, barred, tiles
    )

    attended_low, ogu_parts[1] = after(attended_low, ogu_parts[1])
    output, d_attended, d_resid, grad_gain_two, *grads = feed(
        shard,
        other_swaps(ogu_parts, "fsdp"),
        down_parts,
        tokens_own,
        attended_low,
        blocks,
        gain_two,
    )
    chain = Chain(double_chain(*grads))
    d_attended = gate(d_attended, chain)

    output = output.reshape(seq_count, BLK, width)
    arrived = [to_owner(output[s], s) for s in range(seq_count)]

    halves = []
    for group in range(GROUPS):
        if group:
            d_attended, arrived = gate((d_attended, arrived), chain)
            arrived = jnp.stack(arrived)
            output = jnp.stack([piece(arrived, seq ^ s) for s in range(seq_count)], axis=1)
        *grads, d_bias = attend_back(
            group,
            levels,
            lead,
            low,
            high,
            queries,
            keys,
            values,
            d_attended,
            attended,
            log_total,
            tiles,
            known,
            barred,
            buckets,
        )
        halves.append((grads, d_bias))
        d_attended, _ = lax.optimization_barrier((d_attended, grads[0]))
    d_bias = jnp.concatenate([half[1] for half in halves], axis=0)
    norm_own, halves = gate((norm_own, [half[0] for half in halves]), chain)
    keep, send, d_norm_one = project_back(shard, shards, lead, norm_one, norm_own, qkv, halves)
    qkv_chain = Chain(single_chain(keep, send))
    d_norm_one = gate(d_norm_one, qkv_chain, chain)

    vocab_rows = -(-vocab // 16) * 16
    d_resid = d_resid.reshape(seq_count, BLK, width)
    small = byte_backward(
        lead,
        phases,
        tokens,
        d_norm_one,
        d_resid,
        conv,
        mix,
        table,
        vocab_rows,
        conv_w,
        score_row,
        gain_row,
        total_bytes,
    )
    bias_grad = jnp.transpose(d_bias[:, : heads // GROUPS].reshape(heads, levels)).reshape(1, levels * heads)
    bias_grad = jnp.pad(bias_grad, ((0, 0), (0, width - levels * heads)))
    small = jnp.concatenate([small[: vocab_rows + 6], grad_gain_two, bias_grad], axis=0)
    small = jnp.pad(small, ((0, -small.shape[0] % (8 * ctx_count)), (0, 0))).astype(bf16)
    small = gate(small, qkv_chain, chain)
    shard_rows, tall = query_master.shape[0], down_master.shape[0]
    ctx_row = ctx_index[None]

    def finish(mine, other):
        return unpack(
            functools.partial(unpack_joined_kernel, hidden_width),
            ctx_row,
            mine,
            other,
            [(shard_rows, width)] + [(shard_rows, hidden_width)] * 2 + [(tall, width)],
            [pltpu.VMEM((shard_rows, hidden_width), f32)],
            "unpack_joined",
        )

    small, ffn_grads = reduce_small(small, qkv_chain, chain, finish)
    small = small.astype(f32)
    qkv_grads = unpack(
        unpack_three_kernel,
        ctx_row,
        *qkv_chain.finish(),
        [(shard_rows, width)] * 3,
        [],
        "unpack_three",
    )
    top = vocab_rows
    return (
        output,
        small[:vocab],
        small[top : top + 4],
        small[top + 4],
        small[top + 5],
        small[top + 6],
        small[top + 7, : levels * heads].reshape(levels, heads),
        *qkv_grads,
        *ffn_grads,
    )


def solution(mesh):
    placed = (
        P("fsdp", "ctx"),
        P("fsdp", "ctx"),
        P(),
        P(),
        P(),
        P(),
        P(),
        P(),
        P(),
        P("fsdp", None),
        P("fsdp", None),
        P("fsdp", None),
        P("fsdp", None),
        P("fsdp", None),
        P("fsdp", None),
        P("fsdp", None),
        P("ctx", "fsdp", None),
    )
    return jax.shard_map(
        local,
        mesh=mesh,
        in_specs=placed,
        out_specs=(
            P("ctx", "fsdp", None),
            P(),
            P(),
            P(),
            P(),
            P(),
            P(),
            P("fsdp", None),
            P("fsdp", None),
            P("fsdp", None),
            P("fsdp", None),
            P("fsdp", None),
            P("fsdp", None),
            P("fsdp", None),
        ),
        check_vma=False,
    )
```

```python
import functools

import jax
import jax.numpy as jnp
from jax import lax
from jax.experimental import pallas as pl
from jax.experimental.pallas import tpu as pltpu
from jax.sharding import PartitionSpec as P

f32 = jnp.float32
bf16 = jnp.bfloat16
LANE = 128
BLK = 128
VMEM_CAP = 60 * 1024 * 1024
HIGH = lax.Precision.HIGHEST
NT = (((1,), (1,)), ((), ()))
NN = (((1,), (0,)), ((), ()))
LIGHT = pl.CostEstimate(flops=1, transcendentals=0, bytes_accessed=1)


STEP = 16
NORM_ROWS = 128


def lane_iota(rows):
    return lax.broadcasted_iota(jnp.int32, (rows, LANE), 1)


def block_sum(value, width, lane):
    def ahead(v, n):
        return pltpu.roll(v, LANE - n, 1)

    def behind(v, n):
        return pltpu.roll(v, n, 1)

    if width == 1:
        return value
    if width == 3:
        lead = value + ahead(value, 1) + ahead(value, 2)
        phase = lane % 3
        return jnp.where(phase == 0, lead, jnp.where(phase == 1, behind(lead, 1), behind(lead, 2)))
    pair = value + jnp.where(lane % 2 == 0, ahead(value, 1), behind(value, 1))
    if width == 2:
        return pair
    return pair + jnp.where(lane % 4 < 2, ahead(pair, 2), behind(pair, 2))


def pick(value, lane_index):
    return value[:, lane_index : lane_index + 1]


def byte_forward_kernel(
    total_bytes,
    seq_ref,
    lead_ref,
    both_ref,
    table_ref,
    conv_w_ref,
    score_ref,
    gain_ref,
    tok_ref,
    norm_ref,
    norm_own_ref,
    tok_own_ref,
    conv_ref,
    mix_ref,
    ids_ref,
    known_ref,
    barred_ref,
    hi_ref,
    lo_ref,
    emb,
    flat,
    spread,
):
    groups = conv_ref.shape[1]
    width = conv_ref.shape[2]
    tiles = width // LANE
    token_count = norm_ref.shape[0]
    vocab_pad = hi_ref.shape[0]
    row_lanes = ids_ref.shape[1]
    seq = seq_ref[0]
    vocab = table_ref.shape[0]
    whole_rows = vocab // 128 * 128
    rest = jnp.zeros((vocab_pad - whole_rows, width), f32)
    rest_row = lax.broadcasted_iota(jnp.int32, rest.shape, 0)
    for row in range(whole_rows, vocab):
        rest = jnp.where(rest_row == row - whole_rows, table_ref[row : row + 1, :], rest)
    for here, value in ((0, table_ref[0:whole_rows, :]), (whole_rows, rest)):
        high = value.astype(bf16)
        hi_ref[here : here + value.shape[0], :] = high
        lo_ref[here : here + value.shape[0], :] = (value - high.astype(f32)).astype(bf16)
    lane_f = lane_iota(BLK).astype(f32)
    chunk_bytes = both_ref.shape[3]

    def lay(kind, first):
        for block in range(both_ref.shape[0]):
            row = both_ref[block, seq, kind : kind + 1, :].astype(f32)
            for half in range(chunk_bytes // LANE):
                part = jnp.broadcast_to(row[:, half * LANE : (half + 1) * LANE], (LANE, LANE))
                start = first + block * chunk_bytes + half * LANE
                spread[start : start + LANE, :] = jnp.transpose(part)

    lay(1, 0)
    for block in range(token_count // BLK):
        docs = spread[pl.ds(block * 2 * BLK, BLK, stride=2), :]
        same = docs == lane_f
        rows = slice(block * BLK, (block + 1) * BLK)
        known_ref[rows, :] = same.astype(bf16)
        barred_ref[rows, :] = jnp.where(same | (lane_f >= 16.0), 0.0, -1e30).astype(bf16)
    lay(0, 16)
    none = jnp.full((16, LANE), -1.0, f32)
    spread[0:16, :] = none
    tail = spread.shape[0] - total_bytes - 16
    spread[total_bytes + 16 :, :] = jnp.full((tail, LANE), -1.0, f32)
    lane_g = lane_iota(groups).astype(f32)
    for r in range(15):
        here = spread[pl.ds(13 + r, row_lanes, stride=12), :]
        turned = [
            jnp.transpose(here[n * LANE : (n + 1) * LANE, :])[0:1, :]
            for n in range(row_lanes // LANE)
        ]
        ids_ref[r : r + 1, :] = jnp.concatenate(turned, axis=1)
        onehot = jnp.concatenate(
            [
                (here[0:groups, :] == lane_g + n * LANE).astype(bf16)
                for n in range(vocab_pad // LANE)
            ],
            axis=1,
        )
        emb[r] = jnp.dot(onehot, hi_ref[...], preferred_element_type=f32) + jnp.dot(
            onehot, lo_ref[...], preferred_element_type=f32
        )
    ids_ref[15:16, :] = jnp.full((1, row_lanes), -1.0, f32)
    lane = lane_iota(STEP)

    def chunk(i, masked):
        r0 = pl.multiple_of(i * STEP, STEP)
        rows = pl.ds(r0, STEP)
        sums = [jnp.zeros((STEP, LANE), f32) for _ in range(12)]
        for tile in range(tiles):
            cols = slice(tile * LANE, (tile + 1) * LANE)
            taps = [conv_w_ref[k : k + 1, cols] for k in range(4)]
            piece = [emb[r, rows, cols] for r in range(15)]
            score = score_ref[0:1, cols]
            for r in range(12):
                value = (
                    piece[r] * taps[0]
                    + piece[r + 1] * taps[1]
                    + piece[r + 2] * taps[2]
                    + piece[r + 3] * taps[3]
                )
                if masked:
                    group = r0 + lax.broadcasted_iota(jnp.int32, (STEP, LANE), 0)
                    value = jnp.where(group * 12 + r < total_bytes, value, 0.0)
                conv_ref[r, rows, cols] = value
                sums[r] = sums[r] + value * score
        packed = jnp.zeros((STEP, LANE), f32)
        for r in range(12):
            packed = jnp.where(lane == r, jnp.sum(sums[r], axis=1, keepdims=True), packed)
        logits = [block_sum(packed, b, lane) * (1.0 / b) for b in range(1, 5)]
        best = jnp.maximum(jnp.maximum(logits[0], logits[1]), jnp.maximum(logits[2], logits[3]))
        parts = [jnp.exp(value - best) for value in logits]
        total = parts[0] + parts[1] + parts[2] + parts[3]
        mix = [part / total for part in parts]
        for b in range(4):
            mix_ref[b, rows, :] = mix[b]
        half_one = mix[0] * 0.5
        pair_two = block_sum(mix[1], 2, lane) * 0.25
        single_three = mix[2] * (1.0 / 6.0)
        pair_three = block_sum(mix[2], 2, lane) * (1.0 / 6.0)
        pair_four = block_sum(mix[3], 2, lane) * 0.125
        coef_one = [pick(half_one, r) for r in range(12)]
        coef_two = [pick(pair_two, 2 * j) for j in range(6)]
        coef_four = [pick(pair_four, 2 * j) for j in range(6)]
        coef_three = []
        for j in range(6):
            if j % 3 == 1:
                coef_three.append((pick(single_three, 2 * j), pick(single_three, 2 * j + 1)))
            else:
                coef_three.append((pick(pair_three, 2 * j), None))
        for tile in range(tiles):
            cols = slice(tile * LANE, (tile + 1) * LANE)
            conv = [conv_ref[r, rows, cols] for r in range(12)]
            two = [conv[2 * j] + conv[2 * j + 1] for j in range(6)]
            three = [conv[3 * q] + conv[3 * q + 1] + conv[3 * q + 2] for q in range(4)]
            four = [two[2 * q] + two[2 * q + 1] for q in range(3)]
            for j in range(6):
                a, b = 2 * j, 2 * j + 1
                value = coef_one[a] * conv[a] + coef_one[b] * conv[b]
                value = value + coef_two[j] * two[j] + coef_four[j] * four[j // 2]
                value = value + coef_three[j][0] * three[a // 3]
                if j % 3 == 1:
                    value = value + coef_three[j][1] * three[b // 3]
                flat[tile, pl.ds(6 * r0 + j, STEP, stride=6), :] = value

    whole = (total_bytes // 12) // STEP

    def plain(i, carry):
        chunk(i, False)
        return carry

    lax.fori_loop(0, whole, plain, 0)
    for i in range(whole, groups // STEP):
        chunk(i, True)

    def norm(i, carry):
        rows = pl.ds(pl.multiple_of(i * NORM_ROWS, NORM_ROWS), NORM_ROWS)
        value = jnp.concatenate([flat[tile, rows, :] for tile in range(tiles)], axis=1)
        tok_ref[rows, :] = value
        scale = lax.rsqrt(jnp.mean(value * value, axis=1, keepdims=True) + 1e-06)
        norm_ref[rows, :] = (value * scale * gain_ref[...]).astype(bf16)
        return carry

    lax.fori_loop(0, token_count // NORM_ROWS, norm, 0)
    for slot in range(norm_own_ref.shape[0] // BLK):
        start = pl.multiple_of(lead_ref[slot] * BLK, BLK)
        norm_own_ref[slot * BLK : (slot + 1) * BLK, :] = norm_ref[pl.ds(start, BLK), :]
        tok_own_ref[slot * BLK : (slot + 1) * BLK, :] = tok_ref[pl.ds(start, BLK), :]


def byte_forward(seq, lead, both, table, conv_w, score_w, gain_one, total_bytes):
    width = conv_w.shape[1]
    token_count = total_bytes // 2
    least = -(-total_bytes // 12)
    groups = -(-least // 16) * 16
    row_lanes = -(-least // LANE) * LANE
    vocab_pad = -(-table.shape[0] // LANE) * LANE
    smem = pl.BlockSpec(memory_space=pltpu.SMEM)
    vmem = pl.BlockSpec(memory_space=pltpu.VMEM)
    return pl.pallas_call(
        functools.partial(byte_forward_kernel, total_bytes),
        out_shape=(
            jax.ShapeDtypeStruct((token_count, width), f32),
            jax.ShapeDtypeStruct((token_count, width), bf16),
            jax.ShapeDtypeStruct((lead.shape[0] * BLK, width), bf16),
            jax.ShapeDtypeStruct((lead.shape[0] * BLK, width), f32),
            jax.ShapeDtypeStruct((12, groups, width), f32),
            jax.ShapeDtypeStruct((4, groups, LANE), f32),
            jax.ShapeDtypeStruct((16, row_lanes), f32),
            jax.ShapeDtypeStruct((token_count, LANE), bf16),
            jax.ShapeDtypeStruct((token_count, LANE), bf16),
        ),
        in_specs=[smem, smem] + [vmem] * 5,
        scratch_shapes=[
            pltpu.VMEM((vocab_pad, width), bf16),
            pltpu.VMEM((vocab_pad, width), bf16),
            pltpu.VMEM((15, groups, width), f32),
            pltpu.VMEM((width // LANE, 6 * groups, LANE), f32),
            pltpu.VMEM((12 * row_lanes + 32, LANE), f32),
        ],
        compiler_params=pltpu.CompilerParams(vmem_limit_bytes=VMEM_CAP),
        cost_estimate=LIGHT,
        name="byte_forward",
    )(
        seq,
        lead,
        both,
        table,
        conv_w,
        score_w,
        gain_one,
    )


def byte_backward_kernel(
    total_bytes,
    first_ref,
    ids_ref,
    tok_ref,
    dnorm_ref,
    dres_ref,
    conv_ref,
    mix_ref,
    table_ref,
    conv_w_ref,
    score_ref,
    gain_ref,
    out_ref,
    dtok,
    dconv,
    onehot,
):
    groups = conv_ref.shape[1]
    width = conv_ref.shape[2]
    tiles = width // LANE
    token_count = dnorm_ref.shape[0]
    vocab_rows = onehot.shape[0]
    lanes = ids_ref.shape[1]
    gain = gain_ref[...]

    def norm_back(i, acc):
        rows = pl.ds(pl.multiple_of(i * NORM_ROWS, NORM_ROWS), NORM_ROWS)
        value = tok_ref[rows, :]
        grad = dnorm_ref[rows, :]
        scale = lax.rsqrt(jnp.mean(value * value, axis=1, keepdims=True) + 1e-06)
        grad_gain = grad * gain
        inner = jnp.mean(value * grad_gain, axis=1, keepdims=True)
        total = 0.5 * scale * grad_gain - value * (0.5 * scale * scale * scale * inner)
        for tile in range(tiles):
            dtok[tile, rows, :] = total[:, tile * LANE : (tile + 1) * LANE]
        product = (grad * value * scale).reshape(NORM_ROWS // 8, 8, width)
        return acc + jnp.sum(product, axis=0)

    gain_acc = lax.fori_loop(0, token_count // NORM_ROWS, norm_back, jnp.zeros((8, width), f32))
    rest = dtok.shape[1] - token_count
    dtok[:, token_count:, :] = jnp.zeros((tiles, rest, LANE), f32)
    for slot in range(dres_ref.shape[0]):
        start = pl.multiple_of(first_ref[slot] * BLK, BLK)

        def add(i, carry, slot=slot, start=start):
            r = pl.multiple_of(i * 32, 32)
            rows = pl.ds(pl.multiple_of(start + r, 32), 32)
            more = 0.5 * dres_ref[slot, pl.ds(r, 32), :]
            for tile in range(tiles):
                dtok[tile, rows, :] = (
                    dtok[tile, rows, :] + more[:, tile * LANE : (tile + 1) * LANE]
                )
            return carry

        lax.fori_loop(0, BLK // 32, add, 0)
    vocab = lax.broadcasted_iota(jnp.int32, (vocab_rows, lanes), 0).astype(f32)
    for r in range(15):
        onehot[:, r * lanes : (r + 1) * lanes] = (vocab == ids_ref[r : r + 1, :]).astype(bf16)
    for r in range(12):
        dconv[r * lanes + groups : (r + 1) * lanes, :] = jnp.zeros((lanes - groups, width), bf16)
    lane = lane_iota(8)

    def scalars(r0):
        rows = pl.ds(r0, 8)
        one = [jnp.zeros((8, LANE), f32) for _ in range(12)]
        cross = [jnp.zeros((8, LANE), f32) for _ in range(6)]
        tri = [jnp.zeros((8, LANE), f32) for _ in range(8)]
        for tile in range(tiles):
            cols = slice(tile * LANE, (tile + 1) * LANE)
            conv = [conv_ref[r, rows, cols] for r in range(12)]
            grad = [dtok[tile, pl.ds(6 * r0 + j, 8, stride=6), :] for j in range(6)]
            two = [conv[2 * j] + conv[2 * j + 1] for j in range(6)]
            three = [conv[3 * q] + conv[3 * q + 1] + conv[3 * q + 2] for q in range(4)]
            for r in range(12):
                one[r] = one[r] + conv[r] * grad[r // 2]
            slot = 0
            for j in range(6):
                cross[j] = cross[j] + two[j ^ 1] * grad[j]
                for q in sorted({(2 * j) // 3, (2 * j + 1) // 3}):
                    tri[slot] = tri[slot] + three[q] * grad[j]
                    slot += 1
        inner_one = jnp.zeros((8, LANE), f32)
        for r in range(12):
            inner_one = jnp.where(lane == r, jnp.sum(one[r], axis=1, keepdims=True), inner_one)
        inner_cross = jnp.zeros((8, LANE), f32)
        for j in range(6):
            inner_cross = jnp.where(
                lane // 2 == j, jnp.sum(cross[j], axis=1, keepdims=True), inner_cross
            )
        inner_three = jnp.zeros((8, LANE), f32)
        slot = 0
        for j in range(6):
            for q in sorted({(2 * j) // 3, (2 * j + 1) // 3}):
                here = (lane // 2 == j) & (lane // 3 == q)
                inner_three = jnp.where(
                    here, jnp.sum(tri[slot], axis=1, keepdims=True), inner_three
                )
                slot += 1
        inner_two = block_sum(inner_one, 2, lane)
        mix = [mix_ref[b, rows, :] for b in range(4)]
        d_mix = [
            inner_one,
            inner_two * 0.5,
            inner_three * (1.0 / 3.0),
            (inner_two + inner_cross) * 0.25,
        ]
        mean = mix[0] * d_mix[0] + mix[1] * d_mix[1] + mix[2] * d_mix[2] + mix[3] * d_mix[3]
        d_logit = [mix[b] * (d_mix[b] - mean) for b in range(4)]
        d_logit = [jnp.where(lane < 12, value, 0.0) for value in d_logit]
        slope = d_logit[0]
        for b in range(2, 5):
            slope = slope + block_sum(d_logit[b - 1], b, lane) * (1.0 / b)
        pair_two = block_sum(mix[1], 2, lane) * 0.5
        single_three = mix[2] * (1.0 / 3.0)
        pair_three = block_sum(mix[2], 2, lane) * (1.0 / 3.0)
        pair_four = block_sum(mix[3], 2, lane) * 0.25
        return mix[0], pair_two, single_three, pair_three, pair_four, slope

    def spread(r0, coefs, tile, masked, score_acc):
        one, pair_two, single_three, pair_three, pair_four, slope = coefs
        rows = pl.ds(r0, 8)
        cols = slice(tile * LANE, (tile + 1) * LANE)
        grad = [dtok[tile, pl.ds(6 * r0 + j, 8, stride=6), :] for j in range(6)]
        score = score_ref[0:1, cols]
        four = [
            pick(pair_four, 4 * q) * grad[2 * q] + pick(pair_four, 4 * q + 2) * grad[2 * q + 1]
            for q in range(3)
        ]
        three = []
        for q in range(4):
            a = 3 * q
            if a % 2 == 0:
                three.append(
                    pick(pair_three, a) * grad[a // 2]
                    + pick(single_three, a + 2) * grad[a // 2 + 1]
                )
            else:
                three.append(
                    pick(single_three, a) * grad[a // 2]
                    + pick(pair_three, a + 1) * grad[a // 2 + 1]
                )
        result = []
        for r in range(12):
            weight = pick(slope, r)
            own = (pick(one, r) + pick(pair_two, r)) * grad[r // 2]
            value = own + three[r // 3] + four[r // 4] + weight * score
            score_acc = score_acc + weight * conv_ref[r, rows, cols]
            if masked:
                group = r0 + lax.broadcasted_iota(jnp.int32, (8, LANE), 0)
                value = jnp.where(group * 12 + r < total_bytes, value, 0.0)
            result.append(value)
        return result, score_acc

    def chunk(i, accs, masked):
        r0 = pl.multiple_of(i * 16, 16)
        r1 = pl.multiple_of(i * 16 + 8, 8)
        low_coefs = scalars(r0)
        high_coefs = scalars(r1)
        new = []
        for tile in range(tiles):
            cols = slice(tile * LANE, (tile + 1) * LANE)
            low, acc = spread(r0, low_coefs, tile, masked, accs[tile])
            high, acc = spread(r1, high_coefs, tile, masked, acc)
            new.append(acc)
            for r in range(12):
                both = jnp.concatenate([low[r], high[r]], axis=0).astype(bf16)
                dconv[pl.ds(pl.multiple_of(r * lanes + r0, 16), 16), cols] = both
        return tuple(new)

    accs = tuple(jnp.zeros((8, LANE), f32) for _ in range(tiles))
    whole = (total_bytes // 12) // 16
    accs = lax.fori_loop(0, whole, lambda i, a: chunk(i, a, False), accs)
    for i in range(whole, groups // 16):
        accs = chunk(i, accs, True)
    tail = [jnp.zeros((1, width), f32) for _ in range(8)]
    for k in range(4):
        part = jnp.dot(
            onehot[:, k * lanes : (k + 12) * lanes], dconv[...], preferred_element_type=f32
        )
        if k == 0:
            out_ref[0:vocab_rows, :] = part * conv_w_ref[k : k + 1, :]
        else:
            out_ref[0:vocab_rows, :] = out_ref[0:vocab_rows, :] + part * conv_w_ref[k : k + 1, :]
        vocab = table_ref.shape[0]
        whole_rows = vocab // 8 * 8
        tail[k] = jnp.sum(part[:whole_rows] * table_ref[0:whole_rows, :], axis=0, keepdims=True)
        for row in range(whole_rows, vocab):
            tail[k] = tail[k] + part[row : row + 1] * table_ref[row : row + 1, :]
    tail[4] = jnp.sum(jnp.concatenate(accs, axis=1), axis=0, keepdims=True)
    tail[5] = jnp.sum(gain_acc, axis=0, keepdims=True)
    out_ref[vocab_rows:, :] = jnp.concatenate(tail, axis=0)


def byte_backward(
    first,
    ids,
    tokens,
    d_norm,
    d_resid,
    conv,
    mix,
    table,
    vocab_rows,
    conv_w,
    score_w,
    gain_one,
    total_bytes,
):
    width = conv.shape[2]
    groups = conv.shape[1]
    lanes = ids.shape[1]
    return pl.pallas_call(
        functools.partial(byte_backward_kernel, total_bytes),
        out_shape=jax.ShapeDtypeStruct((vocab_rows + 8, width), f32),
        in_specs=[pl.BlockSpec(memory_space=pltpu.SMEM)]
        + [pl.BlockSpec(memory_space=pltpu.VMEM)] * 10,
        scratch_shapes=[
            pltpu.VMEM((width // LANE, 6 * groups, LANE), f32),
            pltpu.VMEM((12 * lanes, width), bf16),
            pltpu.VMEM((vocab_rows, 15 * lanes), bf16),
        ],
        compiler_params=pltpu.CompilerParams(vmem_limit_bytes=VMEM_CAP),
        cost_estimate=LIGHT,
        name="byte_backward",
    )(
        first,
        ids,
        tokens,
        d_norm,
        d_resid,
        conv,
        mix,
        table,
        conv_w,
        score_w,
        gain_one,
    )


def head_mask(value, head):
    half = value.shape[1] // 2
    lane = lax.broadcasted_iota(jnp.int32, value.shape, 1)
    keep = lane < half if head == 0 else lane >= half
    return jnp.where(keep, value, jnp.zeros_like(value))


def two_heads(value):
    return jnp.concatenate([head_mask(value, 0), head_mask(value, 1)], axis=0)


def bucket_row(buckets_ref, n, reach):
    row = buckets_ref.shape[0] // 2 - 1 - (n - reach)
    return jnp.concatenate([buckets_ref[row : row + 1, :], buckets_ref[row + 1 : row + 2, :]], axis=1)


def bias_tiles(buckets_ref, rel, tiles):
    count = tiles.shape[1]
    levels = rel.shape[1]
    level = lax.broadcasted_iota(jnp.int32, (levels, 2 * BLK), 0)
    for n in range(count):
        onehot = (level == bucket_row(buckets_ref, n, count // 2)).astype(f32)
        values = lax.dot_general(rel, onehot, NN, precision=HIGH, preferred_element_type=f32)
        for head in range(2 * tiles.shape[0]):
            spread = jnp.broadcast_to(values[head : head + 1, :], (BLK, 2 * BLK))
            rolled = pltpu.roll(spread, BLK + 1, 1, stride=1, stride_axis=0)
            half = slice(head % 2 * BLK, head % 2 * BLK + BLK)
            tiles[head // 2, n, :, half] = rolled[:, :BLK]


def fold_rows(value, op):
    return op(value.reshape(BLK // 8, 8, value.shape[1]), axis=0)


def attend_kernel(
    lead_ref,
    low_ref,
    high_ref,
    q_ref,
    k_ref,
    v_ref,
    known,
    barred,
    tiles,
    out_ref,
    low_out_ref,
    log_ref,
    v_turned,
    *scratch,
):
    pairs = tiles.shape[0]
    held, accum = scratch[:pairs], scratch[pairs:]
    reach = tiles.shape[1] // 2
    slots = q_ref.shape[0] // BLK
    half = BLK // 2
    v_turned[...] = jnp.transpose(v_ref[...])
    cols = [slice(p * BLK, (p + 1) * BLK) for p in range(pairs)]
    for slot in range(slots):
        block = lead_ref[slot]
        first = low_ref[slot]
        last = high_ref[slot]
        base = pl.multiple_of(block * BLK, BLK)
        own = slice(slot * BLK, (slot + 1) * BLK)
        bar = barred[pl.ds(base, BLK), :]
        bar = jnp.concatenate([bar, bar], axis=0)
        q_full = [jnp.concatenate([two_heads(q_ref[own, c]), bar], axis=1) for c in cols]

        def score(kb, best):
            rows = pl.ds(pl.multiple_of(kb * BLK, BLK), BLK)
            mark = known[rows, :]
            values = [
                lax.dot_general(
                    jnp.concatenate([k_ref[rows, c], mark], axis=1),
                    q_full[p],
                    NT,
                    preferred_element_type=f32,
                )
                + tiles[p, kb - block + reach]
                for p, c in enumerate(cols)
            ]
            for p in range(pairs):
                held[p][kb - first] = values[p]
            return tuple(jnp.maximum(best[p], fold_rows(values[p], jnp.max)) for p in range(pairs))

        lowest = jnp.full((8, 2 * BLK), -3e38, f32)
        best = lax.fori_loop(first, last, score, (lowest,) * pairs)
        best = [jnp.max(value, axis=0, keepdims=True) for value in best]
        for p in range(pairs):
            accum[p][...] = jnp.zeros((BLK, 2 * BLK), f32)

        def gather(kb, total):
            keys = pl.ds(pl.multiple_of(kb * BLK, BLK), BLK)
            weights = [jnp.exp(held[p][kb - first] - best[p]) for p in range(pairs)]
            products = [
                jnp.dot(v_turned[c, keys], weights[p].astype(bf16), preferred_element_type=f32)
                for p, c in enumerate(cols)
            ]
            for p in range(pairs):
                accum[p][...] += products[p]
            return tuple(total[p] + fold_rows(weights[p], jnp.sum) for p in range(pairs))

        none = jnp.zeros((8, 2 * BLK), f32)
        total = lax.fori_loop(first, last, gather, (none,) * pairs)
        for p in range(pairs):
            row_total = jnp.sum(total[p], axis=0, keepdims=True)
            value = accum[p][...] / row_total
            both = jnp.concatenate([value[:half, :BLK], value[half:, BLK:]], axis=0)
            both = jnp.transpose(both)
            out_ref[own, cols[p]] = both
            low_out_ref[own, cols[p]] = both.astype(bf16)
            log_ref[0, slot, p : p + 1, :] = best[p] + jnp.log(row_total)


def tiles_kernel(buckets_ref, rel_ref, tiles):
    groups = rel_ref.shape[0]
    pairs = tiles.shape[0] // groups
    for group in range(groups):
        bias_tiles(
            buckets_ref, rel_ref[group], tiles.at[group * pairs : (group + 1) * pairs]
        )


def make_tiles(buckets, rel):
    groups, heads, levels = rel.shape
    shape = (heads // 2, 2 * (buckets.shape[0] // 4) + 1, BLK, 2 * BLK)
    return pl.pallas_call(
        tiles_kernel,
        out_shape=jax.ShapeDtypeStruct((groups * shape[0],) + shape[1:], f32),
        compiler_params=pltpu.CompilerParams(vmem_limit_bytes=VMEM_CAP),
        cost_estimate=LIGHT,
        name="bias_tiles",
    )(buckets, rel)


def attend(lead, low, high, q, k, v, known, barred, tiles):
    rows, width = q.shape
    keys = k.shape[0]
    pairs = tiles.shape[0] // GROUPS
    groups = GROUPS
    blocks = keys // BLK
    slots = rows // BLK
    count = tiles.shape[1]
    smem = pl.BlockSpec(memory_space=pltpu.SMEM)

    def cols(size):
        return pl.BlockSpec((size, pairs * BLK), lambda i: (0, i))

    def whole(array):
        return pl.BlockSpec(array.shape, lambda i: (0,) * array.ndim)

    return pl.pallas_call(
        attend_kernel,
        grid=(groups,),
        out_shape=(
            jax.ShapeDtypeStruct((rows, width), f32),
            jax.ShapeDtypeStruct((rows, width), bf16),
            jax.ShapeDtypeStruct((groups, slots, pairs, 2 * BLK), f32),
        ),
        in_specs=[
            smem,
            smem,
            smem,
            cols(rows),
            cols(keys),
            cols(keys),
            whole(known),
            whole(barred),
            pl.BlockSpec((pairs, count, BLK, 2 * BLK), lambda i: (i, 0, 0, 0)),
        ],
        out_specs=(
            cols(rows),
            cols(rows),
            pl.BlockSpec((1, slots, pairs, 2 * BLK), lambda i: (i, 0, 0, 0)),
        ),
        scratch_shapes=[pltpu.VMEM((pairs * BLK, keys), bf16)]
        + [pltpu.VMEM((blocks, BLK, 2 * BLK), f32)] * pairs
        + [pltpu.VMEM((BLK, 2 * BLK), f32)] * pairs,
        compiler_params=pltpu.CompilerParams(vmem_limit_bytes=VMEM_CAP),
        cost_estimate=LIGHT,
        name="attend",
    )(lead, low, high, q, k, v, known, barred, tiles)


def attend_back_kernel(
    lead_ref,
    low_ref,
    high_ref,
    q_ref,
    k_ref,
    v_ref,
    g_ref,
    out_ref,
    log_ref,
    tiles,
    known,
    barred,
    buckets_ref,
    dq_ref,
    dk_ref,
    dv_ref,
    dbias_ref,
    k_turned,
    *scratch,
):
    pairs, count = tiles.shape[:2]
    dk_acc, dv_acc, d_tiles, dq_acc = (scratch[n * pairs : (n + 1) * pairs] for n in range(4))
    reach = count // 2
    slots = q_ref.shape[0] // BLK
    half = BLK // 2
    k_turned[...] = jnp.transpose(k_ref[...])
    for p in range(pairs):
        dk_acc[p][...] = jnp.zeros(dk_acc[p].shape, f32)
        dv_acc[p][...] = jnp.zeros(dv_acc[p].shape, f32)
        d_tiles[p][...] = jnp.zeros(d_tiles[p].shape, f32)
    sub = lax.broadcasted_iota(jnp.int32, (8, BLK), 0)
    chooser = jnp.where((lane_iota(8) // half) == sub, 1.0, 0.0).astype(bf16)
    cols = [slice(p * BLK, (p + 1) * BLK) for p in range(pairs)]
    for slot in range(slots):
        block = lead_ref[slot]
        first = low_ref[slot]
        last = high_ref[slot]
        base = pl.multiple_of(block * BLK, BLK)
        own = slice(slot * BLK, (slot + 1) * BLK)
        bar = barred[pl.ds(base, BLK), :]
        bar = jnp.concatenate([bar, bar], axis=0)
        q_two = [two_heads(q_ref[own, c]) for c in cols]
        q_full = [jnp.concatenate([value, bar], axis=1) for value in q_two]
        g_two = [two_heads(g_ref[own, c]) for c in cols]
        deltas = []
        for p, c in enumerate(cols):
            product = g_ref[own, c].astype(f32) * out_ref[own, c]
            high_part = product.astype(bf16)
            low_part = (product - high_part.astype(f32)).astype(bf16)
            delta = lax.dot_general(
                chooser, high_part, NT, preferred_element_type=f32
            ) + lax.dot_general(chooser, low_part, NT, preferred_element_type=f32)
            deltas.append(jnp.concatenate([delta[0:1, :], delta[1:2, :]], axis=1))
            dq_acc[p][...] = jnp.zeros((BLK, 2 * BLK), f32)
        logs = [log_ref[0, slot, p : p + 1, :] for p in range(pairs)]

        def step(kb, carry):
            rows = pl.ds(pl.multiple_of(kb * BLK, BLK), BLK)
            at = kb - block + reach
            mark = known[rows, :]
            values = [
                lax.dot_general(
                    jnp.concatenate([k_ref[rows, c], mark], axis=1),
                    q_full[p],
                    NT,
                    preferred_element_type=f32,
                )
                for p, c in enumerate(cols)
            ]
            d_probs = [
                lax.dot_general(v_ref[rows, c], g_two[p], NT, preferred_element_type=f32)
                for p, c in enumerate(cols)
            ]
            probs = [jnp.exp(values[p] + (tiles[p, at] - logs[p])) for p in range(pairs)]
            d_scores = [probs[p] * (d_probs[p] - deltas[p]) for p in range(pairs)]
            lows = [value.astype(bf16) for value in d_scores]
            dvs = [
                jnp.dot(probs[p].astype(bf16), g_two[p], preferred_element_type=f32)
                for p in range(pairs)
            ]
            dks = [jnp.dot(lows[p], q_two[p], preferred_element_type=f32) for p in range(pairs)]
            dqs = [
                jnp.dot(k_turned[c, rows], lows[p], preferred_element_type=f32)
                for p, c in enumerate(cols)
            ]
            for p in range(pairs):
                d_tiles[p][at] += d_scores[p]
                dv_acc[p][rows, :] += dvs[p]
                dk_acc[p][rows, :] += dks[p]
                dq_acc[p][...] += dqs[p]
            return carry

        lax.fori_loop(first, last, step, 0)
        for p in range(pairs):
            dq = dq_acc[p][...]
            both = jnp.concatenate([dq[:half, :BLK], dq[half:, BLK:]], axis=0)
            dq_ref[own, cols[p]] = jnp.transpose(both).astype(bf16)
    for p in range(pairs):
        dk_ref[:, cols[p]] = dk_acc[p][...].astype(bf16)
        dv_ref[:, cols[p]] = dv_acc[p][...].astype(bf16)
    levels = dbias_ref.shape[2]
    level = lax.broadcasted_iota(jnp.int32, (levels, 2 * BLK), 0)
    pad = jnp.zeros((BLK, BLK), f32)
    mirror = (
        lax.broadcasted_iota(jnp.int32, (BLK, BLK), 0)
        + lax.broadcasted_iota(jnp.int32, (BLK, BLK), 1)
        == BLK - 1
    ).astype(bf16)
    total = jnp.zeros((8, levels), f32)
    for n in range(count):
        onehot = (level == bucket_row(buckets_ref, n, reach)).astype(f32)
        sums = []
        for p in range(pairs):
            flipped = jnp.dot(mirror, d_tiles[p][n].astype(bf16), preferred_element_type=f32)
            for head in range(2):
                wide = jnp.concatenate([flipped[:, head * BLK : (head + 1) * BLK], pad], axis=1)
                rolled = pltpu.roll(wide, 0, 1, stride=1, stride_axis=0)
                sums.append(jnp.sum(rolled, axis=0, keepdims=True))
        rest = jnp.zeros((8 - 2 * pairs, 2 * BLK), f32)
        total = total + lax.dot_general(
            jnp.concatenate(sums + [rest], axis=0),
            onehot,
            NT,
            precision=HIGH,
            preferred_element_type=f32,
        )
    dbias_ref[0] = total


def attend_back(
    group, levels, lead, low, high, q, k, v, g, out, log, tiles, known, barred, buckets
):
    rows = q.shape[0]
    keys = k.shape[0]
    slots, pairs = log.shape[1:3]
    count = tiles.shape[1]
    width = pairs * BLK
    smem = pl.BlockSpec(memory_space=pltpu.SMEM)

    def cols(size):
        return pl.BlockSpec((size, width), lambda i: (0, group))

    def whole(array):
        return pl.BlockSpec(array.shape, lambda i: (0,) * array.ndim)

    def fresh(*shape):
        return pl.BlockSpec(shape, lambda i: (0,) * len(shape))

    return pl.pallas_call(
        attend_back_kernel,
        grid=(1,),
        out_shape=(
            jax.ShapeDtypeStruct((rows, width), bf16),
            jax.ShapeDtypeStruct((keys, width), bf16),
            jax.ShapeDtypeStruct((keys, width), bf16),
            jax.ShapeDtypeStruct((1, 8, levels), f32),
        ),
        in_specs=[
            smem,
            smem,
            smem,
            cols(rows),
            cols(keys),
            cols(keys),
            cols(rows),
            cols(rows),
            pl.BlockSpec((1, slots, pairs, 2 * BLK), lambda i: (group, 0, 0, 0)),
            pl.BlockSpec((pairs, count, BLK, 2 * BLK), lambda i: (group, 0, 0, 0)),
            whole(known),
            whole(barred),
            whole(buckets),
        ],
        out_specs=(
            fresh(rows, width),
            fresh(keys, width),
            fresh(keys, width),
            fresh(1, 8, levels),
        ),
        scratch_shapes=[pltpu.VMEM((width, keys), bf16)]
        + [pltpu.VMEM((keys, BLK), f32)] * (2 * pairs)
        + [pltpu.VMEM((count, BLK, 2 * BLK), f32)] * pairs
        + [pltpu.VMEM((BLK, 2 * BLK), f32)] * pairs,
        compiler_params=pltpu.CompilerParams(vmem_limit_bytes=VMEM_CAP),
        cost_estimate=LIGHT,
        name="attend_back",
    )(lead, low, high, q, k, v, g, out, log, tiles, known, barred, buckets)


GROUPS = 2


def attention_tables(starts, ends, rel_bucket, rel_bias, lead):
    blocks = starts.shape[0]
    mine = (lead[:, None] == jnp.arange(blocks)[None, :]).astype(jnp.int32)
    own_start = jnp.sum(mine * starts[None, :], axis=1)
    own_end = jnp.sum(mine * ends[None, :], axis=1)
    low = jnp.sum((ends[None, :] < own_start[:, None]).astype(jnp.int32), axis=1)
    high = jnp.sum((starts[None, :] <= own_end[:, None]).astype(jnp.int32), axis=1)
    buckets = jnp.pad(jnp.flip(rel_bucket), (0, 1)).reshape(2 * blocks, BLK)
    levels, heads = rel_bias.shape
    rel = jnp.transpose(rel_bias).reshape(GROUPS, heads // GROUPS, levels)
    return low, high, buckets, rel


def pack_kernel(*refs):
    outs = [ref for ref in refs if ref.dtype == bf16]
    masters = [ref for ref in refs if ref.dtype == f32]
    at = 0
    for out in outs:
        col = 0
        while col < out.shape[1]:
            wide = masters[at].shape[1]
            out[:, col : col + wide] = masters[at][...].astype(bf16)
            col += wide
            at += 1


def pack(groups):
    steps = 1
    while all(group[0].shape[0] % (32 * steps) == 0 for group in groups) and steps < 4:
        steps *= 2

    def spec(array):
        return pl.BlockSpec((array.shape[0] // steps, array.shape[1]), lambda i: (i, 0))

    outs = tuple(
        jax.ShapeDtypeStruct((group[0].shape[0], sum(a.shape[1] for a in group)), bf16)
        for group in groups
    )
    arrays = [array for group in groups for array in group]
    return pl.pallas_call(
        pack_kernel,
        grid=(steps,),
        out_shape=outs,
        in_specs=[spec(array) for array in arrays],
        out_specs=tuple(spec(out) for out in outs),
        compiler_params=pltpu.CompilerParams(vmem_limit_bytes=VMEM_CAP),
        cost_estimate=LIGHT,
        name="pack",
    )(*arrays)


TN = (((0,), (0,)), ((), ()))


def fetch_rows(index, parts, whole, sems):
    rows = parts[0].shape[0]
    copies = []
    for j, part in enumerate(parts):
        start = pl.multiple_of((index ^ j) * rows, rows)
        copies.append(pltpu.make_async_copy(part, whole.at[pl.ds(start, rows), :], sems.at[j]))
    return copies


def project_kernel(count, index_ref, *refs):
    parts = refs[:count]
    norm_ref, own_ref, q_ref, k_ref, v_ref, whole_ref, whole, sems, done = refs[count:]
    width = norm_ref.shape[1]
    copies = fetch_rows(index_ref[0], parts, whole, sems)
    for copy in copies:
        copy.start()
    for copy in copies:
        copy.wait()
    keep = pltpu.make_async_copy(whole, whole_ref, done)
    keep.start()
    for out, rows, col in ((q_ref, own_ref, 0), (k_ref, norm_ref, 1), (v_ref, norm_ref, 2)):
        weight = whole[:, col * width : (col + 1) * width]
        for block in range(rows.shape[0] // 256):
            part = slice(block * 256, (block + 1) * 256)
            out[part, :] = jnp.dot(rows[part, :], weight, preferred_element_type=f32).astype(bf16)
    keep.wait()


def project(index, parts, norm, own):
    count = len(parts)
    width = norm.shape[1]
    full = (parts[0].shape[0] * count, parts[0].shape[1])
    vmem = pl.BlockSpec(memory_space=pltpu.VMEM)
    anywhere = pl.BlockSpec(memory_space=pl.ANY)
    return pl.pallas_call(
        functools.partial(project_kernel, count),
        out_shape=(
            jax.ShapeDtypeStruct(own.shape, bf16),
            jax.ShapeDtypeStruct(norm.shape, bf16),
            jax.ShapeDtypeStruct(norm.shape, bf16),
            jax.ShapeDtypeStruct(full, bf16),
        ),
        in_specs=[pl.BlockSpec(memory_space=pltpu.SMEM)] + [anywhere] * count + [vmem] * 2,
        out_specs=(vmem, vmem, vmem, anywhere),
        scratch_shapes=[
            pltpu.VMEM(full, bf16),
            pltpu.SemaphoreType.DMA((count,)),
            pltpu.SemaphoreType.DMA,
        ],
        compiler_params=pltpu.CompilerParams(vmem_limit_bytes=VMEM_CAP),
        cost_estimate=LIGHT,
        name="project",
    )(index, *parts, norm, own)


def project_back_kernel(count, halves, index_ref, lead_ref, norm_ref, own_ref, whole_ref, *refs):
    keep_ref, send_ref, dnorm_ref, grad_ref, sems = refs[3 * halves :]
    width = norm_ref.shape[1]
    part_width = width // halves
    for half in range(halves):
        for col in range(3):
            rows = own_ref if col == 0 else norm_ref
            here = slice(col * width + half * part_width, col * width + (half + 1) * part_width)
            grad_ref[:, here] = lax.dot_general(
                rows[...], refs[3 * half + col][...], TN, preferred_element_type=f32
            ).astype(bf16)
    waits = scatter_rows(
        index_ref[0], count, (grad_ref, 0, grad_ref.shape[1]), (keep_ref, send_ref, 0), sems, 0
    )
    for block in range(norm_ref.shape[0] // 256):
        part = slice(block * 256, (block + 1) * 256)
        total = None
        for half in range(halves):
            for col in (1, 2):
                here = slice(col * width + half * part_width, col * width + (half + 1) * part_width)
                term = lax.dot_general(
                    refs[3 * half + col][part, :],
                    whole_ref[:, here],
                    NT,
                    preferred_element_type=f32,
                )
                total = term if total is None else total + term
        dnorm_ref[part, :] = total
    for slot in range(own_ref.shape[0] // BLK):
        rows = pl.ds(pl.multiple_of(lead_ref[slot] * BLK, BLK), BLK)
        total = dnorm_ref[rows, :]
        for half in range(halves):
            total = total + lax.dot_general(
                refs[3 * half][slot * BLK : (slot + 1) * BLK, :],
                whole_ref[:, half * part_width : (half + 1) * part_width],
                NT,
                preferred_element_type=f32,
            )
        dnorm_ref[rows, :] = total
    for wait in waits:
        wait.wait()


def project_back(index, count, lead, norm, own, whole, halves):
    vmem = pl.BlockSpec(memory_space=pltpu.VMEM)
    anywhere = pl.BlockSpec(memory_space=pl.ANY)
    smem = pl.BlockSpec(memory_space=pltpu.SMEM)
    grads = [grad for half in halves for grad in half]
    part = jax.ShapeDtypeStruct((count // 2, whole.shape[0] // count, whole.shape[1]), bf16)
    return pl.pallas_call(
        functools.partial(project_back_kernel, count, len(halves)),
        out_shape=(part, part, jax.ShapeDtypeStruct(norm.shape, f32)),
        in_specs=[smem] * 2 + [vmem] * (3 + len(grads)),
        out_specs=(anywhere, anywhere, vmem),
        scratch_shapes=[pltpu.VMEM(whole.shape, bf16), pltpu.SemaphoreType.DMA((count,))],
        compiler_params=pltpu.CompilerParams(vmem_limit_bytes=VMEM_CAP),
        cost_estimate=LIGHT,
        name="project_back",
    )(index, lead, norm, own, whole, *grads)


ROOT = 0.7978845608028654
CUBE = 0.044715


def feed_kernel(count, index_ref, *refs):
    upper = refs[:count]
    lower = refs[count : 2 * count]
    blocks = refs[2 * count].shape[0] // BLK
    cot_blocks = refs[2 * count + 3 : 2 * count + 3 + blocks]
    refs = refs[: 2 * count + 3] + refs[2 * count + 3 + blocks :]
    (
        tok_ref,
        att_ref,
        gain_ref,
        out_ref,
        d_att_ref,
        d_resid_ref,
        gain_grad_ref,
        keep_ref,
        send_ref,
        ogu,
        down,
        store,
        cot_ref,
        resid,
        norm,
        d_norm,
        total,
        hid,
        d_gate,
        d_up,
        sems_upper,
        sems_lower,
        sems_store,
    ) = refs[2 * count :]
    rows, width = tok_ref.shape
    hidden = down.shape[0]
    copies_upper = fetch_rows(index_ref[0], upper, ogu, sems_upper)
    copies_lower = fetch_rows(index_ref[0], lower, down, sems_lower)
    for copy in copies_upper + copies_lower:
        copy.start()
    for n, block in enumerate(cot_blocks):
        cot_ref[n * BLK : (n + 1) * BLK, :] = block[...]
    for copy in copies_upper:
        copy.wait()
    gain = gain_ref[...]
    row_step = 128
    tile = 512
    for block in range(rows // row_step):
        part = slice(block * row_step, (block + 1) * row_step)
        value = tok_ref[part, :] + jnp.dot(
            att_ref[part, :], ogu[:, :width], preferred_element_type=f32
        )
        resid[part, :] = value
        scale = lax.rsqrt(jnp.mean(value * value, axis=1, keepdims=True) + 1e-06)
        norm[part, :] = (value * scale * gain).astype(bf16)
    for copy in copies_lower:
        copy.wait()
    waits = []

    def put(first, last):
        half = store.shape[1] // 2
        for side, begin, end in ((0, first, min(last, half)), (1, max(first, half), last)):
            if begin < end:
                waits.extend(
                    scatter_rows(
                        index_ref[0],
                        count,
                        (store, begin, end),
                        (keep_ref.at[side], send_ref.at[side], begin - side * half),
                        sems_store,
                        len(waits),
                    )
                )

    for n in range(hidden // tile):
        here = slice(n * tile, (n + 1) * tile)
        gate_cols = slice(width + n * tile, width + (n + 1) * tile)
        up_cols = slice(width + hidden + n * tile, width + hidden + (n + 1) * tile)
        for block in range(rows // row_step):
            part = slice(block * row_step, (block + 1) * row_step)
            gate_pre = jnp.dot(norm[part, :], ogu[:, gate_cols], preferred_element_type=f32)
            up_pre = jnp.dot(norm[part, :], ogu[:, up_cols], preferred_element_type=f32)
            d_hidden = lax.dot_general(
                cot_ref[part, :], down[here, :], NT, preferred_element_type=f32
            )
            square = gate_pre * gate_pre
            bent = jnp.tanh(ROOT * gate_pre * (1.0 + CUBE * square))
            half = 0.5 + 0.5 * bent
            gelu = gate_pre * half
            slope = half + (0.5 * ROOT) * gate_pre * (1.0 - bent * bent) * (
                1.0 + (3.0 * CUBE) * square
            )
            low = (gelu * up_pre).astype(bf16)
            d_gate_low = (d_hidden * up_pre * slope).astype(bf16)
            d_up_low = (d_hidden * gelu).astype(bf16)
            hid[part, :] = low
            d_gate[part, :] = d_gate_low
            d_up[part, :] = d_up_low
            add = jnp.dot(low, down[here, :], preferred_element_type=f32)
            back = lax.dot_general(
                d_gate_low, ogu[:, gate_cols], NT, preferred_element_type=f32
            ) + lax.dot_general(d_up_low, ogu[:, up_cols], NT, preferred_element_type=f32)
            if n == 0:
                total[part, :] = resid[part, :] + add
                d_norm[part, :] = back
            else:
                total[part, :] = total[part, :] + add
                d_norm[part, :] = d_norm[part, :] + back
        store[:, gate_cols] = lax.dot_general(
            norm[...], d_gate[...], TN, preferred_element_type=f32
        ).astype(bf16)
        store[:, up_cols] = lax.dot_general(
            norm[...], d_up[...], TN, preferred_element_type=f32
        ).astype(bf16)
        put(width + n * tile, width + (n + 1) * tile)
        put(width + hidden + n * tile, width + hidden + (n + 1) * tile)
        part = lax.dot_general(
            hid[...], cot_ref[...], TN, preferred_element_type=f32
        ).astype(bf16)
        for low_row, low_col, row, size in down_pieces(width // count, hidden // count, width):
            for device in range(count):
                source = device * (hidden // count) + low_row
                if n * tile <= source < (n + 1) * tile:
                    source = source - n * tile
                    target = device * (width // count) + row
                    col = width + 2 * hidden + low_col[1]
                    store[target : target + size, col : col + LANE] = part[
                        source : source + size, low_col[0] : low_col[0] + LANE
                    ]
    gain_sum = jnp.zeros((1, width), f32)
    for block in range(rows // row_step):
        part = slice(block * row_step, (block + 1) * row_step)
        out_ref[part, :] = total[part, :].astype(bf16)
        value = resid[part, :]
        grad = d_norm[part, :]
        scale = lax.rsqrt(jnp.mean(value * value, axis=1, keepdims=True) + 1e-06)
        scaled = grad * gain
        inner = jnp.mean(value * scaled, axis=1, keepdims=True)
        d_value = (
            cot_ref[part, :].astype(f32)
            + scale * scaled
            - value * (scale * scale * scale * inner)
        )
        gain_sum = gain_sum + jnp.sum(grad * value * scale, axis=0, keepdims=True)
        d_resid_ref[part, :] = d_value
        d_low = d_value.astype(bf16)
        norm[part, :] = d_low
        d_att_ref[part, :] = lax.dot_general(
            d_low, ogu[:, :width], NT, preferred_element_type=f32
        ).astype(bf16)
    gain_grad_ref[...] = gain_sum
    store[:, :width] = lax.dot_general(
        att_ref[...], norm[...], TN, preferred_element_type=f32
    ).astype(bf16)
    put(0, width)
    put(width + 2 * hidden, store.shape[1])
    for wait in waits:
        wait.wait()


def scatter_rows(index, count, source, target, sems, at):
    store, begin, end = source
    keep, send, col = target
    rows = store.shape[0] // count
    cols = slice(col, col + end - begin)
    waits = []
    for device in range(count):
        other = index ^ device
        part = store.at[device * rows : (device + 1) * rows, begin:end]
        sem = sems.at[at + device]

        @pl.when(other % 2 == 0)
        def _():
            pltpu.make_async_copy(part, keep.at[other // 2, :, cols], sem).start()

        @pl.when(other % 2 == 1)
        def _():
            pltpu.make_async_copy(part, send.at[other // 2, :, cols], sem).start()

        waits.append(pltpu.make_async_copy(part, keep.at[0, :, cols], sem))
    return waits


def down_pieces(rows, tall, width):
    size = 16
    while tall % (2 * size) == 0 and rows % (2 * size) == 0:
        size *= 2
    pieces = []
    for q in range(tall * (width // LANE) // size):
        there = (q % (tall // size)) * size
        here = (q % (rows // size)) * size
        pieces.append((there, (q // (tall // size) * LANE, q // (rows // size) * LANE), here, size))
    return pieces


def by_parity(index, mine, other, put):
    rows = mine.shape[1]
    for parity in range(2):

        @pl.when(index % 2 == parity)
        def _():
            for k in range(mine.shape[0]):
                put((2 * k + parity) * rows, mine, k)
                put((2 * k + 1 - parity) * rows, other, k)


def unpack_three_kernel(index_ref, mine, other, *outs):
    rows, width = mine.shape[1], outs[0].shape[1]

    def put(row, array, k):
        for n in range(3):
            outs[n][row : row + rows, :] = array[k, :, n * width : (n + 1) * width].astype(f32)

    by_parity(index_ref[0], mine, other, put)


def unpack_joined_kernel(hidden, index_ref, mine, other, *refs):
    outs, spread = refs[:4], refs[4]
    rows, width = mine.shape[1], outs[0].shape[1]
    spans = ((0, width), (width, width + hidden), (width + hidden, width + 2 * hidden))
    base = width + 2 * hidden

    def put(row, array, k):
        for out, (first, last) in zip(outs[:3], spans):
            out[row : row + rows, :] = array[k, :, first:last].astype(f32)
        spread[row : row + rows, :] = array[k, :, base:].astype(f32)

    by_parity(index_ref[0], mine, other, put)
    tall = outs[3].shape[0]
    for there, (col_there, col_here), here, size in down_pieces(spread.shape[0], tall, width):
        outs[3][there : there + size, col_there : col_there + LANE] = spread[
            here : here + size, col_here : col_here + LANE
        ]


def unpack(kernel, index, mine, other, shapes, scratch, name):
    vmem = pl.BlockSpec(memory_space=pltpu.VMEM)
    return pl.pallas_call(
        kernel,
        out_shape=tuple(jax.ShapeDtypeStruct(shape, f32) for shape in shapes),
        in_specs=[pl.BlockSpec(memory_space=pltpu.SMEM), vmem, vmem],
        scratch_shapes=scratch,
        compiler_params=pltpu.CompilerParams(vmem_limit_bytes=VMEM_CAP),
        cost_estimate=LIGHT,
        name=name,
    )(index, mine, other)


def feed(index, upper, lower, tokens, attended, cotangent, gain):
    count = len(upper)
    rows, width = tokens.shape
    full_upper = (upper[0].shape[0] * count, upper[0].shape[1])
    full_lower = (lower[0].shape[0] * count, width)
    hidden = full_lower[0]
    columns = width + 3 * hidden
    vmem = pl.BlockSpec(memory_space=pltpu.VMEM)
    anywhere = pl.BlockSpec(memory_space=pl.ANY)
    tile = 512
    return pl.pallas_call(
        functools.partial(feed_kernel, count),
        out_shape=(
            jax.ShapeDtypeStruct((rows, width), bf16),
            jax.ShapeDtypeStruct((rows, width), bf16),
            jax.ShapeDtypeStruct((rows, width), f32),
            jax.ShapeDtypeStruct((1, width), f32),
            *[jax.ShapeDtypeStruct((2, count // 2, width // count, columns // 2), bf16)] * 2,
        ),
        in_specs=[pl.BlockSpec(memory_space=pltpu.SMEM)]
        + [anywhere] * (2 * count)
        + [vmem] * (3 + len(cotangent)),
        out_specs=(vmem,) * 4 + (anywhere,) * 2,
        scratch_shapes=[
            pltpu.VMEM(full_upper, bf16),
            pltpu.VMEM(full_lower, bf16),
            pltpu.VMEM((width, columns), bf16),
            pltpu.VMEM((rows, width), bf16),
            pltpu.VMEM((rows, width), f32),
            pltpu.VMEM((rows, width), bf16),
            pltpu.VMEM((rows, width), f32),
            pltpu.VMEM((rows, width), f32),
            pltpu.VMEM((rows, tile), bf16),
            pltpu.VMEM((rows, tile), bf16),
            pltpu.VMEM((rows, tile), bf16),
            pltpu.SemaphoreType.DMA((count,)),
            pltpu.SemaphoreType.DMA((count,)),
            pltpu.SemaphoreType.DMA(((2 * hidden // tile + 4) * count,)),
        ],
        compiler_params=pltpu.CompilerParams(vmem_limit_bytes=VMEM_CAP),
        cost_estimate=LIGHT,
        name="feed",
    )(index, *upper, *lower, tokens, attended, gain.reshape(1, width), *cotangent)


def bits_of(count):
    bits = count.bit_length() - 1
    assert 1 << bits == count
    return bits


def swap(value, axis, bit):
    count = lax.axis_size(axis)
    return lax.ppermute(value, axis, [(i, i ^ (1 << bit)) for i in range(count)])


def ordered(mine, other, index, bit, axis=0):
    upper = ((index >> bit) & 1) == 1
    return jnp.concatenate(
        [jnp.where(upper, other, mine), jnp.where(upper, mine, other)], axis=axis
    )


def gather_small(value, axis):
    index = lax.axis_index(axis)
    value = value[None]
    for bit in range(bits_of(lax.axis_size(axis))):
        value = ordered(value, swap(value, axis, bit), index, bit)
    return value


def first_swap(shard, axis):
    bit = bits_of(lax.axis_size(axis)) - 1
    return [(0, shard), (1 << bit, swap(shard, axis, bit))]


def other_swaps(parts, axis):
    for bit in reversed(range(bits_of(lax.axis_size(axis)) - 1)):
        parts = parts + [(j | (1 << bit), swap(part, axis, bit)) for j, part in parts]
    return [part for _, part in sorted(parts, key=lambda pair: pair[0])]


def after(anchor, part):
    j, array = part
    anchor, array = lax.optimization_barrier((anchor, array))
    return anchor, (j, array)


def add_low(left, right):
    return (left.astype(f32) + right.astype(f32)).astype(bf16)


def piece(value, index, dim=0):
    return lax.dynamic_index_in_dim(value, index, dim, keepdims=False)


def scatter_step(value, axis, bit, dim):
    own = (lax.axis_index(axis) >> bit) & 1
    other = swap(piece(value, 1 - own, dim), axis, bit)
    return add_low(piece(value, own, dim), other)


def rest_sum(value, axis):
    count = lax.axis_size(axis)
    index = lax.axis_index(axis)
    mine = index // 2
    total = piece(value, mine).astype(f32)
    for j in range(1, count // 2):
        pairs = [(i, ((i // 2) ^ j) * 2 + i % 2) for i in range(count)]
        total = total + lax.ppermute(piece(value, mine ^ j), axis, pairs).astype(f32)
    return total.astype(bf16)


def rest_gather(value, axis):
    count = lax.axis_size(axis)
    index = lax.axis_index(axis)
    whole = jnp.zeros((count // 2,) + value.shape, value.dtype)
    for j in range(count // 2):
        part = value
        if j:
            pairs = [(i, ((i // 2) ^ j) * 2 + i % 2) for i in range(count)]
            part = lax.ppermute(value, axis, pairs)
        whole = lax.dynamic_update_index_in_dim(whole, part, (index // 2) ^ j, 0)
    return whole


def fsdp_step(keep, send, bit):
    return add_low(keep, swap(send, "fsdp", bit))


def split_bit(value):
    value = value.reshape((value.shape[0] // 2, 2) + value.shape[1:])
    return value[:, 0], value[:, 1]


def parity_step(value, dim):
    count = lax.axis_size("ctx")
    shape = value.shape
    value = value.reshape(shape[:dim] + (count // 2, 2, shape[dim] // count) + shape[dim + 1 :])
    return scatter_step(value, "ctx", 0, dim + 1)


def rest_of_chain(total):
    total = yield rest_sum(total, "ctx")
    total = yield rest_gather(total, "ctx")
    yield (total, swap(total, "ctx", 0))


def single_chain(keep, send):
    bits = bits_of(lax.axis_size("fsdp"))
    total = yield fsdp_step(keep, send, 0)
    for bit in range(1, bits):
        keep, send = split_bit(total)
        total = yield fsdp_step(keep, send, bit)
    total = yield parity_step(total[0], 0)
    yield from rest_of_chain(total)


def double_chain(keep, send):
    bits = bits_of(lax.axis_size("fsdp"))
    other = swap(send, "fsdp", 0)
    left, right = yield (add_low(keep[0], other[0]), add_low(keep[1], other[1]))
    for bit in range(bits):
        if bit < bits - 1:
            left = fsdp_step(*split_bit(left), bit + 1)
        else:
            left = parity_step(left[0], 0)
        if bit == 0:
            right = parity_step(right, 1)
        else:
            right = fsdp_step(*split_bit(right), bit)
        left, right = yield (left, right)
    joined = jnp.concatenate([left, right[0]], axis=-1)
    yield from rest_of_chain(joined)


class Chain:
    def __init__(self, steps):
        self.steps = steps
        self.value = next(steps)

    def advance(self, value):
        self.value = self.steps.send(value)

    def finish(self):
        while True:
            try:
                self.advance(self.value)
            except StopIteration:
                return self.value


def gate(anchor, *chains):
    joined = lax.optimization_barrier((anchor,) + tuple(chain.value for chain in chains))
    for chain, value in zip(chains, joined[1:]):
        chain.advance(value)
    return joined[0]


def reduce_small(value, chain, joined, finish):
    fsdp_bits = bits_of(lax.axis_size("fsdp"))
    count = lax.axis_size("ctx")
    rows, width = value.shape
    value = value.reshape(2, count // 2, 2 * rows // (2 * count), width)
    value = gate(scatter_step(value, "fsdp", 0, 0), chain)
    value = gate(rest_sum(value, "ctx"), chain)
    value = add_low(value, swap(value, "ctx", 0))
    for bit in range(1, fsdp_bits):
        value = add_low(value, swap(value, "fsdp", bit))
    value, pieces = gate((value, joined.finish()), chain)
    done = finish(*pieces)
    whole = rest_gather(value, "ctx")
    whole = whole.reshape((rows // 2, width))
    whole, chain.value, done = lax.optimization_barrier((whole, chain.value, done))
    return ordered(whole, swap(whole, "fsdp", 0), lax.axis_index("fsdp"), 0), done


def local(
    byte_ids,
    doc_ids,
    rel_bucket,
    table,
    conv_w,
    score_w,
    gain_one,
    gain_two,
    rel_bias,
    query_master,
    key_master,
    value_master,
    out_master,
    gate_master,
    up_master,
    down_master,
    out_cotangent,
):
    ctx_count = lax.axis_size("ctx")
    ctx_index = lax.axis_index("ctx")
    seq_count, byte_count = byte_ids.shape
    total_bytes = byte_count * ctx_count
    width = table.shape[1]
    vocab = table.shape[0]
    hidden_width = gate_master.shape[1]
    levels, heads = rel_bias.shape
    share = ctx_count // seq_count
    assert share * seq_count == ctx_count and byte_count == 2 * BLK
    seq = ctx_index // share
    part = ctx_index % share
    near = [seq ^ slot for slot in range(seq_count)]
    lead = jnp.stack([share * other + part for other in near]).astype(jnp.int32)
    rows = seq_count * BLK

    qkv_low, down_low, ogu_low = pack(
        [[query_master, key_master, value_master], [down_master], [out_master, gate_master, up_master]]
    )
    both = jnp.stack([byte_ids, doc_ids], axis=1)
    both = gather_small(both, "ctx")
    both, qkv_low, down_low = lax.optimization_barrier((both, qkv_low, down_low))
    qkv_parts = first_swap(qkv_low, "fsdp")
    shard = lax.axis_index("fsdp")[None]
    shards = lax.axis_size("fsdp")

    def to_owner(block, slot):
        if slot == 0:
            return block
        pairs = []
        for c in range(ctx_count):
            pairs.append((c, ((c // share) ^ slot) * share + c % share))
        return lax.ppermute(block, "ctx", pairs)

    score_row = score_w.reshape(1, width)
    gain_row = gain_one.reshape(1, width)
    seq_row = seq[None]
    tokens, norm_one, norm_own, tokens_own, conv, mix, phases, known, barred = byte_forward(
        seq_row, lead, both, table, conv_w, score_row, gain_row, total_bytes
    )
    down_parts = first_swap(down_low, "fsdp")
    docs = piece(both[:, :, 1], seq, 1)
    low, high, buckets, rel = attention_tables(
        docs[:, 0], docs[:, 2 * BLK - 2], rel_bucket, rel_bias, lead
    )
    blocks = [to_owner(piece(out_cotangent, near[s], 1), s) for s in range(seq_count)]
    tokens, buckets, rel = lax.optimization_barrier((tokens, buckets, rel))
    tiles = make_tiles(buckets, rel)
    norm_one, crossed, down_crossed, blocks, tiles, ogu_low = lax.optimization_barrier(
        (norm_one, qkv_parts[1][1], down_parts[1][1], blocks, tiles, ogu_low)
    )
    qkv_parts[1] = (qkv_parts[1][0], crossed)
    down_parts[1] = (down_parts[1][0], down_crossed)
    qkv_parts = other_swaps(qkv_parts, "fsdp")
    queries, keys, values, qkv = project(shard, qkv_parts, norm_one, norm_own)
    ogu_parts = first_swap(ogu_low, "fsdp")
    down_parts = other_swaps(down_parts, "fsdp")
    attended, attended_low, log_total = attend(
        lead, low, high, queries, keys, values, known, barred, tiles
    )

    attended_low, ogu_parts[1] = after(attended_low, ogu_parts[1])
    output, d_attended, d_resid, grad_gain_two, *grads = feed(
        shard,
        other_swaps(ogu_parts, "fsdp"),
        down_parts,
        tokens_own,
        attended_low,
        blocks,
        gain_two,
    )
    chain = Chain(double_chain(*grads))
    d_attended = gate(d_attended, chain)

    output = output.reshape(seq_count, BLK, width)
    arrived = [to_owner(output[s], s) for s in range(seq_count)]

    halves = []
    for group in range(GROUPS):
        if group:
            d_attended, arrived = gate((d_attended, arrived), chain)
            arrived = jnp.stack(arrived)
            output = jnp.stack([piece(arrived, seq ^ s) for s in range(seq_count)], axis=1)
        *grads, d_bias = attend_back(
            group,
            levels,
            lead,
            low,
            high,
            queries,
            keys,
            values,
            d_attended,
            attended,
            log_total,
            tiles,
            known,
            barred,
            buckets,
        )
        halves.append((grads, d_bias))
        d_attended, _ = lax.optimization_barrier((d_attended, grads[0]))
    d_bias = jnp.concatenate([half[1] for half in halves], axis=0)
    norm_own, halves = gate((norm_own, [half[0] for half in halves]), chain)
    keep, send, d_norm_one = project_back(shard, shards, lead, norm_one, norm_own, qkv, halves)
    qkv_chain = Chain(single_chain(keep, send))
    d_norm_one = gate(d_norm_one, qkv_chain, chain)

    vocab_rows = -(-vocab // 16) * 16
    d_resid = d_resid.reshape(seq_count, BLK, width)
    small = byte_backward(
        lead,
        phases,
        tokens,
        d_norm_one,
        d_resid,
        conv,
        mix,
        table,
        vocab_rows,
        conv_w,
        score_row,
        gain_row,
        total_bytes,
    )
    bias_grad = jnp.transpose(d_bias[:, : heads // GROUPS].reshape(heads, levels)).reshape(1, levels * heads)
    bias_grad = jnp.pad(bias_grad, ((0, 0), (0, width - levels * heads)))
    small = jnp.concatenate([small[: vocab_rows + 6], grad_gain_two, bias_grad], axis=0)
    small = jnp.pad(small, ((0, -small.shape[0] % (8 * ctx_count)), (0, 0))).astype(bf16)
    small = gate(small, qkv_chain, chain)
    shard_rows, tall = query_master.shape[0], down_master.shape[0]
    ctx_row = ctx_index[None]

    def finish(mine, other):
        return unpack(
            functools.partial(unpack_joined_kernel, hidden_width),
            ctx_row,
            mine,
            other,
            [(shard_rows, width)] + [(shard_rows, hidden_width)] * 2 + [(tall, width)],
            [pltpu.VMEM((shard_rows, hidden_width), f32)],
            "unpack_joined",
        )

    small, ffn_grads = reduce_small(small, qkv_chain, chain, finish)
    small = small.astype(f32)
    qkv_grads = unpack(
        unpack_three_kernel,
        ctx_row,
        *qkv_chain.finish(),
        [(shard_rows, width)] * 3,
        [],
        "unpack_three",
    )
    top = vocab_rows
    return (
        output,
        small[:vocab],
        small[top : top + 4],
        small[top + 4],
        small[top + 5],
        small[top + 6],
        small[top + 7, : levels * heads].reshape(levels, heads),
        *qkv_grads,
        *ffn_grads,
    )


def solution(mesh):
    placed = (
        P("fsdp", "ctx"),
        P("fsdp", "ctx"),
        P(),
        P(),
        P(),
        P(),
        P(),
        P(),
        P(),
        P("fsdp", None),
        P("fsdp", None),
        P("fsdp", None),
        P("fsdp", None),
        P("fsdp", None),
        P("fsdp", None),
        P("fsdp", None),
        P("ctx", "fsdp", None),
    )
    return jax.shard_map(
        local,
        mesh=mesh,
        in_specs=placed,
        out_specs=(
            P("ctx", "fsdp", None),
            P(),
            P(),
            P(),
            P(),
            P(),
            P(),
            P("fsdp", None),
            P("fsdp", None),
            P("fsdp", None),
            P("fsdp", None),
            P("fsdp", None),
            P("fsdp", None),
            P("fsdp", None),
        ),
        check_vma=False,
    )
```
